32 devices in a mesh: dp: 4 (over x, core), row: 2 (over y), col: 4 (over z).
Axes of the slice: x: 2, y: 2, z: 4, core: 2. Of those that a mesh axis runs over, the one named last changes fastest.
Arguments:
- tokens: bfloat16 [4096, 2048], P(('dp', 'row'), 'col'), may hold values from -6 to 6
- parent: int32 [4, 4], P('dp'), may hold values from -1 to 1, as said below
- depth: int32 [4, 4], P('dp'), may hold values from 0 to 2, as said below
- w_qkv: float32 [2048, 6144], P('row', 'col'), may hold values from -0.125 to 0.125
- b_qkv: float32 [6144], P('col'), may hold values from -3 to 3
- w_out: float32 [2048, 2048], P('col', 'row'), may hold values from -0.75 to 0.75
- w_up: float32 [2048, 8192], P('row', 'col'), may hold values from -0.125 to 0.125
- b_up: float32 [8192], P('col'), may hold values from -3 to 3
- w_down: float32 [8192, 2048], P('col', 'row'), may hold values from -0.0625 to 0.0625
- b_res: float32 [2048], P('col'), may hold values from -3 to 3
- ln_gain: float32 [2048], replicated, may hold values from 0.5 to 1.5
- ln_bias: float32 [2048], replicated, may hold values from -2 to 2
- cotangent: bfloat16 [4096, 2048], P(('dp', 'row'), 'col'), may hold values from -6 to 6
Outputs:
- output: bfloat16 [4096, 2048], P(('dp', 'row'), 'col')
- tokens_grad: float32 [4096, 2048], P(('dp', 'row'), 'col')
- w_qkv_grad: float32 [2048, 6144], P('row', 'col')
- b_qkv_grad: float32 [6144], P('col')
- w_out_grad: float32 [2048, 2048], P('col', 'row')
- w_up_grad: float32 [2048, 8192], P('row', 'col')
- b_up_grad: float32 [8192], P('col')
- w_down_grad: float32 [8192, 2048], P('col', 'row')
- b_res_grad: float32 [2048], P('col')
- ln_gain_grad: float32 [2048], replicated
- ln_bias_grad: float32 [2048], replicated
The draws below stay inside these ranges and needn't reach their ends.
Inputs may be any that keep to these rules, and one draw needn't show every extreme that they name: In every tree segments 0 to 1 form a trunk: segment 0 has parent -1 and each other trunk segment j has parent j - 1. Every later segment has a trunk segment as parent, and the last segment's parent is trunk segment 4 // 2 - 1. Segment 0 has depth 0 and every other segment one more than its parent.
All inputs are finite; a program needn't handle non-finite values.
Results may differ from the reference program's by a relative error of at most 0.018.
Values may be sent and summed in bfloat16 or wider, within the bound.
No kernel may reach another device: no remote copies, remote signals or barrier semaphores. Data moves between devices by JAX's collectives and lax.ppermute only.
A program may use at most 256 MiB of HBM per device.

```python
import math
import jax
import jax.numpy as jnp
from jax import lax

D = 2048
H = 32
FF = 8192
HD = 64
ROT = 32
SEG = 256
TREE_TOK = 1024
TREE_SEGS = 4
TREES = 4
TOKENS = 4096


def tree_tables(key):
    base_key = jax.random.fold_in(key, 17)
    seg_count = TREE_SEGS
    trunk_len = seg_count // 2
    labels = jnp.arange(seg_count, dtype=jnp.int32)
    picks = jax.random.randint(base_key, (TREES, seg_count), 0, trunk_len)
    branch_parent = jnp.where(labels[None, :] == seg_count - 1, trunk_len - 1, picks)
    trunk_parent = jnp.broadcast_to(labels[None, :] - 1, (TREES, seg_count))
    parents = jnp.where(labels[None, :] < trunk_len, trunk_parent, branch_parent).astype(jnp.int32)

    def deepen(rounds, depths):
        above = jnp.take_along_axis(depths, jnp.maximum(parents, 0), axis=1)
        return jnp.where(parents < 0, 0, above + 1).astype(jnp.int32)
    depths = lax.fori_loop(0, seg_count, deepen, jnp.zeros((TREES, seg_count), jnp.int32))
    return (parents, depths)


def draw_parent(key, part):
    return tree_tables(key)[0]


def draw_depth(key, part):
    return tree_tables(key)[1]


def block_levels(own_key, extent, split, low, largest):
    factor_of, own = 1.0, jax.random.fold_in(own_key, 6)
    for axis_at, blocks in split:
        draws = jnp.exp(jax.random.uniform(jax.random.fold_in(own, axis_at), (blocks,), jnp.float32, low / len(split), largest / len(split)))
        factor_of = factor_of * jnp.repeat(draws, extent[axis_at] // blocks).reshape([-1 if axis == axis_at else 1 for axis in range(len(extent))])
    return factor_of


def noise(key, dims, spread, most, split=(), held_as=jnp.bfloat16):
    drawn = spread * jax.random.normal(key, dims, jnp.float32)
    if split:
        drawn = drawn * block_levels(key, dims, split, -0.22, 0.18)
    return jnp.clip(drawn, -most, most).astype(held_as)


def setup_inputs(seed: int = 0) -> dict:
    streams_of = jax.random.split(jax.random.key(seed), 14)
    tokens = noise(streams_of[0], (TOKENS, D), 1.0, 6.0, ((0, 8), (1, 4)))
    parent = draw_parent(jax.random.fold_in(streams_of[13], 71), 0)
    depth = draw_depth(jax.random.fold_in(streams_of[13], 71), 0)
    w_qkv = noise(streams_of[3], (D, 3 * D), D ** -0.5, 0.125, ((0, 2), (1, 4)), jnp.float32)
    b_qkv = noise(streams_of[4], (3 * D,), 0.5, 3.0, ((0, 4),), jnp.float32)
    w_out = noise(streams_of[5], (D, D), (D // 32) ** -0.5, 0.75, ((0, 4), (1, 2)), jnp.float32)
    w_up = noise(streams_of[6], (D, FF), D ** -0.5, 0.125, ((0, 2), (1, 4)), jnp.float32)
    b_up = noise(streams_of[7], (FF,), 0.5, 3.0, ((0, 4),), jnp.float32)
    w_down = noise(streams_of[8], (FF, D), FF ** -0.5, 0.0625, ((0, 4), (1, 2)), jnp.float32)
    b_res = noise(streams_of[9], (D,), 0.5, 3.0, ((0, 4),), jnp.float32)
    ln_gain = jnp.clip(1.0 + 0.1 * jax.random.normal(streams_of[10], (D,), jnp.float32), 0.5, 1.5)
    ln_bias = noise(streams_of[11], (D,), 0.3, 2.0, (), jnp.float32)
    cotangent = noise(streams_of[12], (TOKENS, D), 1.0, 6.0, ((0, 8), (1, 4)))
    return dict(tokens=tokens, parent=parent, depth=depth, w_qkv=w_qkv, b_qkv=b_qkv, w_out=w_out, w_up=w_up, b_up=b_up, w_down=w_down, b_res=b_res, ln_gain=ln_gain, ln_bias=ln_bias, cotangent=cotangent)


norm_epsilon = 1e-05
masked_fill = -1e+30
rotary_base = 10000.0

@jax.custom_vjp
def low(v):
    return lax.optimization_barrier(v.astype(jnp.bfloat16)).astype(jnp.float32)

@jax.custom_vjp
def low_back(v):
    return v

def low_keep(v):
    return (low(v), None)

def low_pass(kept, grad):
    return (grad,)

def back_keep(v):
    return (v, None)

def back_low(kept, grad):
    return (low(grad),)
low.defvjp(low_keep, low_pass)
low_back.defvjp(back_keep, back_low)

def matmul(left, right):
    return jnp.dot(left, right, precision=lax.Precision.HIGHEST, preferred_element_type=jnp.float32)

def ancestry(parent_row):
    seg_count = parent_row.shape[0]
    labels = jnp.arange(seg_count, dtype=jnp.int32)
    identity = jnp.eye(seg_count, dtype=jnp.float32)
    parent_hot = (parent_row[:, None] == labels[None, :]).astype(jnp.float32)

    def extend(rounds, reachable):
        return jnp.minimum(identity + matmul(parent_hot, reachable), 1.0)
    return lax.fori_loop(0, seg_count, extend, identity)

def rotate(values, cosines, sines):
    half_rot = ROT // 2
    former = values[..., :half_rot]
    latter = values[..., half_rot:ROT]
    return jnp.concatenate([former * cosines - latter * sines, latter * cosines + former * sines, values[..., ROT:]], axis=-1)

def angles_of(positions):
    frequency = jnp.exp(-math.log(rotary_base) * 2.0 * jnp.arange(ROT // 2, dtype=jnp.float32) / ROT)
    phase_angle = positions[:, None] * frequency[None, :]
    return (jnp.cos(phase_angle)[:, None, :], jnp.sin(phase_angle)[:, None, :])

def tree_mask(reachable, query_index, key_index):
    query_seg = query_index // SEG
    key_seg = key_index // SEG
    linked = reachable[query_seg][:, key_seg] > 0.5
    return linked & ((query_seg[:, None] != key_seg[None, :]) | (query_index[:, None] >= key_index[None, :]))

def attend_block(query_block, block_start, key_rows, value_rows, reachable):
    block_len = query_block.shape[0]
    query_index = block_start + jnp.arange(block_len, dtype=jnp.int32)
    key_index = jnp.arange(key_rows.shape[0], dtype=jnp.int32)
    allowed = tree_mask(reachable, query_index, key_index)
    scores = low_back(jnp.einsum('qhe,khe->hqk', query_block, key_rows, precision=lax.Precision.HIGHEST) * HD ** (-0.5))
    scores = jnp.where(allowed[None], scores, masked_fill)
    softmaxed = low(jax.nn.softmax(scores, axis=-1))
    return jnp.einsum('hqk,khe->qhe', softmaxed, value_rows, precision=lax.Precision.HIGHEST)

def tree_attention(queries, key_rows, value_rows, reachable):
    block_len = math.gcd(TREE_TOK, 512)
    blocks = queries.reshape(TREE_TOK // block_len, block_len, H, HD)
    starts = jnp.arange(TREE_TOK // block_len, dtype=jnp.int32) * block_len

    def one_block(block_item):
        return attend_block(block_item[0], block_item[1], key_rows, value_rows, reachable)
    outcome = lax.map(jax.checkpoint(one_block), (blocks, starts))
    return outcome.reshape(TREE_TOK, H * HD)

def forward(tokens, w_qkv, b_qkv, w_out, w_up, b_up, w_down, b_res, ln_gain, ln_bias, reachable, cosines, sines):
    centred = tokens - lax.optimization_barrier(jnp.mean(tokens, axis=1, keepdims=True))
    normal = centred * lax.rsqrt(lax.optimization_barrier(jnp.mean(centred * centred, axis=1, keepdims=True)) + norm_epsilon)
    normed = low(normal * ln_gain + ln_bias)
    mixed = low_back(matmul(normed, low(w_qkv)) + b_qkv).reshape(TOKENS, H, 3, HD)
    queries = low(rotate(mixed[:, :, 0], cosines, sines))
    key_rows = low(rotate(mixed[:, :, 1], cosines, sines))
    value_rows = low(mixed[:, :, 2])

    def per_tree(tree_item):
        return tree_attention(tree_item[0], tree_item[1], tree_item[2], tree_item[3])
    attended = lax.map(per_tree, (queries.reshape(TREES, TREE_TOK, H, HD), key_rows.reshape(TREES, TREE_TOK, H, HD), value_rows.reshape(TREES, TREE_TOK, H, HD), reachable))
    attended = low(low_back(attended.reshape(TOKENS, D)))
    hidden_up = low_back(matmul(normed, low(w_up)) + b_up)
    activated = low(jax.nn.gelu(hidden_up, approximate=True))
    return tokens + (matmul(attended, low(w_out)) + matmul(activated, low(w_down)) + b_res)

def reference(tokens, parent, depth, w_qkv, b_qkv, w_out, w_up, b_up, w_down, b_res, ln_gain, ln_bias, cotangent):
    reachable = jax.vmap(ancestry)(parent)
    token_index = jnp.arange(TOKENS, dtype=jnp.int32)
    local_index = token_index % TREE_TOK
    tree_of = token_index // TREE_TOK
    levels = depth[tree_of, local_index // SEG]
    positions = (levels * SEG + local_index % SEG).astype(jnp.float32)
    cosines, sines = angles_of(positions)

    def wrapped(*inputs):
        return forward(*inputs, reachable, cosines, sines)
    primals = (tokens.astype(jnp.float32), w_qkv, b_qkv, w_out, w_up, b_up, w_down, b_res, ln_gain, ln_bias)
    output, pullback = jax.vjp(wrapped, *primals)
    gradients = pullback(cotangent.astype(jnp.float32))
    return (output.astype(jnp.bfloat16), gradients[0], gradients[1], gradients[2], gradients[3], gradients[4], gradients[5], gradients[6], gradients[7], gradients[8], gradients[9])
```

```python
import functools
import math

import jax
import jax.numpy as jnp
from jax import lax
from jax.experimental import pallas as pl
from jax.experimental.pallas import tpu as pltpu
from jax.sharding import PartitionSpec as P

HD = 64
ROT = 32
SEG = 256


norm_epsilon = 1e-05
masked_fill = -1e30
rotary_base = 10000.0


def precise_dot(left, right):
    return jnp.dot(left, right, precision=lax.Precision.HIGHEST, preferred_element_type=jnp.float32)


def ancestry(parent_row):
    seg_count = parent_row.shape[0]
    labels = jnp.arange(seg_count, dtype=jnp.int32)
    identity = jnp.eye(seg_count, dtype=jnp.float32)
    parent_hot = (parent_row[:, None] == labels[None, :]).astype(jnp.float32)

    def extend(rounds, reachable):
        return jnp.minimum(identity + precise_dot(parent_hot, reachable), 1.0)

    return lax.fori_loop(0, seg_count, extend, identity)


def rotate(values, cosines, sines):
    half_rot = ROT // 2
    former = values[..., :half_rot]
    latter = values[..., half_rot:ROT]
    return jnp.concatenate(
        [former * cosines - latter * sines, latter * cosines + former * sines, values[..., ROT:]],
        axis=-1,
    )


def angles_of(positions):
    frequency = jnp.exp(
        -math.log(rotary_base) * 2.0 * jnp.arange(ROT // 2, dtype=jnp.float32) / ROT
    )
    phase_angle = positions[:, None] * frequency[None, :]
    return (jnp.cos(phase_angle)[:, None, :], jnp.sin(phase_angle)[:, None, :])


def reorder_rows(gradient, row_count, dp_count):
    leading = gradient.shape[0]
    blocked = gradient.reshape(
        row_count, dp_count, leading // (row_count * dp_count), gradient.shape[1]
    )
    return jnp.transpose(blocked, (1, 0, 2, 3)).reshape(leading, gradient.shape[1])


def reorder_cols(gradient, row_count, dp_count):
    trailing = gradient.shape[1]
    blocked = gradient.reshape(
        gradient.shape[0], row_count, dp_count, trailing // (row_count * dp_count)
    )
    return jnp.transpose(blocked, (0, 2, 1, 3)).reshape(gradient.shape[0], trailing)


def general_device(
    tokens,
    parent,
    depth,
    w_qkv,
    b_qkv,
    w_out,
    w_up,
    b_up,
    w_down,
    b_res,
    ln_gain,
    ln_bias,
    cotangent,
):
    tok_rows = tokens.shape[0]
    col_width = tokens.shape[1]
    row_count = lax.axis_size("row")
    dp_count = lax.axis_size("dp")
    row_start = lax.axis_index("row") * tok_rows
    local_heads = w_out.shape[0] // HD
    seg_count = parent.shape[1]
    labels = jnp.arange(seg_count, dtype=jnp.int32)
    reachable = ancestry(parent[0])
    query_index = row_start + jnp.arange(tok_rows, dtype=jnp.int32)
    query_seg = query_index // SEG
    query_hot = (query_seg[:, None] == labels[None, :]).astype(jnp.float32)
    query_reach = precise_dot(query_hot, reachable)
    levels = precise_dot(query_hot, depth[0].astype(jnp.float32)[:, None])[:, 0]
    positions = levels * SEG + (query_index % SEG).astype(jnp.float32)
    cosines, sines = angles_of(positions)
    score_scale = HD ** (-0.5)

    def permit(key_len):
        key_index = jnp.arange(key_len, dtype=jnp.int32)
        key_seg = key_index // SEG
        key_hot = (key_seg[:, None] == labels[None, :]).astype(jnp.float32)
        linked = precise_dot(query_reach, key_hot.T) > 0.5
        return linked & (
            (query_seg[:, None] != key_seg[None, :]) | (query_index[:, None] >= key_index[None, :])
        )

    whole = lax.all_gather(tokens, "col", axis=1, tiled=True).astype(jnp.float32)
    centred = whole - jnp.mean(whole, axis=1, keepdims=True)
    inv_scale = lax.rsqrt(jnp.mean(centred * centred, axis=1, keepdims=True) + norm_epsilon)
    normal = centred * inv_scale
    normed = (normal * ln_gain + ln_bias).astype(jnp.bfloat16)
    qkv_full, up_full, out_full, down_full = (
        lax.all_gather(w_qkv.astype(jnp.bfloat16), "row", axis=0, tiled=True),
        lax.all_gather(w_up.astype(jnp.bfloat16), "row", axis=0, tiled=True),
        lax.all_gather(w_out.astype(jnp.bfloat16), "row", axis=1, tiled=True),
        lax.all_gather(w_down.astype(jnp.bfloat16), "row", axis=1, tiled=True),
    )
    mixed = (jnp.dot(normed, qkv_full, preferred_element_type=jnp.float32) + b_qkv).reshape(
        tok_rows, local_heads, 3, HD
    )

    def rotate_pair(query_pre, key_pre):
        return (rotate(query_pre, cosines, sines), rotate(key_pre, cosines, sines))

    rotated, rotate_back = jax.vjp(rotate_pair, mixed[:, :, 0], mixed[:, :, 1])
    queries = rotated[0].astype(jnp.bfloat16)
    key_rows = rotated[1].astype(jnp.bfloat16)
    value_rows = mixed[:, :, 2].astype(jnp.bfloat16)
    key_flat = key_rows.reshape(tok_rows, local_heads * HD)
    value_flat = value_rows.reshape(tok_rows, local_heads * HD)

    def scores_for(key_part):
        raw_scores = (
            jnp.einsum("qhe,khe->hqk", queries, key_part, preferred_element_type=jnp.float32)
            * score_scale
        )
        allowed = permit(key_part.shape[0])
        return (jnp.where(allowed[None], raw_scores, masked_fill), allowed)

    pieces = (
        lax.all_gather(key_flat, "row", axis=0, tiled=True),
        lax.all_gather(value_flat, "row", axis=0, tiled=True),
    )
    running_top = jnp.full((local_heads, tok_rows), masked_fill, jnp.float32)
    key_len = pieces[0].shape[0]
    key_part = pieces[0].reshape(key_len, local_heads, HD)
    value_part = pieces[1].reshape(key_len, local_heads, HD)
    scores, allowed = scores_for(key_part)
    new_top = jnp.maximum(running_top, jnp.max(scores, axis=2))
    exponent = jnp.where(allowed[None], jnp.exp(scores - new_top[:, :, None]), 0.0)
    running_sum = jnp.sum(exponent, axis=2)
    weighted = jnp.einsum(
        "hqk,khe->hqe",
        exponent.astype(jnp.bfloat16),
        value_part,
        preferred_element_type=jnp.float32,
    )
    running_top, running_sum, weighted = (new_top, running_sum, weighted)
    log_total = running_top + jnp.log(running_sum)
    attn_exact = weighted / running_sum[:, :, None]
    attended = (
        jnp.transpose(attn_exact, (1, 0, 2))
        .reshape(tok_rows, local_heads * HD)
        .astype(jnp.bfloat16)
    )
    hidden_up = jnp.dot(normed, up_full, preferred_element_type=jnp.float32) + b_up
    activated, gelu_back = jax.vjp(functools.partial(jax.nn.gelu, approximate=True), hidden_up)
    activated = activated.astype(jnp.bfloat16)
    branch_terms = jnp.dot(attended, out_full, preferred_element_type=jnp.float32) + jnp.dot(
        activated, down_full, preferred_element_type=jnp.float32
    )
    branch = lax.psum_scatter(
        branch_terms.astype(jnp.bfloat16), "col", scatter_dimension=1, tiled=True
    ).astype(jnp.float32)
    output = (tokens.astype(jnp.float32) + branch + b_res).astype(jnp.bfloat16)
    grad_full = lax.all_gather(cotangent, "col", axis=1, tiled=True)
    res_bias_grad = jnp.sum(cotangent.astype(jnp.float32), axis=0)
    down_grad = jnp.einsum("tf,td->fd", activated, grad_full, preferred_element_type=jnp.float32)
    out_grad = jnp.einsum("te,td->ed", attended, grad_full, preferred_element_type=jnp.float32)
    act_grad = jnp.einsum("td,fd->tf", grad_full, down_full, preferred_element_type=jnp.float32)
    up_grad = gelu_back(act_grad)[0].astype(jnp.bfloat16)
    attn_grad = jnp.einsum(
        "td,ed->te", grad_full, out_full, preferred_element_type=jnp.float32
    ).astype(jnp.bfloat16)
    up_bias_grad = jnp.sum(up_grad.astype(jnp.float32), axis=0)
    up_weight_grad = jnp.einsum("td,tf->df", normed, up_grad, preferred_element_type=jnp.float32)
    out_heads = attn_grad.reshape(tok_rows, local_heads, HD)
    delta_sum = jnp.einsum("qhe,hqe->hq", out_heads.astype(jnp.float32), attn_exact)
    pieces = (
        lax.all_gather(key_flat, "row", axis=0, tiled=True),
        lax.all_gather(value_flat, "row", axis=0, tiled=True),
    )
    key_len = pieces[0].shape[0]
    key_part = pieces[0].reshape(key_len, local_heads, HD)
    value_part = pieces[1].reshape(key_len, local_heads, HD)
    scores, allowed = scores_for(key_part)
    softmaxed = jnp.where(allowed[None], jnp.exp(scores - log_total[:, :, None]), 0.0)
    prob_grad = jnp.einsum(
        "qhe,khe->hqk", out_heads, value_part, preferred_element_type=jnp.float32
    )
    score_grad = (softmaxed * (prob_grad - delta_sum[:, :, None])).astype(jnp.bfloat16)
    query_grad = (
        jnp.einsum("hqk,khe->qhe", score_grad, key_part, preferred_element_type=jnp.float32)
        * score_scale
    )
    key_grad = (
        jnp.einsum("hqk,qhe->khe", score_grad, queries, preferred_element_type=jnp.float32)
        * score_scale
    )
    value_grad = jnp.einsum(
        "hqk,qhe->khe",
        softmaxed.astype(jnp.bfloat16),
        out_heads,
        preferred_element_type=jnp.float32,
    )
    stacked = jnp.stack([key_grad, value_grad], axis=1).reshape(key_len, 2 * local_heads * HD)
    pair_grad = stacked
    query_grad, pair_grad = (query_grad, pair_grad)
    own_pairs = (
        lax.psum_scatter(pair_grad.astype(jnp.bfloat16), "row", scatter_dimension=0, tiled=True)
        .astype(jnp.float32)
        .reshape(tok_rows, 2, local_heads, HD)
    )
    query_pre, key_pre = rotate_back((query_grad, own_pairs[:, 0]))
    mixed_grad = (
        jnp.stack([query_pre, key_pre, own_pairs[:, 1]], axis=2)
        .reshape(tok_rows, 3 * local_heads * HD)
        .astype(jnp.bfloat16)
    )
    qkv_bias_grad = jnp.sum(mixed_grad.astype(jnp.float32), axis=0)
    qkv_weight_grad = jnp.einsum(
        "td,tc->dc", normed, mixed_grad, preferred_element_type=jnp.float32
    )
    norm_part = jnp.einsum(
        "tc,dc->td", mixed_grad, qkv_full, preferred_element_type=jnp.float32
    ) + jnp.einsum("tf,df->td", up_grad, up_full, preferred_element_type=jnp.float32)
    norm_grad = lax.psum(norm_part.astype(jnp.bfloat16), "col").astype(jnp.float32)
    gain_grad = jnp.sum(norm_grad * normal, axis=0)
    shift_grad = jnp.sum(norm_grad, axis=0)
    scaled = norm_grad * ln_gain
    mean_scaled = jnp.mean(scaled, axis=1, keepdims=True)
    mean_mixed = jnp.mean(scaled * normal, axis=1, keepdims=True)
    col_start = lax.axis_index("col") * col_width
    scaled_share = lax.dynamic_slice_in_dim(scaled, col_start, col_width, 1)
    normal_share = lax.dynamic_slice_in_dim(normal, col_start, col_width, 1)
    tokens_grad = inv_scale * (
        scaled_share - mean_scaled - normal_share * mean_mixed
    ) + cotangent.astype(jnp.float32)
    qkv_bias_grad, up_bias_grad, res_bias_grad, gain_grad, shift_grad = (
        lax.psum(qkv_bias_grad.astype(jnp.bfloat16), ("dp", "row")).astype(jnp.float32),
        lax.psum(up_bias_grad.astype(jnp.bfloat16), ("dp", "row")).astype(jnp.float32),
        lax.psum(res_bias_grad.astype(jnp.bfloat16), ("dp", "row")).astype(jnp.float32),
        lax.psum(gain_grad.astype(jnp.bfloat16), ("dp", "row")).astype(jnp.float32),
        lax.psum(shift_grad.astype(jnp.bfloat16), ("dp", "row")).astype(jnp.float32),
    )
    pieces_now = (
        lax.psum_scatter(
            reorder_rows(qkv_weight_grad, row_count, dp_count).astype(jnp.bfloat16),
            ("dp", "row"),
            scatter_dimension=0,
            tiled=True,
        ).astype(jnp.float32),
        lax.psum_scatter(
            reorder_rows(up_weight_grad, row_count, dp_count).astype(jnp.bfloat16),
            ("dp", "row"),
            scatter_dimension=0,
            tiled=True,
        ).astype(jnp.float32),
        lax.psum_scatter(
            reorder_cols(out_grad, row_count, dp_count).astype(jnp.bfloat16),
            ("dp", "row"),
            scatter_dimension=1,
            tiled=True,
        ).astype(jnp.float32),
        lax.psum_scatter(
            reorder_cols(down_grad, row_count, dp_count).astype(jnp.bfloat16),
            ("dp", "row"),
            scatter_dimension=1,
            tiled=True,
        ).astype(jnp.float32),
    )
    qkv_weight_grad, up_weight_grad, out_grad, down_grad = (
        lax.all_gather(pieces_now[0].astype(jnp.bfloat16), "dp", axis=0, tiled=True).astype(
            jnp.float32
        ),
        lax.all_gather(pieces_now[1].astype(jnp.bfloat16), "dp", axis=0, tiled=True).astype(
            jnp.float32
        ),
        lax.all_gather(pieces_now[2].astype(jnp.bfloat16), "dp", axis=1, tiled=True).astype(
            jnp.float32
        ),
        lax.all_gather(pieces_now[3].astype(jnp.bfloat16), "dp", axis=1, tiled=True).astype(
            jnp.float32
        ),
    )
    return (
        output,
        tokens_grad,
        qkv_weight_grad,
        qkv_bias_grad,
        out_grad,
        up_weight_grad,
        up_bias_grad,
        down_grad,
        res_bias_grad,
        gain_grad,
        shift_grad,
    )


SWAP_ROW = [(0, 1), (1, 0)]
SWAP_X = [(0, 2), (2, 0), (1, 3), (3, 1)]
SWAP_CORE = [(0, 1), (1, 0), (2, 3), (3, 2)]


def bf16(values):
    return values.astype(jnp.bfloat16)


def f32(values):
    return values.astype(jnp.float32)


def matmul(left, right, dims=((1,), (0,))):
    return lax.dot_general(left, right, (dims, ((), ())), preferred_element_type=jnp.float32)


def swap_row(values):
    return lax.ppermute(values, "row", SWAP_ROW)


def swap_x(values):
    return lax.ppermute(values, "dp", SWAP_X)


def swap_core(values):
    return lax.ppermute(values, "dp", SWAP_CORE)


def pick(index, first, second):
    return jnp.where(index == 0, first, second)


def pair(index, mine, theirs, axis):
    return pick(
        index,
        jnp.concatenate([mine, theirs], axis=axis),
        jnp.concatenate([theirs, mine], axis=axis),
    )


def gather_line(block, blocks, col):
    count = len(blocks)
    width = block.shape[1]
    to_right, to_left, right, left = [], [], block, block
    for hop in range(1, count):
        right = lax.ppermute(right, "col", [(at, at + 1) for at in range(hop - 1, count - 1)])
        left = lax.ppermute(left, "col", [(at, at - 1) for at in range(1, count - hop + 1)])
        to_right.append(right)
        to_left.append(left)
    slots = jnp.concatenate(to_right[::-1] + [block] + to_left, axis=1)
    return jnp.concatenate(
        [
            lax.dynamic_slice_in_dim(slots, (count - 1 - col + at) * width, width, 1)
            for at in blocks
        ],
        axis=1,
    )


def rotary_tables(positions):
    lane = jnp.arange(2 * HD, dtype=jnp.int32) % HD
    half_rot = ROT // 2
    frequency = jnp.exp(
        -math.log(rotary_base) * 2.0 * (lane % half_rot).astype(jnp.float32) / ROT
    )
    angle = positions[:, None] * frequency[None, :]
    turned = (lane < ROT)[None, :]
    sines = jnp.sin(angle)
    return (
        jnp.where(turned, jnp.cos(angle), 1.0),
        jnp.where((lane < half_rot)[None, :], -sines, 0.0),
        jnp.where(turned & (lane >= half_rot)[None, :], sines, 0.0),
    )


def turn(values, cosines, sines_low, sines_high):
    width = values.shape[1]
    half_rot = ROT // 2
    return (
        values * cosines
        + pltpu.roll(values, width - half_rot, 1) * sines_low
        + pltpu.roll(values, half_rot, 1) * sines_high
    )


def split_kernel(mixed_ref, cos_ref, low_ref, high_ref, query_ref, keyval_ref):
    cosines, low, high = cos_ref[...], low_ref[...], high_ref[...]
    rows = mixed_ref.shape[0]
    half = query_ref.shape[1]
    first = lax.broadcasted_iota(jnp.int32, (rows, 2 * HD), 1) < HD
    scale = HD ** (-0.5)
    for at in range(half // (2 * HD)):
        tiles = [mixed_ref[:, (3 * at + part) * 2 * HD : (3 * at + part + 1) * 2 * HD] for part in range(3)]
        query = jnp.where(first, tiles[0], tiles[1])
        key = jnp.where(first, pltpu.roll(tiles[0], HD, 1), pltpu.roll(tiles[2], HD, 1))
        value = jnp.where(first, tiles[1], tiles[2])
        here = slice(at * 2 * HD, (at + 1) * 2 * HD)
        query_ref[:, here] = bf16(f32(bf16(turn(query, cosines, low, high))) * scale)
        keyval_ref[:, here] = bf16(turn(key, cosines, low, high))
        keyval_ref[:, half + at * 2 * HD : half + (at + 1) * 2 * HD] = bf16(value)


def join_kernel(row_ref, dq_ref, dkv_ref, sent_ref, cos_ref, low_ref, high_ref, out_ref):
    cosines, low, high = cos_ref[...], -low_ref[...], -high_ref[...]
    rows = dq_ref.shape[0]
    half = dq_ref.shape[1]
    first = lax.broadcasted_iota(jnp.int32, (rows, 2 * HD), 1) < HD
    owner = row_ref[0] == 0
    for at in range(half // (2 * HD)):
        here = slice(at * 2 * HD, (at + 1) * 2 * HD)
        there = slice(half + at * 2 * HD, half + (at + 1) * 2 * HD)
        query = turn(dq_ref[:, here], cosines, low, high)
        key = dkv_ref[:, here] + jnp.where(owner, f32(sent_ref[:, here]), 0.0)
        value = dkv_ref[:, there] + jnp.where(owner, f32(sent_ref[:, there]), 0.0)
        key = pltpu.roll(turn(key, cosines, low, high), HD, 1)
        tiles = (jnp.where(first, query, key), jnp.where(first, value, query), jnp.where(first, key, value))
        for part in range(3):
            out_ref[:, (3 * at + part) * 2 * HD : (3 * at + part + 1) * 2 * HD] = bf16(tiles[part])


def tree_kernel(
    parent_ref, row_ref, query_ref, keyval_ref, trunk_ref, grad_ref,
    out_ref, dq_ref, dkv_ref, dtrunk_ref,
    keys, values, dkeys, dvalues,
):
    tree = pl.program_id(0)
    row = row_ref[0]
    rows, half = query_ref.shape
    trunk_len = trunk_ref.shape[0]
    segs = rows // SEG
    trunk_segs = trunk_len // SEG
    seg_count = parent_ref.shape[1]
    first_row = row == 0
    keys[...] = jnp.where(first_row, keyval_ref[:, :half], trunk_ref[:, :half])
    values[...] = jnp.where(first_row, keyval_ref[:, half:], trunk_ref[:, half:])
    dkeys[...] = jnp.zeros_like(dkeys)
    dvalues[...] = jnp.zeros_like(dvalues)
    lane = lax.broadcasted_iota(jnp.int32, (1, half), 1)
    causal = lax.broadcasted_iota(jnp.int32, (SEG, SEG), 0) >= lax.broadcasted_iota(
        jnp.int32, (SEG, SEG), 1
    )
    across = ((1,), (1,))
    down = ((0,), (0,))
    for seg in range(segs):
        here = slice(seg * SEG, (seg + 1) * SEG)
        above = parent_ref[tree, row * segs + seg]
        linked = [above == at for at in range(trunk_segs)]
        for _ in range(seg_count - 2):
            above = jnp.where(above >= 0, parent_ref[tree, jnp.maximum(above, 0)], -1)
            linked = [was | (above == at) for at, was in enumerate(linked)]
        bias = [jnp.where(is_linked, 0.0, masked_fill) for is_linked in linked]
        query, grad = query_ref[here, :], grad_ref[here, :]
        own_key, own_value = keyval_ref[here, :half], keyval_ref[here, half:]
        attended = jnp.zeros((SEG, half), jnp.float32)
        dquery = jnp.zeros((SEG, half), jnp.float32)
        dkey = jnp.zeros((SEG, half), jnp.float32)
        dvalue = jnp.zeros((SEG, half), jnp.float32)
        for head in range(half // HD):
            mine = (lane >= head * HD) & (lane < (head + 1) * HD)
            head_query = jnp.where(mine, query, jnp.zeros_like(query))
            head_grad = jnp.where(mine, grad, jnp.zeros_like(grad))
            scores = [
                matmul(head_query, keys[at * SEG : (at + 1) * SEG, :], across) + bias[at]
                for at in range(trunk_segs)
            ] + [jnp.where(causal, matmul(head_query, own_key, across), masked_fill)]
            top = functools.reduce(jnp.maximum, [jnp.max(s, axis=1, keepdims=True) for s in scores])
            powers = [jnp.exp(s - top) for s in scores]
            total = functools.reduce(jnp.add, [jnp.sum(p, axis=1, keepdims=True) for p in powers])
            probs = [p / total for p in powers]
            low = [bf16(p) for p in probs]
            blocks = [values[at * SEG : (at + 1) * SEG, :] for at in range(trunk_segs)] + [own_value]
            prob_grads = [matmul(head_grad, v, across) for v in blocks]
            delta = functools.reduce(
                jnp.add, [jnp.sum(p * g, axis=1, keepdims=True) for p, g in zip(probs, prob_grads)]
            )
            score_grads = [bf16(p * (g - delta)) for p, g in zip(probs, prob_grads)]
            head_out = functools.reduce(jnp.add, [matmul(p, v) for p, v in zip(low, blocks)])
            attended = jnp.where(mine, head_out, attended)
            key_blocks = [keys[at * SEG : (at + 1) * SEG, :] for at in range(trunk_segs)] + [own_key]
            head_dq = functools.reduce(jnp.add, [matmul(s, u) for s, u in zip(score_grads, key_blocks)])
            dquery = jnp.where(mine, head_dq, dquery)
            dkey = dkey + matmul(score_grads[-1], head_query, down)
            dvalue = dvalue + matmul(low[-1], head_grad, down)
            for at in range(trunk_segs):
                spot = slice(at * SEG, (at + 1) * SEG)
                dkeys[spot, :] += matmul(score_grads[at], head_query, down)
                dvalues[spot, :] += matmul(low[at], head_grad, down)
        out_ref[here, :] = bf16(attended)
        dq_ref[here, :] = dquery * HD ** (-0.5)
        dkv_ref[here, :half] = dkey
        dkv_ref[here, half:] = dvalue
    dtrunk_ref[:, :half] = bf16(dkeys[...])
    dtrunk_ref[:, half:] = bf16(dvalues[...])

    @pl.when(first_row)
    def _():
        dkv_ref[:, :half] += dkeys[...]
        dkv_ref[:, half:] += dvalues[...]


def row_block(rows, width):
    return pl.BlockSpec((rows, width), lambda at, *_: (at, 0))


def split_heads(mixed, tables):
    count, width = mixed.shape
    rows = SEG
    return pl.pallas_call(
        split_kernel,
        grid=(count // rows,),
        in_specs=[row_block(rows, width)] + [row_block(rows, 2 * HD)] * 3,
        out_specs=[row_block(rows, width // 3), row_block(rows, 2 * width // 3)],
        out_shape=[
            jax.ShapeDtypeStruct((count, width // 3), jnp.bfloat16),
            jax.ShapeDtypeStruct((count, 2 * width // 3), jnp.bfloat16),
        ],
        cost_estimate=pl.CostEstimate(flops=20 * count * width, bytes_accessed=8 * count * width, transcendentals=0),
        name="split_heads",
    )(mixed, *tables)


def join_heads(row, dq, dkv, sent, tables):
    count, half = dq.shape
    rows = SEG
    return pl.pallas_call(
        join_kernel,
        grid_spec=pltpu.PrefetchScalarGridSpec(
            num_scalar_prefetch=1,
            grid=(count // rows,),
            in_specs=[row_block(rows, half), row_block(rows, 2 * half), row_block(rows, 2 * half)]
            + [row_block(rows, 2 * HD)] * 3,
            out_specs=row_block(rows, 3 * half),
        ),
        out_shape=jax.ShapeDtypeStruct((count, 3 * half), jnp.bfloat16),
        cost_estimate=pl.CostEstimate(flops=60 * count * half, bytes_accessed=24 * count * half, transcendentals=0),
        name="join_heads",
    )(row, dq, dkv, sent, *tables)


def tree_attention(parents, row, query, keyval, trunk, grad):
    trees = parents.shape[0]
    count, half = query.shape
    rows = count // trees
    keys = trunk.shape[0] // trees
    pairs = count * (keys + SEG) * (half // HD)
    return pl.pallas_call(
        tree_kernel,
        grid_spec=pltpu.PrefetchScalarGridSpec(
            num_scalar_prefetch=2,
            grid=(trees,),
            in_specs=[
                row_block(rows, half),
                row_block(rows, 2 * half),
                row_block(keys, 2 * half),
                row_block(rows, half),
            ],
            out_specs=[
                row_block(rows, half),
                row_block(rows, half),
                row_block(rows, 2 * half),
                row_block(keys, 2 * half),
            ],
            scratch_shapes=[pltpu.VMEM((keys, half), jnp.bfloat16)] * 2
            + [pltpu.VMEM((keys, half), jnp.float32)] * 2,
        ),
        out_shape=[
            jax.ShapeDtypeStruct((count, half), jnp.bfloat16),
            jax.ShapeDtypeStruct((count, half), jnp.float32),
            jax.ShapeDtypeStruct((count, 2 * half), jnp.float32),
            jax.ShapeDtypeStruct((trees * keys, 2 * half), jnp.bfloat16),
        ],
        cost_estimate=pl.CostEstimate(
            flops=12 * pairs * half, bytes_accessed=20 * count * half, transcendentals=pairs
        ),
        name="tree_attention",
    )(parents, row, query, keyval, trunk, grad)


def paired_device(
    tokens,
    parent,
    depth,
    w_qkv,
    b_qkv,
    w_out,
    w_up,
    b_up,
    w_down,
    b_res,
    ln_gain,
    ln_bias,
    cotangent,
):
    count, width = tokens.shape
    row = lax.axis_index("row")
    col = lax.axis_index("col")
    core = lax.axis_index("dp") % 2
    slab = lax.axis_index("dp") // 2
    cols = lax.axis_size("col")
    half = 2 * width
    heads_width = w_out.shape[0] // 2
    hidden = w_up.shape[1] // 2
    blocks = [2 * row, 2 * row + 1, 2 * (1 - row), 2 * (1 - row) + 1]

    def part(values, at, size, axis):
        return lax.dynamic_slice_in_dim(values, at * size, size, axis)

    def other_half(send, axis):
        by_row = swap_row(send)
        by_x = swap_x(by_row)
        return pair(slab, by_row, by_x, axis)

    def whole_weight(master, axis):
        send = bf16(part(master, slab, width, axis))
        return jnp.concatenate([bf16(master), other_half(send, axis)], axis=axis)

    up_full = whole_weight(part(w_up, core, hidden, 1), 0)
    qkv_full = whole_weight(part(w_qkv, core, 3 * heads_width, 1), 0)
    down_full = whole_weight(part(w_down, core, hidden, 0), 1)
    out_full = whole_weight(part(w_out, core, heads_width, 0), 1)

    tables = jnp.concatenate([parent, depth], axis=0)
    tables = jnp.stack([tables, swap_core(tables)])
    parents = tables[:, 0]
    segs = count // SEG
    token = jnp.arange(count, dtype=jnp.int32)
    levels = jnp.zeros((2, count), jnp.float32)
    for seg in range(segs):
        level = lax.dynamic_slice_in_dim(tables[:, 1], row * segs + seg, 1, 1).astype(jnp.float32)
        levels = jnp.where((token // SEG == seg)[None, :], level, levels)
    positions = (levels * SEG + (token % SEG).astype(jnp.float32)[None, :]).reshape(2 * count)
    rotary = rotary_tables(positions)

    whole = f32(gather_line(tokens, blocks, col))
    gain_here = jnp.concatenate([part(ln_gain, at, width, 0) for at in blocks])
    bias_here = jnp.concatenate([part(ln_bias, at, width, 0) for at in blocks])
    mean = jnp.mean(whole, axis=1, keepdims=True)
    centred = whole - mean
    inv_scale = lax.rsqrt(jnp.mean(centred * centred, axis=1, keepdims=True) + norm_epsilon)
    normed = bf16(centred * inv_scale * gain_here + bias_here)
    normed = jnp.concatenate([normed, swap_core(normed)], axis=0)
    grad = gather_line(cotangent, blocks, col)
    grad = jnp.concatenate([grad, swap_core(grad)], axis=0)

    mixed = matmul(normed, qkv_full) + part(b_qkv, core, 3 * heads_width, 0)
    query, keyval = split_heads(mixed, rotary)
    trunk = lax.ppermute(keyval, "row", [(0, 1)])
    hidden_up = matmul(normed, up_full) + part(b_up, core, hidden, 0)
    root = math.sqrt(2.0 / math.pi)
    squared = hidden_up * hidden_up
    bend = jnp.tanh(root * (hidden_up + 0.044715 * squared * hidden_up))
    activated = bf16(0.5 * hidden_up * (1.0 + bend))
    slope = bf16(
        0.5 * (1.0 + bend)
        + 0.5 * hidden_up * (1.0 - bend * bend) * root * (1.0 + 3.0 * 0.044715 * squared)
    )

    def reduced(left, right, name):
        sent = swap_row(bf16(left()))
        both = bf16(right() + f32(sent))
        return bf16(f32(both) + f32(swap_x(both)))

    down_dims = ((0,), (0,))
    across = ((1,), (1,))
    grad_own, grad_other = grad[:, :half], grad[:, half:]
    normed_own, normed_other = normed[:, :half], normed[:, half:]
    cut = hidden // 4
    down_first = reduced(
        lambda: matmul(activated[:, :cut], grad_other, down_dims),
        lambda: matmul(activated[:, :cut], grad_own, down_dims),
        "down_first",
    )
    down_last = reduced(
        lambda: matmul(activated[:, cut:], grad_other, down_dims),
        lambda: matmul(activated[:, cut:], grad_own, down_dims),
        "down_last",
    )
    down_sum = jnp.concatenate([down_first, down_last], axis=0)
    down_grad = f32(pair(core, down_sum, swap_core(down_sum), 0))

    act_grad = matmul(grad, down_full, across)
    up_grad = bf16(act_grad * f32(slope))
    up_sum = reduced(
        lambda: matmul(normed_other, up_grad, down_dims),
        lambda: matmul(normed_own, up_grad, down_dims),
        "up",
    )
    up_weight_grad = f32(pair(core, up_sum, swap_core(up_sum), 1))

    out_heads = bf16(matmul(grad, out_full, across))
    row_table = jnp.reshape(row, (1,)).astype(jnp.int32)
    attended, query_grad, own_grad, trunk_grad = tree_attention(
        parents, row_table, query, keyval, trunk, out_heads
    )
    trunk_sent = lax.ppermute(trunk_grad, "row", [(1, 0)])
    out_sum = reduced(
        lambda: matmul(attended, grad_other, down_dims),
        lambda: matmul(attended, grad_own, down_dims),
        "out",
    )
    out_grad = f32(pair(core, out_sum, swap_core(out_sum), 0))
    mixed_grad = join_heads(row_table, query_grad, own_grad, trunk_sent, rotary)
    qkv_sum = reduced(
        lambda: matmul(normed_other, mixed_grad, down_dims),
        lambda: matmul(normed_own, mixed_grad, down_dims),
        "qkv",
    )
    qkv_weight_grad = f32(pair(core, qkv_sum, swap_core(qkv_sum), 1))

    def spread(terms):
        mine = terms[:count] + f32(swap_core(bf16(terms[count:])))
        mine = bf16(mine)
        ordered = pair(row, mine[:, :half], mine[:, half:], 1)
        stacked = jnp.stack([ordered[:, at * width : (at + 1) * width] for at in range(cols)])
        swapped = lax.all_to_all(stacked, "col", 0, 0, tiled=True)
        return jnp.sum(f32(swapped), axis=0)

    branch = spread(matmul(attended, out_full) + matmul(activated, down_full))
    output = bf16(f32(tokens) + branch + b_res)

    norm_grad = spread(
        matmul(mixed_grad, qkv_full, across) + matmul(up_grad, up_full, across)
    )
    normal = (f32(tokens) - mean) * inv_scale
    scaled = norm_grad * part(ln_gain, col, width, 0)
    sums = jnp.stack([jnp.sum(scaled, axis=1), jnp.sum(scaled * normal, axis=1)])
    shifted = [
        lax.ppermute(sums, "col", [(at, (at + hop) % cols) for at in range(cols)])
        for hop in range(1, cols)
    ]
    sums = functools.reduce(jnp.add, shifted, sums) / (cols * width)
    tokens_grad = inv_scale * (
        scaled - sums[0][:, None] - normal * sums[1][:, None]
    ) + f32(cotangent)

    small = jnp.concatenate(
        [
            jnp.sum(f32(up_grad), axis=0),
            jnp.sum(f32(mixed_grad), axis=0),
            jnp.sum(f32(cotangent), axis=0),
            jnp.sum(norm_grad * normal, axis=0),
            jnp.sum(norm_grad, axis=0),
        ]
    ).reshape(-1, 128)
    small = small + swap_row(small)
    small = small + swap_x(small)
    small, small_other = small.reshape(-1), swap_core(small).reshape(-1)
    bounds = [0, hidden, hidden + 3 * heads_width]
    up_bias_grad = pair(core, small[: bounds[1]], small_other[: bounds[1]], 0)
    qkv_bias_grad = pair(
        core, small[bounds[1] : bounds[2]], small_other[bounds[1] : bounds[2]], 0
    )
    shared = (small + small_other)[bounds[2] :].reshape(3, width)
    res_bias_grad = shared[0]
    norm_sums = shared[1:].reshape(-1, 128)
    arrived = [norm_sums] + [
        lax.ppermute(norm_sums, "col", [(at, (at + hop) % cols) for at in range(cols)])
        for hop in range(1, cols)
    ]
    arrived = arrived[::-1]
    arrived = jnp.stack(arrived + arrived[:-1])
    arrived = lax.dynamic_slice_in_dim(arrived, cols - 1 - col, cols, 0)
    arrived = arrived.reshape(cols, 2, width)
    gain_grad = arrived[:, 0].reshape(-1)
    shift_grad = arrived[:, 1].reshape(-1)
    return (
        output,
        tokens_grad,
        qkv_weight_grad,
        qkv_bias_grad,
        out_grad,
        up_weight_grad,
        up_bias_grad,
        down_grad,
        res_bias_grad,
        gain_grad,
        shift_grad,
    )


def solution(mesh):
    sizes = (mesh.shape["dp"], mesh.shape["row"], mesh.shape["col"])
    per_device = paired_device if sizes == (4, 2, 4) else general_device
    return jax.shard_map(
        per_device,
        mesh=mesh,
        in_specs=(
            P(("dp", "row"), "col"),
            P("dp", None),
            P("dp", None),
            P("row", "col"),
            P("col"),
            P("col", "row"),
            P("row", "col"),
            P("col"),
            P("col", "row"),
            P("col"),
            P(),
            P(),
            P(("dp", "row"), "col"),
        ),
        out_specs=(
            P(("dp", "row"), "col"),
            P(("dp", "row"), "col"),
            P("row", "col"),
            P("col"),
            P("col", "row"),
            P("row", "col"),
            P("col"),
            P("col", "row"),
            P("col"),
            P(),
            P(),
        ),
        check_vma=False,
    )
```

```python
import functools
import math

import jax
import jax.numpy as jnp
from jax import lax
from jax.experimental import pallas as pl
from jax.experimental.pallas import tpu as pltpu
from jax.sharding import PartitionSpec as P

HD = 64
ROT = 32
SEG = 256


norm_epsilon = 1e-05
masked_fill = -1e30
rotary_base = 10000.0


def precise_dot(left, right):
    return jnp.dot(left, right, precision=lax.Precision.HIGHEST, preferred_element_type=jnp.float32)


def ancestry(parent_row):
    seg_count = parent_row.shape[0]
    labels = jnp.arange(seg_count, dtype=jnp.int32)
    identity = jnp.eye(seg_count, dtype=jnp.float32)
    parent_hot = (parent_row[:, None] == labels[None, :]).astype(jnp.float32)

    def extend(rounds, reachable):
        return jnp.minimum(identity + precise_dot(parent_hot, reachable), 1.0)

    return lax.fori_loop(0, seg_count, extend, identity)


def rotate(values, cosines, sines):
    half_rot = ROT // 2
    former = values[..., :half_rot]
    latter = values[..., half_rot:ROT]
    return jnp.concatenate(
        [former * cosines - latter * sines, latter * cosines + former * sines, values[..., ROT:]],
        axis=-1,
    )


def angles_of(positions):
    frequency = jnp.exp(
        -math.log(rotary_base) * 2.0 * jnp.arange(ROT // 2, dtype=jnp.float32) / ROT
    )
    phase_angle = positions[:, None] * frequency[None, :]
    return (jnp.cos(phase_angle)[:, None, :], jnp.sin(phase_angle)[:, None, :])


def reorder_rows(gradient, row_count, dp_count):
    leading = gradient.shape[0]
    blocked = gradient.reshape(
        row_count, dp_count, leading // (row_count * dp_count), gradient.shape[1]
    )
    return jnp.transpose(blocked, (1, 0, 2, 3)).reshape(leading, gradient.shape[1])


def reorder_cols(gradient, row_count, dp_count):
    trailing = gradient.shape[1]
    blocked = gradient.reshape(
        gradient.shape[0], row_count, dp_count, trailing // (row_count * dp_count)
    )
    return jnp.transpose(blocked, (0, 2, 1, 3)).reshape(gradient.shape[0], trailing)


def general_device(
    tokens,
    parent,
    depth,
    w_qkv,
    b_qkv,
    w_out,
    w_up,
    b_up,
    w_down,
    b_res,
    ln_gain,
    ln_bias,
    cotangent,
):
    tok_rows = tokens.shape[0]
    col_width = tokens.shape[1]
    row_count = lax.axis_size("row")
    dp_count = lax.axis_size("dp")
    row_start = lax.axis_index("row") * tok_rows
    local_heads = w_out.shape[0] // HD
    seg_count = parent.shape[1]
    labels = jnp.arange(seg_count, dtype=jnp.int32)
    reachable = ancestry(parent[0])
    query_index = row_start + jnp.arange(tok_rows, dtype=jnp.int32)
    query_seg = query_index // SEG
    query_hot = (query_seg[:, None] == labels[None, :]).astype(jnp.float32)
    query_reach = precise_dot(query_hot, reachable)
    levels = precise_dot(query_hot, depth[0].astype(jnp.float32)[:, None])[:, 0]
    positions = levels * SEG + (query_index % SEG).astype(jnp.float32)
    cosines, sines = angles_of(positions)
    score_scale = HD ** (-0.5)

    def permit(key_len):
        key_index = jnp.arange(key_len, dtype=jnp.int32)
        key_seg = key_index // SEG
        key_hot = (key_seg[:, None] == labels[None, :]).astype(jnp.float32)
        linked = precise_dot(query_reach, key_hot.T) > 0.5
        return linked & (
            (query_seg[:, None] != key_seg[None, :]) | (query_index[:, None] >= key_index[None, :])
        )

    whole = lax.all_gather(tokens, "col", axis=1, tiled=True).astype(jnp.float32)
    centred = whole - jnp.mean(whole, axis=1, keepdims=True)
    inv_scale = lax.rsqrt(jnp.mean(centred * centred, axis=1, keepdims=True) + norm_epsilon)
    normal = centred * inv_scale
    normed = (normal * ln_gain + ln_bias).astype(jnp.bfloat16)
    qkv_full, up_full, out_full, down_full = (
        lax.all_gather(w_qkv.astype(jnp.bfloat16), "row", axis=0, tiled=True),
        lax.all_gather(w_up.astype(jnp.bfloat16), "row", axis=0, tiled=True),
        lax.all_gather(w_out.astype(jnp.bfloat16), "row", axis=1, tiled=True),
        lax.all_gather(w_down.astype(jnp.bfloat16), "row", axis=1, tiled=True),
    )
    mixed = (jnp.dot(normed, qkv_full, preferred_element_type=jnp.float32) + b_qkv).reshape(
        tok_rows, local_heads, 3, HD
    )

    def rotate_pair(query_pre, key_pre):
        return (rotate(query_pre, cosines, sines), rotate(key_pre, cosines, sines))

    rotated, rotate_back = jax.vjp(rotate_pair, mixed[:, :, 0], mixed[:, :, 1])
    queries = rotated[0].astype(jnp.bfloat16)
    key_rows = rotated[1].astype(jnp.bfloat16)
    value_rows = mixed[:, :, 2].astype(jnp.bfloat16)
    key_flat = key_rows.reshape(tok_rows, local_heads * HD)
    value_flat = value_rows.reshape(tok_rows, local_heads * HD)

    def scores_for(key_part):
        raw_scores = (
            jnp.einsum("qhe,khe->hqk", queries, key_part, preferred_element_type=jnp.float32)
            * score_scale
        )
        allowed = permit(key_part.shape[0])
        return (jnp.where(allowed[None], raw_scores, masked_fill), allowed)

    pieces = (
        lax.all_gather(key_flat, "row", axis=0, tiled=True),
        lax.all_gather(value_flat, "row", axis=0, tiled=True),
    )
    running_top = jnp.full((local_heads, tok_rows), masked_fill, jnp.float32)
    key_len = pieces[0].shape[0]
    key_part = pieces[0].reshape(key_len, local_heads, HD)
    value_part = pieces[1].reshape(key_len, local_heads, HD)
    scores, allowed = scores_for(key_part)
    new_top = jnp.maximum(running_top, jnp.max(scores, axis=2))
    exponent = jnp.where(allowed[None], jnp.exp(scores - new_top[:, :, None]), 0.0)
    running_sum = jnp.sum(exponent, axis=2)
    weighted = jnp.einsum(
        "hqk,khe->hqe",
        exponent.astype(jnp.bfloat16),
        value_part,
        preferred_element_type=jnp.float32,
    )
    running_top, running_sum, weighted = (new_top, running_sum, weighted)
    log_total = running_top + jnp.log(running_sum)
    attn_exact = weighted / running_sum[:, :, None]
    attended = (
        jnp.transpose(attn_exact, (1, 0, 2))
        .reshape(tok_rows, local_heads * HD)
        .astype(jnp.bfloat16)
    )
    hidden_up = jnp.dot(normed, up_full, preferred_element_type=jnp.float32) + b_up
    activated, gelu_back = jax.vjp(functools.partial(jax.nn.gelu, approximate=True), hidden_up)
    activated = activated.astype(jnp.bfloat16)
    branch_terms = jnp.dot(attended, out_full, preferred_element_type=jnp.float32) + jnp.dot(
        activated, down_full, preferred_element_type=jnp.float32
    )
    branch = lax.psum_scatter(
        branch_terms.astype(jnp.bfloat16), "col", scatter_dimension=1, tiled=True
    ).astype(jnp.float32)
    output = (tokens.astype(jnp.float32) + branch + b_res).astype(jnp.bfloat16)
    grad_full = lax.all_gather(cotangent, "col", axis=1, tiled=True)
    res_bias_grad = jnp.sum(cotangent.astype(jnp.float32), axis=0)
    down_grad = jnp.einsum("tf,td->fd", activated, grad_full, preferred_element_type=jnp.float32)
    out_grad = jnp.einsum("te,td->ed", attended, grad_full, preferred_element_type=jnp.float32)
    act_grad = jnp.einsum("td,fd->tf", grad_full, down_full, preferred_element_type=jnp.float32)
    up_grad = gelu_back(act_grad)[0].astype(jnp.bfloat16)
    attn_grad = jnp.einsum(
        "td,ed->te", grad_full, out_full, preferred_element_type=jnp.float32
    ).astype(jnp.bfloat16)
    up_bias_grad = jnp.sum(up_grad.astype(jnp.float32), axis=0)
    up_weight_grad = jnp.einsum("td,tf->df", normed, up_grad, preferred_element_type=jnp.float32)
    out_heads = attn_grad.reshape(tok_rows, local_heads, HD)
    delta_sum = jnp.einsum("qhe,hqe->hq", out_heads.astype(jnp.float32), attn_exact)
    pieces = (
        lax.all_gather(key_flat, "row", axis=0, tiled=True),
        lax.all_gather(value_flat, "row", axis=0, tiled=True),
    )
    key_len = pieces[0].shape[0]
    key_part = pieces[0].reshape(key_len, local_heads, HD)
    value_part = pieces[1].reshape(key_len, local_heads, HD)
    scores, allowed = scores_for(key_part)
    softmaxed = jnp.where(allowed[None], jnp.exp(scores - log_total[:, :, None]), 0.0)
    prob_grad = jnp.einsum(
        "qhe,khe->hqk", out_heads, value_part, preferred_element_type=jnp.float32
    )
    score_grad = (softmaxed * (prob_grad - delta_sum[:, :, None])).astype(jnp.bfloat16)
    query_grad = (
        jnp.einsum("hqk,khe->qhe", score_grad, key_part, preferred_element_type=jnp.float32)
        * score_scale
    )
    key_grad = (
        jnp.einsum("hqk,qhe->khe", score_grad, queries, preferred_element_type=jnp.float32)
        * score_scale
    )
    value_grad = jnp.einsum(
        "hqk,qhe->khe",
        softmaxed.astype(jnp.bfloat16),
        out_heads,
        preferred_element_type=jnp.float32,
    )
    stacked = jnp.stack([key_grad, value_grad], axis=1).reshape(key_len, 2 * local_heads * HD)
    pair_grad = stacked
    query_grad, pair_grad = (query_grad, pair_grad)
    own_pairs = (
        lax.psum_scatter(pair_grad.astype(jnp.bfloat16), "row", scatter_dimension=0, tiled=True)
        .astype(jnp.float32)
        .reshape(tok_rows, 2, local_heads, HD)
    )
    query_pre, key_pre = rotate_back((query_grad, own_pairs[:, 0]))
    mixed_grad = (
        jnp.stack([query_pre, key_pre, own_pairs[:, 1]], axis=2)
        .reshape(tok_rows, 3 * local_heads * HD)
        .astype(jnp.bfloat16)
    )
    qkv_bias_grad = jnp.sum(mixed_grad.astype(jnp.float32), axis=0)
    qkv_weight_grad = jnp.einsum(
        "td,tc->dc", normed, mixed_grad, preferred_element_type=jnp.float32
    )
    norm_part = jnp.einsum(
        "tc,dc->td", mixed_grad, qkv_full, preferred_element_type=jnp.float32
    ) + jnp.einsum("tf,df->td", up_grad, up_full, preferred_element_type=jnp.float32)
    norm_grad = lax.psum(norm_part.astype(jnp.bfloat16), "col").astype(jnp.float32)
    gain_grad = jnp.sum(norm_grad * normal, axis=0)
    shift_grad = jnp.sum(norm_grad, axis=0)
    scaled = norm_grad * ln_gain
    mean_scaled = jnp.mean(scaled, axis=1, keepdims=True)
    mean_mixed = jnp.mean(scaled * normal, axis=1, keepdims=True)
    col_start = lax.axis_index("col") * col_width
    scaled_share = lax.dynamic_slice_in_dim(scaled, col_start, col_width, 1)
    normal_share = lax.dynamic_slice_in_dim(normal, col_start, col_width, 1)
    tokens_grad = inv_scale * (
        scaled_share - mean_scaled - normal_share * mean_mixed
    ) + cotangent.astype(jnp.float32)
    qkv_bias_grad, up_bias_grad, res_bias_grad, gain_grad, shift_grad = (
        lax.psum(qkv_bias_grad.astype(jnp.bfloat16), ("dp", "row")).astype(jnp.float32),
        lax.psum(up_bias_grad.astype(jnp.bfloat16), ("dp", "row")).astype(jnp.float32),
        lax.psum(res_bias_grad.astype(jnp.bfloat16), ("dp", "row")).astype(jnp.float32),
        lax.psum(gain_grad.astype(jnp.bfloat16), ("dp", "row")).astype(jnp.float32),
        lax.psum(shift_grad.astype(jnp.bfloat16), ("dp", "row")).astype(jnp.float32),
    )
    pieces_now = (
        lax.psum_scatter(
            reorder_rows(qkv_weight_grad, row_count, dp_count).astype(jnp.bfloat16),
            ("dp", "row"),
            scatter_dimension=0,
            tiled=True,
        ).astype(jnp.float32),
        lax.psum_scatter(
            reorder_rows(up_weight_grad, row_count, dp_count).astype(jnp.bfloat16),
            ("dp", "row"),
            scatter_dimension=0,
            tiled=True,
        ).astype(jnp.float32),
        lax.psum_scatter(
            reorder_cols(out_grad, row_count, dp_count).astype(jnp.bfloat16),
            ("dp", "row"),
            scatter_dimension=1,
            tiled=True,
        ).astype(jnp.float32),
        lax.psum_scatter(
            reorder_cols(down_grad, row_count, dp_count).astype(jnp.bfloat16),
            ("dp", "row"),
            scatter_dimension=1,
            tiled=True,
        ).astype(jnp.float32),
    )
    qkv_weight_grad, up_weight_grad, out_grad, down_grad = (
        lax.all_gather(pieces_now[0].astype(jnp.bfloat16), "dp", axis=0, tiled=True).astype(
            jnp.float32
        ),
        lax.all_gather(pieces_now[1].astype(jnp.bfloat16), "dp", axis=0, tiled=True).astype(
            jnp.float32
        ),
        lax.all_gather(pieces_now[2].astype(jnp.bfloat16), "dp", axis=1, tiled=True).astype(
            jnp.float32
        ),
        lax.all_gather(pieces_now[3].astype(jnp.bfloat16), "dp", axis=1, tiled=True).astype(
            jnp.float32
        ),
    )
    return (
        output,
        tokens_grad,
        qkv_weight_grad,
        qkv_bias_grad,
        out_grad,
        up_weight_grad,
        up_bias_grad,
        down_grad,
        res_bias_grad,
        gain_grad,
        shift_grad,
    )


SWAP_ROW = [(0, 1), (1, 0)]
SWAP_X = [(0, 2), (2, 0), (1, 3), (3, 1)]
SWAP_CORE = [(0, 1), (1, 0), (2, 3), (3, 2)]


def bf16(values):
    return values.astype(jnp.bfloat16)


def f32(values):
    return values.astype(jnp.float32)


def matmul(left, right, dims=((1,), (0,))):
    return lax.dot_general(left, right, (dims, ((), ())), preferred_element_type=jnp.float32)


def swap_row(values):
    return lax.ppermute(values, "row", SWAP_ROW)


def swap_x(values):
    return lax.ppermute(values, "dp", SWAP_X)


def swap_core(values):
    return lax.ppermute(values, "dp", SWAP_CORE)


def pick(index, first, second):
    return jnp.where(index == 0, first, second)


def pair(index, mine, theirs, axis):
    return pick(
        index,
        jnp.concatenate([mine, theirs], axis=axis),
        jnp.concatenate([theirs, mine], axis=axis),
    )


def after(value, *earlier):
    return lax.optimization_barrier((value,) + earlier)[0]


def rotary_tables(positions):
    lane = jnp.arange(2 * HD, dtype=jnp.int32) % HD
    half_rot = ROT // 2
    frequency = jnp.exp(
        -math.log(rotary_base) * 2.0 * (lane % half_rot).astype(jnp.float32) / ROT
    )
    angle = positions[:, None] * frequency[None, :]
    turned = (lane < ROT)[None, :]
    sines = jnp.sin(angle)
    return (
        jnp.where(turned, jnp.cos(angle), 1.0),
        jnp.where((lane < half_rot)[None, :], -sines, 0.0),
        jnp.where(turned & (lane >= half_rot)[None, :], sines, 0.0),
    )


def turn(values, cosines, sines_low, sines_high):
    width = values.shape[1]
    half_rot = ROT // 2
    return (
        values * cosines
        + pltpu.roll(values, width - half_rot, 1) * sines_low
        + pltpu.roll(values, half_rot, 1) * sines_high
    )


def split_kernel(mixed_ref, cos_ref, low_ref, high_ref, query_ref, keyval_ref):
    cosines, low, high = cos_ref[...], low_ref[...], high_ref[...]
    rows = mixed_ref.shape[0]
    half = query_ref.shape[1]
    first = lax.broadcasted_iota(jnp.int32, (rows, 2 * HD), 1) < HD
    scale = HD ** (-0.5)
    for at in range(half // (2 * HD)):
        tiles = [mixed_ref[:, (3 * at + part) * 2 * HD : (3 * at + part + 1) * 2 * HD] for part in range(3)]
        query = jnp.where(first, tiles[0], tiles[1])
        key = jnp.where(first, pltpu.roll(tiles[0], HD, 1), pltpu.roll(tiles[2], HD, 1))
        value = jnp.where(first, tiles[1], tiles[2])
        here = slice(at * 2 * HD, (at + 1) * 2 * HD)
        query_ref[:, here] = bf16(f32(bf16(turn(query, cosines, low, high))) * scale)
        keyval_ref[:, here] = bf16(turn(key, cosines, low, high))
        keyval_ref[:, half + at * 2 * HD : half + (at + 1) * 2 * HD] = bf16(value)


def join_kernel(row_ref, dq_ref, dkv_ref, sent_ref, cos_ref, low_ref, high_ref, out_ref):
    cosines, low, high = cos_ref[...], -low_ref[...], -high_ref[...]
    rows = dq_ref.shape[0]
    half = dq_ref.shape[1]
    first = lax.broadcasted_iota(jnp.int32, (rows, 2 * HD), 1) < HD
    owner = row_ref[0] == 0
    for at in range(half // (2 * HD)):
        here = slice(at * 2 * HD, (at + 1) * 2 * HD)
        there = slice(half + at * 2 * HD, half + (at + 1) * 2 * HD)
        query = turn(dq_ref[:, here], cosines, low, high)
        key = dkv_ref[:, here] + jnp.where(owner, f32(sent_ref[:, here]), 0.0)
        value = dkv_ref[:, there] + jnp.where(owner, f32(sent_ref[:, there]), 0.0)
        key = pltpu.roll(turn(key, cosines, low, high), HD, 1)
        tiles = (jnp.where(first, query, key), jnp.where(first, value, query), jnp.where(first, key, value))
        for part in range(3):
            out_ref[:, (3 * at + part) * 2 * HD : (3 * at + part + 1) * 2 * HD] = bf16(tiles[part])


def tree_kernel(
    parent_ref, row_ref, query_ref, keyval_ref, trunk_ref, grad_ref,
    out_ref, dq_ref, dkv_ref, dtrunk_ref,
    keys, values, dkeys, dvalues,
):
    tree = pl.program_id(0)
    row = row_ref[0]
    rows, half = query_ref.shape
    trunk_len = trunk_ref.shape[0]
    segs = rows // SEG
    trunk_segs = trunk_len // SEG
    seg_count = parent_ref.shape[1]
    first_row = row == 0
    keys[...] = jnp.where(first_row, keyval_ref[:, :half], trunk_ref[:, :half])
    values[...] = jnp.where(first_row, keyval_ref[:, half:], trunk_ref[:, half:])
    dkeys[...] = jnp.zeros_like(dkeys)
    dvalues[...] = jnp.zeros_like(dvalues)
    lane = lax.broadcasted_iota(jnp.int32, (1, half), 1)
    causal = lax.broadcasted_iota(jnp.int32, (SEG, SEG), 0) >= lax.broadcasted_iota(
        jnp.int32, (SEG, SEG), 1
    )
    across = ((1,), (1,))
    down = ((0,), (0,))
    for seg in range(segs):
        here = slice(seg * SEG, (seg + 1) * SEG)
        above = parent_ref[tree, row * segs + seg]
        linked = [above == at for at in range(trunk_segs)]
        for _ in range(seg_count - 2):
            above = jnp.where(above >= 0, parent_ref[tree, jnp.maximum(above, 0)], -1)
            linked = [was | (above == at) for at, was in enumerate(linked)]
        bias = [jnp.where(is_linked, 0.0, masked_fill) for is_linked in linked]
        query, grad = query_ref[here, :], grad_ref[here, :]
        own_key, own_value = keyval_ref[here, :half], keyval_ref[here, half:]
        attended = jnp.zeros((SEG, half), jnp.float32)
        dquery = jnp.zeros((SEG, half), jnp.float32)
        dkey = jnp.zeros((SEG, half), jnp.float32)
        dvalue = jnp.zeros((SEG, half), jnp.float32)
        for head in range(half // HD):
            mine = (lane >= head * HD) & (lane < (head + 1) * HD)
            head_query = jnp.where(mine, query, jnp.zeros_like(query))
            head_grad = jnp.where(mine, grad, jnp.zeros_like(grad))
            scores = [
                matmul(head_query, keys[at * SEG : (at + 1) * SEG, :], across) + bias[at]
                for at in range(trunk_segs)
            ] + [jnp.where(causal, matmul(head_query, own_key, across), masked_fill)]
            top = functools.reduce(jnp.maximum, [jnp.max(s, axis=1, keepdims=True) for s in scores])
            powers = [jnp.exp(s - top) for s in scores]
            total = functools.reduce(jnp.add, [jnp.sum(p, axis=1, keepdims=True) for p in powers])
            probs = [p / total for p in powers]
            low = [bf16(p) for p in probs]
            blocks = [values[at * SEG : (at + 1) * SEG, :] for at in range(trunk_segs)] + [own_value]
            prob_grads = [matmul(head_grad, v, across) for v in blocks]
            delta = functools.reduce(
                jnp.add, [jnp.sum(p * g, axis=1, keepdims=True) for p, g in zip(probs, prob_grads)]
            )
            score_grads = [bf16(p * (g - delta)) for p, g in zip(probs, prob_grads)]
            head_out = functools.reduce(jnp.add, [matmul(p, v) for p, v in zip(low, blocks)])
            attended = jnp.where(mine, head_out, attended)
            key_blocks = [keys[at * SEG : (at + 1) * SEG, :] for at in range(trunk_segs)] + [own_key]
            head_dq = functools.reduce(jnp.add, [matmul(s, u) for s, u in zip(score_grads, key_blocks)])
            dquery = jnp.where(mine, head_dq, dquery)
            dkey = dkey + matmul(score_grads[-1], head_query, down)
            dvalue = dvalue + matmul(low[-1], head_grad, down)
            for at in range(trunk_segs):
                spot = slice(at * SEG, (at + 1) * SEG)
                dkeys[spot, :] += matmul(score_grads[at], head_query, down)
                dvalues[spot, :] += matmul(low[at], head_grad, down)
        out_ref[here, :] = bf16(attended)
        dq_ref[here, :] = dquery * HD ** (-0.5)
        dkv_ref[here, :half] = dkey
        dkv_ref[here, half:] = dvalue
    dtrunk_ref[:, :half] = bf16(dkeys[...])
    dtrunk_ref[:, half:] = bf16(dvalues[...])

    @pl.when(first_row)
    def _():
        dkv_ref[:, :half] += dkeys[...]
        dkv_ref[:, half:] += dvalues[...]


def store_blocks(place_ref, sides, full_ref, plain_ref):
    row, slab = place_ref[1], place_ref[2]
    for side, values in enumerate(sides):
        width = values[0].shape[1]
        for source, value in enumerate(values):
            within = source % 2
            here = row == source // 2

            @pl.when(here)
            def _():
                full_ref[side, :, within * width : (within + 1) * width] = value

            @pl.when(jnp.logical_not(here))
            def _():
                plain_ref[side, :, within * width : (within + 1) * width] = value
                at = (2 + jnp.where(slab == 0, within, 1 - within)) * width
                full_ref[side, :, pl.ds(pl.multiple_of(at, width), width)] = value


def gather_kernel(place_ref, mine_ref, theirs_ref, full_ref, plain_ref):
    sides = [[ref[at] for at in range(ref.shape[0])] for ref in (mine_ref, theirs_ref)]
    store_blocks(place_ref, sides, full_ref, plain_ref)


def norm_kernel(
    place_ref, gain_ref, bias_ref, mine_ref, theirs_ref, full_ref, plain_ref, normal_ref, scale_ref
):
    sides = []
    for side, ref in enumerate((mine_ref, theirs_ref)):
        values = [f32(ref[at]) for at in range(ref.shape[0])]
        features = len(values) * values[0].shape[1]
        mean = functools.reduce(jnp.add, [jnp.sum(v, axis=1, keepdims=True) for v in values]) / features
        centred = [v - mean for v in values]
        square = functools.reduce(jnp.add, [jnp.sum(v * v, axis=1, keepdims=True) for v in centred])
        inv_scale = lax.rsqrt(square / features + norm_epsilon)
        normals = [v * inv_scale for v in centred]
        if side == 0:
            scale_ref[...] = inv_scale
            for source, normal in enumerate(normals):

                @pl.when(place_ref[0] == source)
                def _():
                    normal_ref[...] = normal

        sides.append(
            [
                bf16(normal * gain_ref[source : source + 1, :] + bias_ref[source : source + 1, :])
                for source, normal in enumerate(normals)
            ]
        )
    store_blocks(place_ref, sides, full_ref, plain_ref)


def pair_rows(rows, width):
    return pl.BlockSpec((2, rows, width), lambda at, *_: (0, at, 0))


def gathered(place, mine, theirs, norm=None):
    blocks, count, width = mine.shape
    rows = SEG // 2
    full = blocks * width
    in_specs = [pl.BlockSpec((blocks, rows, width), lambda at, *_: (0, at, 0))] * 2
    out_specs = [pair_rows(rows, full), pair_rows(rows, full // 2)]
    out_shape = [
        jax.ShapeDtypeStruct((2, count, full), jnp.bfloat16),
        jax.ShapeDtypeStruct((2, count, full // 2), jnp.bfloat16),
    ]
    operands = [mine, theirs]
    if norm is not None:
        gain = [values.reshape(blocks, width) for values in norm]
        operands = gain + operands
        in_specs = [pl.BlockSpec((blocks, width), lambda at, *_: (0, 0))] * 2 + in_specs
        out_specs = out_specs + [row_block(rows, width), row_block(rows, 1)]
        out_shape = out_shape + [
            jax.ShapeDtypeStruct((count, width), jnp.float32),
            jax.ShapeDtypeStruct((count, 1), jnp.float32),
        ]
    results = pl.pallas_call(
        gather_kernel if norm is None else norm_kernel,
        grid_spec=pltpu.PrefetchScalarGridSpec(
            num_scalar_prefetch=1, grid=(count // rows,), in_specs=in_specs, out_specs=out_specs
        ),
        out_shape=out_shape,
        cost_estimate=pl.CostEstimate(
            flops=40 * count * width, bytes_accessed=50 * count * width, transcendentals=0
        ),
        name="join_blocks" if norm is None else "norm_blocks",
    )(place, *operands)
    return [values.reshape(2 * count, -1) for values in results[:2]] + list(results[2:])


def stack_kernel(place_ref, terms_ref, arrived_ref, out_ref):
    row, slab = place_ref[1], place_ref[2]
    width = out_ref.shape[2]
    for spot in range(4):
        here = slice(spot * width, (spot + 1) * width)
        value = bf16(terms_ref[:, here] + f32(arrived_ref[:, here]))
        if spot < 2:
            out_ref[2 * row + spot] = value
        else:
            out_ref[2 * (1 - row) + jnp.where(slab == 0, spot - 2, 3 - spot)] = value


def stacked(place, terms, arrived, blocks):
    count, full = arrived.shape
    rows = SEG // 2
    width = full // blocks
    return pl.pallas_call(
        stack_kernel,
        grid_spec=pltpu.PrefetchScalarGridSpec(
            num_scalar_prefetch=1,
            grid=(count // rows,),
            in_specs=[row_block(rows, full), row_block(rows, full)],
            out_specs=pl.BlockSpec((blocks, rows, width), lambda at, *_: (0, at, 0)),
        ),
        out_shape=jax.ShapeDtypeStruct((blocks, count, width), jnp.bfloat16),
        cost_estimate=pl.CostEstimate(flops=count * full, bytes_accessed=8 * count * full, transcendentals=0),
        name="stack_blocks",
    )(place, terms, arrived)


def cast_rows_kernel(place_ref, master_ref, own_ref, send_ref):
    value = bf16(master_ref[...])
    own_ref[...] = value
    half = pl.num_programs(0) // 2

    @pl.when(pl.program_id(0) // half == place_ref[2])
    def _():
        send_ref[...] = value


def cast_cols_kernel(place_ref, master_ref, own_ref, send_ref):
    value = bf16(master_ref[...])
    own_ref[...] = value
    half = value.shape[1] // 2
    send_ref[...] = jnp.where(place_ref[2] == 0, value[:, :half], value[:, half:])


def cast_weight(place, master, axis):
    height, width = master.shape
    rows = SEG
    if axis == 0:
        width = width // 2
        steps = height // rows
        half = steps // 2
        specs = [
            pl.BlockSpec((rows, width), lambda at, place_ref: (at, place_ref[3])),
            pl.BlockSpec((rows, width), lambda at, place_ref: (at, 0)),
            pl.BlockSpec(
                (rows, width), lambda at, place_ref: (jnp.clip(at - half * place_ref[2], 0, half - 1), 0)
            ),
        ]
        send = (height // 2, width)
        whole = (2 * height, width)
    else:
        height = height // 2
        steps = height // rows
        specs = [
            pl.BlockSpec((rows, width), lambda at, place_ref: (at + steps * place_ref[3], 0)),
            pl.BlockSpec((rows, width), lambda at, place_ref: (at, 0)),
            pl.BlockSpec((rows, width // 2), lambda at, place_ref: (at, 0)),
        ]
        send = (height, width // 2)
        whole = (height, 2 * width)
    return pl.pallas_call(
        cast_rows_kernel if axis == 0 else cast_cols_kernel,
        grid_spec=pltpu.PrefetchScalarGridSpec(
            num_scalar_prefetch=1, grid=(steps,), in_specs=specs[:1], out_specs=specs[1:]
        ),
        out_shape=[
            jax.ShapeDtypeStruct(whole, jnp.bfloat16),
            jax.ShapeDtypeStruct(send, jnp.bfloat16),
        ],
        cost_estimate=pl.CostEstimate(flops=height * width, bytes_accessed=7 * height * width, transcendentals=0),
        name="cast_weight",
    )(place, master)


def settle_kernel(place_ref, mine_ref, theirs_ref, *refs):
    out_ref = refs[-1]

    @pl.when(pl.program_id(0) == 0)
    def _():
        out_ref[...] = f32(mine_ref[...])

    @pl.when(pl.program_id(0) == 1)
    def _():
        out_ref[...] = f32(theirs_ref[...])


def settle(place, mine, theirs, shape, axis, offset, dest=None):
    rows, width = SEG, mine.shape[1]
    steps = mine.shape[0] // rows
    first = offset // rows
    per_core = shape[0] // 2 // rows

    def whose(turn, place_ref):
        return place_ref[3] + turn - 2 * place_ref[3] * turn

    def out_at(turn, at, place_ref):
        if axis == 0:
            return (whose(turn, place_ref) * per_core + first + at, 0)
        return (first + at, whose(turn, place_ref))

    in_specs = [
        pl.BlockSpec((rows, width), lambda turn, at, place_ref: (jnp.where(turn == 0, at, steps - 1), 0)),
        pl.BlockSpec((rows, width), lambda turn, at, place_ref: (jnp.where(turn == 0, 0, at), 0)),
    ]
    operands = [place, mine, theirs]
    aliases = {}
    if dest is not None:
        in_specs.append(pl.BlockSpec(memory_space=pl.ANY))
        operands.append(dest)
        aliases = {3: 0}
    return pl.pallas_call(
        settle_kernel,
        grid_spec=pltpu.PrefetchScalarGridSpec(
            num_scalar_prefetch=1,
            grid=(2, steps),
            in_specs=in_specs,
            out_specs=pl.BlockSpec((rows, width), out_at),
        ),
        out_shape=jax.ShapeDtypeStruct(shape, jnp.float32),
        input_output_aliases=aliases,
        cost_estimate=pl.CostEstimate(flops=0, bytes_accessed=12 * mine.size, transcendentals=0),
        name="settle",
    )(*operands)


def row_block(rows, width):
    return pl.BlockSpec((rows, width), lambda at, *_: (at, 0))


def split_heads(mixed, tables):
    count, width = mixed.shape
    rows = SEG
    return pl.pallas_call(
        split_kernel,
        grid=(count // rows,),
        in_specs=[row_block(rows, width)] + [row_block(rows, 2 * HD)] * 3,
        out_specs=[row_block(rows, width // 3), row_block(rows, 2 * width // 3)],
        out_shape=[
            jax.ShapeDtypeStruct((count, width // 3), jnp.bfloat16),
            jax.ShapeDtypeStruct((count, 2 * width // 3), jnp.bfloat16),
        ],
        cost_estimate=pl.CostEstimate(flops=20 * count * width, bytes_accessed=8 * count * width, transcendentals=0),
        name="split_heads",
    )(mixed, *tables)


def join_heads(row, dq, dkv, sent, tables):
    count, half = dq.shape
    rows = SEG
    return pl.pallas_call(
        join_kernel,
        grid_spec=pltpu.PrefetchScalarGridSpec(
            num_scalar_prefetch=1,
            grid=(count // rows,),
            in_specs=[row_block(rows, half), row_block(rows, 2 * half), row_block(rows, 2 * half)]
            + [row_block(rows, 2 * HD)] * 3,
            out_specs=row_block(rows, 3 * half),
        ),
        out_shape=jax.ShapeDtypeStruct((count, 3 * half), jnp.bfloat16),
        cost_estimate=pl.CostEstimate(flops=60 * count * half, bytes_accessed=24 * count * half, transcendentals=0),
        name="join_heads",
    )(row, dq, dkv, sent, *tables)


def tree_attention(parents, row, query, keyval, trunk, grad):
    trees = parents.shape[0]
    count, half = query.shape
    rows = count // trees
    keys = trunk.shape[0] // trees
    pairs = count * (keys + SEG) * (half // HD)
    return pl.pallas_call(
        tree_kernel,
        grid_spec=pltpu.PrefetchScalarGridSpec(
            num_scalar_prefetch=2,
            grid=(trees,),
            in_specs=[
                row_block(rows, half),
                row_block(rows, 2 * half),
                row_block(keys, 2 * half),
                row_block(rows, half),
            ],
            out_specs=[
                row_block(rows, half),
                row_block(rows, half),
                row_block(rows, 2 * half),
                row_block(keys, 2 * half),
            ],
            scratch_shapes=[pltpu.VMEM((keys, half), jnp.bfloat16)] * 2
            + [pltpu.VMEM((keys, half), jnp.float32)] * 2,
        ),
        out_shape=[
            jax.ShapeDtypeStruct((count, half), jnp.bfloat16),
            jax.ShapeDtypeStruct((count, half), jnp.float32),
            jax.ShapeDtypeStruct((count, 2 * half), jnp.float32),
            jax.ShapeDtypeStruct((trees * keys, 2 * half), jnp.bfloat16),
        ],
        cost_estimate=pl.CostEstimate(
            flops=12 * pairs * half, bytes_accessed=20 * count * half, transcendentals=pairs
        ),
        name="tree_attention",
    )(parents, row, query, keyval, trunk, grad)


def paired_device(
    tokens,
    parent,
    depth,
    w_qkv,
    b_qkv,
    w_out,
    w_up,
    b_up,
    w_down,
    b_res,
    ln_gain,
    ln_bias,
    cotangent,
):
    count, width = tokens.shape
    row = lax.axis_index("row")
    col = lax.axis_index("col")
    core = lax.axis_index("dp") % 2
    slab = lax.axis_index("dp") // 2
    cols = lax.axis_size("col")
    half = 2 * width
    heads_width = w_out.shape[0] // 2
    hidden = w_up.shape[1] // 2
    place = jnp.stack([col, row, slab, core]).astype(jnp.int32)
    row_table = jnp.reshape(row, (1,)).astype(jnp.int32)
    down_dims = ((0,), (0,))
    across = ((1,), (1,))

    def part(values, at, size, axis):
        return lax.dynamic_slice_in_dim(values, at * size, size, axis)

    def exchange(stack):
        return lax.all_to_all(stack, "col", 0, 0, tiled=True)

    def to_all(block):
        return exchange(jnp.broadcast_to(block[None], (cols,) + block.shape))

    done = ()

    def step(run, *inputs):
        nonlocal done
        inputs, _ = lax.optimization_barrier((inputs, done))
        result = run(*inputs)
        done = result
        return result

    tokens_near = to_all(tokens)

    def ready(master, axis):
        whole, send = step(lambda weight: cast_weight(place, weight, axis), master)
        return whole, swap_row(send)

    qkv_whole, qkv_row = ready(w_qkv, 0)
    up_whole, up_row = ready(w_up, 0)
    down_whole, down_row = ready(w_down, 1)
    out_whole, out_row = ready(w_out, 1)

    def fill(whole, by_row, axis):
        by_x = swap_x(by_row)
        start = whole.shape[axis] // 2
        whole = lax.dynamic_update_slice_in_dim(whole, by_row, start, axis)
        return lax.dynamic_update_slice_in_dim(whole, by_x, start + by_row.shape[axis], axis)

    tables = jnp.concatenate([parent, depth], axis=0)
    tables = jnp.stack([tables, swap_core(tables)])
    parents = tables[:, 0]
    segs = count // SEG
    token = jnp.arange(count, dtype=jnp.int32)
    levels = jnp.zeros((2, count), jnp.float32)
    for seg in range(segs):
        level = lax.dynamic_slice_in_dim(tables[:, 1], row * segs + seg, 1, 1).astype(jnp.float32)
        levels = jnp.where((token // SEG == seg)[None, :], level, levels)
    positions = (levels * SEG + (token % SEG).astype(jnp.float32)[None, :]).reshape(2 * count)
    rotary = rotary_tables(positions)

    grad_near = to_all(after(cotangent, tokens_near))
    normed, normed_plain, normal, inv_scale = step(
        lambda mine, theirs: gathered(place, mine, theirs, (ln_gain, ln_bias)),
        tokens_near,
        swap_core(tokens_near),
    )
    normed_own = normed[:, :half]

    qkv_full = fill(qkv_whole, qkv_row, 0)
    mixed = step(
        lambda left, right: matmul(left, right) + part(b_qkv, core, 3 * heads_width, 0), normed, qkv_full
    )
    query, keyval = step(lambda values: split_heads(values, rotary), mixed)
    trunk = lax.ppermute(keyval, "row", [(0, 1)])
    root = math.sqrt(2.0 / math.pi)

    def feed(left, right):
        hidden_up = matmul(left, right) + part(b_up, core, hidden, 0)
        squared = hidden_up * hidden_up
        bend = jnp.tanh(root * (hidden_up + 0.044715 * squared * hidden_up))
        return bf16(0.5 * hidden_up * (1.0 + bend)), bf16(
            0.5 * (1.0 + bend)
            + 0.5 * hidden_up * (1.0 - bend * bend) * root * (1.0 + 3.0 * 0.044715 * squared)
        )

    up_full = fill(up_whole, up_row, 0)
    activated, slope = step(feed, normed, up_full)
    down_full = fill(down_whole, down_row, 1)
    out_full = fill(out_whole, out_row, 1)

    grad, grad_plain = step(
        lambda mine, theirs: gathered(place, mine, theirs), grad_near, swap_core(grad_near)
    )
    grad_own = grad[:, :half]

    def cut(values, at):
        size = values.shape[1] // 2
        return values[:, at * size : (at + 1) * size]

    def leaving(left, right):
        return step(lambda a, b: bf16(matmul(a, b, down_dims)), left, right)

    def staying(left, right, sent):
        return step(lambda a, b, c: bf16(matmul(a, b, down_dims) + f32(c)), left, right, sent)

    def crossed(both, arrived):
        mine = step(lambda a, b: bf16(f32(a) + f32(b)), both, arrived)
        return mine, swap_core(mine)

    def settled(pieces, shape, axis, offset, dest):
        operands = pieces if dest is None else pieces + (dest,)
        return step(
            lambda mine, theirs, *rest: settle(place, mine, theirs, shape, axis, offset, *rest), *operands
        )

    down_sent_a = swap_row(leaving(cut(activated, 0), grad_plain))
    down_sent_b = swap_row(leaving(cut(activated, 1), grad_plain))
    out_heads = step(lambda a, b: bf16(matmul(a, b, across)), grad, out_full)
    attended, query_grad, own_grad, trunk_grad = step(
        lambda *operands: tree_attention(parents, row_table, *operands), query, keyval, trunk, out_heads
    )
    trunk_sent = lax.ppermute(trunk_grad, "row", [(1, 0)])
    down_both_a = staying(cut(activated, 0), grad_own, down_sent_a)
    down_cross_a = swap_x(down_both_a)
    up_grad = step(lambda a, b, c: bf16(matmul(a, b, across) * f32(c)), grad, down_full, slope)
    up_sent_a = swap_row(leaving(cut(normed_plain, 0), up_grad))
    down_both_b = staying(cut(activated, 1), grad_own, down_sent_b)
    down_cross_b = swap_x(down_both_b)
    up_sent_b = swap_row(leaving(cut(normed_plain, 1), up_grad))
    out_sent = swap_row(leaving(attended, grad_plain))
    down_a = crossed(down_both_a, down_cross_a)
    branch_terms = step(
        lambda a, b, c, d: matmul(a, b) + matmul(c, d), attended, out_full, activated, down_full
    )
    branch_near = swap_core(step(bf16, branch_terms[count:]))
    mixed_grad = step(
        lambda *operands: join_heads(row_table, *operands, rotary), query_grad, own_grad, trunk_sent
    )
    qkv_sent_a = swap_row(leaving(cut(normed_plain, 0), mixed_grad))
    qkv_sent_b = swap_row(leaving(cut(normed_plain, 1), mixed_grad))
    branch_parts = exchange(step(lambda a, b: stacked(place, a, b, cols), branch_terms, branch_near))
    down_b = crossed(down_both_b, down_cross_b)
    norm_terms = step(
        lambda a, b, c, d: matmul(a, b, across) + matmul(c, d, across),
        mixed_grad, qkv_full, up_grad, up_full,
    )
    norm_near = swap_core(step(bf16, norm_terms[count:]))
    up_both_a = staying(cut(normed_own, 0), up_grad, up_sent_a)
    up_cross_a = swap_x(up_both_a)
    norm_parts = exchange(step(lambda a, b: stacked(place, a, b, cols), norm_terms, norm_near))
    down_grad = settled(down_a, w_down.shape, 0, 0, None)
    down_grad = settled(down_b, w_down.shape, 0, down_both_a.shape[0], down_grad)
    output = step(
        lambda parts, block: bf16(f32(block) + jnp.sum(f32(parts), axis=0) + b_res), branch_parts, tokens
    )
    up_both_b = staying(cut(normed_own, 1), up_grad, up_sent_b)
    up_cross_b = swap_x(up_both_b)
    norm_grad = step(lambda parts: jnp.sum(f32(parts), axis=0), norm_parts)
    scaled = norm_grad * part(ln_gain, col, width, 0)
    sums = jnp.stack([jnp.sum(scaled, axis=1), jnp.sum(scaled * normal, axis=1)])
    for bit in (1, 2):
        sums = sums + lax.ppermute(sums, "col", [(at, at ^ bit) for at in range(cols)])
    up_a = crossed(up_both_a, up_cross_a)
    out_both = staying(attended, grad_own, out_sent)
    out_cross = swap_x(out_both)
    sums = sums / (cols * width)
    tokens_grad = step(
        lambda sums, values: inv_scale
        * (values - sums[0][:, None] - normal * sums[1][:, None])
        + f32(cotangent),
        sums, scaled,
    )
    small = jnp.concatenate(
        [
            jnp.sum(f32(up_grad), axis=0),
            jnp.sum(f32(mixed_grad), axis=0),
            jnp.sum(f32(cotangent), axis=0),
            jnp.sum(norm_grad * normal, axis=0),
            jnp.sum(norm_grad, axis=0),
        ]
    ).reshape(-1, 128)
    shared_at = (hidden + 3 * heads_width) // 128
    small_other = swap_core(small)
    shared = (small + small_other)[shared_at:]
    res_at = width // 128
    ends = shared[res_at:][None]
    for bit in (1, 2):
        ends = pair((col // bit) % 2, ends, lax.ppermute(ends, "col", [(at, at ^ bit) for at in range(cols)]), 0)
    small = jnp.concatenate(
        [
            pair(core, small[: hidden // 128], small_other[: hidden // 128], 0),
            pair(core, small[hidden // 128 : shared_at], small_other[hidden // 128 : shared_at], 0),
            shared[:res_at],
            ends.reshape(-1, 128),
        ]
    )
    up_grad_weight = settled(up_a, w_up.shape, 1, 0, None)
    qkv_both_a = staying(cut(normed_own, 0), mixed_grad, qkv_sent_a)
    qkv_cross_a = swap_x(qkv_both_a)
    up_b = crossed(up_both_b, up_cross_b)
    small = small + swap_row(small)
    qkv_both_b = staying(cut(normed_own, 1), mixed_grad, qkv_sent_b)
    qkv_cross_b = swap_x(qkv_both_b)
    out_mine = crossed(out_both, out_cross)
    up_weight_grad = settled(up_b, w_up.shape, 1, up_both_a.shape[0], up_grad_weight)
    out_grad = settled(out_mine, w_out.shape, 0, 0, None)
    qkv_a = crossed(qkv_both_a, qkv_cross_a)
    qkv_weight_grad = settled(qkv_a, w_qkv.shape, 1, 0, None)
    small = step(jnp.add, small, swap_x(small))
    qkv_b = crossed(qkv_both_b, qkv_cross_b)
    qkv_weight_grad = settled(qkv_b, w_qkv.shape, 1, qkv_both_a.shape[0], qkv_weight_grad)

    bounds = [0, 2 * hidden // 128, (2 * hidden + 6 * heads_width) // 128]
    bounds.append(bounds[-1] + res_at)
    up_bias_grad = small[: bounds[1]].reshape(-1)
    qkv_bias_grad = small[bounds[1] : bounds[2]].reshape(-1)
    res_bias_grad = small[bounds[2] : bounds[3]].reshape(-1)
    ends = small[bounds[3] :].reshape(cols, 2, width)
    gain_grad = ends[:, 0].reshape(-1)
    shift_grad = ends[:, 1].reshape(-1)
    return (
        output,
        tokens_grad,
        qkv_weight_grad,
        qkv_bias_grad,
        out_grad,
        up_weight_grad,
        up_bias_grad,
        down_grad,
        res_bias_grad,
        gain_grad,
        shift_grad,
    )


def solution(mesh):
    sizes = (mesh.shape["dp"], mesh.shape["row"], mesh.shape["col"])
    per_device = paired_device if sizes == (4, 2, 4) else general_device
    return jax.shard_map(
        per_device,
        mesh=mesh,
        in_specs=(
            P(("dp", "row"), "col"),
            P("dp", None),
            P("dp", None),
            P("row", "col"),
            P("col"),
            P("col", "row"),
            P("row", "col"),
            P("col"),
            P("col", "row"),
            P("col"),
            P(),
            P(),
            P(("dp", "row"), "col"),
        ),
        out_specs=(
            P(("dp", "row"), "col"),
            P(("dp", "row"), "col"),
            P("row", "col"),
            P("col"),
            P("col", "row"),
            P("row", "col"),
            P("col"),
            P("col", "row"),
            P("col"),
            P(),
            P(),
        ),
        check_vma=False,
    )
```

```python
import functools
import math

import jax
import jax.numpy as jnp
from jax import lax
from jax.experimental import pallas as pl
from jax.experimental.pallas import tpu as pltpu
from jax.sharding import PartitionSpec as P

HD = 64
ROT = 32
SEG = 256


norm_epsilon = 1e-05
masked_fill = -1e30
rotary_base = 10000.0


def precise_dot(left, right):
    return jnp.dot(left, right, precision=lax.Precision.HIGHEST, preferred_element_type=jnp.float32)


def ancestry(parent_row):
    seg_count = parent_row.shape[0]
    labels = jnp.arange(seg_count, dtype=jnp.int32)
    identity = jnp.eye(seg_count, dtype=jnp.float32)
    parent_hot = (parent_row[:, None] == labels[None, :]).astype(jnp.float32)

    def extend(rounds, reachable):
        return jnp.minimum(identity + precise_dot(parent_hot, reachable), 1.0)

    return lax.fori_loop(0, seg_count, extend, identity)


def rotate(values, cosines, sines):
    half_rot = ROT // 2
    former = values[..., :half_rot]
    latter = values[..., half_rot:ROT]
    return jnp.concatenate(
        [former * cosines - latter * sines, latter * cosines + former * sines, values[..., ROT:]],
        axis=-1,
    )


def angles_of(positions):
    frequency = jnp.exp(
        -math.log(rotary_base) * 2.0 * jnp.arange(ROT // 2, dtype=jnp.float32) / ROT
    )
    phase_angle = positions[:, None] * frequency[None, :]
    return (jnp.cos(phase_angle)[:, None, :], jnp.sin(phase_angle)[:, None, :])


def reorder_rows(gradient, row_count, dp_count):
    leading = gradient.shape[0]
    blocked = gradient.reshape(
        row_count, dp_count, leading // (row_count * dp_count), gradient.shape[1]
    )
    return jnp.transpose(blocked, (1, 0, 2, 3)).reshape(leading, gradient.shape[1])


def reorder_cols(gradient, row_count, dp_count):
    trailing = gradient.shape[1]
    blocked = gradient.reshape(
        gradient.shape[0], row_count, dp_count, trailing // (row_count * dp_count)
    )
    return jnp.transpose(blocked, (0, 2, 1, 3)).reshape(gradient.shape[0], trailing)


def general_device(
    tokens,
    parent,
    depth,
    w_qkv,
    b_qkv,
    w_out,
    w_up,
    b_up,
    w_down,
    b_res,
    ln_gain,
    ln_bias,
    cotangent,
):
    tok_rows = tokens.shape[0]
    col_width = tokens.shape[1]
    row_count = lax.axis_size("row")
    dp_count = lax.axis_size("dp")
    row_start = lax.axis_index("row") * tok_rows
    local_heads = w_out.shape[0] // HD
    seg_count = parent.shape[1]
    labels = jnp.arange(seg_count, dtype=jnp.int32)
    reachable = ancestry(parent[0])
    query_index = row_start + jnp.arange(tok_rows, dtype=jnp.int32)
    query_seg = query_index // SEG
    query_hot = (query_seg[:, None] == labels[None, :]).astype(jnp.float32)
    query_reach = precise_dot(query_hot, reachable)
    levels = precise_dot(query_hot, depth[0].astype(jnp.float32)[:, None])[:, 0]
    positions = levels * SEG + (query_index % SEG).astype(jnp.float32)
    cosines, sines = angles_of(positions)
    score_scale = HD ** (-0.5)

    def permit(key_len):
        key_index = jnp.arange(key_len, dtype=jnp.int32)
        key_seg = key_index // SEG
        key_hot = (key_seg[:, None] == labels[None, :]).astype(jnp.float32)
        linked = precise_dot(query_reach, key_hot.T) > 0.5
        return linked & (
            (query_seg[:, None] != key_seg[None, :]) | (query_index[:, None] >= key_index[None, :])
        )

    whole = lax.all_gather(tokens, "col", axis=1, tiled=True).astype(jnp.float32)
    centred = whole - jnp.mean(whole, axis=1, keepdims=True)
    inv_scale = lax.rsqrt(jnp.mean(centred * centred, axis=1, keepdims=True) + norm_epsilon)
    normal = centred * inv_scale
    normed = (normal * ln_gain + ln_bias).astype(jnp.bfloat16)
    qkv_full, up_full, out_full, down_full = (
        lax.all_gather(w_qkv.astype(jnp.bfloat16), "row", axis=0, tiled=True),
        lax.all_gather(w_up.astype(jnp.bfloat16), "row", axis=0, tiled=True),
        lax.all_gather(w_out.astype(jnp.bfloat16), "row", axis=1, tiled=True),
        lax.all_gather(w_down.astype(jnp.bfloat16), "row", axis=1, tiled=True),
    )
    mixed = (jnp.dot(normed, qkv_full, preferred_element_type=jnp.float32) + b_qkv).reshape(
        tok_rows, local_heads, 3, HD
    )

    def rotate_pair(query_pre, key_pre):
        return (rotate(query_pre, cosines, sines), rotate(key_pre, cosines, sines))

    rotated, rotate_back = jax.vjp(rotate_pair, mixed[:, :, 0], mixed[:, :, 1])
    queries = rotated[0].astype(jnp.bfloat16)
    key_rows = rotated[1].astype(jnp.bfloat16)
    value_rows = mixed[:, :, 2].astype(jnp.bfloat16)
    key_flat = key_rows.reshape(tok_rows, local_heads * HD)
    value_flat = value_rows.reshape(tok_rows, local_heads * HD)

    def scores_for(key_part):
        raw_scores = (
            jnp.einsum("qhe,khe->hqk", queries, key_part, preferred_element_type=jnp.float32)
            * score_scale
        )
        allowed = permit(key_part.shape[0])
        return (jnp.where(allowed[None], raw_scores, masked_fill), allowed)

    pieces = (
        lax.all_gather(key_flat, "row", axis=0, tiled=True),
        lax.all_gather(value_flat, "row", axis=0, tiled=True),
    )
    running_top = jnp.full((local_heads, tok_rows), masked_fill, jnp.float32)
    key_len = pieces[0].shape[0]
    key_part = pieces[0].reshape(key_len, local_heads, HD)
    value_part = pieces[1].reshape(key_len, local_heads, HD)
    scores, allowed = scores_for(key_part)
    new_top = jnp.maximum(running_top, jnp.max(scores, axis=2))
    exponent = jnp.where(allowed[None], jnp.exp(scores - new_top[:, :, None]), 0.0)
    running_sum = jnp.sum(exponent, axis=2)
    weighted = jnp.einsum(
        "hqk,khe->hqe",
        exponent.astype(jnp.bfloat16),
        value_part,
        preferred_element_type=jnp.float32,
    )
    running_top, running_sum, weighted = (new_top, running_sum, weighted)
    log_total = running_top + jnp.log(running_sum)
    attn_exact = weighted / running_sum[:, :, None]
    attended = (
        jnp.transpose(attn_exact, (1, 0, 2))
        .reshape(tok_rows, local_heads * HD)
        .astype(jnp.bfloat16)
    )
    hidden_up = jnp.dot(normed, up_full, preferred_element_type=jnp.float32) + b_up
    activated, gelu_back = jax.vjp(functools.partial(jax.nn.gelu, approximate=True), hidden_up)
    activated = activated.astype(jnp.bfloat16)
    branch_terms = jnp.dot(attended, out_full, preferred_element_type=jnp.float32) + jnp.dot(
        activated, down_full, preferred_element_type=jnp.float32
    )
    branch = lax.psum_scatter(
        branch_terms.astype(jnp.bfloat16), "col", scatter_dimension=1, tiled=True
    ).astype(jnp.float32)
    output = (tokens.astype(jnp.float32) + branch + b_res).astype(jnp.bfloat16)
    grad_full = lax.all_gather(cotangent, "col", axis=1, tiled=True)
    res_bias_grad = jnp.sum(cotangent.astype(jnp.float32), axis=0)
    down_grad = jnp.einsum("tf,td->fd", activated, grad_full, preferred_element_type=jnp.float32)
    out_grad = jnp.einsum("te,td->ed", attended, grad_full, preferred_element_type=jnp.float32)
    act_grad = jnp.einsum("td,fd->tf", grad_full, down_full, preferred_element_type=jnp.float32)
    up_grad = gelu_back(act_grad)[0].astype(jnp.bfloat16)
    attn_grad = jnp.einsum(
        "td,ed->te", grad_full, out_full, preferred_element_type=jnp.float32
    ).astype(jnp.bfloat16)
    up_bias_grad = jnp.sum(up_grad.astype(jnp.float32), axis=0)
    up_weight_grad = jnp.einsum("td,tf->df", normed, up_grad, preferred_element_type=jnp.float32)
    out_heads = attn_grad.reshape(tok_rows, local_heads, HD)
    delta_sum = jnp.einsum("qhe,hqe->hq", out_heads.astype(jnp.float32), attn_exact)
    pieces = (
        lax.all_gather(key_flat, "row", axis=0, tiled=True),
        lax.all_gather(value_flat, "row", axis=0, tiled=True),
    )
    key_len = pieces[0].shape[0]
    key_part = pieces[0].reshape(key_len, local_heads, HD)
    value_part = pieces[1].reshape(key_len, local_heads, HD)
    scores, allowed = scores_for(key_part)
    softmaxed = jnp.where(allowed[None], jnp.exp(scores - log_total[:, :, None]), 0.0)
    prob_grad = jnp.einsum(
        "qhe,khe->hqk", out_heads, value_part, preferred_element_type=jnp.float32
    )
    score_grad = (softmaxed * (prob_grad - delta_sum[:, :, None])).astype(jnp.bfloat16)
    query_grad = (
        jnp.einsum("hqk,khe->qhe", score_grad, key_part, preferred_element_type=jnp.float32)
        * score_scale
    )
    key_grad = (
        jnp.einsum("hqk,qhe->khe", score_grad, queries, preferred_element_type=jnp.float32)
        * score_scale
    )
    value_grad = jnp.einsum(
        "hqk,qhe->khe",
        softmaxed.astype(jnp.bfloat16),
        out_heads,
        preferred_element_type=jnp.float32,
    )
    stacked = jnp.stack([key_grad, value_grad], axis=1).reshape(key_len, 2 * local_heads * HD)
    pair_grad = stacked
    query_grad, pair_grad = (query_grad, pair_grad)
    own_pairs = (
        lax.psum_scatter(pair_grad.astype(jnp.bfloat16), "row", scatter_dimension=0, tiled=True)
        .astype(jnp.float32)
        .reshape(tok_rows, 2, local_heads, HD)
    )
    query_pre, key_pre = rotate_back((query_grad, own_pairs[:, 0]))
    mixed_grad = (
        jnp.stack([query_pre, key_pre, own_pairs[:, 1]], axis=2)
        .reshape(tok_rows, 3 * local_heads * HD)
        .astype(jnp.bfloat16)
    )
    qkv_bias_grad = jnp.sum(mixed_grad.astype(jnp.float32), axis=0)
    qkv_weight_grad = jnp.einsum(
        "td,tc->dc", normed, mixed_grad, preferred_element_type=jnp.float32
    )
    norm_part = jnp.einsum(
        "tc,dc->td", mixed_grad, qkv_full, preferred_element_type=jnp.float32
    ) + jnp.einsum("tf,df->td", up_grad, up_full, preferred_element_type=jnp.float32)
    norm_grad = lax.psum(norm_part.astype(jnp.bfloat16), "col").astype(jnp.float32)
    gain_grad = jnp.sum(norm_grad * normal, axis=0)
    shift_grad = jnp.sum(norm_grad, axis=0)
    scaled = norm_grad * ln_gain
    mean_scaled = jnp.mean(scaled, axis=1, keepdims=True)
    mean_mixed = jnp.mean(scaled * normal, axis=1, keepdims=True)
    col_start = lax.axis_index("col") * col_width
    scaled_share = lax.dynamic_slice_in_dim(scaled, col_start, col_width, 1)
    normal_share = lax.dynamic_slice_in_dim(normal, col_start, col_width, 1)
    tokens_grad = inv_scale * (
        scaled_share - mean_scaled - normal_share * mean_mixed
    ) + cotangent.astype(jnp.float32)
    qkv_bias_grad, up_bias_grad, res_bias_grad, gain_grad, shift_grad = (
        lax.psum(qkv_bias_grad.astype(jnp.bfloat16), ("dp", "row")).astype(jnp.float32),
        lax.psum(up_bias_grad.astype(jnp.bfloat16), ("dp", "row")).astype(jnp.float32),
        lax.psum(res_bias_grad.astype(jnp.bfloat16), ("dp", "row")).astype(jnp.float32),
        lax.psum(gain_grad.astype(jnp.bfloat16), ("dp", "row")).astype(jnp.float32),
        lax.psum(shift_grad.astype(jnp.bfloat16), ("dp", "row")).astype(jnp.float32),
    )
    pieces_now = (
        lax.psum_scatter(
            reorder_rows(qkv_weight_grad, row_count, dp_count).astype(jnp.bfloat16),
            ("dp", "row"),
            scatter_dimension=0,
            tiled=True,
        ).astype(jnp.float32),
        lax.psum_scatter(
            reorder_rows(up_weight_grad, row_count, dp_count).astype(jnp.bfloat16),
            ("dp", "row"),
            scatter_dimension=0,
            tiled=True,
        ).astype(jnp.float32),
        lax.psum_scatter(
            reorder_cols(out_grad, row_count, dp_count).astype(jnp.bfloat16),
            ("dp", "row"),
            scatter_dimension=1,
            tiled=True,
        ).astype(jnp.float32),
        lax.psum_scatter(
            reorder_cols(down_grad, row_count, dp_count).astype(jnp.bfloat16),
            ("dp", "row"),
            scatter_dimension=1,
            tiled=True,
        ).astype(jnp.float32),
    )
    qkv_weight_grad, up_weight_grad, out_grad, down_grad = (
        lax.all_gather(pieces_now[0].astype(jnp.bfloat16), "dp", axis=0, tiled=True).astype(
            jnp.float32
        ),
        lax.all_gather(pieces_now[1].astype(jnp.bfloat16), "dp", axis=0, tiled=True).astype(
            jnp.float32
        ),
        lax.all_gather(pieces_now[2].astype(jnp.bfloat16), "dp", axis=1, tiled=True).astype(
            jnp.float32
        ),
        lax.all_gather(pieces_now[3].astype(jnp.bfloat16), "dp", axis=1, tiled=True).astype(
            jnp.float32
        ),
    )
    return (
        output,
        tokens_grad,
        qkv_weight_grad,
        qkv_bias_grad,
        out_grad,
        up_weight_grad,
        up_bias_grad,
        down_grad,
        res_bias_grad,
        gain_grad,
        shift_grad,
    )


SWAP_ROW = [(0, 1), (1, 0)]
SWAP_X = [(0, 2), (2, 0), (1, 3), (3, 1)]
SWAP_CORE = [(0, 1), (1, 0), (2, 3), (3, 2)]


def bf16(values):
    return values.astype(jnp.bfloat16)


def f32(values):
    return values.astype(jnp.float32)


def matmul(left, right, dims=((1,), (0,))):
    return lax.dot_general(left, right, (dims, ((), ())), preferred_element_type=jnp.float32)


def swap_row(values):
    return lax.ppermute(values, "row", SWAP_ROW)


def swap_x(values):
    return lax.ppermute(values, "dp", SWAP_X)


def swap_core(values):
    return lax.ppermute(values, "dp", SWAP_CORE)


def pick(index, first, second):
    return jnp.where(index == 0, first, second)


def pair(index, mine, theirs, axis):
    return pick(
        index,
        jnp.concatenate([mine, theirs], axis=axis),
        jnp.concatenate([theirs, mine], axis=axis),
    )


def after(value, *earlier):
    return lax.optimization_barrier((value,) + earlier)[0]


def rotary_tables(positions):
    lane = jnp.arange(2 * HD, dtype=jnp.int32) % HD
    half_rot = ROT // 2
    frequency = jnp.exp(
        -math.log(rotary_base) * 2.0 * (lane % half_rot).astype(jnp.float32) / ROT
    )
    angle = positions[:, None] * frequency[None, :]
    turned = (lane < ROT)[None, :]
    sines = jnp.sin(angle)
    return (
        jnp.where(turned, jnp.cos(angle), 1.0),
        jnp.where((lane < half_rot)[None, :], -sines, 0.0),
        jnp.where(turned & (lane >= half_rot)[None, :], sines, 0.0),
    )


def turn(values, cosines, sines_low, sines_high):
    width = values.shape[1]
    half_rot = ROT // 2
    return (
        values * cosines
        + pltpu.roll(values, width - half_rot, 1) * sines_low
        + pltpu.roll(values, half_rot, 1) * sines_high
    )


def split_kernel(mixed_ref, cos_ref, low_ref, high_ref, query_ref, keyval_ref):
    cosines, low, high = cos_ref[...], low_ref[...], high_ref[...]
    rows = mixed_ref.shape[0]
    half = query_ref.shape[1]
    first = lax.broadcasted_iota(jnp.int32, (rows, 2 * HD), 1) < HD
    scale = HD ** (-0.5)
    for at in range(half // (2 * HD)):
        tiles = [mixed_ref[:, (3 * at + part) * 2 * HD : (3 * at + part + 1) * 2 * HD] for part in range(3)]
        query = jnp.where(first, tiles[0], tiles[1])
        key = jnp.where(first, pltpu.roll(tiles[0], HD, 1), pltpu.roll(tiles[2], HD, 1))
        value = jnp.where(first, tiles[1], tiles[2])
        here = slice(at * 2 * HD, (at + 1) * 2 * HD)
        query_ref[:, here] = bf16(f32(bf16(turn(query, cosines, low, high))) * scale)
        keyval_ref[:, here] = bf16(turn(key, cosines, low, high))
        keyval_ref[:, half + at * 2 * HD : half + (at + 1) * 2 * HD] = bf16(value)


def join_kernel(row_ref, dq_ref, dkv_ref, sent_ref, cos_ref, low_ref, high_ref, out_ref):
    cosines, low, high = cos_ref[...], -low_ref[...], -high_ref[...]
    rows = dq_ref.shape[0]
    half = dq_ref.shape[1]
    first = lax.broadcasted_iota(jnp.int32, (rows, 2 * HD), 1) < HD
    owner = row_ref[0] == 0
    for at in range(half // (2 * HD)):
        here = slice(at * 2 * HD, (at + 1) * 2 * HD)
        there = slice(half + at * 2 * HD, half + (at + 1) * 2 * HD)
        query = turn(dq_ref[:, here], cosines, low, high)
        key = dkv_ref[:, here] + jnp.where(owner, f32(sent_ref[:, here]), 0.0)
        value = dkv_ref[:, there] + jnp.where(owner, f32(sent_ref[:, there]), 0.0)
        key = pltpu.roll(turn(key, cosines, low, high), HD, 1)
        tiles = (jnp.where(first, query, key), jnp.where(first, value, query), jnp.where(first, key, value))
        for part in range(3):
            out_ref[:, (3 * at + part) * 2 * HD : (3 * at + part + 1) * 2 * HD] = bf16(tiles[part])


def tree_kernel(
    parent_ref, row_ref, query_ref, keyval_ref, trunk_ref, grad_ref,
    out_ref, dq_ref, dkv_ref, dtrunk_ref,
    keys, values, dkeys, dvalues,
):
    tree = pl.program_id(0)
    row = row_ref[0]
    rows, half = query_ref.shape
    trunk_len = trunk_ref.shape[0]
    segs = rows // SEG
    trunk_segs = trunk_len // SEG
    seg_count = parent_ref.shape[1]
    first_row = row == 0
    keys[...] = jnp.where(first_row, keyval_ref[:, :half], trunk_ref[:, :half])
    values[...] = jnp.where(first_row, keyval_ref[:, half:], trunk_ref[:, half:])
    dkeys[...] = jnp.zeros_like(dkeys)
    dvalues[...] = jnp.zeros_like(dvalues)
    lane = lax.broadcasted_iota(jnp.int32, (1, half), 1)
    causal = lax.broadcasted_iota(jnp.int32, (SEG, SEG), 0) >= lax.broadcasted_iota(
        jnp.int32, (SEG, SEG), 1
    )
    across = ((1,), (1,))
    down = ((0,), (0,))
    for seg in range(segs):
        here = slice(seg * SEG, (seg + 1) * SEG)
        above = parent_ref[tree, row * segs + seg]
        linked = [above == at for at in range(trunk_segs)]
        for _ in range(seg_count - 2):
            above = jnp.where(above >= 0, parent_ref[tree, jnp.maximum(above, 0)], -1)
            linked = [was | (above == at) for at, was in enumerate(linked)]
        bias = [jnp.where(is_linked, 0.0, masked_fill) for is_linked in linked]
        query, grad = query_ref[here, :], grad_ref[here, :]
        own_key, own_value = keyval_ref[here, :half], keyval_ref[here, half:]
        attended = jnp.zeros((SEG, half), jnp.float32)
        dquery = jnp.zeros((SEG, half), jnp.float32)
        dkey = jnp.zeros((SEG, half), jnp.float32)
        dvalue = jnp.zeros((SEG, half), jnp.float32)
        for head in range(half // HD):
            mine = (lane >= head * HD) & (lane < (head + 1) * HD)
            head_query = jnp.where(mine, query, jnp.zeros_like(query))
            head_grad = jnp.where(mine, grad, jnp.zeros_like(grad))
            scores = [
                matmul(head_query, keys[at * SEG : (at + 1) * SEG, :], across) + bias[at]
                for at in range(trunk_segs)
            ] + [jnp.where(causal, matmul(head_query, own_key, across), masked_fill)]
            top = functools.reduce(jnp.maximum, [jnp.max(s, axis=1, keepdims=True) for s in scores])
            powers = [jnp.exp(s - top) for s in scores]
            total = functools.reduce(jnp.add, [jnp.sum(p, axis=1, keepdims=True) for p in powers])
            probs = [p / total for p in powers]
            low = [bf16(p) for p in probs]
            blocks = [values[at * SEG : (at + 1) * SEG, :] for at in range(trunk_segs)] + [own_value]
            prob_grads = [matmul(head_grad, v, across) for v in blocks]
            delta = functools.reduce(
                jnp.add, [jnp.sum(p * g, axis=1, keepdims=True) for p, g in zip(probs, prob_grads)]
            )
            score_grads = [bf16(p * (g - delta)) for p, g in zip(probs, prob_grads)]
            head_out = functools.reduce(jnp.add, [matmul(p, v) for p, v in zip(low, blocks)])
            attended = jnp.where(mine, head_out, attended)
            key_blocks = [keys[at * SEG : (at + 1) * SEG, :] for at in range(trunk_segs)] + [own_key]
            head_dq = functools.reduce(jnp.add, [matmul(s, u) for s, u in zip(score_grads, key_blocks)])
            dquery = jnp.where(mine, head_dq, dquery)
            dkey = dkey + matmul(score_grads[-1], head_query, down)
            dvalue = dvalue + matmul(low[-1], head_grad, down)
            for at in range(trunk_segs):
                spot = slice(at * SEG, (at + 1) * SEG)
                dkeys[spot, :] += matmul(score_grads[at], head_query, down)
                dvalues[spot, :] += matmul(low[at], head_grad, down)
        out_ref[here, :] = bf16(attended)
        dq_ref[here, :] = dquery * HD ** (-0.5)
        dkv_ref[here, :half] = dkey
        dkv_ref[here, half:] = dvalue
    dtrunk_ref[:, :half] = bf16(dkeys[...])
    dtrunk_ref[:, half:] = bf16(dvalues[...])

    @pl.when(first_row)
    def _():
        dkv_ref[:, :half] += dkeys[...]
        dkv_ref[:, half:] += dvalues[...]


def store_blocks(place_ref, sides, full_ref, plain_ref):
    row, slab = place_ref[1], place_ref[2]
    for side, values in enumerate(sides):
        width = values[0].shape[1]
        for source, value in enumerate(values):
            within = source % 2
            here = row == source // 2

            @pl.when(here)
            def _():
                full_ref[side, :, within * width : (within + 1) * width] = value

            @pl.when(jnp.logical_not(here))
            def _():
                plain_ref[side, :, within * width : (within + 1) * width] = value
                at = (2 + jnp.where(slab == 0, within, 1 - within)) * width
                full_ref[side, :, pl.ds(pl.multiple_of(at, width), width)] = value


def gather_kernel(place_ref, mine_ref, theirs_ref, full_ref, plain_ref):
    sides = [[ref[at] for at in range(ref.shape[0])] for ref in (mine_ref, theirs_ref)]
    store_blocks(place_ref, sides, full_ref, plain_ref)


def norm_kernel(
    place_ref, gain_ref, bias_ref, mine_ref, theirs_ref, full_ref, plain_ref, normal_ref, scale_ref
):
    sides = []
    for side, ref in enumerate((mine_ref, theirs_ref)):
        values = [f32(ref[at]) for at in range(ref.shape[0])]
        features = len(values) * values[0].shape[1]
        mean = functools.reduce(jnp.add, [jnp.sum(v, axis=1, keepdims=True) for v in values]) / features
        centred = [v - mean for v in values]
        square = functools.reduce(jnp.add, [jnp.sum(v * v, axis=1, keepdims=True) for v in centred])
        inv_scale = lax.rsqrt(square / features + norm_epsilon)
        normals = [v * inv_scale for v in centred]
        if side == 0:
            scale_ref[...] = inv_scale
            for source, normal in enumerate(normals):

                @pl.when(place_ref[0] == source)
                def _():
                    normal_ref[...] = normal

        sides.append(
            [
                bf16(normal * gain_ref[source : source + 1, :] + bias_ref[source : source + 1, :])
                for source, normal in enumerate(normals)
            ]
        )
    store_blocks(place_ref, sides, full_ref, plain_ref)


def pair_rows(rows, width):
    return pl.BlockSpec((2, rows, width), lambda at, *_: (0, at, 0))


def gathered(place, mine, theirs, norm=None):
    blocks, count, width = mine.shape
    rows = SEG // 2
    full = blocks * width
    in_specs = [pl.BlockSpec((blocks, rows, width), lambda at, *_: (0, at, 0))] * 2
    out_specs = [pair_rows(rows, full), pair_rows(rows, full // 2)]
    out_shape = [
        jax.ShapeDtypeStruct((2, count, full), jnp.bfloat16),
        jax.ShapeDtypeStruct((2, count, full // 2), jnp.bfloat16),
    ]
    operands = [mine, theirs]
    if norm is not None:
        gain = [values.reshape(blocks, width) for values in norm]
        operands = gain + operands
        in_specs = [pl.BlockSpec((blocks, width), lambda at, *_: (0, 0))] * 2 + in_specs
        out_specs = out_specs + [row_block(rows, width), row_block(rows, 1)]
        out_shape = out_shape + [
            jax.ShapeDtypeStruct((count, width), jnp.float32),
            jax.ShapeDtypeStruct((count, 1), jnp.float32),
        ]
    results = pl.pallas_call(
        gather_kernel if norm is None else norm_kernel,
        grid_spec=pltpu.PrefetchScalarGridSpec(
            num_scalar_prefetch=1, grid=(count // rows,), in_specs=in_specs, out_specs=out_specs
        ),
        out_shape=out_shape,
        cost_estimate=pl.CostEstimate(flops=1, bytes_accessed=1, transcendentals=0),
        name="join_blocks" if norm is None else "norm_blocks",
    )(place, *operands)
    return [values.reshape(2 * count, -1) for values in results[:2]] + list(results[2:])


def stack_kernel(place_ref, terms_ref, arrived_ref, out_ref):
    row, slab = place_ref[1], place_ref[2]
    width = out_ref.shape[2]
    for spot in range(4):
        here = slice(spot * width, (spot + 1) * width)
        value = bf16(terms_ref[:, here] + f32(arrived_ref[:, here]))
        if spot < 2:
            out_ref[2 * row + spot] = value
        else:
            out_ref[2 * (1 - row) + jnp.where(slab == 0, spot - 2, 3 - spot)] = value


def stacked(place, terms, arrived, blocks):
    count, full = arrived.shape
    rows = SEG // 2
    width = full // blocks
    return pl.pallas_call(
        stack_kernel,
        grid_spec=pltpu.PrefetchScalarGridSpec(
            num_scalar_prefetch=1,
            grid=(count // rows,),
            in_specs=[row_block(rows, full), row_block(rows, full)],
            out_specs=pl.BlockSpec((blocks, rows, width), lambda at, *_: (0, at, 0)),
        ),
        out_shape=jax.ShapeDtypeStruct((blocks, count, width), jnp.bfloat16),
        cost_estimate=pl.CostEstimate(flops=1, bytes_accessed=1, transcendentals=0),
        name="stack_blocks",
    )(place, terms, arrived)


def cast_rows_kernel(place_ref, master_ref, own_ref, send_ref):
    value = bf16(master_ref[...])
    own_ref[...] = value
    half = pl.num_programs(0) // 2

    @pl.when(pl.program_id(0) // half == place_ref[2])
    def _():
        send_ref[...] = value


def cast_cols_kernel(place_ref, master_ref, own_ref, send_ref):
    value = bf16(master_ref[...])
    own_ref[...] = value
    half = value.shape[1] // 2
    send_ref[...] = jnp.where(place_ref[2] == 0, value[:, :half], value[:, half:])


def cast_weight(place, master, axis):
    height, width = master.shape
    rows = SEG
    if axis == 0:
        width = width // 2
        steps = height // rows
        half = steps // 2
        specs = [
            pl.BlockSpec((rows, width), lambda at, place_ref: (at, place_ref[3])),
            pl.BlockSpec((rows, width), lambda at, place_ref: (at, 0)),
            pl.BlockSpec(
                (rows, width), lambda at, place_ref: (jnp.clip(at - half * place_ref[2], 0, half - 1), 0)
            ),
        ]
        send = (height // 2, width)
        whole = (2 * height, width)
    else:
        height = height // 2
        steps = height // rows
        specs = [
            pl.BlockSpec((rows, width), lambda at, place_ref: (at + steps * place_ref[3], 0)),
            pl.BlockSpec((rows, width), lambda at, place_ref: (at, 0)),
            pl.BlockSpec((rows, width // 2), lambda at, place_ref: (at, 0)),
        ]
        send = (height, width // 2)
        whole = (height, 2 * width)
    return pl.pallas_call(
        cast_rows_kernel if axis == 0 else cast_cols_kernel,
        grid_spec=pltpu.PrefetchScalarGridSpec(
            num_scalar_prefetch=1, grid=(steps,), in_specs=specs[:1], out_specs=specs[1:]
        ),
        out_shape=[
            jax.ShapeDtypeStruct(whole, jnp.bfloat16),
            jax.ShapeDtypeStruct(send, jnp.bfloat16),
        ],
        cost_estimate=pl.CostEstimate(flops=1, bytes_accessed=1, transcendentals=0),
        name="cast_weight",
    )(place, master)


def settle_kernel(place_ref, mine_ref, theirs_ref, *refs):
    out_ref = refs[-1]

    @pl.when(pl.program_id(0) == 0)
    def _():
        out_ref[...] = f32(mine_ref[...])

    @pl.when(pl.program_id(0) == 1)
    def _():
        out_ref[...] = f32(theirs_ref[...])


def settle(place, mine, theirs, shape, axis, offset, dest=None):
    rows, width = SEG, mine.shape[1]
    steps = mine.shape[0] // rows
    first = offset // rows
    per_core = shape[0] // 2 // rows

    def whose(turn, place_ref):
        return place_ref[3] + turn - 2 * place_ref[3] * turn

    def out_at(turn, at, place_ref):
        if axis == 0:
            return (whose(turn, place_ref) * per_core + first + at, 0)
        return (first + at, whose(turn, place_ref))

    in_specs = [
        pl.BlockSpec((rows, width), lambda turn, at, place_ref: (jnp.where(turn == 0, at, steps - 1), 0)),
        pl.BlockSpec((rows, width), lambda turn, at, place_ref: (jnp.where(turn == 0, 0, at), 0)),
    ]
    operands = [place, mine, theirs]
    aliases = {}
    if dest is not None:
        in_specs.append(pl.BlockSpec(memory_space=pl.ANY))
        operands.append(dest)
        aliases = {3: 0}
    return pl.pallas_call(
        settle_kernel,
        grid_spec=pltpu.PrefetchScalarGridSpec(
            num_scalar_prefetch=1,
            grid=(2, steps),
            in_specs=in_specs,
            out_specs=pl.BlockSpec((rows, width), out_at),
        ),
        out_shape=jax.ShapeDtypeStruct(shape, jnp.float32),
        input_output_aliases=aliases,
        cost_estimate=pl.CostEstimate(flops=1, bytes_accessed=1, transcendentals=0),
        name="settle",
    )(*operands)


def row_block(rows, width):
    return pl.BlockSpec((rows, width), lambda at, *_: (at, 0))


def split_heads(mixed, tables):
    count, width = mixed.shape
    rows = SEG
    return pl.pallas_call(
        split_kernel,
        grid=(count // rows,),
        in_specs=[row_block(rows, width)] + [row_block(rows, 2 * HD)] * 3,
        out_specs=[row_block(rows, width // 3), row_block(rows, 2 * width // 3)],
        out_shape=[
            jax.ShapeDtypeStruct((count, width // 3), jnp.bfloat16),
            jax.ShapeDtypeStruct((count, 2 * width // 3), jnp.bfloat16),
        ],
        cost_estimate=pl.CostEstimate(flops=1, bytes_accessed=1, transcendentals=0),
        name="split_heads",
    )(mixed, *tables)


def join_heads(row, dq, dkv, sent, tables):
    count, half = dq.shape
    rows = SEG
    return pl.pallas_call(
        join_kernel,
        grid_spec=pltpu.PrefetchScalarGridSpec(
            num_scalar_prefetch=1,
            grid=(count // rows,),
            in_specs=[row_block(rows, half), row_block(rows, 2 * half), row_block(rows, 2 * half)]
            + [row_block(rows, 2 * HD)] * 3,
            out_specs=row_block(rows, 3 * half),
        ),
        out_shape=jax.ShapeDtypeStruct((count, 3 * half), jnp.bfloat16),
        cost_estimate=pl.CostEstimate(flops=1, bytes_accessed=1, transcendentals=0),
        name="join_heads",
    )(row, dq, dkv, sent, *tables)


def tree_attention(parents, row, query, keyval, trunk, grad):
    trees = parents.shape[0]
    count, half = query.shape
    rows = count // trees
    keys = trunk.shape[0] // trees
    pairs = count * (keys + SEG) * (half // HD)
    return pl.pallas_call(
        tree_kernel,
        grid_spec=pltpu.PrefetchScalarGridSpec(
            num_scalar_prefetch=2,
            grid=(trees,),
            in_specs=[
                row_block(rows, half),
                row_block(rows, 2 * half),
                row_block(keys, 2 * half),
                row_block(rows, half),
            ],
            out_specs=[
                row_block(rows, half),
                row_block(rows, half),
                row_block(rows, 2 * half),
                row_block(keys, 2 * half),
            ],
            scratch_shapes=[pltpu.VMEM((keys, half), jnp.bfloat16)] * 2
            + [pltpu.VMEM((keys, half), jnp.float32)] * 2,
        ),
        out_shape=[
            jax.ShapeDtypeStruct((count, half), jnp.bfloat16),
            jax.ShapeDtypeStruct((count, half), jnp.float32),
            jax.ShapeDtypeStruct((count, 2 * half), jnp.float32),
            jax.ShapeDtypeStruct((trees * keys, 2 * half), jnp.bfloat16),
        ],
        cost_estimate=pl.CostEstimate(flops=1, bytes_accessed=1, transcendentals=0),
        name="tree_attention",
    )(parents, row, query, keyval, trunk, grad)


def paired_device(
    tokens,
    parent,
    depth,
    w_qkv,
    b_qkv,
    w_out,
    w_up,
    b_up,
    w_down,
    b_res,
    ln_gain,
    ln_bias,
    cotangent,
):
    count, width = tokens.shape
    row = lax.axis_index("row")
    col = lax.axis_index("col")
    core = lax.axis_index("dp") % 2
    slab = lax.axis_index("dp") // 2
    cols = lax.axis_size("col")
    half = 2 * width
    heads_width = w_out.shape[0] // 2
    hidden = w_up.shape[1] // 2
    place = jnp.stack([col, row, slab, core]).astype(jnp.int32)
    row_table = jnp.reshape(row, (1,)).astype(jnp.int32)
    down_dims = ((0,), (0,))
    across = ((1,), (1,))

    def part(values, at, size, axis):
        return lax.dynamic_slice_in_dim(values, at * size, size, axis)

    def exchange(stack):
        return lax.all_to_all(stack, "col", 0, 0, tiled=True)

    def to_all(block):
        return exchange(jnp.broadcast_to(block[None], (cols,) + block.shape))

    done = ()

    def step(run, *inputs):
        nonlocal done
        inputs, _ = lax.optimization_barrier((inputs, done))
        result = run(*inputs)
        done = result
        return result

    def wait(value):
        return step(lambda arrived: arrived, value)

    tokens_near = to_all(tokens)
    grad_near = lax.all_gather(cotangent, "col", axis=0)

    def ready(master, axis):
        whole, send = step(lambda weight: cast_weight(place, weight, axis), master)
        return whole, swap_row(send)

    def fill(whole, by_row, by_x, axis):
        start = whole.shape[axis] // 2
        whole = lax.dynamic_update_slice_in_dim(whole, by_row, start, axis)
        return lax.dynamic_update_slice_in_dim(whole, by_x, start + by_row.shape[axis], axis)

    tables = jnp.concatenate([parent, depth], axis=0)
    tables = jnp.stack([tables, swap_core(tables)])
    parents = tables[:, 0]
    segs = count // SEG
    token = jnp.arange(count, dtype=jnp.int32)
    levels = jnp.zeros((2, count), jnp.float32)
    for seg in range(segs):
        level = lax.dynamic_slice_in_dim(tables[:, 1], row * segs + seg, 1, 1).astype(jnp.float32)
        levels = jnp.where((token // SEG == seg)[None, :], level, levels)
    positions = (levels * SEG + (token % SEG).astype(jnp.float32)[None, :]).reshape(2 * count)
    rotary = rotary_tables(positions)

    qkv_whole, qkv_row = ready(w_qkv, 0)
    up_whole, up_row = ready(w_up, 0)
    qkv_row = wait(qkv_row)
    qkv_x = swap_x(qkv_row)
    out_whole, out_row = ready(w_out, 1)
    down_whole, down_row = ready(w_down, 1)
    rotary = step(lambda *tables: tables, *rotary)
    up_row = wait(up_row)
    up_x = swap_x(up_row)
    qkv_x = wait(qkv_x)
    tokens_near = wait(tokens_near)
    tokens_far = swap_core(tokens_near)
    out_row = wait(out_row)
    out_x = swap_x(out_row)
    normed, normed_plain, normal, inv_scale = step(
        lambda mine, theirs: gathered(place, mine, theirs, (ln_gain, ln_bias)), tokens_near, tokens_far
    )
    normed_own = normed[:, :half]
    grad_far = swap_core(grad_near)
    qkv_full = step(lambda *parts: fill(*parts, 0), qkv_whole, qkv_row, qkv_x)
    mixed = step(
        lambda left, right: matmul(left, right) + part(b_qkv, core, 3 * heads_width, 0), normed, qkv_full
    )
    query, keyval = step(lambda values: split_heads(values, rotary), mixed)
    trunk = lax.ppermute(keyval, "row", [(0, 1)])
    root = math.sqrt(2.0 / math.pi)

    def feed(left, right):
        hidden_up = matmul(left, right) + part(b_up, core, hidden, 0)
        squared = hidden_up * hidden_up
        bend = jnp.tanh(root * (hidden_up + 0.044715 * squared * hidden_up))
        return bf16(0.5 * hidden_up * (1.0 + bend)), bf16(
            0.5 * (1.0 + bend)
            + 0.5 * hidden_up * (1.0 - bend * bend) * root * (1.0 + 3.0 * 0.044715 * squared)
        )

    up_full = step(lambda *parts: fill(*parts, 0), up_whole, up_row, up_x)
    activated, slope = step(feed, normed, up_full)
    down_row = wait(down_row)
    down_x = swap_x(down_row)
    grad, grad_plain = step(lambda mine, theirs: gathered(place, mine, theirs), grad_near, grad_far)
    grad_own = grad[:, :half]

    def cut(values, at):
        size = values.shape[1] // 2
        return values[:, at * size : (at + 1) * size]

    def leaving(left, right):
        return step(lambda a, b: bf16(matmul(a, b, down_dims)), left, right)

    def staying(left, right, sent):
        return step(lambda a, b, c: bf16(matmul(a, b, down_dims) + f32(c)), left, right, sent)

    def crossed(both, arrived):
        mine = step(lambda a, b: bf16(f32(a) + f32(b)), both, arrived)
        return mine, swap_core(mine)

    def settled(pieces, shape, axis, offset, dest):
        operands = pieces if dest is None else pieces + (dest,)
        return step(
            lambda mine, theirs, *rest: settle(place, mine, theirs, shape, axis, offset, *rest), *operands
        )

    down_sent_a = swap_row(leaving(cut(activated, 0), grad_plain))
    down_sent_b = swap_row(leaving(cut(activated, 1), grad_plain))
    out_full = step(lambda *parts: fill(*parts, 1), out_whole, out_row, out_x)
    out_heads = step(lambda a, b: bf16(matmul(a, b, across)), grad, out_full)
    attended, query_grad, own_grad, trunk_grad = step(
        lambda *operands: tree_attention(parents, row_table, *operands), query, keyval, trunk, out_heads
    )
    trunk_sent = lax.ppermute(trunk_grad, "row", [(1, 0)])
    down_both_a = staying(cut(activated, 0), grad_own, down_sent_a)
    down_cross_a = swap_x(down_both_a)
    down_full = step(lambda *parts: fill(*parts, 1), down_whole, down_row, down_x)
    up_grad = step(lambda a, b, c: bf16(matmul(a, b, across) * f32(c)), grad, down_full, slope)
    up_sent_a = swap_row(leaving(cut(normed_plain, 0), up_grad))
    down_both_b = staying(cut(activated, 1), grad_own, down_sent_b)
    down_cross_b = swap_x(down_both_b)
    up_sent_b = swap_row(leaving(cut(normed_plain, 1), up_grad))
    down_a = crossed(down_both_a, down_cross_a)
    branch_terms = step(
        lambda a, b, c, d: matmul(a, b) + matmul(c, d), attended, out_full, activated, down_full
    )
    down_grad = settled(down_a, w_down.shape, 0, 0, None)
    mixed_grad = step(
        lambda *operands: join_heads(row_table, *operands, rotary), query_grad, own_grad, trunk_sent
    )
    qkv_sent_a = swap_row(leaving(cut(normed_plain, 0), mixed_grad))
    down_b = crossed(down_both_b, down_cross_b)
    qkv_sent_b = swap_row(leaving(cut(normed_plain, 1), mixed_grad))
    down_grad = settled(down_b, w_down.shape, 0, down_both_a.shape[0], down_grad)
    branch_near = swap_core(step(bf16, branch_terms[count:]))
    up_both_a = staying(cut(normed_own, 0), up_grad, up_sent_a)
    up_cross_a = swap_x(up_both_a)
    norm_terms = step(
        lambda a, b, c, d: matmul(a, b, across) + matmul(c, d, across),
        mixed_grad, qkv_full, up_grad, up_full,
    )
    branch_parts = exchange(step(lambda a, b: stacked(place, a, b, cols), branch_terms, branch_near))
    norm_near = swap_core(step(bf16, norm_terms[count:]))
    up_both_b = staying(cut(normed_own, 1), up_grad, up_sent_b)
    up_cross_b = swap_x(up_both_b)
    up_a = crossed(up_both_a, up_cross_a)
    qkv_both_a = staying(cut(normed_own, 0), mixed_grad, qkv_sent_a)
    qkv_cross_a = swap_x(qkv_both_a)
    norm_parts = exchange(step(lambda a, b: stacked(place, a, b, cols), norm_terms, norm_near))
    out_sent = swap_row(leaving(attended, grad_plain))
    up_weight_grad = settled(up_a, w_up.shape, 1, 0, None)
    up_b = crossed(up_both_b, up_cross_b)
    output = step(
        lambda parts, block: bf16(f32(block) + jnp.sum(f32(parts), axis=0) + b_res), branch_parts, tokens
    )
    qkv_both_b = staying(cut(normed_own, 1), mixed_grad, qkv_sent_b)
    qkv_cross_b = swap_x(qkv_both_b)
    up_weight_grad = settled(up_b, w_up.shape, 1, up_both_a.shape[0], up_weight_grad)
    gain_here = part(ln_gain, col, width, 0)

    def norm_sums(parts):
        total = jnp.sum(f32(parts), axis=0)
        scaled = total * gain_here
        return (
            total,
            jnp.stack([jnp.sum(scaled, axis=1), jnp.sum(scaled * normal, axis=1)]),
            jnp.sum(total * normal, axis=0),
            jnp.sum(total, axis=0),
        )

    norm_grad, sums, gain_sum, shift_sum = step(norm_sums, norm_parts)

    def line_step(values, bit):
        return lax.ppermute(values, "col", [(at, at ^ bit) for at in range(cols)])

    small = jnp.concatenate(
        [
            jnp.sum(f32(up_grad), axis=0),
            jnp.sum(f32(mixed_grad), axis=0),
            jnp.sum(f32(cotangent), axis=0),
            gain_sum,
            shift_sum,
        ]
    ).reshape(-1, 128)
    shared_at = (hidden + 3 * heads_width) // 128
    res_at = width // 128
    sums_next = line_step(sums, 1)
    small_other = swap_core(small)
    qkv_a = crossed(qkv_both_a, qkv_cross_a)
    sums, shared = step(
        lambda sums, arrived, small, other: (sums + arrived, (small + other)[shared_at:]),
        sums, sums_next, small, small_other,
    )
    sums_next = line_step(sums, 2)
    ends = shared[res_at:][None]
    ends_next = line_step(ends, 1)
    out_both = staying(attended, grad_own, out_sent)
    out_cross = swap_x(out_both)
    ends = step(lambda ends, arrived: pair(col % 2, ends, arrived, 0), ends, ends_next)
    ends_next = line_step(ends, 2)
    qkv_weight_grad = settled(qkv_a, w_qkv.shape, 1, 0, None)
    sums = (sums + sums_next) / (cols * width)
    tokens_grad = step(
        lambda sums, total: inv_scale
        * (total * gain_here - sums[0][:, None] - normal * sums[1][:, None])
        + f32(cotangent),
        sums, norm_grad,
    )

    def gather_small(small, other, shared, ends, arrived):
        return jnp.concatenate(
            [
                pair(core, small[: hidden // 128], other[: hidden // 128], 0),
                pair(core, small[hidden // 128 : shared_at], other[hidden // 128 : shared_at], 0),
                shared[:res_at],
                pair(col // 2, ends, arrived, 0).reshape(-1, 128),
            ]
        )

    small = step(gather_small, small, small_other, shared, ends, ends_next)
    small_next = swap_row(small)
    qkv_b = crossed(qkv_both_b, qkv_cross_b)
    small = step(jnp.add, small, small_next)
    small_next = swap_x(small)
    out_mine = crossed(out_both, out_cross)
    qkv_weight_grad = settled(qkv_b, w_qkv.shape, 1, qkv_both_a.shape[0], qkv_weight_grad)
    out_grad = settled(out_mine, w_out.shape, 0, 0, None)
    small = step(jnp.add, small, small_next)

    bounds = [0, 2 * hidden // 128, (2 * hidden + 6 * heads_width) // 128]
    bounds.append(bounds[-1] + res_at)
    up_bias_grad = small[: bounds[1]].reshape(-1)
    qkv_bias_grad = small[bounds[1] : bounds[2]].reshape(-1)
    res_bias_grad = small[bounds[2] : bounds[3]].reshape(-1)
    ends = small[bounds[3] :].reshape(cols, 2, width)
    gain_grad = ends[:, 0].reshape(-1)
    shift_grad = ends[:, 1].reshape(-1)
    return (
        output,
        tokens_grad,
        qkv_weight_grad,
        qkv_bias_grad,
        out_grad,
        up_weight_grad,
        up_bias_grad,
        down_grad,
        res_bias_grad,
        gain_grad,
        shift_grad,
    )


def solution(mesh):
    sizes = (mesh.shape["dp"], mesh.shape["row"], mesh.shape["col"])
    per_device = paired_device if sizes == (4, 2, 4) else general_device
    return jax.shard_map(
        per_device,
        mesh=mesh,
        in_specs=(
            P(("dp", "row"), "col"),
            P("dp", None),
            P("dp", None),
            P("row", "col"),
            P("col"),
            P("col", "row"),
            P("row", "col"),
            P("col"),
            P("col", "row"),
            P("col"),
            P(),
            P(),
            P(("dp", "row"), "col"),
        ),
        out_specs=(
            P(("dp", "row"), "col"),
            P(("dp", "row"), "col"),
            P("row", "col"),
            P("col"),
            P("col", "row"),
            P("row", "col"),
            P("col"),
            P("col", "row"),
            P("col"),
            P(),
            P(),
        ),
        check_vma=False,
    )
```

```python
import functools
import math

import jax
import jax.numpy as jnp
from jax import lax
from jax.experimental import pallas as pl
from jax.experimental.pallas import tpu as pltpu
from jax.sharding import PartitionSpec as P

HD = 64
ROT = 32
SEG = 256


norm_epsilon = 1e-05
masked_fill = -1e30
rotary_base = 10000.0


def precise_dot(left, right):
    return jnp.dot(left, right, precision=lax.Precision.HIGHEST, preferred_element_type=jnp.float32)


def ancestry(parent_row):
    seg_count = parent_row.shape[0]
    labels = jnp.arange(seg_count, dtype=jnp.int32)
    identity = jnp.eye(seg_count, dtype=jnp.float32)
    parent_hot = (parent_row[:, None] == labels[None, :]).astype(jnp.float32)

    def extend(rounds, reachable):
        return jnp.minimum(identity + precise_dot(parent_hot, reachable), 1.0)

    return lax.fori_loop(0, seg_count, extend, identity)


def rotate(values, cosines, sines):
    half_rot = ROT // 2
    former = values[..., :half_rot]
    latter = values[..., half_rot:ROT]
    return jnp.concatenate(
        [former * cosines - latter * sines, latter * cosines + former * sines, values[..., ROT:]],
        axis=-1,
    )


def angles_of(positions):
    frequency = jnp.exp(
        -math.log(rotary_base) * 2.0 * jnp.arange(ROT // 2, dtype=jnp.float32) / ROT
    )
    phase_angle = positions[:, None] * frequency[None, :]
    return (jnp.cos(phase_angle)[:, None, :], jnp.sin(phase_angle)[:, None, :])


def reorder_rows(gradient, row_count, dp_count):
    leading = gradient.shape[0]
    blocked = gradient.reshape(
        row_count, dp_count, leading // (row_count * dp_count), gradient.shape[1]
    )
    return jnp.transpose(blocked, (1, 0, 2, 3)).reshape(leading, gradient.shape[1])


def reorder_cols(gradient, row_count, dp_count):
    trailing = gradient.shape[1]
    blocked = gradient.reshape(
        gradient.shape[0], row_count, dp_count, trailing // (row_count * dp_count)
    )
    return jnp.transpose(blocked, (0, 2, 1, 3)).reshape(gradient.shape[0], trailing)


def general_device(
    tokens,
    parent,
    depth,
    w_qkv,
    b_qkv,
    w_out,
    w_up,
    b_up,
    w_down,
    b_res,
    ln_gain,
    ln_bias,
    cotangent,
):
    tok_rows = tokens.shape[0]
    col_width = tokens.shape[1]
    row_count = lax.axis_size("row")
    dp_count = lax.axis_size("dp")
    row_start = lax.axis_index("row") * tok_rows
    local_heads = w_out.shape[0] // HD
    seg_count = parent.shape[1]
    labels = jnp.arange(seg_count, dtype=jnp.int32)
    reachable = ancestry(parent[0])
    query_index = row_start + jnp.arange(tok_rows, dtype=jnp.int32)
    query_seg = query_index // SEG
    query_hot = (query_seg[:, None] == labels[None, :]).astype(jnp.float32)
    query_reach = precise_dot(query_hot, reachable)
    levels = precise_dot(query_hot, depth[0].astype(jnp.float32)[:, None])[:, 0]
    positions = levels * SEG + (query_index % SEG).astype(jnp.float32)
    cosines, sines = angles_of(positions)
    score_scale = HD ** (-0.5)

    def permit(key_len):
        key_index = jnp.arange(key_len, dtype=jnp.int32)
        key_seg = key_index // SEG
        key_hot = (key_seg[:, None] == labels[None, :]).astype(jnp.float32)
        linked = precise_dot(query_reach, key_hot.T) > 0.5
        return linked & (
            (query_seg[:, None] != key_seg[None, :]) | (query_index[:, None] >= key_index[None, :])
        )

    whole = lax.all_gather(tokens, "col", axis=1, tiled=True).astype(jnp.float32)
    centred = whole - jnp.mean(whole, axis=1, keepdims=True)
    inv_scale = lax.rsqrt(jnp.mean(centred * centred, axis=1, keepdims=True) + norm_epsilon)
    normal = centred * inv_scale
    normed = (normal * ln_gain + ln_bias).astype(jnp.bfloat16)
    qkv_full, up_full, out_full, down_full = (
        lax.all_gather(w_qkv.astype(jnp.bfloat16), "row", axis=0, tiled=True),
        lax.all_gather(w_up.astype(jnp.bfloat16), "row", axis=0, tiled=True),
        lax.all_gather(w_out.astype(jnp.bfloat16), "row", axis=1, tiled=True),
        lax.all_gather(w_down.astype(jnp.bfloat16), "row", axis=1, tiled=True),
    )
    mixed = (jnp.dot(normed, qkv_full, preferred_element_type=jnp.float32) + b_qkv).reshape(
        tok_rows, local_heads, 3, HD
    )

    def rotate_pair(query_pre, key_pre):
        return (rotate(query_pre, cosines, sines), rotate(key_pre, cosines, sines))

    rotated, rotate_back = jax.vjp(rotate_pair, mixed[:, :, 0], mixed[:, :, 1])
    queries = rotated[0].astype(jnp.bfloat16)
    key_rows = rotated[1].astype(jnp.bfloat16)
    value_rows = mixed[:, :, 2].astype(jnp.bfloat16)
    key_flat = key_rows.reshape(tok_rows, local_heads * HD)
    value_flat = value_rows.reshape(tok_rows, local_heads * HD)

    def scores_for(key_part):
        raw_scores = (
            jnp.einsum("qhe,khe->hqk", queries, key_part, preferred_element_type=jnp.float32)
            * score_scale
        )
        allowed = permit(key_part.shape[0])
        return (jnp.where(allowed[None], raw_scores, masked_fill), allowed)

    pieces = (
        lax.all_gather(key_flat, "row", axis=0, tiled=True),
        lax.all_gather(value_flat, "row", axis=0, tiled=True),
    )
    running_top = jnp.full((local_heads, tok_rows), masked_fill, jnp.float32)
    key_len = pieces[0].shape[0]
    key_part = pieces[0].reshape(key_len, local_heads, HD)
    value_part = pieces[1].reshape(key_len, local_heads, HD)
    scores, allowed = scores_for(key_part)
    new_top = jnp.maximum(running_top, jnp.max(scores, axis=2))
    exponent = jnp.where(allowed[None], jnp.exp(scores - new_top[:, :, None]), 0.0)
    running_sum = jnp.sum(exponent, axis=2)
    weighted = jnp.einsum(
        "hqk,khe->hqe",
        exponent.astype(jnp.bfloat16),
        value_part,
        preferred_element_type=jnp.float32,
    )
    running_top, running_sum, weighted = (new_top, running_sum, weighted)
    log_total = running_top + jnp.log(running_sum)
    attn_exact = weighted / running_sum[:, :, None]
    attended = (
        jnp.transpose(attn_exact, (1, 0, 2))
        .reshape(tok_rows, local_heads * HD)
        .astype(jnp.bfloat16)
    )
    hidden_up = jnp.dot(normed, up_full, preferred_element_type=jnp.float32) + b_up
    activated, gelu_back = jax.vjp(functools.partial(jax.nn.gelu, approximate=True), hidden_up)
    activated = activated.astype(jnp.bfloat16)
    branch_terms = jnp.dot(attended, out_full, preferred_element_type=jnp.float32) + jnp.dot(
        activated, down_full, preferred_element_type=jnp.float32
    )
    branch = lax.psum_scatter(
        branch_terms.astype(jnp.bfloat16), "col", scatter_dimension=1, tiled=True
    ).astype(jnp.float32)
    output = (tokens.astype(jnp.float32) + branch + b_res).astype(jnp.bfloat16)
    grad_full = lax.all_gather(cotangent, "col", axis=1, tiled=True)
    res_bias_grad = jnp.sum(cotangent.astype(jnp.float32), axis=0)
    down_grad = jnp.einsum("tf,td->fd", activated, grad_full, preferred_element_type=jnp.float32)
    out_grad = jnp.einsum("te,td->ed", attended, grad_full, preferred_element_type=jnp.float32)
    act_grad = jnp.einsum("td,fd->tf", grad_full, down_full, preferred_element_type=jnp.float32)
    up_grad = gelu_back(act_grad)[0].astype(jnp.bfloat16)
    attn_grad = jnp.einsum(
        "td,ed->te", grad_full, out_full, preferred_element_type=jnp.float32
    ).astype(jnp.bfloat16)
    up_bias_grad = jnp.sum(up_grad.astype(jnp.float32), axis=0)
    up_weight_grad = jnp.einsum("td,tf->df", normed, up_grad, preferred_element_type=jnp.float32)
    out_heads = attn_grad.reshape(tok_rows, local_heads, HD)
    delta_sum = jnp.einsum("qhe,hqe->hq", out_heads.astype(jnp.float32), attn_exact)
    pieces = (
        lax.all_gather(key_flat, "row", axis=0, tiled=True),
        lax.all_gather(value_flat, "row", axis=0, tiled=True),
    )
    key_len = pieces[0].shape[0]
    key_part = pieces[0].reshape(key_len, local_heads, HD)
    value_part = pieces[1].reshape(key_len, local_heads, HD)
    scores, allowed = scores_for(key_part)
    softmaxed = jnp.where(allowed[None], jnp.exp(scores - log_total[:, :, None]), 0.0)
    prob_grad = jnp.einsum(
        "qhe,khe->hqk", out_heads, value_part, preferred_element_type=jnp.float32
    )
    score_grad = (softmaxed * (prob_grad - delta_sum[:, :, None])).astype(jnp.bfloat16)
    query_grad = (
        jnp.einsum("hqk,khe->qhe", score_grad, key_part, preferred_element_type=jnp.float32)
        * score_scale
    )
    key_grad = (
        jnp.einsum("hqk,qhe->khe", score_grad, queries, preferred_element_type=jnp.float32)
        * score_scale
    )
    value_grad = jnp.einsum(
        "hqk,qhe->khe",
        softmaxed.astype(jnp.bfloat16),
        out_heads,
        preferred_element_type=jnp.float32,
    )
    stacked = jnp.stack([key_grad, value_grad], axis=1).reshape(key_len, 2 * local_heads * HD)
    pair_grad = stacked
    query_grad, pair_grad = (query_grad, pair_grad)
    own_pairs = (
        lax.psum_scatter(pair_grad.astype(jnp.bfloat16), "row", scatter_dimension=0, tiled=True)
        .astype(jnp.float32)
        .reshape(tok_rows, 2, local_heads, HD)
    )
    query_pre, key_pre = rotate_back((query_grad, own_pairs[:, 0]))
    mixed_grad = (
        jnp.stack([query_pre, key_pre, own_pairs[:, 1]], axis=2)
        .reshape(tok_rows, 3 * local_heads * HD)
        .astype(jnp.bfloat16)
    )
    qkv_bias_grad = jnp.sum(mixed_grad.astype(jnp.float32), axis=0)
    qkv_weight_grad = jnp.einsum(
        "td,tc->dc", normed, mixed_grad, preferred_element_type=jnp.float32
    )
    norm_part = jnp.einsum(
        "tc,dc->td", mixed_grad, qkv_full, preferred_element_type=jnp.float32
    ) + jnp.einsum("tf,df->td", up_grad, up_full, preferred_element_type=jnp.float32)
    norm_grad = lax.psum(norm_part.astype(jnp.bfloat16), "col").astype(jnp.float32)
    gain_grad = jnp.sum(norm_grad * normal, axis=0)
    shift_grad = jnp.sum(norm_grad, axis=0)
    scaled = norm_grad * ln_gain
    mean_scaled = jnp.mean(scaled, axis=1, keepdims=True)
    mean_mixed = jnp.mean(scaled * normal, axis=1, keepdims=True)
    col_start = lax.axis_index("col") * col_width
    scaled_share = lax.dynamic_slice_in_dim(scaled, col_start, col_width, 1)
    normal_share = lax.dynamic_slice_in_dim(normal, col_start, col_width, 1)
    tokens_grad = inv_scale * (
        scaled_share - mean_scaled - normal_share * mean_mixed
    ) + cotangent.astype(jnp.float32)
    qkv_bias_grad, up_bias_grad, res_bias_grad, gain_grad, shift_grad = (
        lax.psum(qkv_bias_grad.astype(jnp.bfloat16), ("dp", "row")).astype(jnp.float32),
        lax.psum(up_bias_grad.astype(jnp.bfloat16), ("dp", "row")).astype(jnp.float32),
        lax.psum(res_bias_grad.astype(jnp.bfloat16), ("dp", "row")).astype(jnp.float32),
        lax.psum(gain_grad.astype(jnp.bfloat16), ("dp", "row")).astype(jnp.float32),
        lax.psum(shift_grad.astype(jnp.bfloat16), ("dp", "row")).astype(jnp.float32),
    )
    pieces_now = (
        lax.psum_scatter(
            reorder_rows(qkv_weight_grad, row_count, dp_count).astype(jnp.bfloat16),
            ("dp", "row"),
            scatter_dimension=0,
            tiled=True,
        ).astype(jnp.float32),
        lax.psum_scatter(
            reorder_rows(up_weight_grad, row_count, dp_count).astype(jnp.bfloat16),
            ("dp", "row"),
            scatter_dimension=0,
            tiled=True,
        ).astype(jnp.float32),
        lax.psum_scatter(
            reorder_cols(out_grad, row_count, dp_count).astype(jnp.bfloat16),
            ("dp", "row"),
            scatter_dimension=1,
            tiled=True,
        ).astype(jnp.float32),
        lax.psum_scatter(
            reorder_cols(down_grad, row_count, dp_count).astype(jnp.bfloat16),
            ("dp", "row"),
            scatter_dimension=1,
            tiled=True,
        ).astype(jnp.float32),
    )
    qkv_weight_grad, up_weight_grad, out_grad, down_grad = (
        lax.all_gather(pieces_now[0].astype(jnp.bfloat16), "dp", axis=0, tiled=True).astype(
            jnp.float32
        ),
        lax.all_gather(pieces_now[1].astype(jnp.bfloat16), "dp", axis=0, tiled=True).astype(
            jnp.float32
        ),
        lax.all_gather(pieces_now[2].astype(jnp.bfloat16), "dp", axis=1, tiled=True).astype(
            jnp.float32
        ),
        lax.all_gather(pieces_now[3].astype(jnp.bfloat16), "dp", axis=1, tiled=True).astype(
            jnp.float32
        ),
    )
    return (
        output,
        tokens_grad,
        qkv_weight_grad,
        qkv_bias_grad,
        out_grad,
        up_weight_grad,
        up_bias_grad,
        down_grad,
        res_bias_grad,
        gain_grad,
        shift_grad,
    )


SWAP_ROW = [(0, 1), (1, 0)]
SWAP_X = [(0, 2), (2, 0), (1, 3), (3, 1)]
SWAP_CORE = [(0, 1), (1, 0), (2, 3), (3, 2)]


def bf16(values):
    return values.astype(jnp.bfloat16)


def f32(values):
    return values.astype(jnp.float32)


def matmul(left, right, dims=((1,), (0,))):
    return lax.dot_general(left, right, (dims, ((), ())), preferred_element_type=jnp.float32)


def swap_row(values):
    return lax.ppermute(values, "row", SWAP_ROW)


def swap_x(values):
    return lax.ppermute(values, "dp", SWAP_X)


def swap_core(values):
    return lax.ppermute(values, "dp", SWAP_CORE)


def pick(index, first, second):
    return jnp.where(index == 0, first, second)


def pair(index, mine, theirs, axis):
    return pick(
        index,
        jnp.concatenate([mine, theirs], axis=axis),
        jnp.concatenate([theirs, mine], axis=axis),
    )


def after(value, *earlier):
    return lax.optimization_barrier((value,) + earlier)[0]


def rotary_tables(positions):
    lane = jnp.arange(2 * HD, dtype=jnp.int32) % HD
    half_rot = ROT // 2
    frequency = jnp.exp(
        -math.log(rotary_base) * 2.0 * (lane % half_rot).astype(jnp.float32) / ROT
    )
    angle = positions[:, None] * frequency[None, :]
    turned = (lane < ROT)[None, :]
    sines = jnp.sin(angle)
    return (
        jnp.where(turned, jnp.cos(angle), 1.0),
        jnp.where((lane < half_rot)[None, :], -sines, 0.0),
        jnp.where(turned & (lane >= half_rot)[None, :], sines, 0.0),
    )


def turn(values, cosines, sines_low, sines_high):
    width = values.shape[1]
    half_rot = ROT // 2
    return (
        values * cosines
        + pltpu.roll(values, width - half_rot, 1) * sines_low
        + pltpu.roll(values, half_rot, 1) * sines_high
    )


def split_kernel(mixed_ref, cos_ref, low_ref, high_ref, query_ref, keyval_ref):
    cosines, low, high = cos_ref[...], low_ref[...], high_ref[...]
    rows = mixed_ref.shape[0]
    half = query_ref.shape[1]
    first = lax.broadcasted_iota(jnp.int32, (rows, 2 * HD), 1) < HD
    scale = HD ** (-0.5)
    for at in range(half // (2 * HD)):
        tiles = [mixed_ref[:, (3 * at + part) * 2 * HD : (3 * at + part + 1) * 2 * HD] for part in range(3)]
        query = jnp.where(first, tiles[0], tiles[1])
        key = jnp.where(first, pltpu.roll(tiles[0], HD, 1), pltpu.roll(tiles[2], HD, 1))
        value = jnp.where(first, tiles[1], tiles[2])
        here = slice(at * 2 * HD, (at + 1) * 2 * HD)
        query_ref[:, here] = bf16(f32(bf16(turn(query, cosines, low, high))) * scale)
        keyval_ref[:, here] = bf16(turn(key, cosines, low, high))
        keyval_ref[:, half + at * 2 * HD : half + (at + 1) * 2 * HD] = bf16(value)


def join_kernel(row_ref, dq_ref, dkv_ref, sent_ref, cos_ref, low_ref, high_ref, out_ref):
    cosines, low, high = cos_ref[...], -low_ref[...], -high_ref[...]
    rows = dq_ref.shape[0]
    half = dq_ref.shape[1]
    first = lax.broadcasted_iota(jnp.int32, (rows, 2 * HD), 1) < HD
    owner = row_ref[0] == 0
    for at in range(half // (2 * HD)):
        here = slice(at * 2 * HD, (at + 1) * 2 * HD)
        there = slice(half + at * 2 * HD, half + (at + 1) * 2 * HD)
        query = turn(dq_ref[:, here], cosines, low, high)
        key = dkv_ref[:, here] + jnp.where(owner, f32(sent_ref[:, here]), 0.0)
        value = dkv_ref[:, there] + jnp.where(owner, f32(sent_ref[:, there]), 0.0)
        key = pltpu.roll(turn(key, cosines, low, high), HD, 1)
        tiles = (jnp.where(first, query, key), jnp.where(first, value, query), jnp.where(first, key, value))
        for part in range(3):
            out_ref[:, (3 * at + part) * 2 * HD : (3 * at + part + 1) * 2 * HD] = bf16(tiles[part])


def tree_kernel(
    parent_ref, row_ref, query_ref, keyval_ref, trunk_ref, grad_ref,
    out_ref, dq_ref, dkv_ref, dtrunk_ref,
    keys, values, dkeys, dvalues,
):
    tree = pl.program_id(0)
    row = row_ref[0]
    rows, half = query_ref.shape
    trunk_len = trunk_ref.shape[0]
    segs = rows // SEG
    trunk_segs = trunk_len // SEG
    seg_count = parent_ref.shape[1]
    first_row = row == 0
    keys[...] = jnp.where(first_row, keyval_ref[:, :half], trunk_ref[:, :half])
    values[...] = jnp.where(first_row, keyval_ref[:, half:], trunk_ref[:, half:])
    dkeys[...] = jnp.zeros_like(dkeys)
    dvalues[...] = jnp.zeros_like(dvalues)
    lane = lax.broadcasted_iota(jnp.int32, (1, half), 1)
    causal = lax.broadcasted_iota(jnp.int32, (SEG, SEG), 0) >= lax.broadcasted_iota(
        jnp.int32, (SEG, SEG), 1
    )
    across = ((1,), (1,))
    down = ((0,), (0,))
    for seg in range(segs):
        here = slice(seg * SEG, (seg + 1) * SEG)
        above = parent_ref[tree, row * segs + seg]
        linked = [above == at for at in range(trunk_segs)]
        for _ in range(seg_count - 2):
            above = jnp.where(above >= 0, parent_ref[tree, jnp.maximum(above, 0)], -1)
            linked = [was | (above == at) for at, was in enumerate(linked)]
        bias = [jnp.where(is_linked, 0.0, masked_fill) for is_linked in linked]
        query, grad = query_ref[here, :], grad_ref[here, :]
        own_key, own_value = keyval_ref[here, :half], keyval_ref[here, half:]
        attended = jnp.zeros((SEG, half), jnp.float32)
        dquery = jnp.zeros((SEG, half), jnp.float32)
        dkey = jnp.zeros((SEG, half), jnp.float32)
        dvalue = jnp.zeros((SEG, half), jnp.float32)
        for head in range(half // HD):
            mine = (lane >= head * HD) & (lane < (head + 1) * HD)
            head_query = jnp.where(mine, query, jnp.zeros_like(query))
            head_grad = jnp.where(mine, grad, jnp.zeros_like(grad))
            scores = [
                matmul(head_query, keys[at * SEG : (at + 1) * SEG, :], across) + bias[at]
                for at in range(trunk_segs)
            ] + [jnp.where(causal, matmul(head_query, own_key, across), masked_fill)]
            top = functools.reduce(jnp.maximum, [jnp.max(s, axis=1, keepdims=True) for s in scores])
            powers = [jnp.exp(s - top) for s in scores]
            total = functools.reduce(jnp.add, [jnp.sum(p, axis=1, keepdims=True) for p in powers])
            probs = [p / total for p in powers]
            low = [bf16(p) for p in probs]
            blocks = [values[at * SEG : (at + 1) * SEG, :] for at in range(trunk_segs)] + [own_value]
            prob_grads = [matmul(head_grad, v, across) for v in blocks]
            delta = functools.reduce(
                jnp.add, [jnp.sum(p * g, axis=1, keepdims=True) for p, g in zip(probs, prob_grads)]
            )
            score_grads = [bf16(p * (g - delta)) for p, g in zip(probs, prob_grads)]
            head_out = functools.reduce(jnp.add, [matmul(p, v) for p, v in zip(low, blocks)])
            attended = jnp.where(mine, head_out, attended)
            key_blocks = [keys[at * SEG : (at + 1) * SEG, :] for at in range(trunk_segs)] + [own_key]
            head_dq = functools.reduce(jnp.add, [matmul(s, u) for s, u in zip(score_grads, key_blocks)])
            dquery = jnp.where(mine, head_dq, dquery)
            dkey = dkey + matmul(score_grads[-1], head_query, down)
            dvalue = dvalue + matmul(low[-1], head_grad, down)
            for at in range(trunk_segs):
                spot = slice(at * SEG, (at + 1) * SEG)
                dkeys[spot, :] += matmul(score_grads[at], head_query, down)
                dvalues[spot, :] += matmul(low[at], head_grad, down)
        out_ref[here, :] = bf16(attended)
        dq_ref[here, :] = dquery * HD ** (-0.5)
        dkv_ref[here, :half] = dkey
        dkv_ref[here, half:] = dvalue
    dtrunk_ref[:, :half] = bf16(dkeys[...])
    dtrunk_ref[:, half:] = bf16(dvalues[...])

    @pl.when(first_row)
    def _():
        dkv_ref[:, :half] += dkeys[...]
        dkv_ref[:, half:] += dvalues[...]


def store_blocks(place_ref, sides, full_ref, plain_ref):
    row, slab = place_ref[1], place_ref[2]
    for side, values in enumerate(sides):
        width = values[0].shape[1]
        for source, value in enumerate(values):
            within = source % 2
            here = row == source // 2

            @pl.when(here)
            def _():
                full_ref[side, :, within * width : (within + 1) * width] = value

            @pl.when(jnp.logical_not(here))
            def _():
                plain_ref[side, :, within * width : (within + 1) * width] = value
                at = (2 + jnp.where(slab == 0, within, 1 - within)) * width
                full_ref[side, :, pl.ds(pl.multiple_of(at, width), width)] = value


def gather_kernel(place_ref, mine_ref, theirs_ref, full_ref, plain_ref):
    sides = [[ref[at] for at in range(ref.shape[0])] for ref in (mine_ref, theirs_ref)]
    store_blocks(place_ref, sides, full_ref, plain_ref)


def norm_kernel(
    place_ref, gain_ref, bias_ref, mine_ref, theirs_ref, full_ref, plain_ref, normal_ref, scale_ref
):
    sides = []
    for side, ref in enumerate((mine_ref, theirs_ref)):
        values = [f32(ref[at]) for at in range(ref.shape[0])]
        features = len(values) * values[0].shape[1]
        mean = functools.reduce(jnp.add, [jnp.sum(v, axis=1, keepdims=True) for v in values]) / features
        centred = [v - mean for v in values]
        square = functools.reduce(jnp.add, [jnp.sum(v * v, axis=1, keepdims=True) for v in centred])
        inv_scale = lax.rsqrt(square / features + norm_epsilon)
        normals = [v * inv_scale for v in centred]
        if side == 0:
            scale_ref[...] = inv_scale
            for source, normal in enumerate(normals):

                @pl.when(place_ref[0] == source)
                def _():
                    normal_ref[...] = normal

        sides.append(
            [
                bf16(normal * gain_ref[source : source + 1, :] + bias_ref[source : source + 1, :])
                for source, normal in enumerate(normals)
            ]
        )
    store_blocks(place_ref, sides, full_ref, plain_ref)


def pair_rows(rows, width):
    return pl.BlockSpec((2, rows, width), lambda at, *_: (0, at, 0))


def gathered(place, mine, theirs, norm=None):
    blocks, count, width = mine.shape
    rows = SEG if norm is None else SEG // 2
    full = blocks * width
    in_specs = [pl.BlockSpec((blocks, rows, width), lambda at, *_: (0, at, 0))] * 2
    out_specs = [pair_rows(rows, full), pair_rows(rows, full // 2)]
    out_shape = [
        jax.ShapeDtypeStruct((2, count, full), jnp.bfloat16),
        jax.ShapeDtypeStruct((2, count, full // 2), jnp.bfloat16),
    ]
    operands = [mine, theirs]
    if norm is not None:
        gain = [values.reshape(blocks, width) for values in norm]
        operands = gain + operands
        in_specs = [pl.BlockSpec((blocks, width), lambda at, *_: (0, 0))] * 2 + in_specs
        out_specs = out_specs + [row_block(rows, width), row_block(rows, 1)]
        out_shape = out_shape + [
            jax.ShapeDtypeStruct((count, width), jnp.float32),
            jax.ShapeDtypeStruct((count, 1), jnp.float32),
        ]
    results = pl.pallas_call(
        gather_kernel if norm is None else norm_kernel,
        grid_spec=pltpu.PrefetchScalarGridSpec(
            num_scalar_prefetch=1, grid=(count // rows,), in_specs=in_specs, out_specs=out_specs
        ),
        out_shape=out_shape,
        cost_estimate=pl.CostEstimate(flops=1, bytes_accessed=1, transcendentals=0),
        name="join_blocks" if norm is None else "norm_blocks",
    )(place, *operands)
    return [values.reshape(2 * count, -1) for values in results[:2]] + list(results[2:])


def stack_kernel(place_ref, terms_ref, arrived_ref, out_ref):
    row, slab = place_ref[1], place_ref[2]
    width = out_ref.shape[2]
    for spot in range(4):
        here = slice(spot * width, (spot + 1) * width)
        value = bf16(terms_ref[:, here] + f32(arrived_ref[:, here]))
        if spot < 2:
            out_ref[2 * row + spot] = value
        else:
            out_ref[2 * (1 - row) + jnp.where(slab == 0, spot - 2, 3 - spot)] = value


def stacked(place, terms, arrived, blocks):
    count, full = arrived.shape
    rows = SEG
    width = full // blocks
    return pl.pallas_call(
        stack_kernel,
        grid_spec=pltpu.PrefetchScalarGridSpec(
            num_scalar_prefetch=1,
            grid=(count // rows,),
            in_specs=[row_block(rows, full), row_block(rows, full)],
            out_specs=pl.BlockSpec((blocks, rows, width), lambda at, *_: (0, at, 0)),
        ),
        out_shape=jax.ShapeDtypeStruct((blocks, count, width), jnp.bfloat16),
        cost_estimate=pl.CostEstimate(flops=1, bytes_accessed=1, transcendentals=0),
        name="stack_blocks",
    )(place, terms, arrived)


def cast_rows_kernel(place_ref, master_ref, own_ref, send_ref):
    value = bf16(master_ref[...])
    own_ref[...] = value
    half = pl.num_programs(0) // 2

    @pl.when(pl.program_id(0) // half == place_ref[2])
    def _():
        send_ref[...] = value


def cast_cols_kernel(place_ref, master_ref, own_ref, send_ref):
    value = bf16(master_ref[...])
    own_ref[...] = value
    half = value.shape[1] // 2
    send_ref[...] = jnp.where(place_ref[2] == 0, value[:, :half], value[:, half:])


def cast_weight(place, master, axis):
    height, width = master.shape
    rows = min(2 * SEG, master.shape[0] // 4)
    if axis == 0:
        width = width // 2
        steps = height // rows
        half = steps // 2
        specs = [
            pl.BlockSpec((rows, width), lambda at, place_ref: (at, place_ref[3])),
            pl.BlockSpec((rows, width), lambda at, place_ref: (at, 0)),
            pl.BlockSpec(
                (rows, width), lambda at, place_ref: (jnp.clip(at - half * place_ref[2], 0, half - 1), 0)
            ),
        ]
        send = (height // 2, width)
        whole = (2 * height, width)
    else:
        height = height // 2
        steps = height // rows
        specs = [
            pl.BlockSpec((rows, width), lambda at, place_ref: (at + steps * place_ref[3], 0)),
            pl.BlockSpec((rows, width), lambda at, place_ref: (at, 0)),
            pl.BlockSpec((rows, width // 2), lambda at, place_ref: (at, 0)),
        ]
        send = (height, width // 2)
        whole = (height, 2 * width)
    return pl.pallas_call(
        cast_rows_kernel if axis == 0 else cast_cols_kernel,
        grid_spec=pltpu.PrefetchScalarGridSpec(
            num_scalar_prefetch=1, grid=(steps,), in_specs=specs[:1], out_specs=specs[1:]
        ),
        out_shape=[
            jax.ShapeDtypeStruct(whole, jnp.bfloat16),
            jax.ShapeDtypeStruct(send, jnp.bfloat16),
        ],
        cost_estimate=pl.CostEstimate(flops=1, bytes_accessed=1, transcendentals=0),
        name="cast_weight",
    )(place, master)


def settle_kernel(axis, place_ref, mine_ref, theirs_ref, *refs):
    out_ref = refs[-1]
    mine, theirs = f32(mine_ref[...]), f32(theirs_ref[...])
    if axis == 0:
        out_ref[place_ref[3]] = mine
        out_ref[1 - place_ref[3]] = theirs
    else:
        width = mine.shape[1]
        first = place_ref[3] == 0
        out_ref[:, :width] = jnp.where(first, mine, theirs)
        out_ref[:, width:] = jnp.where(first, theirs, mine)


def settle(place, mine, theirs, shape, axis, offset, dest=None):
    rows, width = mine.shape
    at = offset // rows
    whole = pl.BlockSpec((rows, width), lambda *_: (0, 0))
    if axis == 0:
        shape = (2, shape[0] // 2, width)
        out_spec = pl.BlockSpec((2, rows, width), lambda *_: (0, at, 0))
    else:
        out_spec = pl.BlockSpec((rows, 2 * width), lambda *_: (at, 0))
    in_specs = [whole, whole]
    operands = [place, mine, theirs]
    aliases = {}
    if dest is not None:
        in_specs.append(pl.BlockSpec(memory_space=pl.ANY))
        operands.append(dest)
        aliases = {3: 0}
    return pl.pallas_call(
        functools.partial(settle_kernel, axis),
        grid_spec=pltpu.PrefetchScalarGridSpec(
            num_scalar_prefetch=1, grid=(1,), in_specs=in_specs, out_specs=out_spec
        ),
        out_shape=jax.ShapeDtypeStruct(shape, jnp.float32),
        input_output_aliases=aliases,
        cost_estimate=pl.CostEstimate(flops=1, bytes_accessed=1, transcendentals=0),
        name="settle",
    )(*operands)


def row_block(rows, width):
    return pl.BlockSpec((rows, width), lambda at, *_: (at, 0))


def split_heads(mixed, tables):
    count, width = mixed.shape
    rows = 2 * SEG
    return pl.pallas_call(
        split_kernel,
        grid=(count // rows,),
        in_specs=[row_block(rows, width)] + [row_block(rows, 2 * HD)] * 3,
        out_specs=[row_block(rows, width // 3), row_block(rows, 2 * width // 3)],
        out_shape=[
            jax.ShapeDtypeStruct((count, width // 3), jnp.bfloat16),
            jax.ShapeDtypeStruct((count, 2 * width // 3), jnp.bfloat16),
        ],
        cost_estimate=pl.CostEstimate(flops=1, bytes_accessed=1, transcendentals=0),
        name="split_heads",
    )(mixed, *tables)


def join_heads(row, dq, dkv, sent, tables):
    count, half = dq.shape
    rows = 2 * SEG
    return pl.pallas_call(
        join_kernel,
        grid_spec=pltpu.PrefetchScalarGridSpec(
            num_scalar_prefetch=1,
            grid=(count // rows,),
            in_specs=[row_block(rows, half), row_block(rows, 2 * half), row_block(rows, 2 * half)]
            + [row_block(rows, 2 * HD)] * 3,
            out_specs=row_block(rows, 3 * half),
        ),
        out_shape=jax.ShapeDtypeStruct((count, 3 * half), jnp.bfloat16),
        cost_estimate=pl.CostEstimate(flops=1, bytes_accessed=1, transcendentals=0),
        name="join_heads",
    )(row, dq, dkv, sent, *tables)


def tree_attention(parents, row, query, keyval, trunk, grad):
    trees = parents.shape[0]
    count, half = query.shape
    rows = count // trees
    keys = trunk.shape[0] // trees
    pairs = count * (keys + SEG) * (half // HD)
    return pl.pallas_call(
        tree_kernel,
        grid_spec=pltpu.PrefetchScalarGridSpec(
            num_scalar_prefetch=2,
            grid=(trees,),
            in_specs=[
                row_block(rows, half),
                row_block(rows, 2 * half),
                row_block(keys, 2 * half),
                row_block(rows, half),
            ],
            out_specs=[
                row_block(rows, half),
                row_block(rows, half),
                row_block(rows, 2 * half),
                row_block(keys, 2 * half),
            ],
            scratch_shapes=[pltpu.VMEM((keys, half), jnp.bfloat16)] * 2
            + [pltpu.VMEM((keys, half), jnp.float32)] * 2,
        ),
        out_shape=[
            jax.ShapeDtypeStruct((count, half), jnp.bfloat16),
            jax.ShapeDtypeStruct((count, half), jnp.float32),
            jax.ShapeDtypeStruct((count, 2 * half), jnp.float32),
            jax.ShapeDtypeStruct((trees * keys, 2 * half), jnp.bfloat16),
        ],
        cost_estimate=pl.CostEstimate(flops=1, bytes_accessed=1, transcendentals=0),
        name="tree_attention",
    )(parents, row, query, keyval, trunk, grad)


def paired_device(
    tokens,
    parent,
    depth,
    w_qkv,
    b_qkv,
    w_out,
    w_up,
    b_up,
    w_down,
    b_res,
    ln_gain,
    ln_bias,
    cotangent,
):
    count, width = tokens.shape
    row = lax.axis_index("row")
    col = lax.axis_index("col")
    core = lax.axis_index("dp") % 2
    slab = lax.axis_index("dp") // 2
    cols = lax.axis_size("col")
    half = 2 * width
    heads_width = w_out.shape[0] // 2
    hidden = w_up.shape[1] // 2
    place = jnp.stack([col, row, slab, core]).astype(jnp.int32)
    row_table = jnp.reshape(row, (1,)).astype(jnp.int32)
    down_dims = ((0,), (0,))
    across = ((1,), (1,))

    def part(values, at, size, axis):
        return lax.dynamic_slice_in_dim(values, at * size, size, axis)

    def exchange(stack):
        return lax.all_to_all(stack, "col", 0, 0, tiled=True)

    def to_all(block):
        return exchange(jnp.broadcast_to(block[None], (cols,) + block.shape))

    done = ()

    def step(run, *inputs):
        nonlocal done
        inputs, _ = lax.optimization_barrier((inputs, done))
        result = run(*inputs)
        done = result
        return result

    def wait(value):
        return step(lambda arrived: arrived, value)

    tokens_near = lax.all_gather(tokens, "col", axis=0)

    def ready(master, axis):
        whole, send = step(lambda weight: cast_weight(place, weight, axis), master)
        return whole, swap_row(send)

    def fill(whole, by_row, by_x, axis):
        start = whole.shape[axis] // 2
        whole = lax.dynamic_update_slice_in_dim(whole, by_row, start, axis)
        return lax.dynamic_update_slice_in_dim(whole, by_x, start + by_row.shape[axis], axis)

    tables = jnp.concatenate([parent, depth], axis=0)
    tables = jnp.stack([tables, swap_core(tables)])
    parents = tables[:, 0]
    segs = count // SEG
    token = jnp.arange(count, dtype=jnp.int32)
    levels = jnp.zeros((2, count), jnp.float32)
    for seg in range(segs):
        level = lax.dynamic_slice_in_dim(tables[:, 1], row * segs + seg, 1, 1).astype(jnp.float32)
        levels = jnp.where((token // SEG == seg)[None, :], level, levels)
    positions = (levels * SEG + (token % SEG).astype(jnp.float32)[None, :]).reshape(2 * count)
    rotary = rotary_tables(positions)

    qkv_whole, qkv_row = ready(w_qkv, 0)
    up_whole, up_row = ready(w_up, 0)
    qkv_row = wait(qkv_row)
    qkv_x = swap_x(qkv_row)
    out_whole, out_row = ready(w_out, 1)
    down_whole, down_row = ready(w_down, 1)
    rotary = step(lambda *tables: tables, *rotary)
    up_row = wait(up_row)
    up_x = swap_x(up_row)
    qkv_x = wait(qkv_x)
    tokens_near = wait(tokens_near)
    tokens_far = swap_core(tokens_near)
    grad_near = to_all(after(cotangent, tokens_near))
    out_row = wait(out_row)
    out_x = swap_x(out_row)
    normed, normed_plain, normal, inv_scale = step(
        lambda mine, theirs: gathered(place, mine, theirs, (ln_gain, ln_bias)), tokens_near, tokens_far
    )
    normed_own = normed[:, :half]
    grad_far = swap_core(grad_near)
    qkv_full = step(lambda *parts: fill(*parts, 0), qkv_whole, qkv_row, qkv_x)
    mixed = step(
        lambda left, right: matmul(left, right) + part(b_qkv, core, 3 * heads_width, 0), normed, qkv_full
    )
    query, keyval = step(lambda values: split_heads(values, rotary), mixed)
    trunk = lax.ppermute(keyval, "row", [(0, 1)])
    root = math.sqrt(2.0 / math.pi)

    def feed(left, right):
        hidden_up = matmul(left, right) + part(b_up, core, hidden, 0)
        squared = hidden_up * hidden_up
        bend = jnp.tanh(root * (hidden_up + 0.044715 * squared * hidden_up))
        return bf16(0.5 * hidden_up * (1.0 + bend)), bf16(
            0.5 * (1.0 + bend)
            + 0.5 * hidden_up * (1.0 - bend * bend) * root * (1.0 + 3.0 * 0.044715 * squared)
        )

    up_full = step(lambda *parts: fill(*parts, 0), up_whole, up_row, up_x)
    activated, slope = step(feed, normed, up_full)
    down_row = wait(down_row)
    down_x = swap_x(down_row)
    grad, grad_plain = step(lambda mine, theirs: gathered(place, mine, theirs), grad_near, grad_far)
    grad_own = grad[:, :half]

    def cut(values, at):
        size = values.shape[1] // 2
        return values[:, at * size : (at + 1) * size]

    def leaving(left, right):
        return step(lambda a, b: bf16(matmul(a, b, down_dims)), left, right)

    def staying(left, right, sent):
        return step(lambda a, b, c: bf16(matmul(a, b, down_dims) + f32(c)), left, right, sent)

    def crossed(both, arrived):
        mine = step(lambda a, b: bf16(f32(a) + f32(b)), both, arrived)
        return mine, swap_core(mine)

    def settled(pieces, shape, axis, offset, dest):
        operands = pieces if dest is None else pieces + (dest,)
        return step(
            lambda mine, theirs, *rest: settle(place, mine, theirs, shape, axis, offset, *rest), *operands
        )

    down_sent_a = swap_row(leaving(cut(activated, 0), grad_plain))
    down_sent_b = swap_row(leaving(cut(activated, 1), grad_plain))
    out_full = step(lambda *parts: fill(*parts, 1), out_whole, out_row, out_x)
    out_heads = step(lambda a, b: bf16(matmul(a, b, across)), grad, out_full)
    attended, query_grad, own_grad, trunk_grad = step(
        lambda *operands: tree_attention(parents, row_table, *operands), query, keyval, trunk, out_heads
    )
    trunk_sent = lax.ppermute(trunk_grad, "row", [(1, 0)])
    down_both_a = staying(cut(activated, 0), grad_own, down_sent_a)
    down_cross_a = swap_x(down_both_a)
    down_full = step(lambda *parts: fill(*parts, 1), down_whole, down_row, down_x)
    up_grad = step(lambda a, b, c: bf16(matmul(a, b, across) * f32(c)), grad, down_full, slope)
    up_sent_a = swap_row(leaving(cut(normed_plain, 0), up_grad))
    down_both_b = staying(cut(activated, 1), grad_own, down_sent_b)
    down_cross_b = swap_x(down_both_b)
    up_sent_b = swap_row(leaving(cut(normed_plain, 1), up_grad))
    down_a = crossed(down_both_a, down_cross_a)
    branch_terms = step(
        lambda a, b, c, d: matmul(a, b) + matmul(c, d), attended, out_full, activated, down_full
    )
    branch_near = swap_core(step(bf16, branch_terms[count:]))
    mixed_grad = step(
        lambda *operands: join_heads(row_table, *operands, rotary), query_grad, own_grad, trunk_sent
    )
    qkv_sent_a = swap_row(leaving(cut(normed_plain, 0), mixed_grad))
    down_b = crossed(down_both_b, down_cross_b)
    qkv_sent_b = swap_row(leaving(cut(normed_plain, 1), mixed_grad))
    norm_terms = step(
        lambda a, b, c, d: matmul(a, b, across) + matmul(c, d, across),
        mixed_grad, qkv_full, up_grad, up_full,
    )
    branch = lax.psum_scatter(
        step(lambda a, b: stacked(place, a, b, cols), branch_terms, branch_near), "col", tiled=False
    )
    up_both_a = staying(cut(normed_own, 0), up_grad, up_sent_a)
    up_cross_a = swap_x(up_both_a)
    norm_near = swap_core(step(bf16, norm_terms[count:]))
    down_grad = settled(down_a, w_down.shape, 0, 0, None)
    norm_parts = exchange(step(lambda a, b: stacked(place, a, b, cols), norm_terms, norm_near))
    up_both_b = staying(cut(normed_own, 1), up_grad, up_sent_b)
    up_cross_b = swap_x(up_both_b)
    down_grad = settled(down_b, w_down.shape, 0, down_both_a.shape[0], down_grad)
    up_a = crossed(up_both_a, up_cross_a)
    qkv_both_a = staying(cut(normed_own, 0), mixed_grad, qkv_sent_a)
    qkv_cross_a = swap_x(qkv_both_a)
    out_sent = swap_row(leaving(attended, grad_plain))
    up_b = crossed(up_both_b, up_cross_b)
    qkv_both_b = staying(cut(normed_own, 1), mixed_grad, qkv_sent_b)
    qkv_cross_b = swap_x(qkv_both_b)
    up_weight_grad = settled(up_a, w_up.shape, 1, 0, None)
    up_weight_grad = settled(up_b, w_up.shape, 1, up_both_a.shape[0], up_weight_grad)
    gain_here = part(ln_gain, col, width, 0)

    def norm_sums(parts):
        total = jnp.sum(f32(parts), axis=0)
        scaled = total * gain_here
        return (
            total,
            jnp.stack([jnp.sum(scaled, axis=1), jnp.sum(scaled * normal, axis=1)]),
            jnp.sum(total * normal, axis=0),
            jnp.sum(total, axis=0),
        )

    norm_grad, sums, gain_sum, shift_sum = step(norm_sums, norm_parts)

    def line_step(values, bit):
        return lax.ppermute(values, "col", [(at, at ^ bit) for at in range(cols)])

    small = jnp.concatenate(
        [
            jnp.sum(f32(up_grad), axis=0),
            jnp.sum(f32(mixed_grad), axis=0),
            jnp.sum(f32(cotangent), axis=0),
            gain_sum,
            shift_sum,
        ]
    ).reshape(-1, 128)
    shared_at = (hidden + 3 * heads_width) // 128
    res_at = width // 128
    sums_next = line_step(sums, 1)
    small_other = swap_core(small)
    qkv_a = crossed(qkv_both_a, qkv_cross_a)
    sums, shared = step(
        lambda sums, arrived, small, other: (sums + arrived, (small + other)[shared_at:]),
        sums, sums_next, small, small_other,
    )
    sums_next = line_step(sums, 2)
    ends = shared[res_at:][None]
    ends_next = line_step(ends, 1)
    out_both = staying(attended, grad_own, out_sent)
    out_cross = swap_x(out_both)
    ends = step(lambda ends, arrived: pair(col % 2, ends, arrived, 0), ends, ends_next)
    ends_next = line_step(ends, 2)
    qkv_weight_grad = settled(qkv_a, w_qkv.shape, 1, 0, None)
    sums = (sums + sums_next) / (cols * width)
    tokens_grad = step(
        lambda sums, total: inv_scale
        * (total * gain_here - sums[0][:, None] - normal * sums[1][:, None])
        + f32(cotangent),
        sums, norm_grad,
    )

    def gather_small(small, other, shared, ends, arrived):
        return jnp.concatenate(
            [
                pair(core, small[: hidden // 128], other[: hidden // 128], 0),
                pair(core, small[hidden // 128 : shared_at], other[hidden // 128 : shared_at], 0),
                shared[:res_at],
                pair(col // 2, ends, arrived, 0).reshape(-1, 128),
            ]
        )

    output = step(lambda parts, block: bf16(f32(block) + f32(parts) + b_res), branch, tokens)
    small = step(gather_small, small, small_other, shared, ends, ends_next)
    small_next = swap_row(small)
    qkv_b = crossed(qkv_both_b, qkv_cross_b)
    small = step(jnp.add, small, small_next)
    small_next = swap_x(small)
    out_mine = crossed(out_both, out_cross)
    qkv_weight_grad = settled(qkv_b, w_qkv.shape, 1, qkv_both_a.shape[0], qkv_weight_grad)
    out_grad = settled(out_mine, w_out.shape, 0, 0, None)
    small = step(jnp.add, small, small_next)

    bounds = [0, 2 * hidden // 128, (2 * hidden + 6 * heads_width) // 128]
    bounds.append(bounds[-1] + res_at)
    up_bias_grad = small[: bounds[1]].reshape(-1)
    qkv_bias_grad = small[bounds[1] : bounds[2]].reshape(-1)
    res_bias_grad = small[bounds[2] : bounds[3]].reshape(-1)
    ends = small[bounds[3] :].reshape(cols, 2, width)
    gain_grad = ends[:, 0].reshape(-1)
    shift_grad = ends[:, 1].reshape(-1)
    return (
        output,
        tokens_grad,
        qkv_weight_grad,
        qkv_bias_grad,
        out_grad.reshape(w_out.shape),
        up_weight_grad,
        up_bias_grad,
        down_grad.reshape(w_down.shape),
        res_bias_grad,
        gain_grad,
        shift_grad,
    )


def solution(mesh):
    sizes = (mesh.shape["dp"], mesh.shape["row"], mesh.shape["col"])
    per_device = paired_device if sizes == (4, 2, 4) else general_device
    return jax.shard_map(
        per_device,
        mesh=mesh,
        in_specs=(
            P(("dp", "row"), "col"),
            P("dp", None),
            P("dp", None),
            P("row", "col"),
            P("col"),
            P("col", "row"),
            P("row", "col"),
            P("col"),
            P("col", "row"),
            P("col"),
            P(),
            P(),
            P(("dp", "row"), "col"),
        ),
        out_specs=(
            P(("dp", "row"), "col"),
            P(("dp", "row"), "col"),
            P("row", "col"),
            P("col"),
            P("col", "row"),
            P("row", "col"),
            P("col"),
            P("col", "row"),
            P("col"),
            P(),
            P(),
        ),
        check_vma=False,
    )
```

```python
import functools
import math

import jax
import jax.numpy as jnp
from jax import lax
from jax.experimental import pallas as pl
from jax.experimental.pallas import tpu as pltpu
from jax.sharding import PartitionSpec as P

HD = 64
ROT = 32
SEG = 256


norm_epsilon = 1e-05
masked_fill = -1e30
rotary_base = 10000.0


def precise_dot(left, right):
    return jnp.dot(left, right, precision=lax.Precision.HIGHEST, preferred_element_type=jnp.float32)


def ancestry(parent_row):
    seg_count = parent_row.shape[0]
    labels = jnp.arange(seg_count, dtype=jnp.int32)
    identity = jnp.eye(seg_count, dtype=jnp.float32)
    parent_hot = (parent_row[:, None] == labels[None, :]).astype(jnp.float32)

    def extend(rounds, reachable):
        return jnp.minimum(identity + precise_dot(parent_hot, reachable), 1.0)

    return lax.fori_loop(0, seg_count, extend, identity)


def rotate(values, cosines, sines):
    half_rot = ROT // 2
    former = values[..., :half_rot]
    latter = values[..., half_rot:ROT]
    return jnp.concatenate(
        [former * cosines - latter * sines, latter * cosines + former * sines, values[..., ROT:]],
        axis=-1,
    )


def angles_of(positions):
    frequency = jnp.exp(
        -math.log(rotary_base) * 2.0 * jnp.arange(ROT // 2, dtype=jnp.float32) / ROT
    )
    phase_angle = positions[:, None] * frequency[None, :]
    return (jnp.cos(phase_angle)[:, None, :], jnp.sin(phase_angle)[:, None, :])


def reorder_rows(gradient, row_count, dp_count):
    leading = gradient.shape[0]
    blocked = gradient.reshape(
        row_count, dp_count, leading // (row_count * dp_count), gradient.shape[1]
    )
    return jnp.transpose(blocked, (1, 0, 2, 3)).reshape(leading, gradient.shape[1])


def reorder_cols(gradient, row_count, dp_count):
    trailing = gradient.shape[1]
    blocked = gradient.reshape(
        gradient.shape[0], row_count, dp_count, trailing // (row_count * dp_count)
    )
    return jnp.transpose(blocked, (0, 2, 1, 3)).reshape(gradient.shape[0], trailing)


def general_device(
    tokens,
    parent,
    depth,
    w_qkv,
    b_qkv,
    w_out,
    w_up,
    b_up,
    w_down,
    b_res,
    ln_gain,
    ln_bias,
    cotangent,
):
    tok_rows = tokens.shape[0]
    col_width = tokens.shape[1]
    row_count = lax.axis_size("row")
    dp_count = lax.axis_size("dp")
    row_start = lax.axis_index("row") * tok_rows
    local_heads = w_out.shape[0] // HD
    seg_count = parent.shape[1]
    labels = jnp.arange(seg_count, dtype=jnp.int32)
    reachable = ancestry(parent[0])
    query_index = row_start + jnp.arange(tok_rows, dtype=jnp.int32)
    query_seg = query_index // SEG
    query_hot = (query_seg[:, None] == labels[None, :]).astype(jnp.float32)
    query_reach = precise_dot(query_hot, reachable)
    levels = precise_dot(query_hot, depth[0].astype(jnp.float32)[:, None])[:, 0]
    positions = levels * SEG + (query_index % SEG).astype(jnp.float32)
    cosines, sines = angles_of(positions)
    score_scale = HD ** (-0.5)

    def permit(key_len):
        key_index = jnp.arange(key_len, dtype=jnp.int32)
        key_seg = key_index // SEG
        key_hot = (key_seg[:, None] == labels[None, :]).astype(jnp.float32)
        linked = precise_dot(query_reach, key_hot.T) > 0.5
        return linked & (
            (query_seg[:, None] != key_seg[None, :]) | (query_index[:, None] >= key_index[None, :])
        )

    whole = lax.all_gather(tokens, "col", axis=1, tiled=True).astype(jnp.float32)
    centred = whole - jnp.mean(whole, axis=1, keepdims=True)
    inv_scale = lax.rsqrt(jnp.mean(centred * centred, axis=1, keepdims=True) + norm_epsilon)
    normal = centred * inv_scale
    normed = (normal * ln_gain + ln_bias).astype(jnp.bfloat16)
    qkv_full, up_full, out_full, down_full = (
        lax.all_gather(w_qkv.astype(jnp.bfloat16), "row", axis=0, tiled=True),
        lax.all_gather(w_up.astype(jnp.bfloat16), "row", axis=0, tiled=True),
        lax.all_gather(w_out.astype(jnp.bfloat16), "row", axis=1, tiled=True),
        lax.all_gather(w_down.astype(jnp.bfloat16), "row", axis=1, tiled=True),
    )
    mixed = (jnp.dot(normed, qkv_full, preferred_element_type=jnp.float32) + b_qkv).reshape(
        tok_rows, local_heads, 3, HD
    )

    def rotate_pair(query_pre, key_pre):
        return (rotate(query_pre, cosines, sines), rotate(key_pre, cosines, sines))

    rotated, rotate_back = jax.vjp(rotate_pair, mixed[:, :, 0], mixed[:, :, 1])
    queries = rotated[0].astype(jnp.bfloat16)
    key_rows = rotated[1].astype(jnp.bfloat16)
    value_rows = mixed[:, :, 2].astype(jnp.bfloat16)
    key_flat = key_rows.reshape(tok_rows, local_heads * HD)
    value_flat = value_rows.reshape(tok_rows, local_heads * HD)

    def scores_for(key_part):
        raw_scores = (
            jnp.einsum("qhe,khe->hqk", queries, key_part, preferred_element_type=jnp.float32)
            * score_scale
        )
        allowed = permit(key_part.shape[0])
        return (jnp.where(allowed[None], raw_scores, masked_fill), allowed)

    pieces = (
        lax.all_gather(key_flat, "row", axis=0, tiled=True),
        lax.all_gather(value_flat, "row", axis=0, tiled=True),
    )
    running_top = jnp.full((local_heads, tok_rows), masked_fill, jnp.float32)
    key_len = pieces[0].shape[0]
    key_part = pieces[0].reshape(key_len, local_heads, HD)
    value_part = pieces[1].reshape(key_len, local_heads, HD)
    scores, allowed = scores_for(key_part)
    new_top = jnp.maximum(running_top, jnp.max(scores, axis=2))
    exponent = jnp.where(allowed[None], jnp.exp(scores - new_top[:, :, None]), 0.0)
    running_sum = jnp.sum(exponent, axis=2)
    weighted = jnp.einsum(
        "hqk,khe->hqe",
        exponent.astype(jnp.bfloat16),
        value_part,
        preferred_element_type=jnp.float32,
    )
    running_top, running_sum, weighted = (new_top, running_sum, weighted)
    log_total = running_top + jnp.log(running_sum)
    attn_exact = weighted / running_sum[:, :, None]
    attended = (
        jnp.transpose(attn_exact, (1, 0, 2))
        .reshape(tok_rows, local_heads * HD)
        .astype(jnp.bfloat16)
    )
    hidden_up = jnp.dot(normed, up_full, preferred_element_type=jnp.float32) + b_up
    activated, gelu_back = jax.vjp(functools.partial(jax.nn.gelu, approximate=True), hidden_up)
    activated = activated.astype(jnp.bfloat16)
    branch_terms = jnp.dot(attended, out_full, preferred_element_type=jnp.float32) + jnp.dot(
        activated, down_full, preferred_element_type=jnp.float32
    )
    branch = lax.psum_scatter(
        branch_terms.astype(jnp.bfloat16), "col", scatter_dimension=1, tiled=True
    ).astype(jnp.float32)
    output = (tokens.astype(jnp.float32) + branch + b_res).astype(jnp.bfloat16)
    grad_full = lax.all_gather(cotangent, "col", axis=1, tiled=True)
    res_bias_grad = jnp.sum(cotangent.astype(jnp.float32), axis=0)
    down_grad = jnp.einsum("tf,td->fd", activated, grad_full, preferred_element_type=jnp.float32)
    out_grad = jnp.einsum("te,td->ed", attended, grad_full, preferred_element_type=jnp.float32)
    act_grad = jnp.einsum("td,fd->tf", grad_full, down_full, preferred_element_type=jnp.float32)
    up_grad = gelu_back(act_grad)[0].astype(jnp.bfloat16)
    attn_grad = jnp.einsum(
        "td,ed->te", grad_full, out_full, preferred_element_type=jnp.float32
    ).astype(jnp.bfloat16)
    up_bias_grad = jnp.sum(up_grad.astype(jnp.float32), axis=0)
    up_weight_grad = jnp.einsum("td,tf->df", normed, up_grad, preferred_element_type=jnp.float32)
    out_heads = attn_grad.reshape(tok_rows, local_heads, HD)
    delta_sum = jnp.einsum("qhe,hqe->hq", out_heads.astype(jnp.float32), attn_exact)
    pieces = (
        lax.all_gather(key_flat, "row", axis=0, tiled=True),
        lax.all_gather(value_flat, "row", axis=0, tiled=True),
    )
    key_len = pieces[0].shape[0]
    key_part = pieces[0].reshape(key_len, local_heads, HD)
    value_part = pieces[1].reshape(key_len, local_heads, HD)
    scores, allowed = scores_for(key_part)
    softmaxed = jnp.where(allowed[None], jnp.exp(scores - log_total[:, :, None]), 0.0)
    prob_grad = jnp.einsum(
        "qhe,khe->hqk", out_heads, value_part, preferred_element_type=jnp.float32
    )
    score_grad = (softmaxed * (prob_grad - delta_sum[:, :, None])).astype(jnp.bfloat16)
    query_grad = (
        jnp.einsum("hqk,khe->qhe", score_grad, key_part, preferred_element_type=jnp.float32)
        * score_scale
    )
    key_grad = (
        jnp.einsum("hqk,qhe->khe", score_grad, queries, preferred_element_type=jnp.float32)
        * score_scale
    )
    value_grad = jnp.einsum(
        "hqk,qhe->khe",
        softmaxed.astype(jnp.bfloat16),
        out_heads,
        preferred_element_type=jnp.float32,
    )
    stacked = jnp.stack([key_grad, value_grad], axis=1).reshape(key_len, 2 * local_heads * HD)
    pair_grad = stacked
    query_grad, pair_grad = (query_grad, pair_grad)
    own_pairs = (
        lax.psum_scatter(pair_grad.astype(jnp.bfloat16), "row", scatter_dimension=0, tiled=True)
        .astype(jnp.float32)
        .reshape(tok_rows, 2, local_heads, HD)
    )
    query_pre, key_pre = rotate_back((query_grad, own_pairs[:, 0]))
    mixed_grad = (
        jnp.stack([query_pre, key_pre, own_pairs[:, 1]], axis=2)
        .reshape(tok_rows, 3 * local_heads * HD)
        .astype(jnp.bfloat16)
    )
    qkv_bias_grad = jnp.sum(mixed_grad.astype(jnp.float32), axis=0)
    qkv_weight_grad = jnp.einsum(
        "td,tc->dc", normed, mixed_grad, preferred_element_type=jnp.float32
    )
    norm_part = jnp.einsum(
        "tc,dc->td", mixed_grad, qkv_full, preferred_element_type=jnp.float32
    ) + jnp.einsum("tf,df->td", up_grad, up_full, preferred_element_type=jnp.float32)
    norm_grad = lax.psum(norm_part.astype(jnp.bfloat16), "col").astype(jnp.float32)
    gain_grad = jnp.sum(norm_grad * normal, axis=0)
    shift_grad = jnp.sum(norm_grad, axis=0)
    scaled = norm_grad * ln_gain
    mean_scaled = jnp.mean(scaled, axis=1, keepdims=True)
    mean_mixed = jnp.mean(scaled * normal, axis=1, keepdims=True)
    col_start = lax.axis_index("col") * col_width
    scaled_share = lax.dynamic_slice_in_dim(scaled, col_start, col_width, 1)
    normal_share = lax.dynamic_slice_in_dim(normal, col_start, col_width, 1)
    tokens_grad = inv_scale * (
        scaled_share - mean_scaled - normal_share * mean_mixed
    ) + cotangent.astype(jnp.float32)
    qkv_bias_grad, up_bias_grad, res_bias_grad, gain_grad, shift_grad = (
        lax.psum(qkv_bias_grad.astype(jnp.bfloat16), ("dp", "row")).astype(jnp.float32),
        lax.psum(up_bias_grad.astype(jnp.bfloat16), ("dp", "row")).astype(jnp.float32),
        lax.psum(res_bias_grad.astype(jnp.bfloat16), ("dp", "row")).astype(jnp.float32),
        lax.psum(gain_grad.astype(jnp.bfloat16), ("dp", "row")).astype(jnp.float32),
        lax.psum(shift_grad.astype(jnp.bfloat16), ("dp", "row")).astype(jnp.float32),
    )
    pieces_now = (
        lax.psum_scatter(
            reorder_rows(qkv_weight_grad, row_count, dp_count).astype(jnp.bfloat16),
            ("dp", "row"),
            scatter_dimension=0,
            tiled=True,
        ).astype(jnp.float32),
        lax.psum_scatter(
            reorder_rows(up_weight_grad, row_count, dp_count).astype(jnp.bfloat16),
            ("dp", "row"),
            scatter_dimension=0,
            tiled=True,
        ).astype(jnp.float32),
        lax.psum_scatter(
            reorder_cols(out_grad, row_count, dp_count).astype(jnp.bfloat16),
            ("dp", "row"),
            scatter_dimension=1,
            tiled=True,
        ).astype(jnp.float32),
        lax.psum_scatter(
            reorder_cols(down_grad, row_count, dp_count).astype(jnp.bfloat16),
            ("dp", "row"),
            scatter_dimension=1,
            tiled=True,
        ).astype(jnp.float32),
    )
    qkv_weight_grad, up_weight_grad, out_grad, down_grad = (
        lax.all_gather(pieces_now[0].astype(jnp.bfloat16), "dp", axis=0, tiled=True).astype(
            jnp.float32
        ),
        lax.all_gather(pieces_now[1].astype(jnp.bfloat16), "dp", axis=0, tiled=True).astype(
            jnp.float32
        ),
        lax.all_gather(pieces_now[2].astype(jnp.bfloat16), "dp", axis=1, tiled=True).astype(
            jnp.float32
        ),
        lax.all_gather(pieces_now[3].astype(jnp.bfloat16), "dp", axis=1, tiled=True).astype(
            jnp.float32
        ),
    )
    return (
        output,
        tokens_grad,
        qkv_weight_grad,
        qkv_bias_grad,
        out_grad,
        up_weight_grad,
        up_bias_grad,
        down_grad,
        res_bias_grad,
        gain_grad,
        shift_grad,
    )


SWAP_ROW = [(0, 1), (1, 0)]
SWAP_X = [(0, 2), (2, 0), (1, 3), (3, 1)]
SWAP_CORE = [(0, 1), (1, 0), (2, 3), (3, 2)]


def bf16(values):
    return values.astype(jnp.bfloat16)


def f32(values):
    return values.astype(jnp.float32)


def matmul(left, right, dims=((1,), (0,))):
    return lax.dot_general(left, right, (dims, ((), ())), preferred_element_type=jnp.float32)


def swap_row(values):
    return lax.ppermute(values, "row", SWAP_ROW)


def swap_x(values):
    return lax.ppermute(values, "dp", SWAP_X)


def swap_core(values):
    return lax.ppermute(values, "dp", SWAP_CORE)


def pick(index, first, second):
    return jnp.where(index == 0, first, second)


def pair(index, mine, theirs, axis):
    return pick(
        index,
        jnp.concatenate([mine, theirs], axis=axis),
        jnp.concatenate([theirs, mine], axis=axis),
    )


def after(value, *earlier):
    return lax.optimization_barrier((value,) + earlier)[0]


def rotary_tables(positions):
    lane = jnp.arange(2 * HD, dtype=jnp.int32) % HD
    half_rot = ROT // 2
    frequency = jnp.exp(
        -math.log(rotary_base) * 2.0 * (lane % half_rot).astype(jnp.float32) / ROT
    )
    angle = positions[:, None] * frequency[None, :]
    turned = (lane < ROT)[None, :]
    sines = jnp.sin(angle)
    return (
        jnp.where(turned, jnp.cos(angle), 1.0),
        jnp.where((lane < half_rot)[None, :], -sines, 0.0),
        jnp.where(turned & (lane >= half_rot)[None, :], sines, 0.0),
    )


def turn(values, cosines, sines_low, sines_high):
    width = values.shape[1]
    half_rot = ROT // 2
    return (
        values * cosines
        + pltpu.roll(values, width - half_rot, 1) * sines_low
        + pltpu.roll(values, half_rot, 1) * sines_high
    )


def mixed_kernel(
    normed_ref, weight_ref, bias_ref, cos_ref, low_ref, high_ref, query_ref, keyval_ref
):
    cosines, low, high = cos_ref[...], low_ref[...], high_ref[...]
    rows, half = query_ref.shape
    first = lax.broadcasted_iota(jnp.int32, (rows, 2 * HD), 1) < HD
    scale = HD ** (-0.5)
    mixed = matmul(normed_ref[...], weight_ref[...]) + bias_ref[...]
    for at in range(half // (2 * HD)):
        tiles = [mixed[:, (3 * at + part) * 2 * HD : (3 * at + part + 1) * 2 * HD] for part in range(3)]
        query = jnp.where(first, tiles[0], tiles[1])
        key = jnp.where(first, pltpu.roll(tiles[0], HD, 1), pltpu.roll(tiles[2], HD, 1))
        value = jnp.where(first, tiles[1], tiles[2])
        here = slice(at * 2 * HD, (at + 1) * 2 * HD)
        query_ref[:, here] = bf16(f32(bf16(turn(query, cosines, low, high))) * scale)
        keyval_ref[:, here] = bf16(turn(key, cosines, low, high))
        keyval_ref[:, half + at * 2 * HD : half + (at + 1) * 2 * HD] = bf16(value)


def join_kernel(row_ref, dq_ref, dkv_ref, sent_ref, cos_ref, low_ref, high_ref, out_ref):
    cosines, low, high = cos_ref[...], -low_ref[...], -high_ref[...]
    rows = dq_ref.shape[0]
    half = dq_ref.shape[1]
    first = lax.broadcasted_iota(jnp.int32, (rows, 2 * HD), 1) < HD
    owner = row_ref[0] == 0
    for at in range(half // (2 * HD)):
        here = slice(at * 2 * HD, (at + 1) * 2 * HD)
        there = slice(half + at * 2 * HD, half + (at + 1) * 2 * HD)
        query = turn(dq_ref[:, here], cosines, low, high)
        key = dkv_ref[:, here] + jnp.where(owner, f32(sent_ref[:, here]), 0.0)
        value = dkv_ref[:, there] + jnp.where(owner, f32(sent_ref[:, there]), 0.0)
        key = pltpu.roll(turn(key, cosines, low, high), HD, 1)
        tiles = (jnp.where(first, query, key), jnp.where(first, value, query), jnp.where(first, key, value))
        for part in range(3):
            out_ref[:, (3 * at + part) * 2 * HD : (3 * at + part + 1) * 2 * HD] = bf16(tiles[part])


def tree_kernel(
    parent_ref, row_ref, query_ref, keyval_ref, trunk_ref, grad_ref,
    out_ref, dq_ref, dkv_ref, dtrunk_ref,
    keys, values, dkeys, dvalues,
):
    tree = pl.program_id(0)
    row = row_ref[0]
    rows, half = query_ref.shape
    trunk_len = trunk_ref.shape[0]
    segs = rows // SEG
    trunk_segs = trunk_len // SEG
    seg_count = parent_ref.shape[1]
    first_row = row == 0
    keys[...] = jnp.where(first_row, keyval_ref[:, :half], trunk_ref[:, :half])
    values[...] = jnp.where(first_row, keyval_ref[:, half:], trunk_ref[:, half:])
    dkeys[...] = jnp.zeros_like(dkeys)
    dvalues[...] = jnp.zeros_like(dvalues)
    lane = lax.broadcasted_iota(jnp.int32, (1, half), 1)
    causal = lax.broadcasted_iota(jnp.int32, (SEG, SEG), 0) >= lax.broadcasted_iota(
        jnp.int32, (SEG, SEG), 1
    )
    across = ((1,), (1,))
    down = ((0,), (0,))
    for seg in range(segs):
        here = slice(seg * SEG, (seg + 1) * SEG)
        above = parent_ref[tree, row * segs + seg]
        linked = [above == at for at in range(trunk_segs)]
        for _ in range(seg_count - 2):
            above = jnp.where(above >= 0, parent_ref[tree, jnp.maximum(above, 0)], -1)
            linked = [was | (above == at) for at, was in enumerate(linked)]
        bias = [jnp.where(is_linked, 0.0, masked_fill) for is_linked in linked]
        query, grad = query_ref[here, :], grad_ref[here, :]
        own_key, own_value = keyval_ref[here, :half], keyval_ref[here, half:]
        attended = jnp.zeros((SEG, half), jnp.float32)
        dquery = jnp.zeros((SEG, half), jnp.float32)
        dkey = jnp.zeros((SEG, half), jnp.float32)
        dvalue = jnp.zeros((SEG, half), jnp.float32)
        for head in range(half // HD):
            mine = (lane >= head * HD) & (lane < (head + 1) * HD)
            head_query = jnp.where(mine, query, jnp.zeros_like(query))
            head_grad = jnp.where(mine, grad, jnp.zeros_like(grad))
            scores = [
                matmul(head_query, keys[at * SEG : (at + 1) * SEG, :], across) + bias[at]
                for at in range(trunk_segs)
            ] + [jnp.where(causal, matmul(head_query, own_key, across), masked_fill)]
            top = functools.reduce(jnp.maximum, [jnp.max(s, axis=1, keepdims=True) for s in scores])
            powers = [jnp.exp(s - top) for s in scores]
            total = functools.reduce(jnp.add, [jnp.sum(p, axis=1, keepdims=True) for p in powers])
            probs = [p / total for p in powers]
            low = [bf16(p) for p in probs]
            blocks = [values[at * SEG : (at + 1) * SEG, :] for at in range(trunk_segs)] + [own_value]
            prob_grads = [matmul(head_grad, v, across) for v in blocks]
            delta = functools.reduce(
                jnp.add, [jnp.sum(p * g, axis=1, keepdims=True) for p, g in zip(probs, prob_grads)]
            )
            score_grads = [bf16(p * (g - delta)) for p, g in zip(probs, prob_grads)]
            head_out = functools.reduce(jnp.add, [matmul(p, v) for p, v in zip(low, blocks)])
            attended = jnp.where(mine, head_out, attended)
            key_blocks = [keys[at * SEG : (at + 1) * SEG, :] for at in range(trunk_segs)] + [own_key]
            head_dq = functools.reduce(jnp.add, [matmul(s, u) for s, u in zip(score_grads, key_blocks)])
            dquery = jnp.where(mine, head_dq, dquery)
            dkey = dkey + matmul(score_grads[-1], head_query, down)
            dvalue = dvalue + matmul(low[-1], head_grad, down)
            for at in range(trunk_segs):
                spot = slice(at * SEG, (at + 1) * SEG)
                dkeys[spot, :] += matmul(score_grads[at], head_query, down)
                dvalues[spot, :] += matmul(low[at], head_grad, down)
        out_ref[here, :] = bf16(attended)
        dq_ref[here, :] = dquery * HD ** (-0.5)
        dkv_ref[here, :half] = dkey
        dkv_ref[here, half:] = dvalue
    dtrunk_ref[:, :half] = bf16(dkeys[...])
    dtrunk_ref[:, half:] = bf16(dvalues[...])

    @pl.when(first_row)
    def _():
        dkv_ref[:, :half] += dkeys[...]
        dkv_ref[:, half:] += dvalues[...]


def store_blocks(place_ref, sides, full_ref, own_refs, plain_refs):
    row, slab = place_ref[1], place_ref[2]
    for side, values in enumerate(sides):
        width = values[0].shape[1]
        for source, value in enumerate(values):
            within = source % 2
            here = row == source // 2

            def put(refs):
                if len(refs) == 1:
                    refs[0][side, :, within * width : (within + 1) * width] = value
                else:
                    refs[within][side] = value

            @pl.when(here)
            def _():
                full_ref[side, :, within * width : (within + 1) * width] = value
                put(own_refs)

            @pl.when(jnp.logical_not(here))
            def _():
                put(plain_refs)
                at = (2 + jnp.where(slab == 0, within, 1 - within)) * width
                full_ref[side, :, pl.ds(pl.multiple_of(at, width), width)] = value


def gather_kernel(place_ref, mine_ref, theirs_ref, full_ref, own_ref, plain_ref):
    sides = [[ref[at] for at in range(ref.shape[0])] for ref in (mine_ref, theirs_ref)]
    store_blocks(place_ref, sides, full_ref, [own_ref], [plain_ref])


def norm_kernel(place_ref, gain_ref, bias_ref, mine_ref, theirs_ref, full_ref, *outs):
    normal_ref, scale_ref = outs[4:]
    sides = []
    for side, ref in enumerate((mine_ref, theirs_ref)):
        values = [f32(ref[at]) for at in range(ref.shape[0])]
        features = len(values) * values[0].shape[1]
        mean = functools.reduce(jnp.add, [jnp.sum(v, axis=1, keepdims=True) for v in values]) / features
        centred = [v - mean for v in values]
        square = functools.reduce(jnp.add, [jnp.sum(v * v, axis=1, keepdims=True) for v in centred])
        inv_scale = lax.rsqrt(square / features + norm_epsilon)
        normals = [v * inv_scale for v in centred]
        if side == 0:
            scale_ref[...] = inv_scale
            for source, normal in enumerate(normals):

                @pl.when(place_ref[0] == source)
                def _():
                    normal_ref[...] = normal

        sides.append(
            [
                bf16(normal * gain_ref[source : source + 1, :] + bias_ref[source : source + 1, :])
                for source, normal in enumerate(normals)
            ]
        )
    store_blocks(place_ref, sides, full_ref, outs[:2], outs[2:4])


def pair_rows(rows, width):
    return pl.BlockSpec((2, rows, width), lambda at, *_: (0, at, 0))


def gathered(place, mine, theirs, norm=None):
    blocks, count, width = mine.shape
    rows = SEG if norm is None else SEG // 2
    full = blocks * width
    in_specs = [pl.BlockSpec((blocks, rows, width), lambda at, *_: (0, at, 0))] * 2
    parts = [full // 2] * 2 if norm is None else [width] * 4
    out_specs = [pair_rows(rows, size) for size in [full] + parts]
    out_shape = [
        jax.ShapeDtypeStruct((2, count, size), jnp.bfloat16) for size in [full] + parts
    ]
    operands = [mine, theirs]
    if norm is not None:
        gain = [values.reshape(blocks, width) for values in norm]
        operands = gain + operands
        in_specs = [pl.BlockSpec((blocks, width), lambda at, *_: (0, 0))] * 2 + in_specs
        out_specs = out_specs + [row_block(rows, width), row_block(rows, 1)]
        out_shape = out_shape + [
            jax.ShapeDtypeStruct((count, width), jnp.float32),
            jax.ShapeDtypeStruct((count, 1), jnp.float32),
        ]
    results = pl.pallas_call(
        gather_kernel if norm is None else norm_kernel,
        grid_spec=pltpu.PrefetchScalarGridSpec(
            num_scalar_prefetch=1, grid=(count // rows,), in_specs=in_specs, out_specs=out_specs
        ),
        out_shape=out_shape,
        cost_estimate=pl.CostEstimate(flops=1, bytes_accessed=1, transcendentals=0),
        name="join_blocks" if norm is None else "norm_blocks",
    )(place, *operands)
    last = len(parts) + 1
    return [values.reshape(2 * count, -1) for values in results[:last]] + list(results[last:])


def stack_kernel(place_ref, terms_ref, arrived_ref, out_ref):
    row, slab = place_ref[1], place_ref[2]
    width = out_ref.shape[2]
    for spot in range(4):
        here = slice(spot * width, (spot + 1) * width)
        value = bf16(f32(terms_ref[:, here]) + f32(arrived_ref[:, here]))
        if spot < 2:
            out_ref[2 * row + spot] = value
        else:
            out_ref[2 * (1 - row) + jnp.where(slab == 0, spot - 2, 3 - spot)] = value


def stacked(place, terms, arrived, blocks):
    count, full = arrived.shape
    rows = SEG
    width = full // blocks
    return pl.pallas_call(
        stack_kernel,
        grid_spec=pltpu.PrefetchScalarGridSpec(
            num_scalar_prefetch=1,
            grid=(count // rows,),
            in_specs=[row_block(rows, full), row_block(rows, full)],
            out_specs=pl.BlockSpec((blocks, rows, width), lambda at, *_: (0, at, 0)),
        ),
        out_shape=jax.ShapeDtypeStruct((blocks, count, width), jnp.bfloat16),
        cost_estimate=pl.CostEstimate(flops=1, bytes_accessed=1, transcendentals=0),
        name="stack_blocks",
    )(place, terms, arrived)


def cast_rows_kernel(place_ref, master_ref, own_ref, send_ref):
    value = bf16(master_ref[...])
    own_ref[...] = value
    half = pl.num_programs(0) // 2

    @pl.when(pl.program_id(0) // half == place_ref[2])
    def _():
        send_ref[...] = value


def cast_cols_kernel(place_ref, master_ref, own_ref, send_ref):
    value = bf16(master_ref[...])
    own_ref[...] = value
    half = value.shape[1] // 2
    send_ref[...] = jnp.where(place_ref[2] == 0, value[:, :half], value[:, half:])


def cast_weight(place, master, axis):
    height, width = master.shape
    rows = min(2 * SEG, master.shape[0] // 4)
    if axis == 0:
        width = width // 2
        steps = height // rows
        half = steps // 2
        specs = [
            pl.BlockSpec((rows, width), lambda at, place_ref: (at, place_ref[3])),
            pl.BlockSpec((rows, width), lambda at, place_ref: (at, 0)),
            pl.BlockSpec(
                (rows, width), lambda at, place_ref: (jnp.clip(at - half * place_ref[2], 0, half - 1), 0)
            ),
        ]
        send = (height // 2, width)
        whole = (2 * height, width)
    else:
        height = height // 2
        steps = height // rows
        specs = [
            pl.BlockSpec((rows, width), lambda at, place_ref: (at + steps * place_ref[3], 0)),
            pl.BlockSpec((rows, width), lambda at, place_ref: (at, 0)),
            pl.BlockSpec((rows, width // 2), lambda at, place_ref: (at, 0)),
        ]
        send = (height, width // 2)
        whole = (height, 2 * width)
    return pl.pallas_call(
        cast_rows_kernel if axis == 0 else cast_cols_kernel,
        grid_spec=pltpu.PrefetchScalarGridSpec(
            num_scalar_prefetch=1, grid=(steps,), in_specs=specs[:1], out_specs=specs[1:]
        ),
        out_shape=[
            jax.ShapeDtypeStruct(whole, jnp.bfloat16),
            jax.ShapeDtypeStruct(send, jnp.bfloat16),
        ],
        cost_estimate=pl.CostEstimate(flops=1, bytes_accessed=1, transcendentals=0),
        name="cast_weight",
    )(place, master)


def settle_kernel(axis, place_ref, mine_ref, theirs_ref, *refs):
    out_ref = refs[-1]
    mine, theirs = f32(mine_ref[...]), f32(theirs_ref[...])
    if axis == 0:
        out_ref[place_ref[3]] = mine
        out_ref[1 - place_ref[3]] = theirs
    else:
        width = mine.shape[1]
        first = place_ref[3] == 0
        out_ref[:, :width] = jnp.where(first, mine, theirs)
        out_ref[:, width:] = jnp.where(first, theirs, mine)


def settle(place, mine, theirs, shape, axis, offset, dest=None):
    rows, width = mine.shape
    at = offset // rows
    whole = pl.BlockSpec((rows, width), lambda *_: (0, 0))
    if axis == 0:
        shape = (2, shape[0] // 2, width)
        out_spec = pl.BlockSpec((2, rows, width), lambda *_: (0, at, 0))
    else:
        out_spec = pl.BlockSpec((rows, 2 * width), lambda *_: (at, 0))
    in_specs = [whole, whole]
    operands = [place, mine, theirs]
    aliases = {}
    if dest is not None:
        in_specs.append(pl.BlockSpec(memory_space=pl.ANY))
        operands.append(dest)
        aliases = {3: 0}
    return pl.pallas_call(
        functools.partial(settle_kernel, axis),
        grid_spec=pltpu.PrefetchScalarGridSpec(
            num_scalar_prefetch=1, grid=(1,), in_specs=in_specs, out_specs=out_spec
        ),
        out_shape=jax.ShapeDtypeStruct(shape, jnp.float32),
        input_output_aliases=aliases,
        cost_estimate=pl.CostEstimate(flops=1, bytes_accessed=1, transcendentals=0),
        name="settle",
    )(*operands)


def row_block(rows, width):
    return pl.BlockSpec((rows, width), lambda at, *_: (at, 0))


def mixed_heads(normed, weight, bias, tables):
    count, depth = normed.shape
    width = weight.shape[1]
    rows = SEG
    return pl.pallas_call(
        mixed_kernel,
        grid=(count // rows,),
        in_specs=[
            row_block(rows, depth),
            pl.BlockSpec((depth, width), lambda at: (0, 0)),
            pl.BlockSpec((1, width), lambda at: (0, 0)),
        ]
        + [row_block(rows, 2 * HD)] * 3,
        out_specs=[row_block(rows, width // 3), row_block(rows, 2 * width // 3)],
        out_shape=[
            jax.ShapeDtypeStruct((count, width // 3), jnp.bfloat16),
            jax.ShapeDtypeStruct((count, 2 * width // 3), jnp.bfloat16),
        ],
        cost_estimate=pl.CostEstimate(flops=1, bytes_accessed=1, transcendentals=0),
        name="mixed_heads",
    )(normed, weight, bias.reshape(1, width), *tables)


def join_heads(row, dq, dkv, sent, tables):
    count, half = dq.shape
    rows = 2 * SEG
    return pl.pallas_call(
        join_kernel,
        grid_spec=pltpu.PrefetchScalarGridSpec(
            num_scalar_prefetch=1,
            grid=(count // rows,),
            in_specs=[row_block(rows, half), row_block(rows, 2 * half), row_block(rows, 2 * half)]
            + [row_block(rows, 2 * HD)] * 3,
            out_specs=row_block(rows, 3 * half),
        ),
        out_shape=jax.ShapeDtypeStruct((count, 3 * half), jnp.bfloat16),
        cost_estimate=pl.CostEstimate(flops=1, bytes_accessed=1, transcendentals=0),
        name="join_heads",
    )(row, dq, dkv, sent, *tables)


def tree_attention(parents, row, query, keyval, trunk, grad):
    trees = parents.shape[0]
    count, half = query.shape
    rows = count // trees
    keys = trunk.shape[0] // trees
    pairs = count * (keys + SEG) * (half // HD)
    return pl.pallas_call(
        tree_kernel,
        grid_spec=pltpu.PrefetchScalarGridSpec(
            num_scalar_prefetch=2,
            grid=(trees,),
            in_specs=[
                row_block(rows, half),
                row_block(rows, 2 * half),
                row_block(keys, 2 * half),
                row_block(rows, half),
            ],
            out_specs=[
                row_block(rows, half),
                row_block(rows, half),
                row_block(rows, 2 * half),
                row_block(keys, 2 * half),
            ],
            scratch_shapes=[pltpu.VMEM((keys, half), jnp.bfloat16)] * 2
            + [pltpu.VMEM((keys, half), jnp.float32)] * 2,
        ),
        out_shape=[
            jax.ShapeDtypeStruct((count, half), jnp.bfloat16),
            jax.ShapeDtypeStruct((count, half), jnp.float32),
            jax.ShapeDtypeStruct((count, 2 * half), jnp.float32),
            jax.ShapeDtypeStruct((trees * keys, 2 * half), jnp.bfloat16),
        ],
        cost_estimate=pl.CostEstimate(flops=1, bytes_accessed=1, transcendentals=0),
        name="tree_attention",
    )(parents, row, query, keyval, trunk, grad)


def paired_device(
    tokens,
    parent,
    depth,
    w_qkv,
    b_qkv,
    w_out,
    w_up,
    b_up,
    w_down,
    b_res,
    ln_gain,
    ln_bias,
    cotangent,
):
    count, width = tokens.shape
    row = lax.axis_index("row")
    col = lax.axis_index("col")
    core = lax.axis_index("dp") % 2
    slab = lax.axis_index("dp") // 2
    cols = lax.axis_size("col")
    half = 2 * width
    heads_width = w_out.shape[0] // 2
    hidden = w_up.shape[1] // 2
    place = jnp.stack([col, row, slab, core]).astype(jnp.int32)
    row_table = jnp.reshape(row, (1,)).astype(jnp.int32)
    down_dims = ((0,), (0,))
    across = ((1,), (1,))

    def part(values, at, size, axis):
        return lax.dynamic_slice_in_dim(values, at * size, size, axis)

    def exchange(stack):
        return lax.all_to_all(stack, "col", 0, 0, tiled=True)

    def to_all(block):
        return exchange(jnp.broadcast_to(block[None], (cols,) + block.shape))

    done = ()

    def step(run, *inputs):
        nonlocal done
        inputs, _ = lax.optimization_barrier((inputs, done))
        result = run(*inputs)
        done = result
        return result

    def wait(value):
        return step(lambda arrived: arrived, value)

    tokens_near = lax.all_gather(tokens, "col", axis=0)

    def ready(master, axis):
        whole, send = step(lambda weight: cast_weight(place, weight, axis), master)
        return whole, swap_row(send)

    def fill(whole, part_in, axis, last):
        at = whole.shape[axis] // 2 + (part_in.shape[axis] if last else 0)
        return step(lambda a, b: lax.dynamic_update_slice_in_dim(a, b, at, axis), whole, part_in)

    tables = jnp.concatenate([parent, depth], axis=0)
    tables = jnp.stack([tables, swap_core(tables)])
    parents = tables[:, 0]
    segs = count // SEG
    token = jnp.arange(count, dtype=jnp.int32)
    levels = jnp.zeros((2, count), jnp.float32)
    for seg in range(segs):
        level = lax.dynamic_slice_in_dim(tables[:, 1], row * segs + seg, 1, 1).astype(jnp.float32)
        levels = jnp.where((token // SEG == seg)[None, :], level, levels)
    positions = (levels * SEG + (token % SEG).astype(jnp.float32)[None, :]).reshape(2 * count)
    rotary = rotary_tables(positions)

    qkv_whole, qkv_row = ready(w_qkv, 0)
    up_whole, up_row = ready(w_up, 0)
    qkv_row = wait(qkv_row)
    qkv_x = swap_x(qkv_row)
    out_whole, out_row = ready(w_out, 1)
    down_whole, down_row = ready(w_down, 1)
    rotary = step(lambda *tables: tables, *rotary)
    qkv_whole = fill(qkv_whole, qkv_row, 0, False)
    up_row = wait(up_row)
    up_x = swap_x(up_row)
    qkv_x = wait(qkv_x)
    tokens_near = wait(tokens_near)
    tokens_far = swap_core(tokens_near)
    grad_near = to_all(after(cotangent, tokens_near))
    up_whole = fill(up_whole, up_row, 0, False)
    out_row = wait(out_row)
    out_x = swap_x(out_row)
    out_whole = fill(out_whole, out_row, 1, False)
    normed, own_a, own_b, plain_a, plain_b, normal, inv_scale = step(
        lambda mine, theirs: gathered(place, mine, theirs, (ln_gain, ln_bias)), tokens_near, tokens_far
    )
    qkv_full = fill(qkv_whole, qkv_x, 0, True)
    query, keyval = step(
        lambda left, right: mixed_heads(left, right, part(b_qkv, core, 3 * heads_width, 0), rotary),
        normed, qkv_full,
    )
    trunk = lax.ppermute(keyval, "row", [(0, 1)])
    root = math.sqrt(2.0 / math.pi)

    def feed(left, right):
        hidden_up = matmul(left, right) + part(b_up, core, hidden, 0)
        squared = hidden_up * hidden_up
        bend = jnp.tanh(root * (hidden_up + 0.044715 * squared * hidden_up))
        return bf16(0.5 * hidden_up * (1.0 + bend)), bf16(
            0.5 * (1.0 + bend)
            + 0.5 * hidden_up * (1.0 - bend * bend) * root * (1.0 + 3.0 * 0.044715 * squared)
        )

    out_x = wait(out_x)
    up_full = fill(up_whole, up_x, 0, True)
    down_row = wait(down_row)
    down_x = swap_x(down_row)
    activated, slope = step(feed, normed, up_full)
    grad_near = wait(grad_near)
    grad_far = swap_core(grad_near)
    out_full = fill(out_whole, out_x, 1, True)
    grad, grad_own, grad_plain = step(lambda mine, theirs: gathered(place, mine, theirs), grad_near, grad_far)

    def cut(values, at):
        size = values.shape[1] // 2
        return values[:, at * size : (at + 1) * size]

    def leaving(left, right):
        return step(lambda a, b: bf16(matmul(a, b, down_dims)), left, right)

    def staying(left, right, sent):
        return step(lambda a, b, c: bf16(matmul(a, b, down_dims) + f32(c)), left, right, sent)

    def crossed(both, arrived):
        mine = step(lambda a, b: bf16(f32(a) + f32(b)), both, arrived)
        return mine, swap_core(mine)

    def settled(pieces, shape, axis, offset, dest):
        operands = pieces if dest is None else pieces + (dest,)
        return step(
            lambda mine, theirs, *rest: settle(place, mine, theirs, shape, axis, offset, *rest), *operands
        )

    down_sent_a = swap_row(leaving(cut(activated, 0), grad_plain))
    down_sent_b = swap_row(leaving(cut(activated, 1), grad_plain))
    out_heads = step(lambda a, b: bf16(matmul(a, b, across)), grad, out_full)
    attended, query_grad, own_grad, trunk_grad = step(
        lambda *operands: tree_attention(parents, row_table, *operands), query, keyval, trunk, out_heads
    )
    trunk_sent = lax.ppermute(trunk_grad, "row", [(1, 0)])
    down_both_a = staying(cut(activated, 0), grad_own, down_sent_a)
    down_cross_a = swap_x(down_both_a)
    down_full = fill(fill(down_whole, down_row, 1, False), down_x, 1, True)
    up_grad = step(lambda a, b, c: bf16(matmul(a, b, across) * f32(c)), grad, down_full, slope)
    up_sent_a = swap_row(leaving(plain_a, up_grad))
    down_both_b = staying(cut(activated, 1), grad_own, down_sent_b)
    down_cross_b = swap_x(down_both_b)
    up_sent_b = swap_row(leaving(plain_b, up_grad))
    down_a = crossed(down_both_a, down_cross_a)
    branch_terms = step(
        lambda a, b, c, d: bf16(matmul(a, b) + matmul(c, d)), attended, out_full, activated, down_full
    )
    branch_near = swap_core(branch_terms[count:])
    mixed_grad = step(
        lambda *operands: join_heads(row_table, *operands, rotary), query_grad, own_grad, trunk_sent
    )
    qkv_sent_a = swap_row(leaving(plain_a, mixed_grad))
    down_b = crossed(down_both_b, down_cross_b)
    qkv_sent_b = swap_row(leaving(plain_b, mixed_grad))
    norm_terms = step(
        lambda a, b, c, d: bf16(matmul(a, b, across) + matmul(c, d, across)),
        mixed_grad, qkv_full, up_grad, up_full,
    )
    branch = lax.psum_scatter(
        step(lambda a, b: stacked(place, a, b, cols), branch_terms, branch_near), "col", tiled=False
    )
    up_both_a = staying(own_a, up_grad, up_sent_a)
    up_cross_a = swap_x(up_both_a)
    norm_near = swap_core(step(lambda terms: terms[count:], norm_terms))
    down_grad = settled(down_a, w_down.shape, 0, 0, None)
    norm_parts = exchange(step(lambda a, b: stacked(place, a, b, cols), norm_terms, norm_near))
    up_both_b = staying(own_b, up_grad, up_sent_b)
    up_cross_b = swap_x(up_both_b)
    down_grad = settled(down_b, w_down.shape, 0, down_both_a.shape[0], down_grad)
    up_a = crossed(up_both_a, up_cross_a)
    qkv_both_a = staying(own_a, mixed_grad, qkv_sent_a)
    qkv_cross_a = swap_x(qkv_both_a)
    out_sent = swap_row(leaving(attended, grad_plain))
    output = step(lambda parts, block: bf16(f32(block) + f32(parts) + b_res), branch, tokens)
    up_b = crossed(up_both_b, up_cross_b)
    qkv_both_b = staying(own_b, mixed_grad, qkv_sent_b)
    qkv_cross_b = swap_x(qkv_both_b)
    up_weight_grad = settled(up_a, w_up.shape, 1, 0, None)
    up_weight_grad = settled(up_b, w_up.shape, 1, up_both_a.shape[0], up_weight_grad)
    gain_here = part(ln_gain, col, width, 0)

    def norm_sums(parts):
        total = jnp.sum(f32(parts), axis=0)
        scaled = total * gain_here
        return (
            total,
            jnp.stack([jnp.sum(scaled, axis=1), jnp.sum(scaled * normal, axis=1)]),
            jnp.sum(total * normal, axis=0),
            jnp.sum(total, axis=0),
        )

    norm_grad, sums, gain_sum, shift_sum = step(norm_sums, norm_parts)

    def line_step(values, bit):
        return lax.ppermute(values, "col", [(at, at ^ bit) for at in range(cols)])

    small = jnp.concatenate(
        [
            jnp.sum(f32(up_grad), axis=0),
            jnp.sum(f32(mixed_grad), axis=0),
            jnp.sum(f32(cotangent), axis=0),
            gain_sum,
            shift_sum,
        ]
    ).reshape(-1, 128)
    shared_at = (hidden + 3 * heads_width) // 128
    res_at = width // 128
    sums_next = line_step(sums, 1)
    small_other = swap_core(small)
    qkv_a = crossed(qkv_both_a, qkv_cross_a)
    sums, shared = step(
        lambda sums, arrived, small, other: (sums + arrived, (small + other)[shared_at:]),
        sums, sums_next, small, small_other,
    )
    sums_next = line_step(sums, 2)
    ends = shared[res_at:][None]
    ends_next = line_step(ends, 1)
    out_both = staying(attended, grad_own, out_sent)
    out_cross = swap_x(out_both)
    ends = step(lambda ends, arrived: pair(col % 2, ends, arrived, 0), ends, ends_next)
    ends_next = line_step(ends, 2)
    qkv_weight_grad = settled(qkv_a, w_qkv.shape, 1, 0, None)
    sums = (sums + sums_next) / (cols * width)
    tokens_grad = step(
        lambda sums, total: inv_scale
        * (total * gain_here - sums[0][:, None] - normal * sums[1][:, None])
        + f32(cotangent),
        sums, norm_grad,
    )

    def gather_small(small, other, shared, ends, arrived):
        return jnp.concatenate(
            [
                pair(core, small[: hidden // 128], other[: hidden // 128], 0),
                pair(core, small[hidden // 128 : shared_at], other[hidden // 128 : shared_at], 0),
                shared[:res_at],
                pair(col // 2, ends, arrived, 0).reshape(-1, 128),
            ]
        )

    small = step(gather_small, small, small_other, shared, ends, ends_next)
    small_next = swap_row(small)
    qkv_b = crossed(qkv_both_b, qkv_cross_b)
    small = step(jnp.add, small, small_next)
    small_next = swap_x(small)
    out_mine = crossed(out_both, out_cross)
    qkv_weight_grad = settled(qkv_b, w_qkv.shape, 1, qkv_both_a.shape[0], qkv_weight_grad)
    out_grad = settled(out_mine, w_out.shape, 0, 0, None)
    small = step(jnp.add, small, small_next)

    bounds = [0, 2 * hidden // 128, (2 * hidden + 6 * heads_width) // 128]
    bounds.append(bounds[-1] + res_at)
    up_bias_grad = small[: bounds[1]].reshape(-1)
    qkv_bias_grad = small[bounds[1] : bounds[2]].reshape(-1)
    res_bias_grad = small[bounds[2] : bounds[3]].reshape(-1)
    ends = small[bounds[3] :].reshape(cols, 2, width)
    gain_grad = ends[:, 0].reshape(-1)
    shift_grad = ends[:, 1].reshape(-1)
    return (
        output,
        tokens_grad,
        qkv_weight_grad,
        qkv_bias_grad,
        out_grad.reshape(w_out.shape),
        up_weight_grad,
        up_bias_grad,
        down_grad.reshape(w_down.shape),
        res_bias_grad,
        gain_grad,
        shift_grad,
    )


def solution(mesh):
    sizes = (mesh.shape["dp"], mesh.shape["row"], mesh.shape["col"])
    per_device = paired_device if sizes == (4, 2, 4) else general_device
    return jax.shard_map(
        per_device,
        mesh=mesh,
        in_specs=(
            P(("dp", "row"), "col"),
            P("dp", None),
            P("dp", None),
            P("row", "col"),
            P("col"),
            P("col", "row"),
            P("row", "col"),
            P("col"),
            P("col", "row"),
            P("col"),
            P(),
            P(),
            P(("dp", "row"), "col"),
        ),
        out_specs=(
            P(("dp", "row"), "col"),
            P(("dp", "row"), "col"),
            P("row", "col"),
            P("col"),
            P("col", "row"),
            P("row", "col"),
            P("col"),
            P("col", "row"),
            P("col"),
            P(),
            P(),
        ),
        check_vma=False,
    )
```

```python
import functools
import math

import jax
import jax.numpy as jnp
from jax import lax
from jax.experimental import pallas as pl
from jax.experimental.pallas import tpu as pltpu
from jax.sharding import PartitionSpec as P

HD = 64
ROT = 32
SEG = 256


norm_epsilon = 1e-05
masked_fill = -1e30
rotary_base = 10000.0


def precise_dot(left, right):
    return jnp.dot(left, right, precision=lax.Precision.HIGHEST, preferred_element_type=jnp.float32)


def ancestry(parent_row):
    seg_count = parent_row.shape[0]
    labels = jnp.arange(seg_count, dtype=jnp.int32)
    identity = jnp.eye(seg_count, dtype=jnp.float32)
    parent_hot = (parent_row[:, None] == labels[None, :]).astype(jnp.float32)

    def extend(rounds, reachable):
        return jnp.minimum(identity + precise_dot(parent_hot, reachable), 1.0)

    return lax.fori_loop(0, seg_count, extend, identity)


def rotate(values, cosines, sines):
    half_rot = ROT // 2
    former = values[..., :half_rot]
    latter = values[..., half_rot:ROT]
    return jnp.concatenate(
        [former * cosines - latter * sines, latter * cosines + former * sines, values[..., ROT:]],
        axis=-1,
    )


def angles_of(positions):
    frequency = jnp.exp(
        -math.log(rotary_base) * 2.0 * jnp.arange(ROT // 2, dtype=jnp.float32) / ROT
    )
    phase_angle = positions[:, None] * frequency[None, :]
    return (jnp.cos(phase_angle)[:, None, :], jnp.sin(phase_angle)[:, None, :])


def reorder_rows(gradient, row_count, dp_count):
    leading = gradient.shape[0]
    blocked = gradient.reshape(
        row_count, dp_count, leading // (row_count * dp_count), gradient.shape[1]
    )
    return jnp.transpose(blocked, (1, 0, 2, 3)).reshape(leading, gradient.shape[1])


def reorder_cols(gradient, row_count, dp_count):
    trailing = gradient.shape[1]
    blocked = gradient.reshape(
        gradient.shape[0], row_count, dp_count, trailing // (row_count * dp_count)
    )
    return jnp.transpose(blocked, (0, 2, 1, 3)).reshape(gradient.shape[0], trailing)


def general_device(
    tokens,
    parent,
    depth,
    w_qkv,
    b_qkv,
    w_out,
    w_up,
    b_up,
    w_down,
    b_res,
    ln_gain,
    ln_bias,
    cotangent,
):
    tok_rows = tokens.shape[0]
    col_width = tokens.shape[1]
    row_count = lax.axis_size("row")
    dp_count = lax.axis_size("dp")
    row_start = lax.axis_index("row") * tok_rows
    local_heads = w_out.shape[0] // HD
    seg_count = parent.shape[1]
    labels = jnp.arange(seg_count, dtype=jnp.int32)
    reachable = ancestry(parent[0])
    query_index = row_start + jnp.arange(tok_rows, dtype=jnp.int32)
    query_seg = query_index // SEG
    query_hot = (query_seg[:, None] == labels[None, :]).astype(jnp.float32)
    query_reach = precise_dot(query_hot, reachable)
    levels = precise_dot(query_hot, depth[0].astype(jnp.float32)[:, None])[:, 0]
    positions = levels * SEG + (query_index % SEG).astype(jnp.float32)
    cosines, sines = angles_of(positions)
    score_scale = HD ** (-0.5)

    def permit(key_len):
        key_index = jnp.arange(key_len, dtype=jnp.int32)
        key_seg = key_index // SEG
        key_hot = (key_seg[:, None] == labels[None, :]).astype(jnp.float32)
        linked = precise_dot(query_reach, key_hot.T) > 0.5
        return linked & (
            (query_seg[:, None] != key_seg[None, :]) | (query_index[:, None] >= key_index[None, :])
        )

    whole = lax.all_gather(tokens, "col", axis=1, tiled=True).astype(jnp.float32)
    centred = whole - jnp.mean(whole, axis=1, keepdims=True)
    inv_scale = lax.rsqrt(jnp.mean(centred * centred, axis=1, keepdims=True) + norm_epsilon)
    normal = centred * inv_scale
    normed = (normal * ln_gain + ln_bias).astype(jnp.bfloat16)
    qkv_full, up_full, out_full, down_full = (
        lax.all_gather(w_qkv.astype(jnp.bfloat16), "row", axis=0, tiled=True),
        lax.all_gather(w_up.astype(jnp.bfloat16), "row", axis=0, tiled=True),
        lax.all_gather(w_out.astype(jnp.bfloat16), "row", axis=1, tiled=True),
        lax.all_gather(w_down.astype(jnp.bfloat16), "row", axis=1, tiled=True),
    )
    mixed = (jnp.dot(normed, qkv_full, preferred_element_type=jnp.float32) + b_qkv).reshape(
        tok_rows, local_heads, 3, HD
    )

    def rotate_pair(query_pre, key_pre):
        return (rotate(query_pre, cosines, sines), rotate(key_pre, cosines, sines))

    rotated, rotate_back = jax.vjp(rotate_pair, mixed[:, :, 0], mixed[:, :, 1])
    queries = rotated[0].astype(jnp.bfloat16)
    key_rows = rotated[1].astype(jnp.bfloat16)
    value_rows = mixed[:, :, 2].astype(jnp.bfloat16)
    key_flat = key_rows.reshape(tok_rows, local_heads * HD)
    value_flat = value_rows.reshape(tok_rows, local_heads * HD)

    def scores_for(key_part):
        raw_scores = (
            jnp.einsum("qhe,khe->hqk", queries, key_part, preferred_element_type=jnp.float32)
            * score_scale
        )
        allowed = permit(key_part.shape[0])
        return (jnp.where(allowed[None], raw_scores, masked_fill), allowed)

    pieces = (
        lax.all_gather(key_flat, "row", axis=0, tiled=True),
        lax.all_gather(value_flat, "row", axis=0, tiled=True),
    )
    running_top = jnp.full((local_heads, tok_rows), masked_fill, jnp.float32)
    key_len = pieces[0].shape[0]
    key_part = pieces[0].reshape(key_len, local_heads, HD)
    value_part = pieces[1].reshape(key_len, local_heads, HD)
    scores, allowed = scores_for(key_part)
    new_top = jnp.maximum(running_top, jnp.max(scores, axis=2))
    exponent = jnp.where(allowed[None], jnp.exp(scores - new_top[:, :, None]), 0.0)
    running_sum = jnp.sum(exponent, axis=2)
    weighted = jnp.einsum(
        "hqk,khe->hqe",
        exponent.astype(jnp.bfloat16),
        value_part,
        preferred_element_type=jnp.float32,
    )
    running_top, running_sum, weighted = (new_top, running_sum, weighted)
    log_total = running_top + jnp.log(running_sum)
    attn_exact = weighted / running_sum[:, :, None]
    attended = (
        jnp.transpose(attn_exact, (1, 0, 2))
        .reshape(tok_rows, local_heads * HD)
        .astype(jnp.bfloat16)
    )
    hidden_up = jnp.dot(normed, up_full, preferred_element_type=jnp.float32) + b_up
    activated, gelu_back = jax.vjp(functools.partial(jax.nn.gelu, approximate=True), hidden_up)
    activated = activated.astype(jnp.bfloat16)
    branch_terms = jnp.dot(attended, out_full, preferred_element_type=jnp.float32) + jnp.dot(
        activated, down_full, preferred_element_type=jnp.float32
    )
    branch = lax.psum_scatter(
        branch_terms.astype(jnp.bfloat16), "col", scatter_dimension=1, tiled=True
    ).astype(jnp.float32)
    output = (tokens.astype(jnp.float32) + branch + b_res).astype(jnp.bfloat16)
    grad_full = lax.all_gather(cotangent, "col", axis=1, tiled=True)
    res_bias_grad = jnp.sum(cotangent.astype(jnp.float32), axis=0)
    down_grad = jnp.einsum("tf,td->fd", activated, grad_full, preferred_element_type=jnp.float32)
    out_grad = jnp.einsum("te,td->ed", attended, grad_full, preferred_element_type=jnp.float32)
    act_grad = jnp.einsum("td,fd->tf", grad_full, down_full, preferred_element_type=jnp.float32)
    up_grad = gelu_back(act_grad)[0].astype(jnp.bfloat16)
    attn_grad = jnp.einsum(
        "td,ed->te", grad_full, out_full, preferred_element_type=jnp.float32
    ).astype(jnp.bfloat16)
    up_bias_grad = jnp.sum(up_grad.astype(jnp.float32), axis=0)
    up_weight_grad = jnp.einsum("td,tf->df", normed, up_grad, preferred_element_type=jnp.float32)
    out_heads = attn_grad.reshape(tok_rows, local_heads, HD)
    delta_sum = jnp.einsum("qhe,hqe->hq", out_heads.astype(jnp.float32), attn_exact)
    pieces = (
        lax.all_gather(key_flat, "row", axis=0, tiled=True),
        lax.all_gather(value_flat, "row", axis=0, tiled=True),
    )
    key_len = pieces[0].shape[0]
    key_part = pieces[0].reshape(key_len, local_heads, HD)
    value_part = pieces[1].reshape(key_len, local_heads, HD)
    scores, allowed = scores_for(key_part)
    softmaxed = jnp.where(allowed[None], jnp.exp(scores - log_total[:, :, None]), 0.0)
    prob_grad = jnp.einsum(
        "qhe,khe->hqk", out_heads, value_part, preferred_element_type=jnp.float32
    )
    score_grad = (softmaxed * (prob_grad - delta_sum[:, :, None])).astype(jnp.bfloat16)
    query_grad = (
        jnp.einsum("hqk,khe->qhe", score_grad, key_part, preferred_element_type=jnp.float32)
        * score_scale
    )
    key_grad = (
        jnp.einsum("hqk,qhe->khe", score_grad, queries, preferred_element_type=jnp.float32)
        * score_scale
    )
    value_grad = jnp.einsum(
        "hqk,qhe->khe",
        softmaxed.astype(jnp.bfloat16),
        out_heads,
        preferred_element_type=jnp.float32,
    )
    stacked = jnp.stack([key_grad, value_grad], axis=1).reshape(key_len, 2 * local_heads * HD)
    pair_grad = stacked
    query_grad, pair_grad = (query_grad, pair_grad)
    own_pairs = (
        lax.psum_scatter(pair_grad.astype(jnp.bfloat16), "row", scatter_dimension=0, tiled=True)
        .astype(jnp.float32)
        .reshape(tok_rows, 2, local_heads, HD)
    )
    query_pre, key_pre = rotate_back((query_grad, own_pairs[:, 0]))
    mixed_grad = (
        jnp.stack([query_pre, key_pre, own_pairs[:, 1]], axis=2)
        .reshape(tok_rows, 3 * local_heads * HD)
        .astype(jnp.bfloat16)
    )
    qkv_bias_grad = jnp.sum(mixed_grad.astype(jnp.float32), axis=0)
    qkv_weight_grad = jnp.einsum(
        "td,tc->dc", normed, mixed_grad, preferred_element_type=jnp.float32
    )
    norm_part = jnp.einsum(
        "tc,dc->td", mixed_grad, qkv_full, preferred_element_type=jnp.float32
    ) + jnp.einsum("tf,df->td", up_grad, up_full, preferred_element_type=jnp.float32)
    norm_grad = lax.psum(norm_part.astype(jnp.bfloat16), "col").astype(jnp.float32)
    gain_grad = jnp.sum(norm_grad * normal, axis=0)
    shift_grad = jnp.sum(norm_grad, axis=0)
    scaled = norm_grad * ln_gain
    mean_scaled = jnp.mean(scaled, axis=1, keepdims=True)
    mean_mixed = jnp.mean(scaled * normal, axis=1, keepdims=True)
    col_start = lax.axis_index("col") * col_width
    scaled_share = lax.dynamic_slice_in_dim(scaled, col_start, col_width, 1)
    normal_share = lax.dynamic_slice_in_dim(normal, col_start, col_width, 1)
    tokens_grad = inv_scale * (
        scaled_share - mean_scaled - normal_share * mean_mixed
    ) + cotangent.astype(jnp.float32)
    qkv_bias_grad, up_bias_grad, res_bias_grad, gain_grad, shift_grad = (
        lax.psum(qkv_bias_grad.astype(jnp.bfloat16), ("dp", "row")).astype(jnp.float32),
        lax.psum(up_bias_grad.astype(jnp.bfloat16), ("dp", "row")).astype(jnp.float32),
        lax.psum(res_bias_grad.astype(jnp.bfloat16), ("dp", "row")).astype(jnp.float32),
        lax.psum(gain_grad.astype(jnp.bfloat16), ("dp", "row")).astype(jnp.float32),
        lax.psum(shift_grad.astype(jnp.bfloat16), ("dp", "row")).astype(jnp.float32),
    )
    pieces_now = (
        lax.psum_scatter(
            reorder_rows(qkv_weight_grad, row_count, dp_count).astype(jnp.bfloat16),
            ("dp", "row"),
            scatter_dimension=0,
            tiled=True,
        ).astype(jnp.float32),
        lax.psum_scatter(
            reorder_rows(up_weight_grad, row_count, dp_count).astype(jnp.bfloat16),
            ("dp", "row"),
            scatter_dimension=0,
            tiled=True,
        ).astype(jnp.float32),
        lax.psum_scatter(
            reorder_cols(out_grad, row_count, dp_count).astype(jnp.bfloat16),
            ("dp", "row"),
            scatter_dimension=1,
            tiled=True,
        ).astype(jnp.float32),
        lax.psum_scatter(
            reorder_cols(down_grad, row_count, dp_count).astype(jnp.bfloat16),
            ("dp", "row"),
            scatter_dimension=1,
            tiled=True,
        ).astype(jnp.float32),
    )
    qkv_weight_grad, up_weight_grad, out_grad, down_grad = (
        lax.all_gather(pieces_now[0].astype(jnp.bfloat16), "dp", axis=0, tiled=True).astype(
            jnp.float32
        ),
        lax.all_gather(pieces_now[1].astype(jnp.bfloat16), "dp", axis=0, tiled=True).astype(
            jnp.float32
        ),
        lax.all_gather(pieces_now[2].astype(jnp.bfloat16), "dp", axis=1, tiled=True).astype(
            jnp.float32
        ),
        lax.all_gather(pieces_now[3].astype(jnp.bfloat16), "dp", axis=1, tiled=True).astype(
            jnp.float32
        ),
    )
    return (
        output,
        tokens_grad,
        qkv_weight_grad,
        qkv_bias_grad,
        out_grad,
        up_weight_grad,
        up_bias_grad,
        down_grad,
        res_bias_grad,
        gain_grad,
        shift_grad,
    )


SWAP_ROW = [(0, 1), (1, 0)]
SWAP_X = [(0, 2), (2, 0), (1, 3), (3, 1)]
SWAP_CORE = [(0, 1), (1, 0), (2, 3), (3, 2)]


def bf16(values):
    return values.astype(jnp.bfloat16)


def f32(values):
    return values.astype(jnp.float32)


def matmul(left, right, dims=((1,), (0,))):
    return lax.dot_general(left, right, (dims, ((), ())), preferred_element_type=jnp.float32)


def swap_row(values):
    return lax.ppermute(values, "row", SWAP_ROW)


def swap_x(values):
    return lax.ppermute(values, "dp", SWAP_X)


def swap_core(values):
    return lax.ppermute(values, "dp", SWAP_CORE)


def pick(index, first, second):
    return jnp.where(index == 0, first, second)


def pair(index, mine, theirs, axis):
    return pick(
        index,
        jnp.concatenate([mine, theirs], axis=axis),
        jnp.concatenate([theirs, mine], axis=axis),
    )


def after(value, *earlier):
    return lax.optimization_barrier((value,) + earlier)[0]


def rotary_tables(positions):
    lane = jnp.arange(2 * HD, dtype=jnp.int32) % HD
    half_rot = ROT // 2
    frequency = jnp.exp(
        -math.log(rotary_base) * 2.0 * (lane % half_rot).astype(jnp.float32) / ROT
    )
    angle = positions[:, None] * frequency[None, :]
    turned = (lane < ROT)[None, :]
    sines = jnp.sin(angle)
    return (
        jnp.where(turned, jnp.cos(angle), 1.0),
        jnp.where((lane < half_rot)[None, :], -sines, 0.0),
        jnp.where(turned & (lane >= half_rot)[None, :], sines, 0.0),
    )


def turn(values, cosines, sines_low, sines_high):
    width = values.shape[1]
    half_rot = ROT // 2
    return (
        values * cosines
        + pltpu.roll(values, width - half_rot, 1) * sines_low
        + pltpu.roll(values, half_rot, 1) * sines_high
    )


def mixed_kernel(
    normed_ref, weight_ref, bias_ref, cos_ref, low_ref, high_ref, query_ref, keyval_ref
):
    cosines, low, high = cos_ref[...], low_ref[...], high_ref[...]
    rows, half = query_ref.shape
    first = lax.broadcasted_iota(jnp.int32, (rows, 2 * HD), 1) < HD
    scale = HD ** (-0.5)
    mixed = matmul(normed_ref[...], weight_ref[...]) + bias_ref[...]
    for at in range(half // (2 * HD)):
        tiles = [mixed[:, (3 * at + part) * 2 * HD : (3 * at + part + 1) * 2 * HD] for part in range(3)]
        query = jnp.where(first, tiles[0], tiles[1])
        key = jnp.where(first, pltpu.roll(tiles[0], HD, 1), pltpu.roll(tiles[2], HD, 1))
        value = jnp.where(first, tiles[1], tiles[2])
        here = slice(at * 2 * HD, (at + 1) * 2 * HD)
        query_ref[:, here] = bf16(f32(bf16(turn(query, cosines, low, high))) * scale)
        keyval_ref[:, here] = bf16(turn(key, cosines, low, high))
        keyval_ref[:, half + at * 2 * HD : half + (at + 1) * 2 * HD] = bf16(value)


def join_kernel(row_ref, dq_ref, dkv_ref, sent_ref, cos_ref, low_ref, high_ref, out_ref):
    cosines, low, high = cos_ref[...], -low_ref[...], -high_ref[...]
    rows = dq_ref.shape[0]
    half = dq_ref.shape[1]
    first = lax.broadcasted_iota(jnp.int32, (rows, 2 * HD), 1) < HD
    owner = row_ref[0] == 0
    for at in range(half // (2 * HD)):
        here = slice(at * 2 * HD, (at + 1) * 2 * HD)
        there = slice(half + at * 2 * HD, half + (at + 1) * 2 * HD)
        query = turn(dq_ref[:, here], cosines, low, high)
        key = dkv_ref[:, here] + jnp.where(owner, f32(sent_ref[:, here]), 0.0)
        value = dkv_ref[:, there] + jnp.where(owner, f32(sent_ref[:, there]), 0.0)
        key = pltpu.roll(turn(key, cosines, low, high), HD, 1)
        tiles = (jnp.where(first, query, key), jnp.where(first, value, query), jnp.where(first, key, value))
        for part in range(3):
            out_ref[:, (3 * at + part) * 2 * HD : (3 * at + part + 1) * 2 * HD] = bf16(tiles[part])


def tree_kernel(
    parent_ref, row_ref, query_ref, keyval_ref, trunk_ref, grad_ref,
    out_ref, dq_ref, dkv_ref, dtrunk_ref,
    keys, values, dkeys, dvalues,
):
    tree = pl.program_id(0)
    row = row_ref[0]
    rows, half = query_ref.shape
    trunk_len = trunk_ref.shape[0]
    segs = rows // SEG
    trunk_segs = trunk_len // SEG
    seg_count = parent_ref.shape[1]
    first_row = row == 0
    keys[...] = jnp.where(first_row, keyval_ref[:, :half], trunk_ref[:, :half])
    values[...] = jnp.where(first_row, keyval_ref[:, half:], trunk_ref[:, half:])
    dkeys[...] = jnp.zeros_like(dkeys)
    dvalues[...] = jnp.zeros_like(dvalues)
    lane = lax.broadcasted_iota(jnp.int32, (1, half), 1)
    causal = lax.broadcasted_iota(jnp.int32, (SEG, SEG), 0) >= lax.broadcasted_iota(
        jnp.int32, (SEG, SEG), 1
    )
    across = ((1,), (1,))
    down = ((0,), (0,))
    for seg in range(segs):
        here = slice(seg * SEG, (seg + 1) * SEG)
        above = parent_ref[tree, row * segs + seg]
        linked = [above == at for at in range(trunk_segs)]
        for _ in range(seg_count - 2):
            above = jnp.where(above >= 0, parent_ref[tree, jnp.maximum(above, 0)], -1)
            linked = [was | (above == at) for at, was in enumerate(linked)]
        bias = [jnp.where(is_linked, 0.0, masked_fill) for is_linked in linked]
        query, grad = query_ref[here, :], grad_ref[here, :]
        own_key, own_value = keyval_ref[here, :half], keyval_ref[here, half:]
        attended = jnp.zeros((SEG, half), jnp.float32)
        dquery = jnp.zeros((SEG, half), jnp.float32)
        dkey = jnp.zeros((SEG, half), jnp.float32)
        dvalue = jnp.zeros((SEG, half), jnp.float32)
        for head in range(half // HD):
            mine = (lane >= head * HD) & (lane < (head + 1) * HD)
            head_query = jnp.where(mine, query, jnp.zeros_like(query))
            head_grad = jnp.where(mine, grad, jnp.zeros_like(grad))
            scores = [
                matmul(head_query, keys[at * SEG : (at + 1) * SEG, :], across) + bias[at]
                for at in range(trunk_segs)
            ] + [jnp.where(causal, matmul(head_query, own_key, across), masked_fill)]
            top = functools.reduce(jnp.maximum, [jnp.max(s, axis=1, keepdims=True) for s in scores])
            powers = [jnp.exp(s - top) for s in scores]
            total = functools.reduce(jnp.add, [jnp.sum(p, axis=1, keepdims=True) for p in powers])
            probs = [p / total for p in powers]
            low = [bf16(p) for p in probs]
            blocks = [values[at * SEG : (at + 1) * SEG, :] for at in range(trunk_segs)] + [own_value]
            prob_grads = [matmul(head_grad, v, across) for v in blocks]
            delta = functools.reduce(
                jnp.add, [jnp.sum(p * g, axis=1, keepdims=True) for p, g in zip(probs, prob_grads)]
            )
            score_grads = [bf16(p * (g - delta)) for p, g in zip(probs, prob_grads)]
            head_out = functools.reduce(jnp.add, [matmul(p, v) for p, v in zip(low, blocks)])
            attended = jnp.where(mine, head_out, attended)
            key_blocks = [keys[at * SEG : (at + 1) * SEG, :] for at in range(trunk_segs)] + [own_key]
            head_dq = functools.reduce(jnp.add, [matmul(s, u) for s, u in zip(score_grads, key_blocks)])
            dquery = jnp.where(mine, head_dq, dquery)
            dkey = dkey + matmul(score_grads[-1], head_query, down)
            dvalue = dvalue + matmul(low[-1], head_grad, down)
            for at in range(trunk_segs):
                spot = slice(at * SEG, (at + 1) * SEG)
                dkeys[spot, :] += matmul(score_grads[at], head_query, down)
                dvalues[spot, :] += matmul(low[at], head_grad, down)
        out_ref[here, :] = bf16(attended)
        dq_ref[here, :] = dquery * HD ** (-0.5)
        dkv_ref[here, :half] = dkey
        dkv_ref[here, half:] = dvalue
    dtrunk_ref[:, :half] = bf16(dkeys[...])
    dtrunk_ref[:, half:] = bf16(dvalues[...])

    @pl.when(first_row)
    def _():
        dkv_ref[:, :half] += dkeys[...]
        dkv_ref[:, half:] += dvalues[...]


def store_blocks(place_ref, sides, full_ref, own_refs, plain_refs):
    row, slab = place_ref[1], place_ref[2]
    for side, values in enumerate(sides):
        width = values[0].shape[1]
        for source, value in enumerate(values):
            within = source % 2
            here = row == source // 2

            def put(refs):
                if len(refs) == 1:
                    refs[0][side, :, within * width : (within + 1) * width] = value
                else:
                    refs[within][side] = value

            @pl.when(here)
            def _():
                full_ref[side, :, within * width : (within + 1) * width] = value
                put(own_refs)

            @pl.when(jnp.logical_not(here))
            def _():
                put(plain_refs)
                at = (2 + jnp.where(slab == 0, within, 1 - within)) * width
                full_ref[side, :, pl.ds(pl.multiple_of(at, width), width)] = value


def gather_kernel(place_ref, mine_ref, theirs_ref, full_ref, own_ref, plain_ref):
    sides = [[ref[at] for at in range(ref.shape[0])] for ref in (mine_ref, theirs_ref)]
    store_blocks(place_ref, sides, full_ref, [own_ref], [plain_ref])


def norm_kernel(place_ref, gain_ref, bias_ref, mine_ref, theirs_ref, full_ref, *outs):
    normal_ref, scale_ref = outs[4:]
    sides = []
    for side, ref in enumerate((mine_ref, theirs_ref)):
        values = [f32(ref[at]) for at in range(ref.shape[0])]
        features = len(values) * values[0].shape[1]
        mean = functools.reduce(jnp.add, [jnp.sum(v, axis=1, keepdims=True) for v in values]) / features
        centred = [v - mean for v in values]
        square = functools.reduce(jnp.add, [jnp.sum(v * v, axis=1, keepdims=True) for v in centred])
        inv_scale = lax.rsqrt(square / features + norm_epsilon)
        normals = [v * inv_scale for v in centred]
        if side == 0:
            scale_ref[...] = inv_scale
            for source, normal in enumerate(normals):

                @pl.when(place_ref[0] == source)
                def _():
                    normal_ref[...] = normal

        sides.append(
            [
                bf16(normal * gain_ref[source : source + 1, :] + bias_ref[source : source + 1, :])
                for source, normal in enumerate(normals)
            ]
        )
    store_blocks(place_ref, sides, full_ref, outs[:2], outs[2:4])


def pair_rows(rows, width):
    return pl.BlockSpec((2, rows, width), lambda at, *_: (0, at, 0))


def gathered(place, mine, theirs, norm=None):
    blocks, count, width = mine.shape
    rows = SEG if norm is None else SEG // 2
    full = blocks * width
    in_specs = [pl.BlockSpec((blocks, rows, width), lambda at, *_: (0, at, 0))] * 2
    parts = [full // 2] * 2 if norm is None else [width] * 4
    out_specs = [pair_rows(rows, size) for size in [full] + parts]
    out_shape = [
        jax.ShapeDtypeStruct((2, count, size), jnp.bfloat16) for size in [full] + parts
    ]
    operands = [mine, theirs]
    if norm is not None:
        gain = [values.reshape(blocks, width) for values in norm]
        operands = gain + operands
        in_specs = [pl.BlockSpec((blocks, width), lambda at, *_: (0, 0))] * 2 + in_specs
        out_specs = out_specs + [row_block(rows, width), row_block(rows, 1)]
        out_shape = out_shape + [
            jax.ShapeDtypeStruct((count, width), jnp.float32),
            jax.ShapeDtypeStruct((count, 1), jnp.float32),
        ]
    results = pl.pallas_call(
        gather_kernel if norm is None else norm_kernel,
        grid_spec=pltpu.PrefetchScalarGridSpec(
            num_scalar_prefetch=1, grid=(count // rows,), in_specs=in_specs, out_specs=out_specs
        ),
        out_shape=out_shape,
        cost_estimate=pl.CostEstimate(flops=1, bytes_accessed=1, transcendentals=0),
        name="join_blocks" if norm is None else "norm_blocks",
    )(place, *operands)
    last = len(parts) + 1
    return [values.reshape(2 * count, -1) for values in results[:last]] + list(results[last:])


def stack_kernel(place_ref, terms_ref, arrived_ref, out_ref):
    row, slab = place_ref[1], place_ref[2]
    width = out_ref.shape[2]
    for spot in range(4):
        here = slice(spot * width, (spot + 1) * width)
        value = bf16(f32(terms_ref[:, here]) + f32(arrived_ref[:, here]))
        if spot < 2:
            out_ref[2 * row + spot] = value
        else:
            out_ref[2 * (1 - row) + jnp.where(slab == 0, spot - 2, 3 - spot)] = value


def stacked(place, terms, arrived, blocks):
    count, full = arrived.shape
    rows = SEG
    width = full // blocks
    return pl.pallas_call(
        stack_kernel,
        grid_spec=pltpu.PrefetchScalarGridSpec(
            num_scalar_prefetch=1,
            grid=(count // rows,),
            in_specs=[row_block(rows, full), row_block(rows, full)],
            out_specs=pl.BlockSpec((blocks, rows, width), lambda at, *_: (0, at, 0)),
        ),
        out_shape=jax.ShapeDtypeStruct((blocks, count, width), jnp.bfloat16),
        cost_estimate=pl.CostEstimate(flops=1, bytes_accessed=1, transcendentals=0),
        name="stack_blocks",
    )(place, terms, arrived)


def cast_rows_kernel(place_ref, master_ref, own_ref, send_ref):
    value = bf16(master_ref[...])
    own_ref[...] = value
    half = pl.num_programs(0) // 2

    @pl.when(pl.program_id(0) // half == place_ref[2])
    def _():
        send_ref[...] = value


def cast_cols_kernel(place_ref, master_ref, own_ref, send_ref):
    value = bf16(master_ref[...])
    own_ref[...] = value
    half = value.shape[1] // 2
    send_ref[...] = jnp.where(place_ref[2] == 0, value[:, :half], value[:, half:])


def cast_weight(place, master, axis):
    height, width = master.shape
    rows = min(2 * SEG, master.shape[0] // 4)
    if axis == 0:
        width = width // 2
        steps = height // rows
        half = steps // 2
        specs = [
            pl.BlockSpec((rows, width), lambda at, place_ref: (at, place_ref[3])),
            pl.BlockSpec((rows, width), lambda at, place_ref: (at, 0)),
            pl.BlockSpec(
                (rows, width), lambda at, place_ref: (jnp.clip(at - half * place_ref[2], 0, half - 1), 0)
            ),
        ]
        send = (height // 2, width)
        whole = (2 * height, width)
    else:
        height = height // 2
        steps = height // rows
        specs = [
            pl.BlockSpec((rows, width), lambda at, place_ref: (at + steps * place_ref[3], 0)),
            pl.BlockSpec((rows, width), lambda at, place_ref: (at, 0)),
            pl.BlockSpec((rows, width // 2), lambda at, place_ref: (at, 0)),
        ]
        send = (height, width // 2)
        whole = (height, 2 * width)
    return pl.pallas_call(
        cast_rows_kernel if axis == 0 else cast_cols_kernel,
        grid_spec=pltpu.PrefetchScalarGridSpec(
            num_scalar_prefetch=1, grid=(steps,), in_specs=specs[:1], out_specs=specs[1:]
        ),
        out_shape=[
            jax.ShapeDtypeStruct(whole, jnp.bfloat16),
            jax.ShapeDtypeStruct(send, jnp.bfloat16),
        ],
        cost_estimate=pl.CostEstimate(flops=1, bytes_accessed=1, transcendentals=0),
        name="cast_weight",
    )(place, master)


def settle_store(axis, place_ref, mine, theirs, out_ref):
    if axis == 0:
        out_ref[place_ref[3]] = mine
        out_ref[1 - place_ref[3]] = theirs
    else:
        width = mine.shape[1]
        first = place_ref[3] == 0
        out_ref[:, :width] = jnp.where(first, mine, theirs)
        out_ref[:, width:] = jnp.where(first, theirs, mine)


def settle_kernel(axis, place_ref, mine_ref, theirs_ref, *refs):
    settle_store(axis, place_ref, f32(mine_ref[...]), f32(theirs_ref[...]), refs[-1])


def settle_both_kernel(axis, place_ref, *refs):
    for at in range(2):

        @pl.when(pl.program_id(0) == at)
        def _():
            settle_store(axis, place_ref, f32(refs[2 * at][...]), f32(refs[2 * at + 1][...]), refs[-1])


def settle_both(place, first, last, shape, axis):
    rows, width = first[0].shape
    if axis == 0:
        shape = (2, shape[0] // 2, width)
        out_spec = pl.BlockSpec((2, rows, width), lambda at, *_: (0, at, 0))
    else:
        out_spec = pl.BlockSpec((rows, 2 * width), lambda at, *_: (at, 0))
    return pl.pallas_call(
        functools.partial(settle_both_kernel, axis),
        grid_spec=pltpu.PrefetchScalarGridSpec(
            num_scalar_prefetch=1,
            grid=(2,),
            in_specs=[pl.BlockSpec((rows, width), lambda *_: (0, 0))] * 4,
            out_specs=out_spec,
        ),
        out_shape=jax.ShapeDtypeStruct(shape, jnp.float32),
        cost_estimate=pl.CostEstimate(flops=1, bytes_accessed=1, transcendentals=0),
        name="settle_both",
    )(place, *first, *last)


def settle(place, mine, theirs, shape, axis, offset, dest=None):
    rows, width = mine.shape
    at = offset // rows
    whole = pl.BlockSpec((rows, width), lambda *_: (0, 0))
    if axis == 0:
        shape = (2, shape[0] // 2, width)
        out_spec = pl.BlockSpec((2, rows, width), lambda *_: (0, at, 0))
    else:
        out_spec = pl.BlockSpec((rows, 2 * width), lambda *_: (at, 0))
    in_specs = [whole, whole]
    operands = [place, mine, theirs]
    aliases = {}
    if dest is not None:
        in_specs.append(pl.BlockSpec(memory_space=pl.ANY))
        operands.append(dest)
        aliases = {3: 0}
    return pl.pallas_call(
        functools.partial(settle_kernel, axis),
        grid_spec=pltpu.PrefetchScalarGridSpec(
            num_scalar_prefetch=1, grid=(1,), in_specs=in_specs, out_specs=out_spec
        ),
        out_shape=jax.ShapeDtypeStruct(shape, jnp.float32),
        input_output_aliases=aliases,
        cost_estimate=pl.CostEstimate(flops=1, bytes_accessed=1, transcendentals=0),
        name="settle",
    )(*operands)


def row_block(rows, width):
    return pl.BlockSpec((rows, width), lambda at, *_: (at, 0))


def mixed_heads(normed, weight, bias, tables):
    count, depth = normed.shape
    width = weight.shape[1]
    rows = SEG
    return pl.pallas_call(
        mixed_kernel,
        grid=(count // rows,),
        in_specs=[
            row_block(rows, depth),
            pl.BlockSpec((depth, width), lambda at: (0, 0)),
            pl.BlockSpec((1, width), lambda at: (0, 0)),
        ]
        + [row_block(rows, 2 * HD)] * 3,
        out_specs=[row_block(rows, width // 3), row_block(rows, 2 * width // 3)],
        out_shape=[
            jax.ShapeDtypeStruct((count, width // 3), jnp.bfloat16),
            jax.ShapeDtypeStruct((count, 2 * width // 3), jnp.bfloat16),
        ],
        cost_estimate=pl.CostEstimate(flops=1, bytes_accessed=1, transcendentals=0),
        name="mixed_heads",
    )(normed, weight, bias.reshape(1, width), *tables)


def join_heads(row, dq, dkv, sent, tables):
    count, half = dq.shape
    rows = 2 * SEG
    return pl.pallas_call(
        join_kernel,
        grid_spec=pltpu.PrefetchScalarGridSpec(
            num_scalar_prefetch=1,
            grid=(count // rows,),
            in_specs=[row_block(rows, half), row_block(rows, 2 * half), row_block(rows, 2 * half)]
            + [row_block(rows, 2 * HD)] * 3,
            out_specs=row_block(rows, 3 * half),
        ),
        out_shape=jax.ShapeDtypeStruct((count, 3 * half), jnp.bfloat16),
        cost_estimate=pl.CostEstimate(flops=1, bytes_accessed=1, transcendentals=0),
        name="join_heads",
    )(row, dq, dkv, sent, *tables)


def tree_attention(parents, row, query, keyval, trunk, grad):
    trees = parents.shape[0]
    count, half = query.shape
    rows = count // trees
    keys = trunk.shape[0] // trees
    pairs = count * (keys + SEG) * (half // HD)
    return pl.pallas_call(
        tree_kernel,
        grid_spec=pltpu.PrefetchScalarGridSpec(
            num_scalar_prefetch=2,
            grid=(trees,),
            in_specs=[
                row_block(rows, half),
                row_block(rows, 2 * half),
                row_block(keys, 2 * half),
                row_block(rows, half),
            ],
            out_specs=[
                row_block(rows, half),
                row_block(rows, half),
                row_block(rows, 2 * half),
                row_block(keys, 2 * half),
            ],
            scratch_shapes=[pltpu.VMEM((keys, half), jnp.bfloat16)] * 2
            + [pltpu.VMEM((keys, half), jnp.float32)] * 2,
        ),
        out_shape=[
            jax.ShapeDtypeStruct((count, half), jnp.bfloat16),
            jax.ShapeDtypeStruct((count, half), jnp.float32),
            jax.ShapeDtypeStruct((count, 2 * half), jnp.float32),
            jax.ShapeDtypeStruct((trees * keys, 2 * half), jnp.bfloat16),
        ],
        cost_estimate=pl.CostEstimate(flops=1, bytes_accessed=1, transcendentals=0),
        name="tree_attention",
    )(parents, row, query, keyval, trunk, grad)


def paired_device(
    tokens,
    parent,
    depth,
    w_qkv,
    b_qkv,
    w_out,
    w_up,
    b_up,
    w_down,
    b_res,
    ln_gain,
    ln_bias,
    cotangent,
):
    count, width = tokens.shape
    row = lax.axis_index("row")
    col = lax.axis_index("col")
    core = lax.axis_index("dp") % 2
    slab = lax.axis_index("dp") // 2
    cols = lax.axis_size("col")
    half = 2 * width
    heads_width = w_out.shape[0] // 2
    hidden = w_up.shape[1] // 2
    place = jnp.stack([col, row, slab, core]).astype(jnp.int32)
    row_table = jnp.reshape(row, (1,)).astype(jnp.int32)
    down_dims = ((0,), (0,))
    across = ((1,), (1,))

    def part(values, at, size, axis):
        return lax.dynamic_slice_in_dim(values, at * size, size, axis)

    def exchange(stack):
        return lax.all_to_all(stack, "col", 0, 0, tiled=True)

    done = ()

    def step(run, *inputs):
        nonlocal done
        inputs, _ = lax.optimization_barrier((inputs, done))
        result = run(*inputs)
        done = result
        return result

    def wait(value):
        return step(lambda arrived: arrived, value)

    tokens_near = lax.all_gather(tokens, "col", axis=0)
    grad_stack = jnp.broadcast_to(cotangent[None], (cols,) + cotangent.shape)

    def ready(master, axis):
        whole, send = step(lambda weight: cast_weight(place, weight, axis), master)
        return whole, swap_row(send)

    def fill(whole, part_in, axis, last):
        at = whole.shape[axis] // 2 + (part_in.shape[axis] if last else 0)
        return step(lambda a, b: lax.dynamic_update_slice_in_dim(a, b, at, axis), whole, part_in)

    tables = jnp.concatenate([parent, depth], axis=0)
    tables = jnp.stack([tables, swap_core(tables)])
    parents = tables[:, 0]
    segs = count // SEG
    token = jnp.arange(count, dtype=jnp.int32)
    levels = jnp.zeros((2, count), jnp.float32)
    for seg in range(segs):
        level = lax.dynamic_slice_in_dim(tables[:, 1], row * segs + seg, 1, 1).astype(jnp.float32)
        levels = jnp.where((token // SEG == seg)[None, :], level, levels)
    positions = (levels * SEG + (token % SEG).astype(jnp.float32)[None, :]).reshape(2 * count)
    rotary = rotary_tables(positions)

    qkv_whole, qkv_row = ready(w_qkv, 0)
    up_whole, up_row = ready(w_up, 0)
    qkv_row = wait(qkv_row)
    qkv_x = swap_x(qkv_row)
    out_whole, out_row = ready(w_out, 1)
    down_whole, down_row = ready(w_down, 1)
    rotary = step(lambda *tables: tables, *rotary)
    qkv_whole = fill(qkv_whole, qkv_row, 0, False)
    up_row = wait(up_row)
    up_x = swap_x(up_row)
    qkv_x = wait(qkv_x)
    tokens_near = wait(tokens_near)
    tokens_far = swap_core(tokens_near)
    grad_near = exchange(after(grad_stack, tokens_near))
    up_whole = fill(up_whole, up_row, 0, False)
    normed, own_a, own_b, plain_a, plain_b, normal, inv_scale = step(
        lambda mine, theirs: gathered(place, mine, theirs, (ln_gain, ln_bias)), tokens_near, tokens_far
    )
    qkv_full = fill(qkv_whole, qkv_x, 0, True)
    query, keyval = step(
        lambda left, right: mixed_heads(left, right, part(b_qkv, core, 3 * heads_width, 0), rotary),
        normed, qkv_full,
    )
    trunk = lax.ppermute(keyval, "row", [(0, 1)])
    root = math.sqrt(2.0 / math.pi)

    def feed(left, right):
        hidden_up = matmul(left, right) + part(b_up, core, hidden, 0)
        squared = hidden_up * hidden_up
        bend = jnp.tanh(root * (hidden_up + 0.044715 * squared * hidden_up))
        return bf16(0.5 * hidden_up * (1.0 + bend)), bf16(
            0.5 * (1.0 + bend)
            + 0.5 * hidden_up * (1.0 - bend * bend) * root * (1.0 + 3.0 * 0.044715 * squared)
        )

    out_row = wait(out_row)
    out_x = swap_x(out_row)
    up_full = fill(up_whole, up_x, 0, True)
    down_row = wait(down_row)
    down_x = swap_x(down_row)
    activated, slope = step(feed, normed, up_full)
    out_whole = fill(out_whole, out_row, 1, False)
    down_whole = fill(down_whole, down_row, 1, False)
    out_full = fill(out_whole, out_x, 1, True)
    trunk = wait(trunk)
    grad_near = wait(grad_near)
    grad_far = swap_core(grad_near)
    grad, grad_own, grad_plain = step(lambda mine, theirs: gathered(place, mine, theirs), grad_near, grad_far)

    def cut(values, at):
        size = values.shape[1] // 2
        return values[:, at * size : (at + 1) * size]

    def leaving(left, right):
        return step(lambda a, b: bf16(matmul(a, b, down_dims)), left, right)

    def staying(left, right, sent):
        return step(lambda a, b, c: bf16(matmul(a, b, down_dims) + f32(c)), left, right, sent)

    def crossed(both, arrived):
        mine = step(lambda a, b: bf16(f32(a) + f32(b)), both, arrived)
        return mine, swap_core(mine)

    def settled(pieces, shape, axis, offset, dest):
        operands = pieces if dest is None else pieces + (dest,)
        return step(
            lambda mine, theirs, *rest: settle(place, mine, theirs, shape, axis, offset, *rest), *operands
        )

    down_sent_a = swap_row(leaving(cut(activated, 0), grad_plain))
    down_sent_b = swap_row(leaving(cut(activated, 1), grad_plain))
    out_heads = step(lambda a, b: bf16(matmul(a, b, across)), grad, out_full)
    attended, query_grad, own_grad, trunk_grad = step(
        lambda *operands: tree_attention(parents, row_table, *operands), query, keyval, trunk, out_heads
    )
    trunk_sent = lax.ppermute(trunk_grad, "row", [(1, 0)])
    down_both_a = staying(cut(activated, 0), grad_own, down_sent_a)
    down_cross_a = swap_x(down_both_a)
    down_full = fill(down_whole, down_x, 1, True)
    up_grad = step(lambda a, b, c: bf16(matmul(a, b, across) * f32(c)), grad, down_full, slope)
    up_sent_a = swap_row(leaving(plain_a, up_grad))
    down_both_b = staying(cut(activated, 1), grad_own, down_sent_b)
    down_cross_b = swap_x(down_both_b)
    up_sent_b = swap_row(leaving(plain_b, up_grad))
    down_a = crossed(down_both_a, down_cross_a)
    branch_terms = step(
        lambda a, b, c, d: bf16(matmul(a, b) + matmul(c, d)), attended, out_full, activated, down_full
    )
    branch_near = swap_core(branch_terms[count:])
    mixed_grad = step(
        lambda *operands: join_heads(row_table, *operands, rotary), query_grad, own_grad, trunk_sent
    )
    qkv_sent_a = swap_row(leaving(plain_a, mixed_grad))
    down_b = crossed(down_both_b, down_cross_b)
    qkv_sent_b = swap_row(leaving(plain_b, mixed_grad))
    norm_terms = step(
        lambda a, b, c, d: bf16(matmul(a, b, across) + matmul(c, d, across)),
        mixed_grad, qkv_full, up_grad, up_full,
    )
    up_both_a = staying(own_a, up_grad, up_sent_a)
    up_cross_a = swap_x(up_both_a)
    norm_near = swap_core(step(lambda terms: terms[count:], norm_terms))
    down_grad = step(lambda first, last: settle_both(place, first, last, w_down.shape, 0), down_a, down_b)
    norm_parts = exchange(step(lambda a, b: stacked(place, a, b, cols), norm_terms, norm_near))
    up_a = crossed(up_both_a, up_cross_a)
    up_both_b = staying(own_b, up_grad, up_sent_b)
    up_cross_b = swap_x(up_both_b)
    branch = lax.psum_scatter(
        step(lambda a, b: stacked(place, a, b, cols), branch_terms, branch_near), "col", tiled=False
    )
    qkv_both_a = staying(own_a, mixed_grad, qkv_sent_a)
    qkv_cross_a = swap_x(qkv_both_a)
    out_sent = swap_row(leaving(attended, grad_plain))
    up_b = crossed(up_both_b, up_cross_b)
    qkv_both_b = staying(own_b, mixed_grad, qkv_sent_b)
    qkv_cross_b = swap_x(qkv_both_b)
    gain_here = part(ln_gain, col, width, 0)

    def norm_sums(parts):
        total = jnp.sum(f32(parts), axis=0)
        scaled = total * gain_here
        return (
            total,
            jnp.stack([jnp.sum(scaled, axis=1), jnp.sum(scaled * normal, axis=1)]),
            jnp.sum(total * normal, axis=0),
            jnp.sum(total, axis=0),
        )

    norm_grad, sums, gain_sum, shift_sum = step(norm_sums, norm_parts)
    up_weight_grad = step(lambda first, last: settle_both(place, first, last, w_up.shape, 1), up_a, up_b)

    def line_step(values, bit):
        return lax.ppermute(values, "col", [(at, at ^ bit) for at in range(cols)])

    small = jnp.concatenate(
        [
            jnp.sum(f32(up_grad), axis=0),
            jnp.sum(f32(mixed_grad), axis=0),
            jnp.sum(f32(cotangent), axis=0),
            gain_sum,
            shift_sum,
        ]
    ).reshape(-1, 128)
    shared_at = (hidden + 3 * heads_width) // 128
    res_at = width // 128
    sums_next = line_step(sums, 1)
    small_other = swap_core(small)
    qkv_a = crossed(qkv_both_a, qkv_cross_a)
    sums, shared = step(
        lambda sums, arrived, small, other: (sums + arrived, (small + other)[shared_at:]),
        sums, sums_next, small, small_other,
    )
    sums_next = line_step(sums, 2)
    ends = shared[res_at:][None]
    ends_next = line_step(ends, 1)
    out_both = staying(attended, grad_own, out_sent)
    out_cross = swap_x(out_both)
    ends = step(lambda ends, arrived: pair(col % 2, ends, arrived, 0), ends, ends_next)
    ends_next = line_step(ends, 2)
    qkv_weight_grad = settled(qkv_a, w_qkv.shape, 1, 0, None)
    sums = (sums + sums_next) / (cols * width)
    tokens_grad = step(
        lambda sums, total: inv_scale
        * (total * gain_here - sums[0][:, None] - normal * sums[1][:, None])
        + f32(cotangent),
        sums, norm_grad,
    )

    def gather_small(small, other, shared, ends, arrived):
        return jnp.concatenate(
            [
                pair(core, small[: hidden // 128], other[: hidden // 128], 0),
                pair(core, small[hidden // 128 : shared_at], other[hidden // 128 : shared_at], 0),
                shared[:res_at],
                pair(col // 2, ends, arrived, 0).reshape(-1, 128),
            ]
        )

    output = step(lambda parts, block: bf16(f32(block) + f32(parts) + b_res), branch, tokens)
    small = step(gather_small, small, small_other, shared, ends, ends_next)
    small_next = swap_row(small)
    qkv_b = crossed(qkv_both_b, qkv_cross_b)
    small = step(jnp.add, small, small_next)
    small_next = swap_x(small)
    out_mine = crossed(out_both, out_cross)
    qkv_weight_grad = settled(qkv_b, w_qkv.shape, 1, qkv_both_a.shape[0], qkv_weight_grad)
    out_grad = settled(out_mine, w_out.shape, 0, 0, None)
    small = step(jnp.add, small, small_next)

    bounds = [0, 2 * hidden // 128, (2 * hidden + 6 * heads_width) // 128]
    bounds.append(bounds[-1] + res_at)
    up_bias_grad = small[: bounds[1]].reshape(-1)
    qkv_bias_grad = small[bounds[1] : bounds[2]].reshape(-1)
    res_bias_grad = small[bounds[2] : bounds[3]].reshape(-1)
    ends = small[bounds[3] :].reshape(cols, 2, width)
    gain_grad = ends[:, 0].reshape(-1)
    shift_grad = ends[:, 1].reshape(-1)
    return (
        output,
        tokens_grad,
        qkv_weight_grad,
        qkv_bias_grad,
        out_grad.reshape(w_out.shape),
        up_weight_grad,
        up_bias_grad,
        down_grad.reshape(w_down.shape),
        res_bias_grad,
        gain_grad,
        shift_grad,
    )


def solution(mesh):
    sizes = (mesh.shape["dp"], mesh.shape["row"], mesh.shape["col"])
    per_device = paired_device if sizes == (4, 2, 4) else general_device
    return jax.shard_map(
        per_device,
        mesh=mesh,
        in_specs=(
            P(("dp", "row"), "col"),
            P("dp", None),
            P("dp", None),
            P("row", "col"),
            P("col"),
            P("col", "row"),
            P("row", "col"),
            P("col"),
            P("col", "row"),
            P("col"),
            P(),
            P(),
            P(("dp", "row"), "col"),
        ),
        out_specs=(
            P(("dp", "row"), "col"),
            P(("dp", "row"), "col"),
            P("row", "col"),
            P("col"),
            P("col", "row"),
            P("row", "col"),
            P("col"),
            P("col", "row"),
            P("col"),
            P(),
            P(),
        ),
        check_vma=False,
    )
```

```python
import functools
import math

import jax
import jax.numpy as jnp
from jax import lax
from jax.experimental import pallas as pl
from jax.experimental.pallas import tpu as pltpu
from jax.sharding import PartitionSpec as P

HD = 64
ROT = 32
SEG = 256


norm_epsilon = 1e-05
masked_fill = -1e30
rotary_base = 10000.0


def precise_dot(left, right):
    return jnp.dot(left, right, precision=lax.Precision.HIGHEST, preferred_element_type=jnp.float32)


def ancestry(parent_row):
    seg_count = parent_row.shape[0]
    labels = jnp.arange(seg_count, dtype=jnp.int32)
    identity = jnp.eye(seg_count, dtype=jnp.float32)
    parent_hot = (parent_row[:, None] == labels[None, :]).astype(jnp.float32)

    def extend(rounds, reachable):
        return jnp.minimum(identity + precise_dot(parent_hot, reachable), 1.0)

    return lax.fori_loop(0, seg_count, extend, identity)


def rotate(values, cosines, sines):
    half_rot = ROT // 2
    former = values[..., :half_rot]
    latter = values[..., half_rot:ROT]
    return jnp.concatenate(
        [former * cosines - latter * sines, latter * cosines + former * sines, values[..., ROT:]],
        axis=-1,
    )


def angles_of(positions):
    frequency = jnp.exp(
        -math.log(rotary_base) * 2.0 * jnp.arange(ROT // 2, dtype=jnp.float32) / ROT
    )
    phase_angle = positions[:, None] * frequency[None, :]
    return (jnp.cos(phase_angle)[:, None, :], jnp.sin(phase_angle)[:, None, :])


def reorder_rows(gradient, row_count, dp_count):
    leading = gradient.shape[0]
    blocked = gradient.reshape(
        row_count, dp_count, leading // (row_count * dp_count), gradient.shape[1]
    )
    return jnp.transpose(blocked, (1, 0, 2, 3)).reshape(leading, gradient.shape[1])


def reorder_cols(gradient, row_count, dp_count):
    trailing = gradient.shape[1]
    blocked = gradient.reshape(
        gradient.shape[0], row_count, dp_count, trailing // (row_count * dp_count)
    )
    return jnp.transpose(blocked, (0, 2, 1, 3)).reshape(gradient.shape[0], trailing)


def general_device(
    tokens,
    parent,
    depth,
    w_qkv,
    b_qkv,
    w_out,
    w_up,
    b_up,
    w_down,
    b_res,
    ln_gain,
    ln_bias,
    cotangent,
):
    tok_rows = tokens.shape[0]
    col_width = tokens.shape[1]
    row_count = lax.axis_size("row")
    dp_count = lax.axis_size("dp")
    row_start = lax.axis_index("row") * tok_rows
    local_heads = w_out.shape[0] // HD
    seg_count = parent.shape[1]
    labels = jnp.arange(seg_count, dtype=jnp.int32)
    reachable = ancestry(parent[0])
    query_index = row_start + jnp.arange(tok_rows, dtype=jnp.int32)
    query_seg = query_index // SEG
    query_hot = (query_seg[:, None] == labels[None, :]).astype(jnp.float32)
    query_reach = precise_dot(query_hot, reachable)
    levels = precise_dot(query_hot, depth[0].astype(jnp.float32)[:, None])[:, 0]
    positions = levels * SEG + (query_index % SEG).astype(jnp.float32)
    cosines, sines = angles_of(positions)
    score_scale = HD ** (-0.5)

    def permit(key_len):
        key_index = jnp.arange(key_len, dtype=jnp.int32)
        key_seg = key_index // SEG
        key_hot = (key_seg[:, None] == labels[None, :]).astype(jnp.float32)
        linked = precise_dot(query_reach, key_hot.T) > 0.5
        return linked & (
            (query_seg[:, None] != key_seg[None, :]) | (query_index[:, None] >= key_index[None, :])
        )

    whole = lax.all_gather(tokens, "col", axis=1, tiled=True).astype(jnp.float32)
    centred = whole - jnp.mean(whole, axis=1, keepdims=True)
    inv_scale = lax.rsqrt(jnp.mean(centred * centred, axis=1, keepdims=True) + norm_epsilon)
    normal = centred * inv_scale
    normed = (normal * ln_gain + ln_bias).astype(jnp.bfloat16)
    qkv_full, up_full, out_full, down_full = (
        lax.all_gather(w_qkv.astype(jnp.bfloat16), "row", axis=0, tiled=True),
        lax.all_gather(w_up.astype(jnp.bfloat16), "row", axis=0, tiled=True),
        lax.all_gather(w_out.astype(jnp.bfloat16), "row", axis=1, tiled=True),
        lax.all_gather(w_down.astype(jnp.bfloat16), "row", axis=1, tiled=True),
    )
    mixed = (jnp.dot(normed, qkv_full, preferred_element_type=jnp.float32) + b_qkv).reshape(
        tok_rows, local_heads, 3, HD
    )

    def rotate_pair(query_pre, key_pre):
        return (rotate(query_pre, cosines, sines), rotate(key_pre, cosines, sines))

    rotated, rotate_back = jax.vjp(rotate_pair, mixed[:, :, 0], mixed[:, :, 1])
    queries = rotated[0].astype(jnp.bfloat16)
    key_rows = rotated[1].astype(jnp.bfloat16)
    value_rows = mixed[:, :, 2].astype(jnp.bfloat16)
    key_flat = key_rows.reshape(tok_rows, local_heads * HD)
    value_flat = value_rows.reshape(tok_rows, local_heads * HD)

    def scores_for(key_part):
        raw_scores = (
            jnp.einsum("qhe,khe->hqk", queries, key_part, preferred_element_type=jnp.float32)
            * score_scale
        )
        allowed = permit(key_part.shape[0])
        return (jnp.where(allowed[None], raw_scores, masked_fill), allowed)

    pieces = (
        lax.all_gather(key_flat, "row", axis=0, tiled=True),
        lax.all_gather(value_flat, "row", axis=0, tiled=True),
    )
    running_top = jnp.full((local_heads, tok_rows), masked_fill, jnp.float32)
    key_len = pieces[0].shape[0]
    key_part = pieces[0].reshape(key_len, local_heads, HD)
    value_part = pieces[1].reshape(key_len, local_heads, HD)
    scores, allowed = scores_for(key_part)
    new_top = jnp.maximum(running_top, jnp.max(scores, axis=2))
    exponent = jnp.where(allowed[None], jnp.exp(scores - new_top[:, :, None]), 0.0)
    running_sum = jnp.sum(exponent, axis=2)
    weighted = jnp.einsum(
        "hqk,khe->hqe",
        exponent.astype(jnp.bfloat16),
        value_part,
        preferred_element_type=jnp.float32,
    )
    running_top, running_sum, weighted = (new_top, running_sum, weighted)
    log_total = running_top + jnp.log(running_sum)
    attn_exact = weighted / running_sum[:, :, None]
    attended = (
        jnp.transpose(attn_exact, (1, 0, 2))
        .reshape(tok_rows, local_heads * HD)
        .astype(jnp.bfloat16)
    )
    hidden_up = jnp.dot(normed, up_full, preferred_element_type=jnp.float32) + b_up
    activated, gelu_back = jax.vjp(functools.partial(jax.nn.gelu, approximate=True), hidden_up)
    activated = activated.astype(jnp.bfloat16)
    branch_terms = jnp.dot(attended, out_full, preferred_element_type=jnp.float32) + jnp.dot(
        activated, down_full, preferred_element_type=jnp.float32
    )
    branch = lax.psum_scatter(
        branch_terms.astype(jnp.bfloat16), "col", scatter_dimension=1, tiled=True
    ).astype(jnp.float32)
    output = (tokens.astype(jnp.float32) + branch + b_res).astype(jnp.bfloat16)
    grad_full = lax.all_gather(cotangent, "col", axis=1, tiled=True)
    res_bias_grad = jnp.sum(cotangent.astype(jnp.float32), axis=0)
    down_grad = jnp.einsum("tf,td->fd", activated, grad_full, preferred_element_type=jnp.float32)
    out_grad = jnp.einsum("te,td->ed", attended, grad_full, preferred_element_type=jnp.float32)
    act_grad = jnp.einsum("td,fd->tf", grad_full, down_full, preferred_element_type=jnp.float32)
    up_grad = gelu_back(act_grad)[0].astype(jnp.bfloat16)
    attn_grad = jnp.einsum(
        "td,ed->te", grad_full, out_full, preferred_element_type=jnp.float32
    ).astype(jnp.bfloat16)
    up_bias_grad = jnp.sum(up_grad.astype(jnp.float32), axis=0)
    up_weight_grad = jnp.einsum("td,tf->df", normed, up_grad, preferred_element_type=jnp.float32)
    out_heads = attn_grad.reshape(tok_rows, local_heads, HD)
    delta_sum = jnp.einsum("qhe,hqe->hq", out_heads.astype(jnp.float32), attn_exact)
    pieces = (
        lax.all_gather(key_flat, "row", axis=0, tiled=True),
        lax.all_gather(value_flat, "row", axis=0, tiled=True),
    )
    key_len = pieces[0].shape[0]
    key_part = pieces[0].reshape(key_len, local_heads, HD)
    value_part = pieces[1].reshape(key_len, local_heads, HD)
    scores, allowed = scores_for(key_part)
    softmaxed = jnp.where(allowed[None], jnp.exp(scores - log_total[:, :, None]), 0.0)
    prob_grad = jnp.einsum(
        "qhe,khe->hqk", out_heads, value_part, preferred_element_type=jnp.float32
    )
    score_grad = (softmaxed * (prob_grad - delta_sum[:, :, None])).astype(jnp.bfloat16)
    query_grad = (
        jnp.einsum("hqk,khe->qhe", score_grad, key_part, preferred_element_type=jnp.float32)
        * score_scale
    )
    key_grad = (
        jnp.einsum("hqk,qhe->khe", score_grad, queries, preferred_element_type=jnp.float32)
        * score_scale
    )
    value_grad = jnp.einsum(
        "hqk,qhe->khe",
        softmaxed.astype(jnp.bfloat16),
        out_heads,
        preferred_element_type=jnp.float32,
    )
    stacked = jnp.stack([key_grad, value_grad], axis=1).reshape(key_len, 2 * local_heads * HD)
    pair_grad = stacked
    query_grad, pair_grad = (query_grad, pair_grad)
    own_pairs = (
        lax.psum_scatter(pair_grad.astype(jnp.bfloat16), "row", scatter_dimension=0, tiled=True)
        .astype(jnp.float32)
        .reshape(tok_rows, 2, local_heads, HD)
    )
    query_pre, key_pre = rotate_back((query_grad, own_pairs[:, 0]))
    mixed_grad = (
        jnp.stack([query_pre, key_pre, own_pairs[:, 1]], axis=2)
        .reshape(tok_rows, 3 * local_heads * HD)
        .astype(jnp.bfloat16)
    )
    qkv_bias_grad = jnp.sum(mixed_grad.astype(jnp.float32), axis=0)
    qkv_weight_grad = jnp.einsum(
        "td,tc->dc", normed, mixed_grad, preferred_element_type=jnp.float32
    )
    norm_part = jnp.einsum(
        "tc,dc->td", mixed_grad, qkv_full, preferred_element_type=jnp.float32
    ) + jnp.einsum("tf,df->td", up_grad, up_full, preferred_element_type=jnp.float32)
    norm_grad = lax.psum(norm_part.astype(jnp.bfloat16), "col").astype(jnp.float32)
    gain_grad = jnp.sum(norm_grad * normal, axis=0)
    shift_grad = jnp.sum(norm_grad, axis=0)
    scaled = norm_grad * ln_gain
    mean_scaled = jnp.mean(scaled, axis=1, keepdims=True)
    mean_mixed = jnp.mean(scaled * normal, axis=1, keepdims=True)
    col_start = lax.axis_index("col") * col_width
    scaled_share = lax.dynamic_slice_in_dim(scaled, col_start, col_width, 1)
    normal_share = lax.dynamic_slice_in_dim(normal, col_start, col_width, 1)
    tokens_grad = inv_scale * (
        scaled_share - mean_scaled - normal_share * mean_mixed
    ) + cotangent.astype(jnp.float32)
    qkv_bias_grad, up_bias_grad, res_bias_grad, gain_grad, shift_grad = (
        lax.psum(qkv_bias_grad.astype(jnp.bfloat16), ("dp", "row")).astype(jnp.float32),
        lax.psum(up_bias_grad.astype(jnp.bfloat16), ("dp", "row")).astype(jnp.float32),
        lax.psum(res_bias_grad.astype(jnp.bfloat16), ("dp", "row")).astype(jnp.float32),
        lax.psum(gain_grad.astype(jnp.bfloat16), ("dp", "row")).astype(jnp.float32),
        lax.psum(shift_grad.astype(jnp.bfloat16), ("dp", "row")).astype(jnp.float32),
    )
    pieces_now = (
        lax.psum_scatter(
            reorder_rows(qkv_weight_grad, row_count, dp_count).astype(jnp.bfloat16),
            ("dp", "row"),
            scatter_dimension=0,
            tiled=True,
        ).astype(jnp.float32),
        lax.psum_scatter(
            reorder_rows(up_weight_grad, row_count, dp_count).astype(jnp.bfloat16),
            ("dp", "row"),
            scatter_dimension=0,
            tiled=True,
        ).astype(jnp.float32),
        lax.psum_scatter(
            reorder_cols(out_grad, row_count, dp_count).astype(jnp.bfloat16),
            ("dp", "row"),
            scatter_dimension=1,
            tiled=True,
        ).astype(jnp.float32),
        lax.psum_scatter(
            reorder_cols(down_grad, row_count, dp_count).astype(jnp.bfloat16),
            ("dp", "row"),
            scatter_dimension=1,
            tiled=True,
        ).astype(jnp.float32),
    )
    qkv_weight_grad, up_weight_grad, out_grad, down_grad = (
        lax.all_gather(pieces_now[0].astype(jnp.bfloat16), "dp", axis=0, tiled=True).astype(
            jnp.float32
        ),
        lax.all_gather(pieces_now[1].astype(jnp.bfloat16), "dp", axis=0, tiled=True).astype(
            jnp.float32
        ),
        lax.all_gather(pieces_now[2].astype(jnp.bfloat16), "dp", axis=1, tiled=True).astype(
            jnp.float32
        ),
        lax.all_gather(pieces_now[3].astype(jnp.bfloat16), "dp", axis=1, tiled=True).astype(
            jnp.float32
        ),
    )
    return (
        output,
        tokens_grad,
        qkv_weight_grad,
        qkv_bias_grad,
        out_grad,
        up_weight_grad,
        up_bias_grad,
        down_grad,
        res_bias_grad,
        gain_grad,
        shift_grad,
    )


SWAP_ROW = [(0, 1), (1, 0)]
SWAP_X = [(0, 2), (2, 0), (1, 3), (3, 1)]
SWAP_CORE = [(0, 1), (1, 0), (2, 3), (3, 2)]


def bf16(values):
    return values.astype(jnp.bfloat16)


def f32(values):
    return values.astype(jnp.float32)


def matmul(left, right, dims=((1,), (0,))):
    return lax.dot_general(left, right, (dims, ((), ())), preferred_element_type=jnp.float32)


def swap_row(values):
    return lax.ppermute(values, "row", SWAP_ROW)


def swap_x(values):
    return lax.ppermute(values, "dp", SWAP_X)


def swap_core(values):
    return lax.ppermute(values, "dp", SWAP_CORE)


def pick(index, first, second):
    return jnp.where(index == 0, first, second)


def pair(index, mine, theirs, axis):
    return pick(
        index,
        jnp.concatenate([mine, theirs], axis=axis),
        jnp.concatenate([theirs, mine], axis=axis),
    )


def after(value, *earlier):
    return lax.optimization_barrier((value,) + earlier)[0]


def rotary_tables(positions):
    lane = jnp.arange(2 * HD, dtype=jnp.int32) % HD
    half_rot = ROT // 2
    frequency = jnp.exp(
        -math.log(rotary_base) * 2.0 * (lane % half_rot).astype(jnp.float32) / ROT
    )
    angle = positions[:, None] * frequency[None, :]
    turned = (lane < ROT)[None, :]
    sines = jnp.sin(angle)
    return (
        jnp.where(turned, jnp.cos(angle), 1.0),
        jnp.where((lane < half_rot)[None, :], -sines, 0.0),
        jnp.where(turned & (lane >= half_rot)[None, :], sines, 0.0),
    )


def turn(values, cosines, sines_low, sines_high):
    width = values.shape[1]
    half_rot = ROT // 2
    return (
        values * cosines
        + pltpu.roll(values, width - half_rot, 1) * sines_low
        + pltpu.roll(values, half_rot, 1) * sines_high
    )


def mixed_kernel(
    normed_ref, weight_ref, bias_ref, cos_ref, low_ref, high_ref, query_ref, keyval_ref
):
    cosines, low, high = cos_ref[...], low_ref[...], high_ref[...]
    rows, half = query_ref.shape
    first = lax.broadcasted_iota(jnp.int32, (rows, 2 * HD), 1) < HD
    scale = HD ** (-0.5)
    mixed = matmul(normed_ref[...], weight_ref[...]) + bias_ref[...]
    for at in range(half // (2 * HD)):
        tiles = [mixed[:, (3 * at + part) * 2 * HD : (3 * at + part + 1) * 2 * HD] for part in range(3)]
        query = jnp.where(first, tiles[0], tiles[1])
        key = jnp.where(first, pltpu.roll(tiles[0], HD, 1), pltpu.roll(tiles[2], HD, 1))
        value = jnp.where(first, tiles[1], tiles[2])
        here = slice(at * 2 * HD, (at + 1) * 2 * HD)
        query_ref[:, here] = bf16(f32(bf16(turn(query, cosines, low, high))) * scale)
        keyval_ref[:, here] = bf16(turn(key, cosines, low, high))
        keyval_ref[:, half + at * 2 * HD : half + (at + 1) * 2 * HD] = bf16(value)


def join_kernel(row_ref, dq_ref, dkv_ref, sent_ref, cos_ref, low_ref, high_ref, out_ref):
    cosines, low, high = cos_ref[...], -low_ref[...], -high_ref[...]
    rows = dq_ref.shape[0]
    half = dq_ref.shape[1]
    first = lax.broadcasted_iota(jnp.int32, (rows, 2 * HD), 1) < HD
    owner = row_ref[0] == 0
    for at in range(half // (2 * HD)):
        here = slice(at * 2 * HD, (at + 1) * 2 * HD)
        there = slice(half + at * 2 * HD, half + (at + 1) * 2 * HD)
        query = turn(dq_ref[:, here], cosines, low, high)
        key = dkv_ref[:, here] + jnp.where(owner, f32(sent_ref[:, here]), 0.0)
        value = dkv_ref[:, there] + jnp.where(owner, f32(sent_ref[:, there]), 0.0)
        key = pltpu.roll(turn(key, cosines, low, high), HD, 1)
        tiles = (jnp.where(first, query, key), jnp.where(first, value, query), jnp.where(first, key, value))
        for part in range(3):
            out_ref[:, (3 * at + part) * 2 * HD : (3 * at + part + 1) * 2 * HD] = bf16(tiles[part])


def tree_kernel(
    parent_ref, row_ref, query_ref, keyval_ref, trunk_ref, grad_ref,
    out_ref, dq_ref, dkv_ref, dtrunk_ref,
    keys, values, dkeys, dvalues,
):
    tree = pl.program_id(0)
    row = row_ref[0]
    rows, half = query_ref.shape
    trunk_len = trunk_ref.shape[0]
    segs = rows // SEG
    trunk_segs = trunk_len // SEG
    seg_count = parent_ref.shape[1]
    first_row = row == 0
    keys[...] = jnp.where(first_row, keyval_ref[:, :half], trunk_ref[:, :half])
    values[...] = jnp.where(first_row, keyval_ref[:, half:], trunk_ref[:, half:])
    dkeys[...] = jnp.zeros_like(dkeys)
    dvalues[...] = jnp.zeros_like(dvalues)
    lane = lax.broadcasted_iota(jnp.int32, (1, half), 1)
    causal = lax.broadcasted_iota(jnp.int32, (SEG, SEG), 0) >= lax.broadcasted_iota(
        jnp.int32, (SEG, SEG), 1
    )
    across = ((1,), (1,))
    down = ((0,), (0,))
    for seg in range(segs):
        here = slice(seg * SEG, (seg + 1) * SEG)
        above = parent_ref[tree, row * segs + seg]
        linked = [above == at for at in range(trunk_segs)]
        for _ in range(seg_count - 2):
            above = jnp.where(above >= 0, parent_ref[tree, jnp.maximum(above, 0)], -1)
            linked = [was | (above == at) for at, was in enumerate(linked)]
        bias = [jnp.where(is_linked, 0.0, masked_fill) for is_linked in linked]
        query, grad = query_ref[here, :], grad_ref[here, :]
        own_key, own_value = keyval_ref[here, :half], keyval_ref[here, half:]
        attended = jnp.zeros((SEG, half), jnp.float32)
        dquery = jnp.zeros((SEG, half), jnp.float32)
        dkey = jnp.zeros((SEG, half), jnp.float32)
        dvalue = jnp.zeros((SEG, half), jnp.float32)
        for head in range(half // HD):
            mine = (lane >= head * HD) & (lane < (head + 1) * HD)
            head_query = jnp.where(mine, query, jnp.zeros_like(query))
            head_grad = jnp.where(mine, grad, jnp.zeros_like(grad))
            scores = [
                matmul(head_query, keys[at * SEG : (at + 1) * SEG, :], across) + bias[at]
                for at in range(trunk_segs)
            ] + [jnp.where(causal, matmul(head_query, own_key, across), masked_fill)]
            top = functools.reduce(jnp.maximum, [jnp.max(s, axis=1, keepdims=True) for s in scores])
            powers = [jnp.exp(s - top) for s in scores]
            total = functools.reduce(jnp.add, [jnp.sum(p, axis=1, keepdims=True) for p in powers])
            probs = [p / total for p in powers]
            low = [bf16(p) for p in probs]
            blocks = [values[at * SEG : (at + 1) * SEG, :] for at in range(trunk_segs)] + [own_value]
            prob_grads = [matmul(head_grad, v, across) for v in blocks]
            delta = functools.reduce(
                jnp.add, [jnp.sum(p * g, axis=1, keepdims=True) for p, g in zip(probs, prob_grads)]
            )
            score_grads = [bf16(p * (g - delta)) for p, g in zip(probs, prob_grads)]
            head_out = functools.reduce(jnp.add, [matmul(p, v) for p, v in zip(low, blocks)])
            attended = jnp.where(mine, head_out, attended)
            key_blocks = [keys[at * SEG : (at + 1) * SEG, :] for at in range(trunk_segs)] + [own_key]
            head_dq = functools.reduce(jnp.add, [matmul(s, u) for s, u in zip(score_grads, key_blocks)])
            dquery = jnp.where(mine, head_dq, dquery)
            dkey = dkey + matmul(score_grads[-1], head_query, down)
            dvalue = dvalue + matmul(low[-1], head_grad, down)
            for at in range(trunk_segs):
                spot = slice(at * SEG, (at + 1) * SEG)
                dkeys[spot, :] += matmul(score_grads[at], head_query, down)
                dvalues[spot, :] += matmul(low[at], head_grad, down)
        out_ref[here, :] = bf16(attended)
        dq_ref[here, :] = dquery * HD ** (-0.5)
        dkv_ref[here, :half] = dkey
        dkv_ref[here, half:] = dvalue
    dtrunk_ref[:, :half] = bf16(dkeys[...])
    dtrunk_ref[:, half:] = bf16(dvalues[...])

    @pl.when(first_row)
    def _():
        dkv_ref[:, :half] += dkeys[...]
        dkv_ref[:, half:] += dvalues[...]


def store_blocks(place_ref, sides, full_ref, own_refs, plain_refs):
    row, slab = place_ref[1], place_ref[2]
    for side, values in enumerate(sides):
        width = values[0].shape[1]
        for source, value in enumerate(values):
            within = source % 2
            here = row == source // 2

            def put(refs):
                if len(refs) == 1:
                    refs[0][side, :, within * width : (within + 1) * width] = value
                else:
                    refs[within][side] = value

            @pl.when(here)
            def _():
                full_ref[side, :, within * width : (within + 1) * width] = value
                put(own_refs)

            @pl.when(jnp.logical_not(here))
            def _():
                put(plain_refs)
                at = (2 + jnp.where(slab == 0, within, 1 - within)) * width
                full_ref[side, :, pl.ds(pl.multiple_of(at, width), width)] = value


def gather_kernel(place_ref, mine_ref, theirs_ref, full_ref, own_ref, plain_ref):
    sides = [[ref[at] for at in range(ref.shape[0])] for ref in (mine_ref, theirs_ref)]
    store_blocks(place_ref, sides, full_ref, [own_ref], [plain_ref])


def norm_kernel(place_ref, gain_ref, bias_ref, mine_ref, theirs_ref, full_ref, *outs):
    normal_ref, scale_ref = outs[4:]
    sides = []
    for side, ref in enumerate((mine_ref, theirs_ref)):
        values = [f32(ref[at]) for at in range(ref.shape[0])]
        features = len(values) * values[0].shape[1]
        mean = functools.reduce(jnp.add, [jnp.sum(v, axis=1, keepdims=True) for v in values]) / features
        centred = [v - mean for v in values]
        square = functools.reduce(jnp.add, [jnp.sum(v * v, axis=1, keepdims=True) for v in centred])
        inv_scale = lax.rsqrt(square / features + norm_epsilon)
        normals = [v * inv_scale for v in centred]
        if side == 0:
            scale_ref[...] = inv_scale
            for source, normal in enumerate(normals):

                @pl.when(place_ref[0] == source)
                def _():
                    normal_ref[...] = normal

        sides.append(
            [
                bf16(normal * gain_ref[source : source + 1, :] + bias_ref[source : source + 1, :])
                for source, normal in enumerate(normals)
            ]
        )
    store_blocks(place_ref, sides, full_ref, outs[:2], outs[2:4])


def pair_rows(rows, width):
    return pl.BlockSpec((2, rows, width), lambda at, *_: (0, at, 0))


def gathered(place, mine, theirs, norm=None):
    blocks, count, width = mine.shape
    rows = SEG if norm is None else SEG // 2
    full = blocks * width
    in_specs = [pl.BlockSpec((blocks, rows, width), lambda at, *_: (0, at, 0))] * 2
    parts = [full // 2] * 2 if norm is None else [width] * 4
    out_specs = [pair_rows(rows, size) for size in [full] + parts]
    out_shape = [
        jax.ShapeDtypeStruct((2, count, size), jnp.bfloat16) for size in [full] + parts
    ]
    operands = [mine, theirs]
    if norm is not None:
        gain = [values.reshape(blocks, width) for values in norm]
        operands = gain + operands
        in_specs = [pl.BlockSpec((blocks, width), lambda at, *_: (0, 0))] * 2 + in_specs
        out_specs = out_specs + [row_block(rows, width), row_block(rows, 1)]
        out_shape = out_shape + [
            jax.ShapeDtypeStruct((count, width), jnp.float32),
            jax.ShapeDtypeStruct((count, 1), jnp.float32),
        ]
    results = pl.pallas_call(
        gather_kernel if norm is None else norm_kernel,
        grid_spec=pltpu.PrefetchScalarGridSpec(
            num_scalar_prefetch=1, grid=(count // rows,), in_specs=in_specs, out_specs=out_specs
        ),
        out_shape=out_shape,
        cost_estimate=pl.CostEstimate(flops=1, bytes_accessed=1, transcendentals=0),
        name="join_blocks" if norm is None else "norm_blocks",
    )(place, *operands)
    last = len(parts) + 1
    return [values.reshape(2 * count, -1) for values in results[:last]] + list(results[last:])


def stack_kernel(place_ref, terms_ref, arrived_ref, out_ref):
    row, slab = place_ref[1], place_ref[2]
    width = out_ref.shape[2]
    for spot in range(4):
        here = slice(spot * width, (spot + 1) * width)
        value = bf16(f32(terms_ref[:, here]) + f32(arrived_ref[:, here]))
        if spot < 2:
            out_ref[2 * row + spot] = value
        else:
            out_ref[2 * (1 - row) + jnp.where(slab == 0, spot - 2, 3 - spot)] = value


def stacked(place, terms, arrived, blocks):
    count, full = arrived.shape
    rows = SEG
    width = full // blocks
    return pl.pallas_call(
        stack_kernel,
        grid_spec=pltpu.PrefetchScalarGridSpec(
            num_scalar_prefetch=1,
            grid=(count // rows,),
            in_specs=[row_block(rows, full), row_block(rows, full)],
            out_specs=pl.BlockSpec((blocks, rows, width), lambda at, *_: (0, at, 0)),
        ),
        out_shape=jax.ShapeDtypeStruct((blocks, count, width), jnp.bfloat16),
        cost_estimate=pl.CostEstimate(flops=1, bytes_accessed=1, transcendentals=0),
        name="stack_blocks",
    )(place, terms, arrived)


def cast_rows_kernel(place_ref, master_ref, own_ref, send_ref):
    value = bf16(master_ref[...])
    own_ref[...] = value
    half = pl.num_programs(0) // 2

    @pl.when(pl.program_id(0) // half == place_ref[2])
    def _():
        send_ref[...] = value


def cast_cols_kernel(place_ref, master_ref, own_ref, send_ref):
    value = bf16(master_ref[...])
    own_ref[...] = value
    half = value.shape[1] // 2
    send_ref[...] = jnp.where(place_ref[2] == 0, value[:, :half], value[:, half:])


def cast_weight(place, master, axis):
    height, width = master.shape
    rows = min(2 * SEG, master.shape[0] // 4)
    if axis == 0:
        width = width // 2
        steps = height // rows
        half = steps // 2
        specs = [
            pl.BlockSpec((rows, width), lambda at, place_ref: (at, place_ref[3])),
            pl.BlockSpec((rows, width), lambda at, place_ref: (at, 0)),
            pl.BlockSpec(
                (rows, width), lambda at, place_ref: (jnp.clip(at - half * place_ref[2], 0, half - 1), 0)
            ),
        ]
        send = (height // 2, width)
        whole = (2 * height, width)
    else:
        height = height // 2
        steps = height // rows
        specs = [
            pl.BlockSpec((rows, width), lambda at, place_ref: (at + steps * place_ref[3], 0)),
            pl.BlockSpec((rows, width), lambda at, place_ref: (at, 0)),
            pl.BlockSpec((rows, width // 2), lambda at, place_ref: (at, 0)),
        ]
        send = (height, width // 2)
        whole = (height, 2 * width)
    return pl.pallas_call(
        cast_rows_kernel if axis == 0 else cast_cols_kernel,
        grid_spec=pltpu.PrefetchScalarGridSpec(
            num_scalar_prefetch=1, grid=(steps,), in_specs=specs[:1], out_specs=specs[1:]
        ),
        out_shape=[
            jax.ShapeDtypeStruct(whole, jnp.bfloat16),
            jax.ShapeDtypeStruct(send, jnp.bfloat16),
        ],
        cost_estimate=pl.CostEstimate(flops=1, bytes_accessed=1, transcendentals=0),
        name="cast_weight",
    )(place, master)


def settle_store(axis, place_ref, mine, theirs, out_ref):
    if axis == 0:
        out_ref[place_ref[3]] = mine
        out_ref[1 - place_ref[3]] = theirs
    else:
        width = mine.shape[1]
        first = place_ref[3] == 0
        out_ref[:, :width] = jnp.where(first, mine, theirs)
        out_ref[:, width:] = jnp.where(first, theirs, mine)


def settle_kernel(axis, place_ref, mine_ref, theirs_ref, *refs):
    settle_store(axis, place_ref, f32(mine_ref[...]), f32(theirs_ref[...]), refs[-1])


def settle_both_kernel(axis, place_ref, *refs):
    for at in range(2):

        @pl.when(pl.program_id(0) == at)
        def _():
            settle_store(axis, place_ref, f32(refs[2 * at][...]), f32(refs[2 * at + 1][...]), refs[-1])


def settle_both(place, first, last, shape, axis):
    rows, width = first[0].shape
    if axis == 0:
        shape = (2, shape[0] // 2, width)
        out_spec = pl.BlockSpec((2, rows, width), lambda at, *_: (0, at, 0))
    else:
        out_spec = pl.BlockSpec((rows, 2 * width), lambda at, *_: (at, 0))
    return pl.pallas_call(
        functools.partial(settle_both_kernel, axis),
        grid_spec=pltpu.PrefetchScalarGridSpec(
            num_scalar_prefetch=1,
            grid=(2,),
            in_specs=[pl.BlockSpec((rows, width), lambda *_: (0, 0))] * 4,
            out_specs=out_spec,
        ),
        out_shape=jax.ShapeDtypeStruct(shape, jnp.float32),
        cost_estimate=pl.CostEstimate(flops=1, bytes_accessed=1, transcendentals=0),
        name="settle_both",
    )(place, *first, *last)


def settle(place, mine, theirs, shape, axis, offset, dest=None):
    rows, width = mine.shape
    at = offset // rows
    whole = pl.BlockSpec((rows, width), lambda *_: (0, 0))
    if axis == 0:
        shape = (2, shape[0] // 2, width)
        out_spec = pl.BlockSpec((2, rows, width), lambda *_: (0, at, 0))
    else:
        out_spec = pl.BlockSpec((rows, 2 * width), lambda *_: (at, 0))
    in_specs = [whole, whole]
    operands = [place, mine, theirs]
    aliases = {}
    if dest is not None:
        in_specs.append(pl.BlockSpec(memory_space=pl.ANY))
        operands.append(dest)
        aliases = {3: 0}
    return pl.pallas_call(
        functools.partial(settle_kernel, axis),
        grid_spec=pltpu.PrefetchScalarGridSpec(
            num_scalar_prefetch=1, grid=(1,), in_specs=in_specs, out_specs=out_spec
        ),
        out_shape=jax.ShapeDtypeStruct(shape, jnp.float32),
        input_output_aliases=aliases,
        cost_estimate=pl.CostEstimate(flops=1, bytes_accessed=1, transcendentals=0),
        name="settle",
    )(*operands)


def row_block(rows, width):
    return pl.BlockSpec((rows, width), lambda at, *_: (at, 0))


def mixed_heads(normed, weight, bias, tables):
    count, depth = normed.shape
    width = weight.shape[1]
    rows = SEG
    return pl.pallas_call(
        mixed_kernel,
        grid=(count // rows,),
        in_specs=[
            row_block(rows, depth),
            pl.BlockSpec((depth, width), lambda at: (0, 0)),
            pl.BlockSpec((1, width), lambda at: (0, 0)),
        ]
        + [row_block(rows, 2 * HD)] * 3,
        out_specs=[row_block(rows, width // 3), row_block(rows, 2 * width // 3)],
        out_shape=[
            jax.ShapeDtypeStruct((count, width // 3), jnp.bfloat16),
            jax.ShapeDtypeStruct((count, 2 * width // 3), jnp.bfloat16),
        ],
        cost_estimate=pl.CostEstimate(flops=1, bytes_accessed=1, transcendentals=0),
        name="mixed_heads",
    )(normed, weight, bias.reshape(1, width), *tables)


def join_heads(row, dq, dkv, sent, tables):
    count, half = dq.shape
    rows = 2 * SEG
    return pl.pallas_call(
        join_kernel,
        grid_spec=pltpu.PrefetchScalarGridSpec(
            num_scalar_prefetch=1,
            grid=(count // rows,),
            in_specs=[row_block(rows, half), row_block(rows, 2 * half), row_block(rows, 2 * half)]
            + [row_block(rows, 2 * HD)] * 3,
            out_specs=row_block(rows, 3 * half),
        ),
        out_shape=jax.ShapeDtypeStruct((count, 3 * half), jnp.bfloat16),
        cost_estimate=pl.CostEstimate(flops=1, bytes_accessed=1, transcendentals=0),
        name="join_heads",
    )(row, dq, dkv, sent, *tables)


def tree_attention(parents, row, query, keyval, trunk, grad):
    trees = parents.shape[0]
    count, half = query.shape
    rows = count // trees
    keys = trunk.shape[0] // trees
    pairs = count * (keys + SEG) * (half // HD)
    return pl.pallas_call(
        tree_kernel,
        grid_spec=pltpu.PrefetchScalarGridSpec(
            num_scalar_prefetch=2,
            grid=(trees,),
            in_specs=[
                row_block(rows, half),
                row_block(rows, 2 * half),
                row_block(keys, 2 * half),
                row_block(rows, half),
            ],
            out_specs=[
                row_block(rows, half),
                row_block(rows, half),
                row_block(rows, 2 * half),
                row_block(keys, 2 * half),
            ],
            scratch_shapes=[pltpu.VMEM((keys, half), jnp.bfloat16)] * 2
            + [pltpu.VMEM((keys, half), jnp.float32)] * 2,
        ),
        out_shape=[
            jax.ShapeDtypeStruct((count, half), jnp.bfloat16),
            jax.ShapeDtypeStruct((count, half), jnp.float32),
            jax.ShapeDtypeStruct((count, 2 * half), jnp.float32),
            jax.ShapeDtypeStruct((trees * keys, 2 * half), jnp.bfloat16),
        ],
        cost_estimate=pl.CostEstimate(flops=1, bytes_accessed=1, transcendentals=0),
        name="tree_attention",
    )(parents, row, query, keyval, trunk, grad)


def paired_device(
    tokens,
    parent,
    depth,
    w_qkv,
    b_qkv,
    w_out,
    w_up,
    b_up,
    w_down,
    b_res,
    ln_gain,
    ln_bias,
    cotangent,
):
    count, width = tokens.shape
    row = lax.axis_index("row")
    col = lax.axis_index("col")
    core = lax.axis_index("dp") % 2
    slab = lax.axis_index("dp") // 2
    cols = lax.axis_size("col")
    half = 2 * width
    heads_width = w_out.shape[0] // 2
    hidden = w_up.shape[1] // 2
    place = jnp.stack([col, row, slab, core]).astype(jnp.int32)
    row_table = jnp.reshape(row, (1,)).astype(jnp.int32)
    down_dims = ((0,), (0,))
    across = ((1,), (1,))

    def part(values, at, size, axis):
        return lax.dynamic_slice_in_dim(values, at * size, size, axis)

    def exchange(stack):
        return lax.all_to_all(stack, "col", 0, 0, tiled=True)

    done = ()

    def step(run, *inputs):
        nonlocal done
        inputs, _ = lax.optimization_barrier((inputs, done))
        result = run(*inputs)
        done = result
        return result

    def wait(value):
        return step(lambda arrived: arrived, value)

    tokens_near = lax.all_gather(tokens, "col", axis=0)
    grad_stack = jnp.broadcast_to(cotangent[None], (cols,) + cotangent.shape)

    def ready(master, axis):
        whole, send = step(lambda weight: cast_weight(place, weight, axis), master)
        return whole, swap_row(send)

    def fill(whole, part_in, axis, last):
        at = whole.shape[axis] // 2 + (part_in.shape[axis] if last else 0)
        return step(lambda a, b: lax.dynamic_update_slice_in_dim(a, b, at, axis), whole, part_in)

    tables = jnp.concatenate([parent, depth], axis=0)
    tables = jnp.stack([tables, swap_core(tables)])
    parents = tables[:, 0]
    segs = count // SEG
    token = jnp.arange(count, dtype=jnp.int32)
    levels = jnp.zeros((2, count), jnp.float32)
    for seg in range(segs):
        level = lax.dynamic_slice_in_dim(tables[:, 1], row * segs + seg, 1, 1).astype(jnp.float32)
        levels = jnp.where((token // SEG == seg)[None, :], level, levels)
    positions = (levels * SEG + (token % SEG).astype(jnp.float32)[None, :]).reshape(2 * count)
    rotary = rotary_tables(positions)

    qkv_whole, qkv_row = ready(w_qkv, 0)
    up_whole, up_row = ready(w_up, 0)
    qkv_row = wait(qkv_row)
    qkv_x = swap_x(qkv_row)
    out_whole, out_row = ready(w_out, 1)
    down_whole, down_row = ready(w_down, 1)
    rotary = step(lambda *tables: tables, *rotary)
    qkv_whole = fill(qkv_whole, qkv_row, 0, False)
    up_row = wait(up_row)
    up_x = swap_x(up_row)
    qkv_x = wait(qkv_x)
    tokens_near = wait(tokens_near)
    tokens_far = swap_core(tokens_near)
    grad_near = exchange(after(grad_stack, tokens_near))
    up_whole = fill(up_whole, up_row, 0, False)
    normed, own_a, own_b, plain_a, plain_b, normal, inv_scale = step(
        lambda mine, theirs: gathered(place, mine, theirs, (ln_gain, ln_bias)), tokens_near, tokens_far
    )
    qkv_full = fill(qkv_whole, qkv_x, 0, True)
    query, keyval = step(
        lambda left, right: mixed_heads(left, right, part(b_qkv, core, 3 * heads_width, 0), rotary),
        normed, qkv_full,
    )
    trunk = lax.ppermute(keyval, "row", [(0, 1)])
    root = math.sqrt(2.0 / math.pi)

    def feed(left, right):
        hidden_up = matmul(left, right) + part(b_up, core, hidden, 0)
        squared = hidden_up * hidden_up
        bend = jnp.tanh(root * (hidden_up + 0.044715 * squared * hidden_up))
        return bf16(0.5 * hidden_up * (1.0 + bend)), bf16(
            0.5 * (1.0 + bend)
            + 0.5 * hidden_up * (1.0 - bend * bend) * root * (1.0 + 3.0 * 0.044715 * squared)
        )

    out_row = wait(out_row)
    out_x = swap_x(out_row)
    up_full = fill(up_whole, up_x, 0, True)
    down_row = wait(down_row)
    down_x = swap_x(down_row)
    activated, slope = step(feed, normed, up_full)
    out_whole = fill(out_whole, out_row, 1, False)
    down_whole = fill(down_whole, down_row, 1, False)
    out_full = fill(out_whole, out_x, 1, True)
    trunk = wait(trunk)
    grad_near = wait(grad_near)
    grad_far = swap_core(grad_near)
    grad, grad_own, grad_plain = step(lambda mine, theirs: gathered(place, mine, theirs), grad_near, grad_far)

    def cut(values, at):
        size = values.shape[1] // 2
        return values[:, at * size : (at + 1) * size]

    def leaving(left, right):
        return step(lambda a, b: bf16(matmul(a, b, down_dims)), left, right)

    def staying(left, right, sent):
        return step(lambda a, b, c: bf16(matmul(a, b, down_dims) + f32(c)), left, right, sent)

    def crossed(both, arrived):
        mine = step(lambda a, b: bf16(f32(a) + f32(b)), both, arrived)
        return mine, swap_core(mine)

    def settled(pieces, shape, axis, offset, dest):
        operands = pieces if dest is None else pieces + (dest,)
        return step(
            lambda mine, theirs, *rest: settle(place, mine, theirs, shape, axis, offset, *rest), *operands
        )

    down_sent_a = swap_row(leaving(cut(activated, 0), grad_plain))
    down_sent_b = swap_row(leaving(cut(activated, 1), grad_plain))
    out_heads = step(lambda a, b: bf16(matmul(a, b, across)), grad, out_full)
    attended, query_grad, own_grad, trunk_grad = step(
        lambda *operands: tree_attention(parents, row_table, *operands), query, keyval, trunk, out_heads
    )
    trunk_sent = lax.ppermute(trunk_grad, "row", [(1, 0)])
    down_both_a = staying(cut(activated, 0), grad_own, down_sent_a)
    down_cross_a = swap_x(down_both_a)
    down_full = fill(down_whole, down_x, 1, True)
    up_grad = step(lambda a, b, c: bf16(matmul(a, b, across) * f32(c)), grad, down_full, slope)
    up_sent_a = swap_row(leaving(plain_a, up_grad))
    down_both_b = staying(cut(activated, 1), grad_own, down_sent_b)
    down_cross_b = swap_x(down_both_b)
    up_sent_b = swap_row(leaving(plain_b, up_grad))
    down_a = crossed(down_both_a, down_cross_a)
    branch_terms = step(
        lambda a, b, c, d: bf16(matmul(a, b) + matmul(c, d)), attended, out_full, activated, down_full
    )
    branch_near = swap_core(branch_terms[count:])
    mixed_grad = step(
        lambda *operands: join_heads(row_table, *operands, rotary), query_grad, own_grad, trunk_sent
    )
    qkv_sent_a = swap_row(leaving(plain_a, mixed_grad))
    down_b = crossed(down_both_b, down_cross_b)
    qkv_sent_b = swap_row(leaving(plain_b, mixed_grad))
    norm_terms = step(
        lambda a, b, c, d: bf16(matmul(a, b, across) + matmul(c, d, across)),
        mixed_grad, qkv_full, up_grad, up_full,
    )
    branch = lax.psum_scatter(
        step(lambda a, b: stacked(place, a, b, cols), branch_terms, branch_near), "col", tiled=False
    )
    up_both_a = staying(own_a, up_grad, up_sent_a)
    up_cross_a = swap_x(up_both_a)
    norm_near = swap_core(step(lambda terms: terms[count:], norm_terms))
    norm_parts = exchange(step(lambda a, b: stacked(place, a, b, cols), norm_terms, norm_near))
    down_grad = step(lambda first, last: settle_both(place, first, last, w_down.shape, 0), down_a, down_b)
    up_a = crossed(up_both_a, up_cross_a)
    up_both_b = staying(own_b, up_grad, up_sent_b)
    up_cross_b = swap_x(up_both_b)
    qkv_both_a = staying(own_a, mixed_grad, qkv_sent_a)
    qkv_cross_a = swap_x(qkv_both_a)
    out_sent = swap_row(leaving(attended, grad_plain))
    up_b = crossed(up_both_b, up_cross_b)
    qkv_both_b = staying(own_b, mixed_grad, qkv_sent_b)
    qkv_cross_b = swap_x(qkv_both_b)
    output = step(lambda parts, block: bf16(f32(block) + f32(parts) + b_res), branch, tokens)
    gain_here = part(ln_gain, col, width, 0)

    def norm_sums(parts):
        total = jnp.sum(f32(parts), axis=0)
        scaled = total * gain_here
        return (
            total,
            jnp.stack([jnp.sum(scaled, axis=1), jnp.sum(scaled * normal, axis=1)]),
            jnp.sum(total * normal, axis=0),
            jnp.sum(total, axis=0),
        )

    norm_grad, sums, gain_sum, shift_sum = step(norm_sums, norm_parts)
    up_weight_grad = step(lambda first, last: settle_both(place, first, last, w_up.shape, 1), up_a, up_b)

    def line_step(values, bit):
        return lax.ppermute(values, "col", [(at, at ^ bit) for at in range(cols)])

    small = jnp.concatenate(
        [
            jnp.sum(f32(up_grad), axis=0),
            jnp.sum(f32(mixed_grad), axis=0),
            jnp.sum(f32(cotangent), axis=0),
            gain_sum,
            shift_sum,
        ]
    ).reshape(-1, 128)
    shared_at = (hidden + 3 * heads_width) // 128
    res_at = width // 128
    sums_next = line_step(sums, 1)
    small_other = swap_core(small)
    qkv_a = crossed(qkv_both_a, qkv_cross_a)
    sums, shared = step(
        lambda sums, arrived, small, other: (sums + arrived, (small + other)[shared_at:]),
        sums, sums_next, small, small_other,
    )
    sums_next = line_step(sums, 2)
    ends = shared[res_at:][None]
    ends_next = line_step(ends, 1)
    out_both = staying(attended, grad_own, out_sent)
    out_cross = swap_x(out_both)
    ends = step(lambda ends, arrived: pair(col % 2, ends, arrived, 0), ends, ends_next)
    ends_next = line_step(ends, 2)
    qkv_weight_grad = settled(qkv_a, w_qkv.shape, 1, 0, None)
    sums = (sums + sums_next) / (cols * width)
    tokens_grad = step(
        lambda sums, total: inv_scale
        * (total * gain_here - sums[0][:, None] - normal * sums[1][:, None])
        + f32(cotangent),
        sums, norm_grad,
    )

    def gather_small(small, other, shared, ends, arrived):
        return jnp.concatenate(
            [
                pair(core, small[: hidden // 128], other[: hidden // 128], 0),
                pair(core, small[hidden // 128 : shared_at], other[hidden // 128 : shared_at], 0),
                shared[:res_at],
                pair(col // 2, ends, arrived, 0).reshape(-1, 128),
            ]
        )

    small = step(gather_small, small, small_other, shared, ends, ends_next)
    small_next = swap_row(small)
    qkv_b = crossed(qkv_both_b, qkv_cross_b)
    small = step(jnp.add, small, small_next)
    small_next = swap_x(small)
    out_mine = crossed(out_both, out_cross)
    qkv_weight_grad = settled(qkv_b, w_qkv.shape, 1, qkv_both_a.shape[0], qkv_weight_grad)
    out_grad = settled(out_mine, w_out.shape, 0, 0, None)
    small = step(jnp.add, small, small_next)

    bounds = [0, 2 * hidden // 128, (2 * hidden + 6 * heads_width) // 128]
    bounds.append(bounds[-1] + res_at)
    up_bias_grad = small[: bounds[1]].reshape(-1)
    qkv_bias_grad = small[bounds[1] : bounds[2]].reshape(-1)
    res_bias_grad = small[bounds[2] : bounds[3]].reshape(-1)
    ends = small[bounds[3] :].reshape(cols, 2, width)
    gain_grad = ends[:, 0].reshape(-1)
    shift_grad = ends[:, 1].reshape(-1)
    return (
        output,
        tokens_grad,
        qkv_weight_grad,
        qkv_bias_grad,
        out_grad.reshape(w_out.shape),
        up_weight_grad,
        up_bias_grad,
        down_grad.reshape(w_down.shape),
        res_bias_grad,
        gain_grad,
        shift_grad,
    )


def solution(mesh):
    sizes = (mesh.shape["dp"], mesh.shape["row"], mesh.shape["col"])
    per_device = paired_device if sizes == (4, 2, 4) else general_device
    return jax.shard_map(
        per_device,
        mesh=mesh,
        in_specs=(
            P(("dp", "row"), "col"),
            P("dp", None),
            P("dp", None),
            P("row", "col"),
            P("col"),
            P("col", "row"),
            P("row", "col"),
            P("col"),
            P("col", "row"),
            P("col"),
            P(),
            P(),
            P(("dp", "row"), "col"),
        ),
        out_specs=(
            P(("dp", "row"), "col"),
            P(("dp", "row"), "col"),
            P("row", "col"),
            P("col"),
            P("col", "row"),
            P("row", "col"),
            P("col"),
            P("col", "row"),
            P("col"),
            P(),
            P(),
        ),
        check_vma=False,
    )
```

```python
import functools
import math

import jax
import jax.numpy as jnp
from jax import lax
from jax.experimental import pallas as pl
from jax.experimental.pallas import tpu as pltpu
from jax.sharding import PartitionSpec as P

HD = 64
ROT = 32
SEG = 256


norm_epsilon = 1e-05
masked_fill = -1e30
rotary_base = 10000.0


def precise_dot(left, right):
    return jnp.dot(left, right, precision=lax.Precision.HIGHEST, preferred_element_type=jnp.float32)


def ancestry(parent_row):
    seg_count = parent_row.shape[0]
    labels = jnp.arange(seg_count, dtype=jnp.int32)
    identity = jnp.eye(seg_count, dtype=jnp.float32)
    parent_hot = (parent_row[:, None] == labels[None, :]).astype(jnp.float32)

    def extend(rounds, reachable):
        return jnp.minimum(identity + precise_dot(parent_hot, reachable), 1.0)

    return lax.fori_loop(0, seg_count, extend, identity)


def rotate(values, cosines, sines):
    half_rot = ROT // 2
    former = values[..., :half_rot]
    latter = values[..., half_rot:ROT]
    return jnp.concatenate(
        [former * cosines - latter * sines, latter * cosines + former * sines, values[..., ROT:]],
        axis=-1,
    )


def angles_of(positions):
    frequency = jnp.exp(
        -math.log(rotary_base) * 2.0 * jnp.arange(ROT // 2, dtype=jnp.float32) / ROT
    )
    phase_angle = positions[:, None] * frequency[None, :]
    return (jnp.cos(phase_angle)[:, None, :], jnp.sin(phase_angle)[:, None, :])


def reorder_rows(gradient, row_count, dp_count):
    leading = gradient.shape[0]
    blocked = gradient.reshape(
        row_count, dp_count, leading // (row_count * dp_count), gradient.shape[1]
    )
    return jnp.transpose(blocked, (1, 0, 2, 3)).reshape(leading, gradient.shape[1])


def reorder_cols(gradient, row_count, dp_count):
    trailing = gradient.shape[1]
    blocked = gradient.reshape(
        gradient.shape[0], row_count, dp_count, trailing // (row_count * dp_count)
    )
    return jnp.transpose(blocked, (0, 2, 1, 3)).reshape(gradient.shape[0], trailing)


def general_device(
    tokens,
    parent,
    depth,
    w_qkv,
    b_qkv,
    w_out,
    w_up,
    b_up,
    w_down,
    b_res,
    ln_gain,
    ln_bias,
    cotangent,
):
    tok_rows = tokens.shape[0]
    col_width = tokens.shape[1]
    row_count = lax.axis_size("row")
    dp_count = lax.axis_size("dp")
    row_start = lax.axis_index("row") * tok_rows
    local_heads = w_out.shape[0] // HD
    seg_count = parent.shape[1]
    labels = jnp.arange(seg_count, dtype=jnp.int32)
    reachable = ancestry(parent[0])
    query_index = row_start + jnp.arange(tok_rows, dtype=jnp.int32)
    query_seg = query_index // SEG
    query_hot = (query_seg[:, None] == labels[None, :]).astype(jnp.float32)
    query_reach = precise_dot(query_hot, reachable)
    levels = precise_dot(query_hot, depth[0].astype(jnp.float32)[:, None])[:, 0]
    positions = levels * SEG + (query_index % SEG).astype(jnp.float32)
    cosines, sines = angles_of(positions)
    score_scale = HD ** (-0.5)

    def permit(key_len):
        key_index = jnp.arange(key_len, dtype=jnp.int32)
        key_seg = key_index // SEG
        key_hot = (key_seg[:, None] == labels[None, :]).astype(jnp.float32)
        linked = precise_dot(query_reach, key_hot.T) > 0.5
        return linked & (
            (query_seg[:, None] != key_seg[None, :]) | (query_index[:, None] >= key_index[None, :])
        )

    whole = lax.all_gather(tokens, "col", axis=1, tiled=True).astype(jnp.float32)
    centred = whole - jnp.mean(whole, axis=1, keepdims=True)
    inv_scale = lax.rsqrt(jnp.mean(centred * centred, axis=1, keepdims=True) + norm_epsilon)
    normal = centred * inv_scale
    normed = (normal * ln_gain + ln_bias).astype(jnp.bfloat16)
    qkv_full, up_full, out_full, down_full = (
        lax.all_gather(w_qkv.astype(jnp.bfloat16), "row", axis=0, tiled=True),
        lax.all_gather(w_up.astype(jnp.bfloat16), "row", axis=0, tiled=True),
        lax.all_gather(w_out.astype(jnp.bfloat16), "row", axis=1, tiled=True),
        lax.all_gather(w_down.astype(jnp.bfloat16), "row", axis=1, tiled=True),
    )
    mixed = (jnp.dot(normed, qkv_full, preferred_element_type=jnp.float32) + b_qkv).reshape(
        tok_rows, local_heads, 3, HD
    )

    def rotate_pair(query_pre, key_pre):
        return (rotate(query_pre, cosines, sines), rotate(key_pre, cosines, sines))

    rotated, rotate_back = jax.vjp(rotate_pair, mixed[:, :, 0], mixed[:, :, 1])
    queries = rotated[0].astype(jnp.bfloat16)
    key_rows = rotated[1].astype(jnp.bfloat16)
    value_rows = mixed[:, :, 2].astype(jnp.bfloat16)
    key_flat = key_rows.reshape(tok_rows, local_heads * HD)
    value_flat = value_rows.reshape(tok_rows, local_heads * HD)

    def scores_for(key_part):
        raw_scores = (
            jnp.einsum("qhe,khe->hqk", queries, key_part, preferred_element_type=jnp.float32)
            * score_scale
        )
        allowed = permit(key_part.shape[0])
        return (jnp.where(allowed[None], raw_scores, masked_fill), allowed)

    pieces = (
        lax.all_gather(key_flat, "row", axis=0, tiled=True),
        lax.all_gather(value_flat, "row", axis=0, tiled=True),
    )
    running_top = jnp.full((local_heads, tok_rows), masked_fill, jnp.float32)
    key_len = pieces[0].shape[0]
    key_part = pieces[0].reshape(key_len, local_heads, HD)
    value_part = pieces[1].reshape(key_len, local_heads, HD)
    scores, allowed = scores_for(key_part)
    new_top = jnp.maximum(running_top, jnp.max(scores, axis=2))
    exponent = jnp.where(allowed[None], jnp.exp(scores - new_top[:, :, None]), 0.0)
    running_sum = jnp.sum(exponent, axis=2)
    weighted = jnp.einsum(
        "hqk,khe->hqe",
        exponent.astype(jnp.bfloat16),
        value_part,
        preferred_element_type=jnp.float32,
    )
    running_top, running_sum, weighted = (new_top, running_sum, weighted)
    log_total = running_top + jnp.log(running_sum)
    attn_exact = weighted / running_sum[:, :, None]
    attended = (
        jnp.transpose(attn_exact, (1, 0, 2))
        .reshape(tok_rows, local_heads * HD)
        .astype(jnp.bfloat16)
    )
    hidden_up = jnp.dot(normed, up_full, preferred_element_type=jnp.float32) + b_up
    activated, gelu_back = jax.vjp(functools.partial(jax.nn.gelu, approximate=True), hidden_up)
    activated = activated.astype(jnp.bfloat16)
    branch_terms = jnp.dot(attended, out_full, preferred_element_type=jnp.float32) + jnp.dot(
        activated, down_full, preferred_element_type=jnp.float32
    )
    branch = lax.psum_scatter(
        branch_terms.astype(jnp.bfloat16), "col", scatter_dimension=1, tiled=True
    ).astype(jnp.float32)
    output = (tokens.astype(jnp.float32) + branch + b_res).astype(jnp.bfloat16)
    grad_full = lax.all_gather(cotangent, "col", axis=1, tiled=True)
    res_bias_grad = jnp.sum(cotangent.astype(jnp.float32), axis=0)
    down_grad = jnp.einsum("tf,td->fd", activated, grad_full, preferred_element_type=jnp.float32)
    out_grad = jnp.einsum("te,td->ed", attended, grad_full, preferred_element_type=jnp.float32)
    act_grad = jnp.einsum("td,fd->tf", grad_full, down_full, preferred_element_type=jnp.float32)
    up_grad = gelu_back(act_grad)[0].astype(jnp.bfloat16)
    attn_grad = jnp.einsum(
        "td,ed->te", grad_full, out_full, preferred_element_type=jnp.float32
    ).astype(jnp.bfloat16)
    up_bias_grad = jnp.sum(up_grad.astype(jnp.float32), axis=0)
    up_weight_grad = jnp.einsum("td,tf->df", normed, up_grad, preferred_element_type=jnp.float32)
    out_heads = attn_grad.reshape(tok_rows, local_heads, HD)
    delta_sum = jnp.einsum("qhe,hqe->hq", out_heads.astype(jnp.float32), attn_exact)
    pieces = (
        lax.all_gather(key_flat, "row", axis=0, tiled=True),
        lax.all_gather(value_flat, "row", axis=0, tiled=True),
    )
    key_len = pieces[0].shape[0]
    key_part = pieces[0].reshape(key_len, local_heads, HD)
    value_part = pieces[1].reshape(key_len, local_heads, HD)
    scores, allowed = scores_for(key_part)
    softmaxed = jnp.where(allowed[None], jnp.exp(scores - log_total[:, :, None]), 0.0)
    prob_grad = jnp.einsum(
        "qhe,khe->hqk", out_heads, value_part, preferred_element_type=jnp.float32
    )
    score_grad = (softmaxed * (prob_grad - delta_sum[:, :, None])).astype(jnp.bfloat16)
    query_grad = (
        jnp.einsum("hqk,khe->qhe", score_grad, key_part, preferred_element_type=jnp.float32)
        * score_scale
    )
    key_grad = (
        jnp.einsum("hqk,qhe->khe", score_grad, queries, preferred_element_type=jnp.float32)
        * score_scale
    )
    value_grad = jnp.einsum(
        "hqk,qhe->khe",
        softmaxed.astype(jnp.bfloat16),
        out_heads,
        preferred_element_type=jnp.float32,
    )
    stacked = jnp.stack([key_grad, value_grad], axis=1).reshape(key_len, 2 * local_heads * HD)
    pair_grad = stacked
    query_grad, pair_grad = (query_grad, pair_grad)
    own_pairs = (
        lax.psum_scatter(pair_grad.astype(jnp.bfloat16), "row", scatter_dimension=0, tiled=True)
        .astype(jnp.float32)
        .reshape(tok_rows, 2, local_heads, HD)
    )
    query_pre, key_pre = rotate_back((query_grad, own_pairs[:, 0]))
    mixed_grad = (
        jnp.stack([query_pre, key_pre, own_pairs[:, 1]], axis=2)
        .reshape(tok_rows, 3 * local_heads * HD)
        .astype(jnp.bfloat16)
    )
    qkv_bias_grad = jnp.sum(mixed_grad.astype(jnp.float32), axis=0)
    qkv_weight_grad = jnp.einsum(
        "td,tc->dc", normed, mixed_grad, preferred_element_type=jnp.float32
    )
    norm_part = jnp.einsum(
        "tc,dc->td", mixed_grad, qkv_full, preferred_element_type=jnp.float32
    ) + jnp.einsum("tf,df->td", up_grad, up_full, preferred_element_type=jnp.float32)
    norm_grad = lax.psum(norm_part.astype(jnp.bfloat16), "col").astype(jnp.float32)
    gain_grad = jnp.sum(norm_grad * normal, axis=0)
    shift_grad = jnp.sum(norm_grad, axis=0)
    scaled = norm_grad * ln_gain
    mean_scaled = jnp.mean(scaled, axis=1, keepdims=True)
    mean_mixed = jnp.mean(scaled * normal, axis=1, keepdims=True)
    col_start = lax.axis_index("col") * col_width
    scaled_share = lax.dynamic_slice_in_dim(scaled, col_start, col_width, 1)
    normal_share = lax.dynamic_slice_in_dim(normal, col_start, col_width, 1)
    tokens_grad = inv_scale * (
        scaled_share - mean_scaled - normal_share * mean_mixed
    ) + cotangent.astype(jnp.float32)
    qkv_bias_grad, up_bias_grad, res_bias_grad, gain_grad, shift_grad = (
        lax.psum(qkv_bias_grad.astype(jnp.bfloat16), ("dp", "row")).astype(jnp.float32),
        lax.psum(up_bias_grad.astype(jnp.bfloat16), ("dp", "row")).astype(jnp.float32),
        lax.psum(res_bias_grad.astype(jnp.bfloat16), ("dp", "row")).astype(jnp.float32),
        lax.psum(gain_grad.astype(jnp.bfloat16), ("dp", "row")).astype(jnp.float32),
        lax.psum(shift_grad.astype(jnp.bfloat16), ("dp", "row")).astype(jnp.float32),
    )
    pieces_now = (
        lax.psum_scatter(
            reorder_rows(qkv_weight_grad, row_count, dp_count).astype(jnp.bfloat16),
            ("dp", "row"),
            scatter_dimension=0,
            tiled=True,
        ).astype(jnp.float32),
        lax.psum_scatter(
            reorder_rows(up_weight_grad, row_count, dp_count).astype(jnp.bfloat16),
            ("dp", "row"),
            scatter_dimension=0,
            tiled=True,
        ).astype(jnp.float32),
        lax.psum_scatter(
            reorder_cols(out_grad, row_count, dp_count).astype(jnp.bfloat16),
            ("dp", "row"),
            scatter_dimension=1,
            tiled=True,
        ).astype(jnp.float32),
        lax.psum_scatter(
            reorder_cols(down_grad, row_count, dp_count).astype(jnp.bfloat16),
            ("dp", "row"),
            scatter_dimension=1,
            tiled=True,
        ).astype(jnp.float32),
    )
    qkv_weight_grad, up_weight_grad, out_grad, down_grad = (
        lax.all_gather(pieces_now[0].astype(jnp.bfloat16), "dp", axis=0, tiled=True).astype(
            jnp.float32
        ),
        lax.all_gather(pieces_now[1].astype(jnp.bfloat16), "dp", axis=0, tiled=True).astype(
            jnp.float32
        ),
        lax.all_gather(pieces_now[2].astype(jnp.bfloat16), "dp", axis=1, tiled=True).astype(
            jnp.float32
        ),
        lax.all_gather(pieces_now[3].astype(jnp.bfloat16), "dp", axis=1, tiled=True).astype(
            jnp.float32
        ),
    )
    return (
        output,
        tokens_grad,
        qkv_weight_grad,
        qkv_bias_grad,
        out_grad,
        up_weight_grad,
        up_bias_grad,
        down_grad,
        res_bias_grad,
        gain_grad,
        shift_grad,
    )


SWAP_ROW = [(0, 1), (1, 0)]
SWAP_X = [(0, 2), (2, 0), (1, 3), (3, 1)]
SWAP_CORE = [(0, 1), (1, 0), (2, 3), (3, 2)]


def bf16(values):
    return values.astype(jnp.bfloat16)


def f32(values):
    return values.astype(jnp.float32)


def matmul(left, right, dims=((1,), (0,))):
    return lax.dot_general(left, right, (dims, ((), ())), preferred_element_type=jnp.float32)


def swap_row(values):
    return lax.ppermute(values, "row", SWAP_ROW)


def swap_x(values):
    return lax.ppermute(values, "dp", SWAP_X)


def swap_core(values):
    return lax.ppermute(values, "dp", SWAP_CORE)


def pick(index, first, second):
    return jnp.where(index == 0, first, second)


def pair(index, mine, theirs, axis):
    return pick(
        index,
        jnp.concatenate([mine, theirs], axis=axis),
        jnp.concatenate([theirs, mine], axis=axis),
    )


def after(value, *earlier):
    return lax.optimization_barrier((value,) + earlier)[0]


def rotary_tables(positions):
    lane = jnp.arange(2 * HD, dtype=jnp.int32) % HD
    half_rot = ROT // 2
    frequency = jnp.exp(
        -math.log(rotary_base) * 2.0 * (lane % half_rot).astype(jnp.float32) / ROT
    )
    angle = positions[:, None] * frequency[None, :]
    turned = (lane < ROT)[None, :]
    sines = jnp.sin(angle)
    return (
        jnp.where(turned, jnp.cos(angle), 1.0),
        jnp.where((lane < half_rot)[None, :], -sines, 0.0),
        jnp.where(turned & (lane >= half_rot)[None, :], sines, 0.0),
    )


def turn(values, cosines, sines_low, sines_high):
    width = values.shape[1]
    half_rot = ROT // 2
    return (
        values * cosines
        + pltpu.roll(values, width - half_rot, 1) * sines_low
        + pltpu.roll(values, half_rot, 1) * sines_high
    )


def mixed_kernel(
    normed_ref, weight_ref, bias_ref, cos_ref, low_ref, high_ref, query_ref, keyval_ref
):
    cosines, low, high = cos_ref[...], low_ref[...], high_ref[...]
    rows, half = query_ref.shape
    first = lax.broadcasted_iota(jnp.int32, (rows, 2 * HD), 1) < HD
    scale = HD ** (-0.5)
    mixed = matmul(normed_ref[...], weight_ref[...]) + bias_ref[...]
    for at in range(half // (2 * HD)):
        tiles = [mixed[:, (3 * at + part) * 2 * HD : (3 * at + part + 1) * 2 * HD] for part in range(3)]
        query = jnp.where(first, tiles[0], tiles[1])
        key = jnp.where(first, pltpu.roll(tiles[0], HD, 1), pltpu.roll(tiles[2], HD, 1))
        value = jnp.where(first, tiles[1], tiles[2])
        here = slice(at * 2 * HD, (at + 1) * 2 * HD)
        query_ref[:, here] = bf16(f32(bf16(turn(query, cosines, low, high))) * scale)
        keyval_ref[:, here] = bf16(turn(key, cosines, low, high))
        keyval_ref[:, half + at * 2 * HD : half + (at + 1) * 2 * HD] = bf16(value)


def join_kernel(row_ref, dq_ref, dkv_ref, sent_ref, cos_ref, low_ref, high_ref, out_ref):
    cosines, low, high = cos_ref[...], -low_ref[...], -high_ref[...]
    rows = dq_ref.shape[0]
    half = dq_ref.shape[1]
    first = lax.broadcasted_iota(jnp.int32, (rows, 2 * HD), 1) < HD
    owner = row_ref[0] == 0
    for at in range(half // (2 * HD)):
        here = slice(at * 2 * HD, (at + 1) * 2 * HD)
        there = slice(half + at * 2 * HD, half + (at + 1) * 2 * HD)
        query = turn(dq_ref[:, here], cosines, low, high)
        key = dkv_ref[:, here] + jnp.where(owner, f32(sent_ref[:, here]), 0.0)
        value = dkv_ref[:, there] + jnp.where(owner, f32(sent_ref[:, there]), 0.0)
        key = pltpu.roll(turn(key, cosines, low, high), HD, 1)
        tiles = (jnp.where(first, query, key), jnp.where(first, value, query), jnp.where(first, key, value))
        for part in range(3):
            out_ref[:, (3 * at + part) * 2 * HD : (3 * at + part + 1) * 2 * HD] = bf16(tiles[part])


def tree_kernel(
    parent_ref, row_ref, query_ref, keyval_ref, trunk_ref, grad_ref,
    out_ref, dq_ref, dkv_ref, dtrunk_ref,
    keys, values, dkeys, dvalues,
):
    tree = pl.program_id(0)
    row = row_ref[0]
    rows, half = query_ref.shape
    trunk_len = trunk_ref.shape[0]
    segs = rows // SEG
    trunk_segs = trunk_len // SEG
    seg_count = parent_ref.shape[1]
    first_row = row == 0
    keys[...] = jnp.where(first_row, keyval_ref[:, :half], trunk_ref[:, :half])
    values[...] = jnp.where(first_row, keyval_ref[:, half:], trunk_ref[:, half:])
    dkeys[...] = jnp.zeros_like(dkeys)
    dvalues[...] = jnp.zeros_like(dvalues)
    lane = lax.broadcasted_iota(jnp.int32, (1, half), 1)
    causal = lax.broadcasted_iota(jnp.int32, (SEG, SEG), 0) >= lax.broadcasted_iota(
        jnp.int32, (SEG, SEG), 1
    )
    across = ((1,), (1,))
    down = ((0,), (0,))
    for seg in range(segs):
        here = slice(seg * SEG, (seg + 1) * SEG)
        above = parent_ref[tree, row * segs + seg]
        linked = [above == at for at in range(trunk_segs)]
        for _ in range(seg_count - 2):
            above = jnp.where(above >= 0, parent_ref[tree, jnp.maximum(above, 0)], -1)
            linked = [was | (above == at) for at, was in enumerate(linked)]
        bias = [jnp.where(is_linked, 0.0, masked_fill) for is_linked in linked]
        query, grad = query_ref[here, :], grad_ref[here, :]
        own_key, own_value = keyval_ref[here, :half], keyval_ref[here, half:]
        attended = jnp.zeros((SEG, half), jnp.float32)
        dquery = jnp.zeros((SEG, half), jnp.float32)
        dkey = jnp.zeros((SEG, half), jnp.float32)
        dvalue = jnp.zeros((SEG, half), jnp.float32)
        for head in range(half // HD):
            mine = (lane >= head * HD) & (lane < (head + 1) * HD)
            head_query = jnp.where(mine, query, jnp.zeros_like(query))
            head_grad = jnp.where(mine, grad, jnp.zeros_like(grad))
            scores = [
                matmul(head_query, keys[at * SEG : (at + 1) * SEG, :], across) + bias[at]
                for at in range(trunk_segs)
            ] + [jnp.where(causal, matmul(head_query, own_key, across), masked_fill)]
            top = functools.reduce(jnp.maximum, [jnp.max(s, axis=1, keepdims=True) for s in scores])
            powers = [jnp.exp(s - top) for s in scores]
            total = functools.reduce(jnp.add, [jnp.sum(p, axis=1, keepdims=True) for p in powers])
            probs = [p / total for p in powers]
            low = [bf16(p) for p in probs]
            blocks = [values[at * SEG : (at + 1) * SEG, :] for at in range(trunk_segs)] + [own_value]
            prob_grads = [matmul(head_grad, v, across) for v in blocks]
            delta = functools.reduce(
                jnp.add, [jnp.sum(p * g, axis=1, keepdims=True) for p, g in zip(probs, prob_grads)]
            )
            score_grads = [bf16(p * (g - delta)) for p, g in zip(probs, prob_grads)]
            head_out = functools.reduce(jnp.add, [matmul(p, v) for p, v in zip(low, blocks)])
            attended = jnp.where(mine, head_out, attended)
            key_blocks = [keys[at * SEG : (at + 1) * SEG, :] for at in range(trunk_segs)] + [own_key]
            head_dq = functools.reduce(jnp.add, [matmul(s, u) for s, u in zip(score_grads, key_blocks)])
            dquery = jnp.where(mine, head_dq, dquery)
            dkey = dkey + matmul(score_grads[-1], head_query, down)
            dvalue = dvalue + matmul(low[-1], head_grad, down)
            for at in range(trunk_segs):
                spot = slice(at * SEG, (at + 1) * SEG)
                dkeys[spot, :] += matmul(score_grads[at], head_query, down)
                dvalues[spot, :] += matmul(low[at], head_grad, down)
        out_ref[here, :] = bf16(attended)
        dq_ref[here, :] = dquery * HD ** (-0.5)
        dkv_ref[here, :half] = dkey
        dkv_ref[here, half:] = dvalue
    dtrunk_ref[:, :half] = bf16(dkeys[...])
    dtrunk_ref[:, half:] = bf16(dvalues[...])

    @pl.when(first_row)
    def _():
        dkv_ref[:, :half] += dkeys[...]
        dkv_ref[:, half:] += dvalues[...]


def store_blocks(place_ref, sides, full_ref, own_refs, plain_refs):
    row, slab = place_ref[1], place_ref[2]
    for side, values in enumerate(sides):
        width = values[0].shape[1]
        for source, value in enumerate(values):
            within = source % 2
            here = row == source // 2

            def put(refs):
                if len(refs) == 1:
                    refs[0][side, :, within * width : (within + 1) * width] = value
                else:
                    refs[within][side] = value

            @pl.when(here)
            def _():
                full_ref[side, :, within * width : (within + 1) * width] = value
                put(own_refs)

            @pl.when(jnp.logical_not(here))
            def _():
                put(plain_refs)
                at = (2 + jnp.where(slab == 0, within, 1 - within)) * width
                full_ref[side, :, pl.ds(pl.multiple_of(at, width), width)] = value


def gather_kernel(place_ref, mine_ref, theirs_ref, full_ref, own_ref, plain_ref):
    sides = [[ref[at] for at in range(ref.shape[0])] for ref in (mine_ref, theirs_ref)]
    store_blocks(place_ref, sides, full_ref, [own_ref], [plain_ref])


def norm_kernel(place_ref, gain_ref, bias_ref, mine_ref, theirs_ref, full_ref, *outs):
    normal_ref, scale_ref = outs[4:]
    sides = []
    for side, ref in enumerate((mine_ref, theirs_ref)):
        values = [f32(ref[at]) for at in range(ref.shape[0])]
        features = len(values) * values[0].shape[1]
        mean = functools.reduce(jnp.add, [jnp.sum(v, axis=1, keepdims=True) for v in values]) / features
        centred = [v - mean for v in values]
        square = functools.reduce(jnp.add, [jnp.sum(v * v, axis=1, keepdims=True) for v in centred])
        inv_scale = lax.rsqrt(square / features + norm_epsilon)
        normals = [v * inv_scale for v in centred]
        if side == 0:
            scale_ref[...] = inv_scale
            for source, normal in enumerate(normals):

                @pl.when(place_ref[0] == source)
                def _():
                    normal_ref[...] = normal

        sides.append(
            [
                bf16(normal * gain_ref[source : source + 1, :] + bias_ref[source : source + 1, :])
                for source, normal in enumerate(normals)
            ]
        )
    store_blocks(place_ref, sides, full_ref, outs[:2], outs[2:4])


def pair_rows(rows, width):
    return pl.BlockSpec((2, rows, width), lambda at, *_: (0, at, 0))


def gathered(place, mine, theirs, norm=None):
    blocks, count, width = mine.shape
    rows = SEG if norm is None else SEG // 2
    full = blocks * width
    in_specs = [pl.BlockSpec((blocks, rows, width), lambda at, *_: (0, at, 0))] * 2
    parts = [full // 2] * 2 if norm is None else [width] * 4
    out_specs = [pair_rows(rows, size) for size in [full] + parts]
    out_shape = [
        jax.ShapeDtypeStruct((2, count, size), jnp.bfloat16) for size in [full] + parts
    ]
    operands = [mine, theirs]
    if norm is not None:
        gain = [values.reshape(blocks, width) for values in norm]
        operands = gain + operands
        in_specs = [pl.BlockSpec((blocks, width), lambda at, *_: (0, 0))] * 2 + in_specs
        out_specs = out_specs + [row_block(rows, width), row_block(rows, 1)]
        out_shape = out_shape + [
            jax.ShapeDtypeStruct((count, width), jnp.float32),
            jax.ShapeDtypeStruct((count, 1), jnp.float32),
        ]
    results = pl.pallas_call(
        gather_kernel if norm is None else norm_kernel,
        grid_spec=pltpu.PrefetchScalarGridSpec(
            num_scalar_prefetch=1, grid=(count // rows,), in_specs=in_specs, out_specs=out_specs
        ),
        out_shape=out_shape,
        cost_estimate=pl.CostEstimate(flops=1, bytes_accessed=1, transcendentals=0),
        name="join_blocks" if norm is None else "norm_blocks",
    )(place, *operands)
    last = len(parts) + 1
    return [values.reshape(2 * count, -1) for values in results[:last]] + list(results[last:])


def stack_kernel(place_ref, terms_ref, arrived_ref, out_ref):
    row, slab = place_ref[1], place_ref[2]
    width = out_ref.shape[2]
    for spot in range(4):
        here = slice(spot * width, (spot + 1) * width)
        value = bf16(f32(terms_ref[:, here]) + f32(arrived_ref[:, here]))
        if spot < 2:
            out_ref[2 * row + spot] = value
        else:
            out_ref[2 * (1 - row) + jnp.where(slab == 0, spot - 2, 3 - spot)] = value


def stacked(place, terms, arrived, blocks):
    count, full = arrived.shape
    rows = SEG
    width = full // blocks
    return pl.pallas_call(
        stack_kernel,
        grid_spec=pltpu.PrefetchScalarGridSpec(
            num_scalar_prefetch=1,
            grid=(count // rows,),
            in_specs=[row_block(rows, full), row_block(rows, full)],
            out_specs=pl.BlockSpec((blocks, rows, width), lambda at, *_: (0, at, 0)),
        ),
        out_shape=jax.ShapeDtypeStruct((blocks, count, width), jnp.bfloat16),
        cost_estimate=pl.CostEstimate(flops=1, bytes_accessed=1, transcendentals=0),
        name="stack_blocks",
    )(place, terms, arrived)


def cast_rows_kernel(place_ref, master_ref, own_ref, send_ref):
    value = bf16(master_ref[...])
    own_ref[...] = value
    half = pl.num_programs(0) // 2

    @pl.when(pl.program_id(0) // half == place_ref[2])
    def _():
        send_ref[...] = value


def cast_cols_kernel(place_ref, master_ref, own_ref, send_ref):
    value = bf16(master_ref[...])
    own_ref[...] = value
    half = value.shape[1] // 2
    send_ref[...] = jnp.where(place_ref[2] == 0, value[:, :half], value[:, half:])


def cast_weight(place, master, axis):
    height, width = master.shape
    rows = min(2 * SEG, master.shape[0] // 4)
    if axis == 0:
        width = width // 2
        steps = height // rows
        half = steps // 2
        specs = [
            pl.BlockSpec((rows, width), lambda at, place_ref: (at, place_ref[3])),
            pl.BlockSpec((rows, width), lambda at, place_ref: (at, 0)),
            pl.BlockSpec(
                (rows, width), lambda at, place_ref: (jnp.clip(at - half * place_ref[2], 0, half - 1), 0)
            ),
        ]
        send = (height // 2, width)
        whole = (2 * height, width)
    else:
        height = height // 2
        steps = height // rows
        specs = [
            pl.BlockSpec((rows, width), lambda at, place_ref: (at + steps * place_ref[3], 0)),
            pl.BlockSpec((rows, width), lambda at, place_ref: (at, 0)),
            pl.BlockSpec((rows, width // 2), lambda at, place_ref: (at, 0)),
        ]
        send = (height, width // 2)
        whole = (height, 2 * width)
    return pl.pallas_call(
        cast_rows_kernel if axis == 0 else cast_cols_kernel,
        grid_spec=pltpu.PrefetchScalarGridSpec(
            num_scalar_prefetch=1, grid=(steps,), in_specs=specs[:1], out_specs=specs[1:]
        ),
        out_shape=[
            jax.ShapeDtypeStruct(whole, jnp.bfloat16),
            jax.ShapeDtypeStruct(send, jnp.bfloat16),
        ],
        cost_estimate=pl.CostEstimate(flops=1, bytes_accessed=1, transcendentals=0),
        name="cast_weight",
    )(place, master)


def settle_store(axis, place_ref, mine, theirs, out_ref):
    if axis == 0:
        out_ref[place_ref[3]] = mine
        out_ref[1 - place_ref[3]] = theirs
    else:
        width = mine.shape[1]
        first = place_ref[3] == 0
        out_ref[:, :width] = jnp.where(first, mine, theirs)
        out_ref[:, width:] = jnp.where(first, theirs, mine)


def settle_kernel(axis, place_ref, mine_ref, theirs_ref, *refs):
    settle_store(axis, place_ref, f32(mine_ref[...]), f32(theirs_ref[...]), refs[-1])


def settle_both_kernel(axis, place_ref, *refs):
    for at in range(2):

        @pl.when(pl.program_id(0) == at)
        def _():
            settle_store(axis, place_ref, f32(refs[2 * at][...]), f32(refs[2 * at + 1][...]), refs[-1])


def settle_both(place, first, last, shape, axis):
    rows, width = first[0].shape
    if axis == 0:
        shape = (2, shape[0] // 2, width)
        out_spec = pl.BlockSpec((2, rows, width), lambda at, *_: (0, at, 0))
    else:
        out_spec = pl.BlockSpec((rows, 2 * width), lambda at, *_: (at, 0))
    return pl.pallas_call(
        functools.partial(settle_both_kernel, axis),
        grid_spec=pltpu.PrefetchScalarGridSpec(
            num_scalar_prefetch=1,
            grid=(2,),
            in_specs=[pl.BlockSpec((rows, width), lambda *_: (0, 0))] * 4,
            out_specs=out_spec,
        ),
        out_shape=jax.ShapeDtypeStruct(shape, jnp.float32),
        cost_estimate=pl.CostEstimate(flops=1, bytes_accessed=1, transcendentals=0),
        name="settle_both",
    )(place, *first, *last)


def settle(place, mine, theirs, shape, axis, offset, dest=None):
    rows, width = mine.shape
    at = offset // rows
    whole = pl.BlockSpec((rows, width), lambda *_: (0, 0))
    if axis == 0:
        shape = (2, shape[0] // 2, width)
        out_spec = pl.BlockSpec((2, rows, width), lambda *_: (0, at, 0))
    else:
        out_spec = pl.BlockSpec((rows, 2 * width), lambda *_: (at, 0))
    in_specs = [whole, whole]
    operands = [place, mine, theirs]
    aliases = {}
    if dest is not None:
        in_specs.append(pl.BlockSpec(memory_space=pl.ANY))
        operands.append(dest)
        aliases = {3: 0}
    return pl.pallas_call(
        functools.partial(settle_kernel, axis),
        grid_spec=pltpu.PrefetchScalarGridSpec(
            num_scalar_prefetch=1, grid=(1,), in_specs=in_specs, out_specs=out_spec
        ),
        out_shape=jax.ShapeDtypeStruct(shape, jnp.float32),
        input_output_aliases=aliases,
        cost_estimate=pl.CostEstimate(flops=1, bytes_accessed=1, transcendentals=0),
        name="settle",
    )(*operands)


def row_block(rows, width):
    return pl.BlockSpec((rows, width), lambda at, *_: (at, 0))


def mixed_heads(normed, weight, bias, tables):
    count, depth = normed.shape
    width = weight.shape[1]
    rows = SEG
    return pl.pallas_call(
        mixed_kernel,
        grid=(count // rows,),
        in_specs=[
            row_block(rows, depth),
            pl.BlockSpec((depth, width), lambda at: (0, 0)),
            pl.BlockSpec((1, width), lambda at: (0, 0)),
        ]
        + [row_block(rows, 2 * HD)] * 3,
        out_specs=[row_block(rows, width // 3), row_block(rows, 2 * width // 3)],
        out_shape=[
            jax.ShapeDtypeStruct((count, width // 3), jnp.bfloat16),
            jax.ShapeDtypeStruct((count, 2 * width // 3), jnp.bfloat16),
        ],
        cost_estimate=pl.CostEstimate(flops=1, bytes_accessed=1, transcendentals=0),
        name="mixed_heads",
    )(normed, weight, bias.reshape(1, width), *tables)


def join_heads(row, dq, dkv, sent, tables):
    count, half = dq.shape
    rows = 2 * SEG
    return pl.pallas_call(
        join_kernel,
        grid_spec=pltpu.PrefetchScalarGridSpec(
            num_scalar_prefetch=1,
            grid=(count // rows,),
            in_specs=[row_block(rows, half), row_block(rows, 2 * half), row_block(rows, 2 * half)]
            + [row_block(rows, 2 * HD)] * 3,
            out_specs=row_block(rows, 3 * half),
        ),
        out_shape=jax.ShapeDtypeStruct((count, 3 * half), jnp.bfloat16),
        cost_estimate=pl.CostEstimate(flops=1, bytes_accessed=1, transcendentals=0),
        name="join_heads",
    )(row, dq, dkv, sent, *tables)


def tree_attention(parents, row, query, keyval, trunk, grad):
    trees = parents.shape[0]
    count, half = query.shape
    rows = count // trees
    keys = trunk.shape[0] // trees
    pairs = count * (keys + SEG) * (half // HD)
    return pl.pallas_call(
        tree_kernel,
        grid_spec=pltpu.PrefetchScalarGridSpec(
            num_scalar_prefetch=2,
            grid=(trees,),
            in_specs=[
                row_block(rows, half),
                row_block(rows, 2 * half),
                row_block(keys, 2 * half),
                row_block(rows, half),
            ],
            out_specs=[
                row_block(rows, half),
                row_block(rows, half),
                row_block(rows, 2 * half),
                row_block(keys, 2 * half),
            ],
            scratch_shapes=[pltpu.VMEM((keys, half), jnp.bfloat16)] * 2
            + [pltpu.VMEM((keys, half), jnp.float32)] * 2,
        ),
        out_shape=[
            jax.ShapeDtypeStruct((count, half), jnp.bfloat16),
            jax.ShapeDtypeStruct((count, half), jnp.float32),
            jax.ShapeDtypeStruct((count, 2 * half), jnp.float32),
            jax.ShapeDtypeStruct((trees * keys, 2 * half), jnp.bfloat16),
        ],
        cost_estimate=pl.CostEstimate(flops=1, bytes_accessed=1, transcendentals=0),
        name="tree_attention",
    )(parents, row, query, keyval, trunk, grad)


def paired_device(
    tokens,
    parent,
    depth,
    w_qkv,
    b_qkv,
    w_out,
    w_up,
    b_up,
    w_down,
    b_res,
    ln_gain,
    ln_bias,
    cotangent,
):
    count, width = tokens.shape
    row = lax.axis_index("row")
    col = lax.axis_index("col")
    core = lax.axis_index("dp") % 2
    slab = lax.axis_index("dp") // 2
    cols = lax.axis_size("col")
    half = 2 * width
    heads_width = w_out.shape[0] // 2
    hidden = w_up.shape[1] // 2
    place = jnp.stack([col, row, slab, core]).astype(jnp.int32)
    row_table = jnp.reshape(row, (1,)).astype(jnp.int32)
    down_dims = ((0,), (0,))
    across = ((1,), (1,))

    def part(values, at, size, axis):
        return lax.dynamic_slice_in_dim(values, at * size, size, axis)

    def exchange(stack):
        return lax.all_to_all(stack, "col", 0, 0, tiled=True)

    done = ()

    def step(run, *inputs):
        nonlocal done
        inputs, _ = lax.optimization_barrier((inputs, done))
        result = run(*inputs)
        done = result
        return result

    def wait(value):
        return step(lambda arrived: arrived, value)

    tokens_near = lax.all_gather(tokens, "col", axis=0)
    grad_stack = jnp.broadcast_to(cotangent[None], (cols,) + cotangent.shape)

    def ready(master, axis):
        whole, send = step(lambda weight: cast_weight(place, weight, axis), master)
        return whole, swap_row(send)

    def fill(whole, part_in, axis, last):
        at = whole.shape[axis] // 2 + (part_in.shape[axis] if last else 0)
        return step(lambda a, b: lax.dynamic_update_slice_in_dim(a, b, at, axis), whole, part_in)

    tables = jnp.concatenate([parent, depth], axis=0)
    tables = jnp.stack([tables, swap_core(tables)])
    parents = tables[:, 0]
    segs = count // SEG
    token = jnp.arange(count, dtype=jnp.int32)
    levels = jnp.zeros((2, count), jnp.float32)
    for seg in range(segs):
        level = lax.dynamic_slice_in_dim(tables[:, 1], row * segs + seg, 1, 1).astype(jnp.float32)
        levels = jnp.where((token // SEG == seg)[None, :], level, levels)
    positions = (levels * SEG + (token % SEG).astype(jnp.float32)[None, :]).reshape(2 * count)
    rotary = rotary_tables(positions)

    qkv_whole, qkv_row = ready(w_qkv, 0)
    up_whole, up_row = ready(w_up, 0)
    qkv_row = wait(qkv_row)
    qkv_x = swap_x(qkv_row)
    out_whole, out_row = ready(w_out, 1)
    down_whole, down_row = ready(w_down, 1)
    rotary = step(lambda *tables: tables, *rotary)
    qkv_whole = fill(qkv_whole, qkv_row, 0, False)
    up_row = wait(up_row)
    up_x = swap_x(up_row)
    qkv_x = wait(qkv_x)
    tokens_near = wait(tokens_near)
    tokens_far = swap_core(tokens_near)
    grad_near = exchange(after(grad_stack, tokens_near))
    up_whole = fill(up_whole, up_row, 0, False)
    normed, own_a, own_b, plain_a, plain_b, normal, inv_scale = step(
        lambda mine, theirs: gathered(place, mine, theirs, (ln_gain, ln_bias)), tokens_near, tokens_far
    )
    qkv_full = fill(qkv_whole, qkv_x, 0, True)
    query, keyval = step(
        lambda left, right: mixed_heads(left, right, part(b_qkv, core, 3 * heads_width, 0), rotary),
        normed, qkv_full,
    )
    trunk = lax.ppermute(keyval, "row", [(0, 1)])
    root = math.sqrt(2.0 / math.pi)

    def feed(left, right):
        hidden_up = matmul(left, right) + part(b_up, core, hidden, 0)
        squared = hidden_up * hidden_up
        bend = jnp.tanh(root * (hidden_up + 0.044715 * squared * hidden_up))
        return bf16(0.5 * hidden_up * (1.0 + bend)), bf16(
            0.5 * (1.0 + bend)
            + 0.5 * hidden_up * (1.0 - bend * bend) * root * (1.0 + 3.0 * 0.044715 * squared)
        )

    out_row = wait(out_row)
    out_x = swap_x(out_row)
    up_full = fill(up_whole, up_x, 0, True)
    down_row = wait(down_row)
    down_x = swap_x(down_row)
    activated, slope = step(feed, normed, up_full)
    out_whole = fill(out_whole, out_row, 1, False)
    down_whole = fill(down_whole, down_row, 1, False)
    out_full = fill(out_whole, out_x, 1, True)
    trunk = wait(trunk)
    grad_near = wait(grad_near)
    grad_far = swap_core(grad_near)
    grad, grad_own, grad_plain = step(lambda mine, theirs: gathered(place, mine, theirs), grad_near, grad_far)

    def cut(values, at):
        size = values.shape[1] // 2
        return values[:, at * size : (at + 1) * size]

    def leaving(left, right):
        return step(lambda a, b: bf16(matmul(a, b, down_dims)), left, right)

    def staying(left, right, sent):
        return step(lambda a, b, c: bf16(matmul(a, b, down_dims) + f32(c)), left, right, sent)

    def crossed(both, arrived):
        mine = step(lambda a, b: bf16(f32(a) + f32(b)), both, arrived)
        return mine, swap_core(mine)

    def settled(pieces, shape, axis, offset, dest):
        operands = pieces if dest is None else pieces + (dest,)
        return step(
            lambda mine, theirs, *rest: settle(place, mine, theirs, shape, axis, offset, *rest), *operands
        )

    down_sent_a = swap_row(leaving(cut(activated, 0), grad_plain))
    down_sent_b = swap_row(leaving(cut(activated, 1), grad_plain))
    out_heads = step(lambda a, b: bf16(matmul(a, b, across)), grad, out_full)
    attended, query_grad, own_grad, trunk_grad = step(
        lambda *operands: tree_attention(parents, row_table, *operands), query, keyval, trunk, out_heads
    )
    trunk_sent = lax.ppermute(trunk_grad, "row", [(1, 0)])
    down_both_a = staying(cut(activated, 0), grad_own, down_sent_a)
    down_cross_a = swap_x(down_both_a)
    down_full = fill(down_whole, down_x, 1, True)
    branch_terms = step(
        lambda a, b, c, d: bf16(matmul(a, b) + matmul(c, d)), attended, out_full, activated, down_full
    )
    branch_near = swap_core(branch_terms[count:])
    up_grad = step(lambda a, b, c: bf16(matmul(a, b, across) * f32(c)), grad, down_full, slope)
    up_sent_a = swap_row(leaving(plain_a, up_grad))
    down_both_b = staying(cut(activated, 1), grad_own, down_sent_b)
    down_cross_b = swap_x(down_both_b)
    up_sent_b = swap_row(leaving(plain_b, up_grad))
    down_a = crossed(down_both_a, down_cross_a)
    branch = lax.psum_scatter(
        step(lambda a, b: stacked(place, a, b, cols), branch_terms, branch_near), "col", tiled=False
    )
    mixed_grad = step(
        lambda *operands: join_heads(row_table, *operands, rotary), query_grad, own_grad, trunk_sent
    )
    qkv_sent_a = swap_row(leaving(plain_a, mixed_grad))
    down_b = crossed(down_both_b, down_cross_b)
    qkv_sent_b = swap_row(leaving(plain_b, mixed_grad))
    norm_terms = step(
        lambda a, b, c, d: bf16(matmul(a, b, across) + matmul(c, d, across)),
        mixed_grad, qkv_full, up_grad, up_full,
    )
    up_both_a = staying(own_a, up_grad, up_sent_a)
    up_cross_a = swap_x(up_both_a)
    norm_near = swap_core(step(lambda terms: terms[count:], norm_terms))
    output = step(lambda parts, block: bf16(f32(block) + f32(parts) + b_res), branch, tokens)
    norm_parts = exchange(step(lambda a, b: stacked(place, a, b, cols), norm_terms, norm_near))
    down_grad = step(lambda first, last: settle_both(place, first, last, w_down.shape, 0), down_a, down_b)
    up_a = crossed(up_both_a, up_cross_a)
    up_both_b = staying(own_b, up_grad, up_sent_b)
    up_cross_b = swap_x(up_both_b)
    qkv_both_a = staying(own_a, mixed_grad, qkv_sent_a)
    qkv_cross_a = swap_x(qkv_both_a)
    out_sent = swap_row(leaving(attended, grad_plain))
    up_b = crossed(up_both_b, up_cross_b)
    qkv_both_b = staying(own_b, mixed_grad, qkv_sent_b)
    qkv_cross_b = swap_x(qkv_both_b)
    gain_here = part(ln_gain, col, width, 0)

    def norm_sums(parts):
        total = jnp.sum(f32(parts), axis=0)
        scaled = total * gain_here
        return (
            total,
            jnp.stack([jnp.sum(scaled, axis=1), jnp.sum(scaled * normal, axis=1)]),
            jnp.sum(total * normal, axis=0),
            jnp.sum(total, axis=0),
        )

    norm_grad, sums, gain_sum, shift_sum = step(norm_sums, norm_parts)
    up_weight_grad = step(lambda first, last: settle_both(place, first, last, w_up.shape, 1), up_a, up_b)

    def line_step(values, bit):
        return lax.ppermute(values, "col", [(at, at ^ bit) for at in range(cols)])

    small = jnp.concatenate(
        [
            jnp.sum(f32(up_grad), axis=0),
            jnp.sum(f32(mixed_grad), axis=0),
            jnp.sum(f32(cotangent), axis=0),
            gain_sum,
            shift_sum,
        ]
    ).reshape(-1, 128)
    shared_at = (hidden + 3 * heads_width) // 128
    res_at = width // 128
    sums_next = line_step(sums, 1)
    small_other = swap_core(small)
    qkv_a = crossed(qkv_both_a, qkv_cross_a)
    sums, shared = step(
        lambda sums, arrived, small, other: (sums + arrived, (small + other)[shared_at:]),
        sums, sums_next, small, small_other,
    )
    sums_next = line_step(sums, 2)
    ends = shared[res_at:][None]
    ends_next = line_step(ends, 1)
    out_both = staying(attended, grad_own, out_sent)
    out_cross = swap_x(out_both)
    ends = step(lambda ends, arrived: pair(col % 2, ends, arrived, 0), ends, ends_next)
    ends_next = line_step(ends, 2)
    qkv_weight_grad = settled(qkv_a, w_qkv.shape, 1, 0, None)
    sums = (sums + sums_next) / (cols * width)
    tokens_grad = step(
        lambda sums, total: inv_scale
        * (total * gain_here - sums[0][:, None] - normal * sums[1][:, None])
        + f32(cotangent),
        sums, norm_grad,
    )

    def gather_small(small, other, shared, ends, arrived):
        return jnp.concatenate(
            [
                pair(core, small[: hidden // 128], other[: hidden // 128], 0),
                pair(core, small[hidden // 128 : shared_at], other[hidden // 128 : shared_at], 0),
                shared[:res_at],
                pair(col // 2, ends, arrived, 0).reshape(-1, 128),
            ]
        )

    small = step(gather_small, small, small_other, shared, ends, ends_next)
    small_next = swap_row(small)
    qkv_b = crossed(qkv_both_b, qkv_cross_b)
    small = step(jnp.add, small, small_next)
    small_next = swap_x(small)
    out_mine = crossed(out_both, out_cross)
    qkv_weight_grad = settled(qkv_b, w_qkv.shape, 1, qkv_both_a.shape[0], qkv_weight_grad)
    out_grad = settled(out_mine, w_out.shape, 0, 0, None)
    small = step(jnp.add, small, small_next)

    bounds = [0, 2 * hidden // 128, (2 * hidden + 6 * heads_width) // 128]
    bounds.append(bounds[-1] + res_at)
    up_bias_grad = small[: bounds[1]].reshape(-1)
    qkv_bias_grad = small[bounds[1] : bounds[2]].reshape(-1)
    res_bias_grad = small[bounds[2] : bounds[3]].reshape(-1)
    ends = small[bounds[3] :].reshape(cols, 2, width)
    gain_grad = ends[:, 0].reshape(-1)
    shift_grad = ends[:, 1].reshape(-1)
    return (
        output,
        tokens_grad,
        qkv_weight_grad,
        qkv_bias_grad,
        out_grad.reshape(w_out.shape),
        up_weight_grad,
        up_bias_grad,
        down_grad.reshape(w_down.shape),
        res_bias_grad,
        gain_grad,
        shift_grad,
    )


def solution(mesh):
    sizes = (mesh.shape["dp"], mesh.shape["row"], mesh.shape["col"])
    per_device = paired_device if sizes == (4, 2, 4) else general_device
    return jax.shard_map(
        per_device,
        mesh=mesh,
        in_specs=(
            P(("dp", "row"), "col"),
            P("dp", None),
            P("dp", None),
            P("row", "col"),
            P("col"),
            P("col", "row"),
            P("row", "col"),
            P("col"),
            P("col", "row"),
            P("col"),
            P(),
            P(),
            P(("dp", "row"), "col"),
        ),
        out_specs=(
            P(("dp", "row"), "col"),
            P(("dp", "row"), "col"),
            P("row", "col"),
            P("col"),
            P("col", "row"),
            P("row", "col"),
            P("col"),
            P("col", "row"),
            P("col"),
            P(),
            P(),
        ),
        check_vma=False,
    )
```

```python
import functools
import math

import jax
import jax.numpy as jnp
from jax import lax
from jax.experimental import pallas as pl
from jax.experimental.pallas import tpu as pltpu
from jax.sharding import PartitionSpec as P

HD = 64
ROT = 32
SEG = 256


norm_epsilon = 1e-05
masked_fill = -1e30
rotary_base = 10000.0


def precise_dot(left, right):
    return jnp.dot(left, right, precision=lax.Precision.HIGHEST, preferred_element_type=jnp.float32)


def ancestry(parent_row):
    seg_count = parent_row.shape[0]
    labels = jnp.arange(seg_count, dtype=jnp.int32)
    identity = jnp.eye(seg_count, dtype=jnp.float32)
    parent_hot = (parent_row[:, None] == labels[None, :]).astype(jnp.float32)

    def extend(rounds, reachable):
        return jnp.minimum(identity + precise_dot(parent_hot, reachable), 1.0)

    return lax.fori_loop(0, seg_count, extend, identity)


def rotate(values, cosines, sines):
    half_rot = ROT // 2
    former = values[..., :half_rot]
    latter = values[..., half_rot:ROT]
    return jnp.concatenate(
        [former * cosines - latter * sines, latter * cosines + former * sines, values[..., ROT:]],
        axis=-1,
    )


def angles_of(positions):
    frequency = jnp.exp(
        -math.log(rotary_base) * 2.0 * jnp.arange(ROT // 2, dtype=jnp.float32) / ROT
    )
    phase_angle = positions[:, None] * frequency[None, :]
    return (jnp.cos(phase_angle)[:, None, :], jnp.sin(phase_angle)[:, None, :])


def reorder_rows(gradient, row_count, dp_count):
    leading = gradient.shape[0]
    blocked = gradient.reshape(
        row_count, dp_count, leading // (row_count * dp_count), gradient.shape[1]
    )
    return jnp.transpose(blocked, (1, 0, 2, 3)).reshape(leading, gradient.shape[1])


def reorder_cols(gradient, row_count, dp_count):
    trailing = gradient.shape[1]
    blocked = gradient.reshape(
        gradient.shape[0], row_count, dp_count, trailing // (row_count * dp_count)
    )
    return jnp.transpose(blocked, (0, 2, 1, 3)).reshape(gradient.shape[0], trailing)


def general_device(
    tokens,
    parent,
    depth,
    w_qkv,
    b_qkv,
    w_out,
    w_up,
    b_up,
    w_down,
    b_res,
    ln_gain,
    ln_bias,
    cotangent,
):
    tok_rows = tokens.shape[0]
    col_width = tokens.shape[1]
    row_count = lax.axis_size("row")
    dp_count = lax.axis_size("dp")
    row_start = lax.axis_index("row") * tok_rows
    local_heads = w_out.shape[0] // HD
    seg_count = parent.shape[1]
    labels = jnp.arange(seg_count, dtype=jnp.int32)
    reachable = ancestry(parent[0])
    query_index = row_start + jnp.arange(tok_rows, dtype=jnp.int32)
    query_seg = query_index // SEG
    query_hot = (query_seg[:, None] == labels[None, :]).astype(jnp.float32)
    query_reach = precise_dot(query_hot, reachable)
    levels = precise_dot(query_hot, depth[0].astype(jnp.float32)[:, None])[:, 0]
    positions = levels * SEG + (query_index % SEG).astype(jnp.float32)
    cosines, sines = angles_of(positions)
    score_scale = HD ** (-0.5)

    def permit(key_len):
        key_index = jnp.arange(key_len, dtype=jnp.int32)
        key_seg = key_index // SEG
        key_hot = (key_seg[:, None] == labels[None, :]).astype(jnp.float32)
        linked = precise_dot(query_reach, key_hot.T) > 0.5
        return linked & (
            (query_seg[:, None] != key_seg[None, :]) | (query_index[:, None] >= key_index[None, :])
        )

    whole = lax.all_gather(tokens, "col", axis=1, tiled=True).astype(jnp.float32)
    centred = whole - jnp.mean(whole, axis=1, keepdims=True)
    inv_scale = lax.rsqrt(jnp.mean(centred * centred, axis=1, keepdims=True) + norm_epsilon)
    normal = centred * inv_scale
    normed = (normal * ln_gain + ln_bias).astype(jnp.bfloat16)
    qkv_full, up_full, out_full, down_full = (
        lax.all_gather(w_qkv.astype(jnp.bfloat16), "row", axis=0, tiled=True),
        lax.all_gather(w_up.astype(jnp.bfloat16), "row", axis=0, tiled=True),
        lax.all_gather(w_out.astype(jnp.bfloat16), "row", axis=1, tiled=True),
        lax.all_gather(w_down.astype(jnp.bfloat16), "row", axis=1, tiled=True),
    )
    mixed = (jnp.dot(normed, qkv_full, preferred_element_type=jnp.float32) + b_qkv).reshape(
        tok_rows, local_heads, 3, HD
    )

    def rotate_pair(query_pre, key_pre):
        return (rotate(query_pre, cosines, sines), rotate(key_pre, cosines, sines))

    rotated, rotate_back = jax.vjp(rotate_pair, mixed[:, :, 0], mixed[:, :, 1])
    queries = rotated[0].astype(jnp.bfloat16)
    key_rows = rotated[1].astype(jnp.bfloat16)
    value_rows = mixed[:, :, 2].astype(jnp.bfloat16)
    key_flat = key_rows.reshape(tok_rows, local_heads * HD)
    value_flat = value_rows.reshape(tok_rows, local_heads * HD)

    def scores_for(key_part):
        raw_scores = (
            jnp.einsum("qhe,khe->hqk", queries, key_part, preferred_element_type=jnp.float32)
            * score_scale
        )
        allowed = permit(key_part.shape[0])
        return (jnp.where(allowed[None], raw_scores, masked_fill), allowed)

    pieces = (
        lax.all_gather(key_flat, "row", axis=0, tiled=True),
        lax.all_gather(value_flat, "row", axis=0, tiled=True),
    )
    running_top = jnp.full((local_heads, tok_rows), masked_fill, jnp.float32)
    key_len = pieces[0].shape[0]
    key_part = pieces[0].reshape(key_len, local_heads, HD)
    value_part = pieces[1].reshape(key_len, local_heads, HD)
    scores, allowed = scores_for(key_part)
    new_top = jnp.maximum(running_top, jnp.max(scores, axis=2))
    exponent = jnp.where(allowed[None], jnp.exp(scores - new_top[:, :, None]), 0.0)
    running_sum = jnp.sum(exponent, axis=2)
    weighted = jnp.einsum(
        "hqk,khe->hqe",
        exponent.astype(jnp.bfloat16),
        value_part,
        preferred_element_type=jnp.float32,
    )
    running_top, running_sum, weighted = (new_top, running_sum, weighted)
    log_total = running_top + jnp.log(running_sum)
    attn_exact = weighted / running_sum[:, :, None]
    attended = (
        jnp.transpose(attn_exact, (1, 0, 2))
        .reshape(tok_rows, local_heads * HD)
        .astype(jnp.bfloat16)
    )
    hidden_up = jnp.dot(normed, up_full, preferred_element_type=jnp.float32) + b_up
    activated, gelu_back = jax.vjp(functools.partial(jax.nn.gelu, approximate=True), hidden_up)
    activated = activated.astype(jnp.bfloat16)
    branch_terms = jnp.dot(attended, out_full, preferred_element_type=jnp.float32) + jnp.dot(
        activated, down_full, preferred_element_type=jnp.float32
    )
    branch = lax.psum_scatter(
        branch_terms.astype(jnp.bfloat16), "col", scatter_dimension=1, tiled=True
    ).astype(jnp.float32)
    output = (tokens.astype(jnp.float32) + branch + b_res).astype(jnp.bfloat16)
    grad_full = lax.all_gather(cotangent, "col", axis=1, tiled=True)
    res_bias_grad = jnp.sum(cotangent.astype(jnp.float32), axis=0)
    down_grad = jnp.einsum("tf,td->fd", activated, grad_full, preferred_element_type=jnp.float32)
    out_grad = jnp.einsum("te,td->ed", attended, grad_full, preferred_element_type=jnp.float32)
    act_grad = jnp.einsum("td,fd->tf", grad_full, down_full, preferred_element_type=jnp.float32)
    up_grad = gelu_back(act_grad)[0].astype(jnp.bfloat16)
    attn_grad = jnp.einsum(
        "td,ed->te", grad_full, out_full, preferred_element_type=jnp.float32
    ).astype(jnp.bfloat16)
    up_bias_grad = jnp.sum(up_grad.astype(jnp.float32), axis=0)
    up_weight_grad = jnp.einsum("td,tf->df", normed, up_grad, preferred_element_type=jnp.float32)
    out_heads = attn_grad.reshape(tok_rows, local_heads, HD)
    delta_sum = jnp.einsum("qhe,hqe->hq", out_heads.astype(jnp.float32), attn_exact)
    pieces = (
        lax.all_gather(key_flat, "row", axis=0, tiled=True),
        lax.all_gather(value_flat, "row", axis=0, tiled=True),
    )
    key_len = pieces[0].shape[0]
    key_part = pieces[0].reshape(key_len, local_heads, HD)
    value_part = pieces[1].reshape(key_len, local_heads, HD)
    scores, allowed = scores_for(key_part)
    softmaxed = jnp.where(allowed[None], jnp.exp(scores - log_total[:, :, None]), 0.0)
    prob_grad = jnp.einsum(
        "qhe,khe->hqk", out_heads, value_part, preferred_element_type=jnp.float32
    )
    score_grad = (softmaxed * (prob_grad - delta_sum[:, :, None])).astype(jnp.bfloat16)
    query_grad = (
        jnp.einsum("hqk,khe->qhe", score_grad, key_part, preferred_element_type=jnp.float32)
        * score_scale
    )
    key_grad = (
        jnp.einsum("hqk,qhe->khe", score_grad, queries, preferred_element_type=jnp.float32)
        * score_scale
    )
    value_grad = jnp.einsum(
        "hqk,qhe->khe",
        softmaxed.astype(jnp.bfloat16),
        out_heads,
        preferred_element_type=jnp.float32,
    )
    stacked = jnp.stack([key_grad, value_grad], axis=1).reshape(key_len, 2 * local_heads * HD)
    pair_grad = stacked
    query_grad, pair_grad = (query_grad, pair_grad)
    own_pairs = (
        lax.psum_scatter(pair_grad.astype(jnp.bfloat16), "row", scatter_dimension=0, tiled=True)
        .astype(jnp.float32)
        .reshape(tok_rows, 2, local_heads, HD)
    )
    query_pre, key_pre = rotate_back((query_grad, own_pairs[:, 0]))
    mixed_grad = (
        jnp.stack([query_pre, key_pre, own_pairs[:, 1]], axis=2)
        .reshape(tok_rows, 3 * local_heads * HD)
        .astype(jnp.bfloat16)
    )
    qkv_bias_grad = jnp.sum(mixed_grad.astype(jnp.float32), axis=0)
    qkv_weight_grad = jnp.einsum(
        "td,tc->dc", normed, mixed_grad, preferred_element_type=jnp.float32
    )
    norm_part = jnp.einsum(
        "tc,dc->td", mixed_grad, qkv_full, preferred_element_type=jnp.float32
    ) + jnp.einsum("tf,df->td", up_grad, up_full, preferred_element_type=jnp.float32)
    norm_grad = lax.psum(norm_part.astype(jnp.bfloat16), "col").astype(jnp.float32)
    gain_grad = jnp.sum(norm_grad * normal, axis=0)
    shift_grad = jnp.sum(norm_grad, axis=0)
    scaled = norm_grad * ln_gain
    mean_scaled = jnp.mean(scaled, axis=1, keepdims=True)
    mean_mixed = jnp.mean(scaled * normal, axis=1, keepdims=True)
    col_start = lax.axis_index("col") * col_width
    scaled_share = lax.dynamic_slice_in_dim(scaled, col_start, col_width, 1)
    normal_share = lax.dynamic_slice_in_dim(normal, col_start, col_width, 1)
    tokens_grad = inv_scale * (
        scaled_share - mean_scaled - normal_share * mean_mixed
    ) + cotangent.astype(jnp.float32)
    qkv_bias_grad, up_bias_grad, res_bias_grad, gain_grad, shift_grad = (
        lax.psum(qkv_bias_grad.astype(jnp.bfloat16), ("dp", "row")).astype(jnp.float32),
        lax.psum(up_bias_grad.astype(jnp.bfloat16), ("dp", "row")).astype(jnp.float32),
        lax.psum(res_bias_grad.astype(jnp.bfloat16), ("dp", "row")).astype(jnp.float32),
        lax.psum(gain_grad.astype(jnp.bfloat16), ("dp", "row")).astype(jnp.float32),
        lax.psum(shift_grad.astype(jnp.bfloat16), ("dp", "row")).astype(jnp.float32),
    )
    pieces_now = (
        lax.psum_scatter(
            reorder_rows(qkv_weight_grad, row_count, dp_count).astype(jnp.bfloat16),
            ("dp", "row"),
            scatter_dimension=0,
            tiled=True,
        ).astype(jnp.float32),
        lax.psum_scatter(
            reorder_rows(up_weight_grad, row_count, dp_count).astype(jnp.bfloat16),
            ("dp", "row"),
            scatter_dimension=0,
            tiled=True,
        ).astype(jnp.float32),
        lax.psum_scatter(
            reorder_cols(out_grad, row_count, dp_count).astype(jnp.bfloat16),
            ("dp", "row"),
            scatter_dimension=1,
            tiled=True,
        ).astype(jnp.float32),
        lax.psum_scatter(
            reorder_cols(down_grad, row_count, dp_count).astype(jnp.bfloat16),
            ("dp", "row"),
            scatter_dimension=1,
            tiled=True,
        ).astype(jnp.float32),
    )
    qkv_weight_grad, up_weight_grad, out_grad, down_grad = (
        lax.all_gather(pieces_now[0].astype(jnp.bfloat16), "dp", axis=0, tiled=True).astype(
            jnp.float32
        ),
        lax.all_gather(pieces_now[1].astype(jnp.bfloat16), "dp", axis=0, tiled=True).astype(
            jnp.float32
        ),
        lax.all_gather(pieces_now[2].astype(jnp.bfloat16), "dp", axis=1, tiled=True).astype(
            jnp.float32
        ),
        lax.all_gather(pieces_now[3].astype(jnp.bfloat16), "dp", axis=1, tiled=True).astype(
            jnp.float32
        ),
    )
    return (
        output,
        tokens_grad,
        qkv_weight_grad,
        qkv_bias_grad,
        out_grad,
        up_weight_grad,
        up_bias_grad,
        down_grad,
        res_bias_grad,
        gain_grad,
        shift_grad,
    )


SWAP_ROW = [(0, 1), (1, 0)]
SWAP_X = [(0, 2), (2, 0), (1, 3), (3, 1)]
SWAP_CORE = [(0, 1), (1, 0), (2, 3), (3, 2)]


def bf16(values):
    return values.astype(jnp.bfloat16)


def f32(values):
    return values.astype(jnp.float32)


def matmul(left, right, dims=((1,), (0,))):
    return lax.dot_general(left, right, (dims, ((), ())), preferred_element_type=jnp.float32)


def swap_row(values):
    return lax.ppermute(values, "row", SWAP_ROW)


def swap_x(values):
    return lax.ppermute(values, "dp", SWAP_X)


def swap_core(values):
    return lax.ppermute(values, "dp", SWAP_CORE)


def pick(index, first, second):
    return jnp.where(index == 0, first, second)


def pair(index, mine, theirs, axis):
    return pick(
        index,
        jnp.concatenate([mine, theirs], axis=axis),
        jnp.concatenate([theirs, mine], axis=axis),
    )


def after(value, *earlier):
    return lax.optimization_barrier((value,) + earlier)[0]


def rotary_tables(positions):
    lane = jnp.arange(2 * HD, dtype=jnp.int32) % HD
    half_rot = ROT // 2
    frequency = jnp.exp(
        -math.log(rotary_base) * 2.0 * (lane % half_rot).astype(jnp.float32) / ROT
    )
    angle = positions[:, None] * frequency[None, :]
    turned = (lane < ROT)[None, :]
    sines = jnp.sin(angle)
    return (
        jnp.where(turned, jnp.cos(angle), 1.0),
        jnp.where((lane < half_rot)[None, :], -sines, 0.0),
        jnp.where(turned & (lane >= half_rot)[None, :], sines, 0.0),
    )


def turn(values, cosines, sines_low, sines_high):
    width = values.shape[1]
    half_rot = ROT // 2
    return (
        values * cosines
        + pltpu.roll(values, width - half_rot, 1) * sines_low
        + pltpu.roll(values, half_rot, 1) * sines_high
    )


def mixed_kernel(
    normed_ref, weight_ref, bias_ref, cos_ref, low_ref, high_ref, query_ref, keyval_ref
):
    cosines, low, high = cos_ref[...], low_ref[...], high_ref[...]
    rows, half = query_ref.shape
    first = lax.broadcasted_iota(jnp.int32, (rows, 2 * HD), 1) < HD
    scale = HD ** (-0.5)
    mixed = matmul(normed_ref[...], weight_ref[...]) + bias_ref[...]
    for at in range(half // (2 * HD)):
        tiles = [mixed[:, (3 * at + part) * 2 * HD : (3 * at + part + 1) * 2 * HD] for part in range(3)]
        query = jnp.where(first, tiles[0], tiles[1])
        key = jnp.where(first, pltpu.roll(tiles[0], HD, 1), pltpu.roll(tiles[2], HD, 1))
        value = jnp.where(first, tiles[1], tiles[2])
        here = slice(at * 2 * HD, (at + 1) * 2 * HD)
        query_ref[:, here] = bf16(f32(bf16(turn(query, cosines, low, high))) * scale)
        keyval_ref[:, here] = bf16(turn(key, cosines, low, high))
        keyval_ref[:, half + at * 2 * HD : half + (at + 1) * 2 * HD] = bf16(value)


def join_kernel(row_ref, dq_ref, dkv_ref, sent_ref, cos_ref, low_ref, high_ref, out_ref):
    cosines, low, high = cos_ref[...], -low_ref[...], -high_ref[...]
    rows = dq_ref.shape[0]
    half = dq_ref.shape[1]
    first = lax.broadcasted_iota(jnp.int32, (rows, 2 * HD), 1) < HD
    owner = row_ref[0] == 0
    for at in range(half // (2 * HD)):
        here = slice(at * 2 * HD, (at + 1) * 2 * HD)
        there = slice(half + at * 2 * HD, half + (at + 1) * 2 * HD)
        query = turn(dq_ref[:, here], cosines, low, high)
        key = dkv_ref[:, here] + jnp.where(owner, f32(sent_ref[:, here]), 0.0)
        value = dkv_ref[:, there] + jnp.where(owner, f32(sent_ref[:, there]), 0.0)
        key = pltpu.roll(turn(key, cosines, low, high), HD, 1)
        tiles = (jnp.where(first, query, key), jnp.where(first, value, query), jnp.where(first, key, value))
        for part in range(3):
            out_ref[:, (3 * at + part) * 2 * HD : (3 * at + part + 1) * 2 * HD] = bf16(tiles[part])


def tree_kernel(
    parent_ref, row_ref, query_ref, keyval_ref, trunk_ref, grad_ref,
    out_ref, dq_ref, dkv_ref, dtrunk_ref,
    keys, values, dkeys, dvalues,
):
    tree = pl.program_id(0)
    row = row_ref[0]
    rows, half = query_ref.shape
    trunk_len = trunk_ref.shape[0]
    segs = rows // SEG
    trunk_segs = trunk_len // SEG
    seg_count = parent_ref.shape[1]
    first_row = row == 0
    keys[...] = jnp.where(first_row, keyval_ref[:, :half], trunk_ref[:, :half])
    values[...] = jnp.where(first_row, keyval_ref[:, half:], trunk_ref[:, half:])
    dkeys[...] = jnp.zeros_like(dkeys)
    dvalues[...] = jnp.zeros_like(dvalues)
    lane = lax.broadcasted_iota(jnp.int32, (1, half), 1)
    causal = lax.broadcasted_iota(jnp.int32, (SEG, SEG), 0) >= lax.broadcasted_iota(
        jnp.int32, (SEG, SEG), 1
    )
    across = ((1,), (1,))
    down = ((0,), (0,))
    for seg in range(segs):
        here = slice(seg * SEG, (seg + 1) * SEG)
        above = parent_ref[tree, row * segs + seg]
        linked = [above == at for at in range(trunk_segs)]
        for _ in range(seg_count - 2):
            above = jnp.where(above >= 0, parent_ref[tree, jnp.maximum(above, 0)], -1)
            linked = [was | (above == at) for at, was in enumerate(linked)]
        bias = [jnp.where(is_linked, 0.0, masked_fill) for is_linked in linked]
        query, grad = query_ref[here, :], grad_ref[here, :]
        own_key, own_value = keyval_ref[here, :half], keyval_ref[here, half:]
        attended = jnp.zeros((SEG, half), jnp.float32)
        dquery = jnp.zeros((SEG, half), jnp.float32)
        dkey = jnp.zeros((SEG, half), jnp.float32)
        dvalue = jnp.zeros((SEG, half), jnp.float32)
        for head in range(half // HD):
            mine = (lane >= head * HD) & (lane < (head + 1) * HD)
            head_query = jnp.where(mine, query, jnp.zeros_like(query))
            head_grad = jnp.where(mine, grad, jnp.zeros_like(grad))
            scores = [
                matmul(head_query, keys[at * SEG : (at + 1) * SEG, :], across) + bias[at]
                for at in range(trunk_segs)
            ] + [jnp.where(causal, matmul(head_query, own_key, across), masked_fill)]
            top = functools.reduce(jnp.maximum, [jnp.max(s, axis=1, keepdims=True) for s in scores])
            powers = [jnp.exp(s - top) for s in scores]
            total = functools.reduce(jnp.add, [jnp.sum(p, axis=1, keepdims=True) for p in powers])
            probs = [p / total for p in powers]
            low = [bf16(p) for p in probs]
            blocks = [values[at * SEG : (at + 1) * SEG, :] for at in range(trunk_segs)] + [own_value]
            prob_grads = [matmul(head_grad, v, across) for v in blocks]
            delta = functools.reduce(
                jnp.add, [jnp.sum(p * g, axis=1, keepdims=True) for p, g in zip(probs, prob_grads)]
            )
            score_grads = [bf16(p * (g - delta)) for p, g in zip(probs, prob_grads)]
            head_out = functools.reduce(jnp.add, [matmul(p, v) for p, v in zip(low, blocks)])
            attended = jnp.where(mine, head_out, attended)
            key_blocks = [keys[at * SEG : (at + 1) * SEG, :] for at in range(trunk_segs)] + [own_key]
            head_dq = functools.reduce(jnp.add, [matmul(s, u) for s, u in zip(score_grads, key_blocks)])
            dquery = jnp.where(mine, head_dq, dquery)
            dkey = dkey + matmul(score_grads[-1], head_query, down)
            dvalue = dvalue + matmul(low[-1], head_grad, down)
            for at in range(trunk_segs):
                spot = slice(at * SEG, (at + 1) * SEG)
                dkeys[spot, :] += matmul(score_grads[at], head_query, down)
                dvalues[spot, :] += matmul(low[at], head_grad, down)
        out_ref[here, :] = bf16(attended)
        dq_ref[here, :] = dquery * HD ** (-0.5)
        dkv_ref[here, :half] = dkey
        dkv_ref[here, half:] = dvalue
    dtrunk_ref[:, :half] = bf16(dkeys[...])
    dtrunk_ref[:, half:] = bf16(dvalues[...])

    @pl.when(first_row)
    def _():
        dkv_ref[:, :half] += dkeys[...]
        dkv_ref[:, half:] += dvalues[...]


def store_blocks(place_ref, sides, full_ref, own_refs, plain_refs):
    row, slab = place_ref[1], place_ref[2]
    for side, values in enumerate(sides):
        width = values[0].shape[1]
        for source, value in enumerate(values):
            within = source % 2
            here = row == source // 2

            def put(refs):
                if len(refs) == 1:
                    refs[0][side, :, within * width : (within + 1) * width] = value
                else:
                    refs[within][side] = value

            @pl.when(here)
            def _():
                full_ref[side, :, within * width : (within + 1) * width] = value
                put(own_refs)

            @pl.when(jnp.logical_not(here))
            def _():
                put(plain_refs)
                at = (2 + jnp.where(slab == 0, within, 1 - within)) * width
                full_ref[side, :, pl.ds(pl.multiple_of(at, width), width)] = value


def gather_kernel(place_ref, mine_ref, theirs_ref, full_ref, own_ref, plain_ref):
    sides = [[ref[at] for at in range(ref.shape[0])] for ref in (mine_ref, theirs_ref)]
    store_blocks(place_ref, sides, full_ref, [own_ref], [plain_ref])


def norm_kernel(place_ref, gain_ref, bias_ref, mine_ref, theirs_ref, full_ref, *outs):
    normal_ref, scale_ref = outs[4:]
    sides = []
    for side, ref in enumerate((mine_ref, theirs_ref)):
        values = [f32(ref[at]) for at in range(ref.shape[0])]
        features = len(values) * values[0].shape[1]
        mean = functools.reduce(jnp.add, [jnp.sum(v, axis=1, keepdims=True) for v in values]) / features
        centred = [v - mean for v in values]
        square = functools.reduce(jnp.add, [jnp.sum(v * v, axis=1, keepdims=True) for v in centred])
        inv_scale = lax.rsqrt(square / features + norm_epsilon)
        normals = [v * inv_scale for v in centred]
        if side == 0:
            scale_ref[...] = inv_scale
            for source, normal in enumerate(normals):

                @pl.when(place_ref[0] == source)
                def _():
                    normal_ref[...] = normal

        sides.append(
            [
                bf16(normal * gain_ref[source : source + 1, :] + bias_ref[source : source + 1, :])
                for source, normal in enumerate(normals)
            ]
        )
    store_blocks(place_ref, sides, full_ref, outs[:2], outs[2:4])


def pair_rows(rows, width):
    return pl.BlockSpec((2, rows, width), lambda at, *_: (0, at, 0))


def gathered(place, mine, theirs, norm=None):
    blocks, count, width = mine.shape
    rows = SEG if norm is None else SEG // 2
    full = blocks * width
    in_specs = [pl.BlockSpec((blocks, rows, width), lambda at, *_: (0, at, 0))] * 2
    parts = [full // 2] * 2 if norm is None else [width] * 4
    out_specs = [pair_rows(rows, size) for size in [full] + parts]
    out_shape = [
        jax.ShapeDtypeStruct((2, count, size), jnp.bfloat16) for size in [full] + parts
    ]
    operands = [mine, theirs]
    if norm is not None:
        gain = [values.reshape(blocks, width) for values in norm]
        operands = gain + operands
        in_specs = [pl.BlockSpec((blocks, width), lambda at, *_: (0, 0))] * 2 + in_specs
        out_specs = out_specs + [row_block(rows, width), row_block(rows, 1)]
        out_shape = out_shape + [
            jax.ShapeDtypeStruct((count, width), jnp.float32),
            jax.ShapeDtypeStruct((count, 1), jnp.float32),
        ]
    results = pl.pallas_call(
        gather_kernel if norm is None else norm_kernel,
        grid_spec=pltpu.PrefetchScalarGridSpec(
            num_scalar_prefetch=1, grid=(count // rows,), in_specs=in_specs, out_specs=out_specs
        ),
        out_shape=out_shape,
        cost_estimate=pl.CostEstimate(flops=1, bytes_accessed=1, transcendentals=0),
        name="join_blocks" if norm is None else "norm_blocks",
    )(place, *operands)
    last = len(parts) + 1
    return [values.reshape(2 * count, -1) for values in results[:last]] + list(results[last:])


def stack_kernel(place_ref, terms_ref, arrived_ref, out_ref):
    row, slab = place_ref[1], place_ref[2]
    width = out_ref.shape[2]
    for spot in range(4):
        here = slice(spot * width, (spot + 1) * width)
        value = bf16(f32(terms_ref[:, here]) + f32(arrived_ref[:, here]))
        if spot < 2:
            out_ref[2 * row + spot] = value
        else:
            out_ref[2 * (1 - row) + jnp.where(slab == 0, spot - 2, 3 - spot)] = value


def stacked(place, terms, arrived, blocks):
    count, full = arrived.shape
    rows = SEG
    width = full // blocks
    return pl.pallas_call(
        stack_kernel,
        grid_spec=pltpu.PrefetchScalarGridSpec(
            num_scalar_prefetch=1,
            grid=(count // rows,),
            in_specs=[row_block(rows, full), row_block(rows, full)],
            out_specs=pl.BlockSpec((blocks, rows, width), lambda at, *_: (0, at, 0)),
        ),
        out_shape=jax.ShapeDtypeStruct((blocks, count, width), jnp.bfloat16),
        cost_estimate=pl.CostEstimate(flops=1, bytes_accessed=1, transcendentals=0),
        name="stack_blocks",
    )(place, terms, arrived)


def cast_rows_kernel(place_ref, master_ref, own_ref, send_ref):
    value = bf16(master_ref[...])
    own_ref[...] = value
    half = pl.num_programs(0) // 2

    @pl.when(pl.program_id(0) // half == place_ref[2])
    def _():
        send_ref[...] = value


def cast_cols_kernel(place_ref, master_ref, own_ref, send_ref):
    value = bf16(master_ref[...])
    own_ref[...] = value
    half = value.shape[1] // 2
    send_ref[...] = jnp.where(place_ref[2] == 0, value[:, :half], value[:, half:])


def cast_weight(place, master, axis):
    height, width = master.shape
    rows = min(2 * SEG, master.shape[0] // 4)
    if axis == 0:
        width = width // 2
        steps = height // rows
        half = steps // 2
        specs = [
            pl.BlockSpec((rows, width), lambda at, place_ref: (at, place_ref[3])),
            pl.BlockSpec((rows, width), lambda at, place_ref: (at, 0)),
            pl.BlockSpec(
                (rows, width), lambda at, place_ref: (jnp.clip(at - half * place_ref[2], 0, half - 1), 0)
            ),
        ]
        send = (height // 2, width)
        whole = (2 * height, width)
    else:
        height = height // 2
        steps = height // rows
        specs = [
            pl.BlockSpec((rows, width), lambda at, place_ref: (at + steps * place_ref[3], 0)),
            pl.BlockSpec((rows, width), lambda at, place_ref: (at, 0)),
            pl.BlockSpec((rows, width // 2), lambda at, place_ref: (at, 0)),
        ]
        send = (height, width // 2)
        whole = (height, 2 * width)
    return pl.pallas_call(
        cast_rows_kernel if axis == 0 else cast_cols_kernel,
        grid_spec=pltpu.PrefetchScalarGridSpec(
            num_scalar_prefetch=1, grid=(steps,), in_specs=specs[:1], out_specs=specs[1:]
        ),
        out_shape=[
            jax.ShapeDtypeStruct(whole, jnp.bfloat16),
            jax.ShapeDtypeStruct(send, jnp.bfloat16),
        ],
        cost_estimate=pl.CostEstimate(flops=1, bytes_accessed=1, transcendentals=0),
        name="cast_weight",
    )(place, master)


def settle_store(axis, place_ref, mine, theirs, out_ref):
    if axis == 0:
        out_ref[place_ref[3]] = mine
        out_ref[1 - place_ref[3]] = theirs
    else:
        width = mine.shape[1]
        first = place_ref[3] == 0
        out_ref[:, :width] = jnp.where(first, mine, theirs)
        out_ref[:, width:] = jnp.where(first, theirs, mine)


def settle_kernel(axis, place_ref, mine_ref, theirs_ref, *refs):
    settle_store(axis, place_ref, f32(mine_ref[...]), f32(theirs_ref[...]), refs[-1])


def settle_both_kernel(axis, place_ref, *refs):
    for at in range(2):

        @pl.when(pl.program_id(0) == at)
        def _():
            settle_store(axis, place_ref, f32(refs[2 * at][...]), f32(refs[2 * at + 1][...]), refs[-1])


def settle_both(place, first, last, shape, axis):
    rows, width = first[0].shape
    if axis == 0:
        shape = (2, shape[0] // 2, width)
        out_spec = pl.BlockSpec((2, rows, width), lambda at, *_: (0, at, 0))
    else:
        out_spec = pl.BlockSpec((rows, 2 * width), lambda at, *_: (at, 0))
    return pl.pallas_call(
        functools.partial(settle_both_kernel, axis),
        grid_spec=pltpu.PrefetchScalarGridSpec(
            num_scalar_prefetch=1,
            grid=(2,),
            in_specs=[pl.BlockSpec((rows, width), lambda *_: (0, 0))] * 4,
            out_specs=out_spec,
        ),
        out_shape=jax.ShapeDtypeStruct(shape, jnp.float32),
        cost_estimate=pl.CostEstimate(flops=1, bytes_accessed=1, transcendentals=0),
        name="settle_both",
    )(place, *first, *last)


def settle(place, mine, theirs, shape, axis, offset, dest=None):
    rows, width = mine.shape
    at = offset // rows
    whole = pl.BlockSpec((rows, width), lambda *_: (0, 0))
    if axis == 0:
        shape = (2, shape[0] // 2, width)
        out_spec = pl.BlockSpec((2, rows, width), lambda *_: (0, at, 0))
    else:
        out_spec = pl.BlockSpec((rows, 2 * width), lambda *_: (at, 0))
    in_specs = [whole, whole]
    operands = [place, mine, theirs]
    aliases = {}
    if dest is not None:
        in_specs.append(pl.BlockSpec(memory_space=pl.ANY))
        operands.append(dest)
        aliases = {3: 0}
    return pl.pallas_call(
        functools.partial(settle_kernel, axis),
        grid_spec=pltpu.PrefetchScalarGridSpec(
            num_scalar_prefetch=1, grid=(1,), in_specs=in_specs, out_specs=out_spec
        ),
        out_shape=jax.ShapeDtypeStruct(shape, jnp.float32),
        input_output_aliases=aliases,
        cost_estimate=pl.CostEstimate(flops=1, bytes_accessed=1, transcendentals=0),
        name="settle",
    )(*operands)


def row_block(rows, width):
    return pl.BlockSpec((rows, width), lambda at, *_: (at, 0))


def mixed_heads(normed, weight, bias, tables):
    count, depth = normed.shape
    width = weight.shape[1]
    rows = SEG
    return pl.pallas_call(
        mixed_kernel,
        grid=(count // rows,),
        in_specs=[
            row_block(rows, depth),
            pl.BlockSpec((depth, width), lambda at: (0, 0)),
            pl.BlockSpec((1, width), lambda at: (0, 0)),
        ]
        + [row_block(rows, 2 * HD)] * 3,
        out_specs=[row_block(rows, width // 3), row_block(rows, 2 * width // 3)],
        out_shape=[
            jax.ShapeDtypeStruct((count, width // 3), jnp.bfloat16),
            jax.ShapeDtypeStruct((count, 2 * width // 3), jnp.bfloat16),
        ],
        cost_estimate=pl.CostEstimate(flops=1, bytes_accessed=1, transcendentals=0),
        name="mixed_heads",
    )(normed, weight, bias.reshape(1, width), *tables)


def join_heads(row, dq, dkv, sent, tables):
    count, half = dq.shape
    rows = 2 * SEG
    return pl.pallas_call(
        join_kernel,
        grid_spec=pltpu.PrefetchScalarGridSpec(
            num_scalar_prefetch=1,
            grid=(count // rows,),
            in_specs=[row_block(rows, half), row_block(rows, 2 * half), row_block(rows, 2 * half)]
            + [row_block(rows, 2 * HD)] * 3,
            out_specs=row_block(rows, 3 * half),
        ),
        out_shape=jax.ShapeDtypeStruct((count, 3 * half), jnp.bfloat16),
        cost_estimate=pl.CostEstimate(flops=1, bytes_accessed=1, transcendentals=0),
        name="join_heads",
    )(row, dq, dkv, sent, *tables)


def tree_attention(parents, row, query, keyval, trunk, grad):
    trees = parents.shape[0]
    count, half = query.shape
    rows = count // trees
    keys = trunk.shape[0] // trees
    pairs = count * (keys + SEG) * (half // HD)
    return pl.pallas_call(
        tree_kernel,
        grid_spec=pltpu.PrefetchScalarGridSpec(
            num_scalar_prefetch=2,
            grid=(trees,),
            in_specs=[
                row_block(rows, half),
                row_block(rows, 2 * half),
                row_block(keys, 2 * half),
                row_block(rows, half),
            ],
            out_specs=[
                row_block(rows, half),
                row_block(rows, half),
                row_block(rows, 2 * half),
                row_block(keys, 2 * half),
            ],
            scratch_shapes=[pltpu.VMEM((keys, half), jnp.bfloat16)] * 2
            + [pltpu.VMEM((keys, half), jnp.float32)] * 2,
        ),
        out_shape=[
            jax.ShapeDtypeStruct((count, half), jnp.bfloat16),
            jax.ShapeDtypeStruct((count, half), jnp.float32),
            jax.ShapeDtypeStruct((count, 2 * half), jnp.float32),
            jax.ShapeDtypeStruct((trees * keys, 2 * half), jnp.bfloat16),
        ],
        cost_estimate=pl.CostEstimate(flops=1, bytes_accessed=1, transcendentals=0),
        name="tree_attention",
    )(parents, row, query, keyval, trunk, grad)


def paired_device(
    tokens,
    parent,
    depth,
    w_qkv,
    b_qkv,
    w_out,
    w_up,
    b_up,
    w_down,
    b_res,
    ln_gain,
    ln_bias,
    cotangent,
):
    count, width = tokens.shape
    row = lax.axis_index("row")
    col = lax.axis_index("col")
    core = lax.axis_index("dp") % 2
    slab = lax.axis_index("dp") // 2
    cols = lax.axis_size("col")
    half = 2 * width
    heads_width = w_out.shape[0] // 2
    hidden = w_up.shape[1] // 2
    place = jnp.stack([col, row, slab, core]).astype(jnp.int32)
    row_table = jnp.reshape(row, (1,)).astype(jnp.int32)
    down_dims = ((0,), (0,))
    across = ((1,), (1,))

    def part(values, at, size, axis):
        return lax.dynamic_slice_in_dim(values, at * size, size, axis)

    def exchange(stack):
        return lax.all_to_all(stack, "col", 0, 0, tiled=True)

    done = ()

    def step(run, *inputs):
        nonlocal done
        inputs, _ = lax.optimization_barrier((inputs, done))
        result = run(*inputs)
        done = result
        return result

    def wait(value):
        return step(lambda arrived: arrived, value)

    tokens_near = lax.all_gather(tokens, "col", axis=0)
    grad_stack = jnp.broadcast_to(cotangent[None], (cols,) + cotangent.shape)

    def ready(master, axis):
        whole, send = step(lambda weight: cast_weight(place, weight, axis), master)
        return whole, swap_row(send)

    def fill(whole, part_in, axis, last):
        at = whole.shape[axis] // 2 + (part_in.shape[axis] if last else 0)
        return step(lambda a, b: lax.dynamic_update_slice_in_dim(a, b, at, axis), whole, part_in)

    tables = jnp.concatenate([parent, depth], axis=0)
    tables = jnp.stack([tables, swap_core(tables)])
    parents = tables[:, 0]
    segs = count // SEG
    token = jnp.arange(count, dtype=jnp.int32)
    levels = jnp.zeros((2, count), jnp.float32)
    for seg in range(segs):
        level = lax.dynamic_slice_in_dim(tables[:, 1], row * segs + seg, 1, 1).astype(jnp.float32)
        levels = jnp.where((token // SEG == seg)[None, :], level, levels)
    positions = (levels * SEG + (token % SEG).astype(jnp.float32)[None, :]).reshape(2 * count)
    rotary = rotary_tables(positions)

    qkv_whole, qkv_row = ready(w_qkv, 0)
    up_whole, up_row = ready(w_up, 0)
    qkv_row = wait(qkv_row)
    qkv_x = swap_x(qkv_row)
    out_whole, out_row = ready(w_out, 1)
    down_whole, down_row = ready(w_down, 1)
    rotary = step(lambda *tables: tables, *rotary)
    qkv_whole = fill(qkv_whole, qkv_row, 0, False)
    up_row = wait(up_row)
    up_x = swap_x(up_row)
    qkv_x = wait(qkv_x)
    tokens_near = wait(tokens_near)
    tokens_far = swap_core(tokens_near)
    grad_near = exchange(after(grad_stack, tokens_near))
    up_whole = fill(up_whole, up_row, 0, False)
    normed, own_a, own_b, plain_a, plain_b, normal, inv_scale = step(
        lambda mine, theirs: gathered(place, mine, theirs, (ln_gain, ln_bias)), tokens_near, tokens_far
    )
    qkv_full = fill(qkv_whole, qkv_x, 0, True)
    query, keyval = step(
        lambda left, right: mixed_heads(left, right, part(b_qkv, core, 3 * heads_width, 0), rotary),
        normed, qkv_full,
    )
    trunk = lax.ppermute(keyval, "row", [(0, 1)])
    root = math.sqrt(2.0 / math.pi)

    def feed(left, right):
        hidden_up = matmul(left, right) + part(b_up, core, hidden, 0)
        squared = hidden_up * hidden_up
        bend = jnp.tanh(root * (hidden_up + 0.044715 * squared * hidden_up))
        return bf16(0.5 * hidden_up * (1.0 + bend)), bf16(
            0.5 * (1.0 + bend)
            + 0.5 * hidden_up * (1.0 - bend * bend) * root * (1.0 + 3.0 * 0.044715 * squared)
        )

    out_row = wait(out_row)
    out_x = swap_x(out_row)
    up_full = fill(up_whole, up_x, 0, True)
    down_row = wait(down_row)
    down_x = swap_x(down_row)
    activated, slope = step(feed, normed, up_full)
    out_whole = fill(out_whole, out_row, 1, False)
    down_whole = fill(down_whole, down_row, 1, False)
    out_full = fill(out_whole, out_x, 1, True)
    trunk = wait(trunk)
    grad_near = wait(grad_near)
    grad_far = swap_core(grad_near)
    grad, grad_own, grad_plain = step(lambda mine, theirs: gathered(place, mine, theirs), grad_near, grad_far)

    def cut(values, at):
        size = values.shape[1] // 2
        return values[:, at * size : (at + 1) * size]

    def leaving(left, right):
        return step(lambda a, b: bf16(matmul(a, b, down_dims)), left, right)

    def staying(left, right, sent):
        return step(lambda a, b, c: bf16(matmul(a, b, down_dims) + f32(c)), left, right, sent)

    def crossed(both, arrived):
        mine = step(lambda a, b: bf16(f32(a) + f32(b)), both, arrived)
        return mine, swap_core(mine)

    def settled(pieces, shape, axis, offset, dest):
        operands = pieces if dest is None else pieces + (dest,)
        return step(
            lambda mine, theirs, *rest: settle(place, mine, theirs, shape, axis, offset, *rest), *operands
        )

    down_sent_a = swap_row(leaving(cut(activated, 0), grad_plain))
    down_sent_b = swap_row(leaving(cut(activated, 1), grad_plain))
    out_heads = step(lambda a, b: bf16(matmul(a, b, across)), grad, out_full)
    attended, query_grad, own_grad, trunk_grad = step(
        lambda *operands: tree_attention(parents, row_table, *operands), query, keyval, trunk, out_heads
    )
    trunk_sent = lax.ppermute(trunk_grad, "row", [(1, 0)])
    out_sent = swap_row(leaving(attended, grad_plain))
    down_both_a = staying(cut(activated, 0), grad_own, down_sent_a)
    down_cross_a = swap_x(down_both_a)
    down_full = fill(down_whole, down_x, 1, True)
    branch_terms = step(
        lambda a, b, c, d: bf16(matmul(a, b) + matmul(c, d)), attended, out_full, activated, down_full
    )
    branch_near = swap_core(branch_terms[count:])
    up_grad = step(lambda a, b, c: bf16(matmul(a, b, across) * f32(c)), grad, down_full, slope)
    up_sent_a = swap_row(leaving(plain_a, up_grad))
    down_both_b = staying(cut(activated, 1), grad_own, down_sent_b)
    down_cross_b = swap_x(down_both_b)
    out_both = staying(attended, grad_own, out_sent)
    out_cross = swap_x(out_both)
    up_sent_b = swap_row(leaving(plain_b, up_grad))
    down_a = crossed(down_both_a, down_cross_a)
    branch = lax.psum_scatter(
        step(lambda a, b: stacked(place, a, b, cols), branch_terms, branch_near), "col", tiled=False
    )
    mixed_grad = step(
        lambda *operands: join_heads(row_table, *operands, rotary), query_grad, own_grad, trunk_sent
    )
    qkv_sent_a = swap_row(leaving(plain_a, mixed_grad))
    down_b = crossed(down_both_b, down_cross_b)
    qkv_sent_b = swap_row(leaving(plain_b, mixed_grad))
    norm_terms = step(
        lambda a, b, c, d: bf16(matmul(a, b, across) + matmul(c, d, across)),
        mixed_grad, qkv_full, up_grad, up_full,
    )
    up_both_a = staying(own_a, up_grad, up_sent_a)
    up_cross_a = swap_x(up_both_a)
    norm_near = swap_core(step(lambda terms: terms[count:], norm_terms))
    output = step(lambda parts, block: bf16(f32(block) + f32(parts) + b_res), branch, tokens)
    norm_parts = exchange(step(lambda a, b: stacked(place, a, b, cols), norm_terms, norm_near))
    down_grad = step(lambda first, last: settle_both(place, first, last, w_down.shape, 0), down_a, down_b)
    up_a = crossed(up_both_a, up_cross_a)
    up_both_b = staying(own_b, up_grad, up_sent_b)
    up_cross_b = swap_x(up_both_b)
    out_mine = crossed(out_both, out_cross)
    qkv_both_a = staying(own_a, mixed_grad, qkv_sent_a)
    qkv_cross_a = swap_x(qkv_both_a)
    out_grad = settled(out_mine, w_out.shape, 0, 0, None)
    up_b = crossed(up_both_b, up_cross_b)
    gain_here = part(ln_gain, col, width, 0)

    def norm_sums(parts):
        total = jnp.sum(f32(parts), axis=0)
        scaled = total * gain_here
        return (
            total,
            jnp.stack([jnp.sum(scaled, axis=1), jnp.sum(scaled * normal, axis=1)]),
            jnp.sum(total * normal, axis=0),
            jnp.sum(total, axis=0),
        )

    norm_grad, sums, gain_sum, shift_sum = step(norm_sums, norm_parts)
    up_weight_grad = step(lambda first, last: settle_both(place, first, last, w_up.shape, 1), up_a, up_b)

    def line_step(values, bit):
        return lax.ppermute(values, "col", [(at, at ^ bit) for at in range(cols)])

    small = jnp.concatenate(
        [
            jnp.sum(f32(up_grad), axis=0),
            jnp.sum(f32(mixed_grad), axis=0),
            jnp.sum(f32(cotangent), axis=0),
            gain_sum,
            shift_sum,
        ]
    ).reshape(-1, 128)
    shared_at = (hidden + 3 * heads_width) // 128
    res_at = width // 128
    sums_next = line_step(sums, 1)
    small_other = swap_core(small)
    sums, shared = step(
        lambda sums, arrived, small, other: (sums + arrived, (small + other)[shared_at:]),
        sums, sums_next, small, small_other,
    )
    sums_next = line_step(sums, 2)
    ends = shared[res_at:][None]
    ends_next = line_step(ends, 1)
    qkv_both_b = staying(own_b, mixed_grad, qkv_sent_b)
    qkv_cross_b = swap_x(qkv_both_b)
    ends = step(lambda ends, arrived: pair(col % 2, ends, arrived, 0), ends, ends_next)
    ends_next = line_step(ends, 2)
    qkv_a = crossed(qkv_both_a, qkv_cross_a)
    sums = (sums + sums_next) / (cols * width)
    tokens_grad = step(
        lambda sums, total: inv_scale
        * (total * gain_here - sums[0][:, None] - normal * sums[1][:, None])
        + f32(cotangent),
        sums, norm_grad,
    )

    def gather_small(small, other, shared, ends, arrived):
        return jnp.concatenate(
            [
                pair(core, small[: hidden // 128], other[: hidden // 128], 0),
                pair(core, small[hidden // 128 : shared_at], other[hidden // 128 : shared_at], 0),
                shared[:res_at],
                pair(col // 2, ends, arrived, 0).reshape(-1, 128),
            ]
        )

    small = step(gather_small, small, small_other, shared, ends, ends_next)
    small_next = swap_row(small)
    qkv_b = crossed(qkv_both_b, qkv_cross_b)
    small = step(jnp.add, small, small_next)
    small_next = swap_x(small)
    qkv_weight_grad = step(
        lambda first, last: settle_both(place, first, last, w_qkv.shape, 1), qkv_a, qkv_b
    )
    small = step(jnp.add, small, small_next)

    bounds = [0, 2 * hidden // 128, (2 * hidden + 6 * heads_width) // 128]
    bounds.append(bounds[-1] + res_at)
    up_bias_grad = small[: bounds[1]].reshape(-1)
    qkv_bias_grad = small[bounds[1] : bounds[2]].reshape(-1)
    res_bias_grad = small[bounds[2] : bounds[3]].reshape(-1)
    ends = small[bounds[3] :].reshape(cols, 2, width)
    gain_grad = ends[:, 0].reshape(-1)
    shift_grad = ends[:, 1].reshape(-1)
    return (
        output,
        tokens_grad,
        qkv_weight_grad,
        qkv_bias_grad,
        out_grad.reshape(w_out.shape),
        up_weight_grad,
        up_bias_grad,
        down_grad.reshape(w_down.shape),
        res_bias_grad,
        gain_grad,
        shift_grad,
    )


def solution(mesh):
    sizes = (mesh.shape["dp"], mesh.shape["row"], mesh.shape["col"])
    per_device = paired_device if sizes == (4, 2, 4) else general_device
    return jax.shard_map(
        per_device,
        mesh=mesh,
        in_specs=(
            P(("dp", "row"), "col"),
            P("dp", None),
            P("dp", None),
            P("row", "col"),
            P("col"),
            P("col", "row"),
            P("row", "col"),
            P("col"),
            P("col", "row"),
            P("col"),
            P(),
            P(),
            P(("dp", "row"), "col"),
        ),
        out_specs=(
            P(("dp", "row"), "col"),
            P(("dp", "row"), "col"),
            P("row", "col"),
            P("col"),
            P("col", "row"),
            P("row", "col"),
            P("col"),
            P("col", "row"),
            P("col"),
            P(),
            P(),
        ),
        check_vma=False,
    )
```

```python
import functools
import math

import jax
import jax.numpy as jnp
from jax import lax
from jax.experimental import pallas as pl
from jax.experimental.pallas import tpu as pltpu
from jax.sharding import PartitionSpec as P

HD = 64
ROT = 32
SEG = 256


norm_epsilon = 1e-05
masked_fill = -1e30
rotary_base = 10000.0


def precise_dot(left, right):
    return jnp.dot(left, right, precision=lax.Precision.HIGHEST, preferred_element_type=jnp.float32)


def ancestry(parent_row):
    seg_count = parent_row.shape[0]
    labels = jnp.arange(seg_count, dtype=jnp.int32)
    identity = jnp.eye(seg_count, dtype=jnp.float32)
    parent_hot = (parent_row[:, None] == labels[None, :]).astype(jnp.float32)

    def extend(rounds, reachable):
        return jnp.minimum(identity + precise_dot(parent_hot, reachable), 1.0)

    return lax.fori_loop(0, seg_count, extend, identity)


def rotate(values, cosines, sines):
    half_rot = ROT // 2
    former = values[..., :half_rot]
    latter = values[..., half_rot:ROT]
    return jnp.concatenate(
        [former * cosines - latter * sines, latter * cosines + former * sines, values[..., ROT:]],
        axis=-1,
    )


def angles_of(positions):
    frequency = jnp.exp(
        -math.log(rotary_base) * 2.0 * jnp.arange(ROT // 2, dtype=jnp.float32) / ROT
    )
    phase_angle = positions[:, None] * frequency[None, :]
    return (jnp.cos(phase_angle)[:, None, :], jnp.sin(phase_angle)[:, None, :])


def reorder_rows(gradient, row_count, dp_count):
    leading = gradient.shape[0]
    blocked = gradient.reshape(
        row_count, dp_count, leading // (row_count * dp_count), gradient.shape[1]
    )
    return jnp.transpose(blocked, (1, 0, 2, 3)).reshape(leading, gradient.shape[1])


def reorder_cols(gradient, row_count, dp_count):
    trailing = gradient.shape[1]
    blocked = gradient.reshape(
        gradient.shape[0], row_count, dp_count, trailing // (row_count * dp_count)
    )
    return jnp.transpose(blocked, (0, 2, 1, 3)).reshape(gradient.shape[0], trailing)


def general_device(
    tokens,
    parent,
    depth,
    w_qkv,
    b_qkv,
    w_out,
    w_up,
    b_up,
    w_down,
    b_res,
    ln_gain,
    ln_bias,
    cotangent,
):
    tok_rows = tokens.shape[0]
    col_width = tokens.shape[1]
    row_count = lax.axis_size("row")
    dp_count = lax.axis_size("dp")
    row_start = lax.axis_index("row") * tok_rows
    local_heads = w_out.shape[0] // HD
    seg_count = parent.shape[1]
    labels = jnp.arange(seg_count, dtype=jnp.int32)
    reachable = ancestry(parent[0])
    query_index = row_start + jnp.arange(tok_rows, dtype=jnp.int32)
    query_seg = query_index // SEG
    query_hot = (query_seg[:, None] == labels[None, :]).astype(jnp.float32)
    query_reach = precise_dot(query_hot, reachable)
    levels = precise_dot(query_hot, depth[0].astype(jnp.float32)[:, None])[:, 0]
    positions = levels * SEG + (query_index % SEG).astype(jnp.float32)
    cosines, sines = angles_of(positions)
    score_scale = HD ** (-0.5)

    def permit(key_len):
        key_index = jnp.arange(key_len, dtype=jnp.int32)
        key_seg = key_index // SEG
        key_hot = (key_seg[:, None] == labels[None, :]).astype(jnp.float32)
        linked = precise_dot(query_reach, key_hot.T) > 0.5
        return linked & (
            (query_seg[:, None] != key_seg[None, :]) | (query_index[:, None] >= key_index[None, :])
        )

    whole = lax.all_gather(tokens, "col", axis=1, tiled=True).astype(jnp.float32)
    centred = whole - jnp.mean(whole, axis=1, keepdims=True)
    inv_scale = lax.rsqrt(jnp.mean(centred * centred, axis=1, keepdims=True) + norm_epsilon)
    normal = centred * inv_scale
    normed = (normal * ln_gain + ln_bias).astype(jnp.bfloat16)
    qkv_full, up_full, out_full, down_full = (
        lax.all_gather(w_qkv.astype(jnp.bfloat16), "row", axis=0, tiled=True),
        lax.all_gather(w_up.astype(jnp.bfloat16), "row", axis=0, tiled=True),
        lax.all_gather(w_out.astype(jnp.bfloat16), "row", axis=1, tiled=True),
        lax.all_gather(w_down.astype(jnp.bfloat16), "row", axis=1, tiled=True),
    )
    mixed = (jnp.dot(normed, qkv_full, preferred_element_type=jnp.float32) + b_qkv).reshape(
        tok_rows, local_heads, 3, HD
    )

    def rotate_pair(query_pre, key_pre):
        return (rotate(query_pre, cosines, sines), rotate(key_pre, cosines, sines))

    rotated, rotate_back = jax.vjp(rotate_pair, mixed[:, :, 0], mixed[:, :, 1])
    queries = rotated[0].astype(jnp.bfloat16)
    key_rows = rotated[1].astype(jnp.bfloat16)
    value_rows = mixed[:, :, 2].astype(jnp.bfloat16)
    key_flat = key_rows.reshape(tok_rows, local_heads * HD)
    value_flat = value_rows.reshape(tok_rows, local_heads * HD)

    def scores_for(key_part):
        raw_scores = (
            jnp.einsum("qhe,khe->hqk", queries, key_part, preferred_element_type=jnp.float32)
            * score_scale
        )
        allowed = permit(key_part.shape[0])
        return (jnp.where(allowed[None], raw_scores, masked_fill), allowed)

    pieces = (
        lax.all_gather(key_flat, "row", axis=0, tiled=True),
        lax.all_gather(value_flat, "row", axis=0, tiled=True),
    )
    running_top = jnp.full((local_heads, tok_rows), masked_fill, jnp.float32)
    key_len = pieces[0].shape[0]
    key_part = pieces[0].reshape(key_len, local_heads, HD)
    value_part = pieces[1].reshape(key_len, local_heads, HD)
    scores, allowed = scores_for(key_part)
    new_top = jnp.maximum(running_top, jnp.max(scores, axis=2))
    exponent = jnp.where(allowed[None], jnp.exp(scores - new_top[:, :, None]), 0.0)
    running_sum = jnp.sum(exponent, axis=2)
    weighted = jnp.einsum(
        "hqk,khe->hqe",
        exponent.astype(jnp.bfloat16),
        value_part,
        preferred_element_type=jnp.float32,
    )
    running_top, running_sum, weighted = (new_top, running_sum, weighted)
    log_total = running_top + jnp.log(running_sum)
    attn_exact = weighted / running_sum[:, :, None]
    attended = (
        jnp.transpose(attn_exact, (1, 0, 2))
        .reshape(tok_rows, local_heads * HD)
        .astype(jnp.bfloat16)
    )
    hidden_up = jnp.dot(normed, up_full, preferred_element_type=jnp.float32) + b_up
    activated, gelu_back = jax.vjp(functools.partial(jax.nn.gelu, approximate=True), hidden_up)
    activated = activated.astype(jnp.bfloat16)
    branch_terms = jnp.dot(attended, out_full, preferred_element_type=jnp.float32) + jnp.dot(
        activated, down_full, preferred_element_type=jnp.float32
    )
    branch = lax.psum_scatter(
        branch_terms.astype(jnp.bfloat16), "col", scatter_dimension=1, tiled=True
    ).astype(jnp.float32)
    output = (tokens.astype(jnp.float32) + branch + b_res).astype(jnp.bfloat16)
    grad_full = lax.all_gather(cotangent, "col", axis=1, tiled=True)
    res_bias_grad = jnp.sum(cotangent.astype(jnp.float32), axis=0)
    down_grad = jnp.einsum("tf,td->fd", activated, grad_full, preferred_element_type=jnp.float32)
    out_grad = jnp.einsum("te,td->ed", attended, grad_full, preferred_element_type=jnp.float32)
    act_grad = jnp.einsum("td,fd->tf", grad_full, down_full, preferred_element_type=jnp.float32)
    up_grad = gelu_back(act_grad)[0].astype(jnp.bfloat16)
    attn_grad = jnp.einsum(
        "td,ed->te", grad_full, out_full, preferred_element_type=jnp.float32
    ).astype(jnp.bfloat16)
    up_bias_grad = jnp.sum(up_grad.astype(jnp.float32), axis=0)
    up_weight_grad = jnp.einsum("td,tf->df", normed, up_grad, preferred_element_type=jnp.float32)
    out_heads = attn_grad.reshape(tok_rows, local_heads, HD)
    delta_sum = jnp.einsum("qhe,hqe->hq", out_heads.astype(jnp.float32), attn_exact)
    pieces = (
        lax.all_gather(key_flat, "row", axis=0, tiled=True),
        lax.all_gather(value_flat, "row", axis=0, tiled=True),
    )
    key_len = pieces[0].shape[0]
    key_part = pieces[0].reshape(key_len, local_heads, HD)
    value_part = pieces[1].reshape(key_len, local_heads, HD)
    scores, allowed = scores_for(key_part)
    softmaxed = jnp.where(allowed[None], jnp.exp(scores - log_total[:, :, None]), 0.0)
    prob_grad = jnp.einsum(
        "qhe,khe->hqk", out_heads, value_part, preferred_element_type=jnp.float32
    )
    score_grad = (softmaxed * (prob_grad - delta_sum[:, :, None])).astype(jnp.bfloat16)
    query_grad = (
        jnp.einsum("hqk,khe->qhe", score_grad, key_part, preferred_element_type=jnp.float32)
        * score_scale
    )
    key_grad = (
        jnp.einsum("hqk,qhe->khe", score_grad, queries, preferred_element_type=jnp.float32)
        * score_scale
    )
    value_grad = jnp.einsum(
        "hqk,qhe->khe",
        softmaxed.astype(jnp.bfloat16),
        out_heads,
        preferred_element_type=jnp.float32,
    )
    stacked = jnp.stack([key_grad, value_grad], axis=1).reshape(key_len, 2 * local_heads * HD)
    pair_grad = stacked
    query_grad, pair_grad = (query_grad, pair_grad)
    own_pairs = (
        lax.psum_scatter(pair_grad.astype(jnp.bfloat16), "row", scatter_dimension=0, tiled=True)
        .astype(jnp.float32)
        .reshape(tok_rows, 2, local_heads, HD)
    )
    query_pre, key_pre = rotate_back((query_grad, own_pairs[:, 0]))
    mixed_grad = (
        jnp.stack([query_pre, key_pre, own_pairs[:, 1]], axis=2)
        .reshape(tok_rows, 3 * local_heads * HD)
        .astype(jnp.bfloat16)
    )
    qkv_bias_grad = jnp.sum(mixed_grad.astype(jnp.float32), axis=0)
    qkv_weight_grad = jnp.einsum(
        "td,tc->dc", normed, mixed_grad, preferred_element_type=jnp.float32
    )
    norm_part = jnp.einsum(
        "tc,dc->td", mixed_grad, qkv_full, preferred_element_type=jnp.float32
    ) + jnp.einsum("tf,df->td", up_grad, up_full, preferred_element_type=jnp.float32)
    norm_grad = lax.psum(norm_part.astype(jnp.bfloat16), "col").astype(jnp.float32)
    gain_grad = jnp.sum(norm_grad * normal, axis=0)
    shift_grad = jnp.sum(norm_grad, axis=0)
    scaled = norm_grad * ln_gain
    mean_scaled = jnp.mean(scaled, axis=1, keepdims=True)
    mean_mixed = jnp.mean(scaled * normal, axis=1, keepdims=True)
    col_start = lax.axis_index("col") * col_width
    scaled_share = lax.dynamic_slice_in_dim(scaled, col_start, col_width, 1)
    normal_share = lax.dynamic_slice_in_dim(normal, col_start, col_width, 1)
    tokens_grad = inv_scale * (
        scaled_share - mean_scaled - normal_share * mean_mixed
    ) + cotangent.astype(jnp.float32)
    qkv_bias_grad, up_bias_grad, res_bias_grad, gain_grad, shift_grad = (
        lax.psum(qkv_bias_grad.astype(jnp.bfloat16), ("dp", "row")).astype(jnp.float32),
        lax.psum(up_bias_grad.astype(jnp.bfloat16), ("dp", "row")).astype(jnp.float32),
        lax.psum(res_bias_grad.astype(jnp.bfloat16), ("dp", "row")).astype(jnp.float32),
        lax.psum(gain_grad.astype(jnp.bfloat16), ("dp", "row")).astype(jnp.float32),
        lax.psum(shift_grad.astype(jnp.bfloat16), ("dp", "row")).astype(jnp.float32),
    )
    pieces_now = (
        lax.psum_scatter(
            reorder_rows(qkv_weight_grad, row_count, dp_count).astype(jnp.bfloat16),
            ("dp", "row"),
            scatter_dimension=0,
            tiled=True,
        ).astype(jnp.float32),
        lax.psum_scatter(
            reorder_rows(up_weight_grad, row_count, dp_count).astype(jnp.bfloat16),
            ("dp", "row"),
            scatter_dimension=0,
            tiled=True,
        ).astype(jnp.float32),
        lax.psum_scatter(
            reorder_cols(out_grad, row_count, dp_count).astype(jnp.bfloat16),
            ("dp", "row"),
            scatter_dimension=1,
            tiled=True,
        ).astype(jnp.float32),
        lax.psum_scatter(
            reorder_cols(down_grad, row_count, dp_count).astype(jnp.bfloat16),
            ("dp", "row"),
            scatter_dimension=1,
            tiled=True,
        ).astype(jnp.float32),
    )
    qkv_weight_grad, up_weight_grad, out_grad, down_grad = (
        lax.all_gather(pieces_now[0].astype(jnp.bfloat16), "dp", axis=0, tiled=True).astype(
            jnp.float32
        ),
        lax.all_gather(pieces_now[1].astype(jnp.bfloat16), "dp", axis=0, tiled=True).astype(
            jnp.float32
        ),
        lax.all_gather(pieces_now[2].astype(jnp.bfloat16), "dp", axis=1, tiled=True).astype(
            jnp.float32
        ),
        lax.all_gather(pieces_now[3].astype(jnp.bfloat16), "dp", axis=1, tiled=True).astype(
            jnp.float32
        ),
    )
    return (
        output,
        tokens_grad,
        qkv_weight_grad,
        qkv_bias_grad,
        out_grad,
        up_weight_grad,
        up_bias_grad,
        down_grad,
        res_bias_grad,
        gain_grad,
        shift_grad,
    )


SWAP_ROW = [(0, 1), (1, 0)]
SWAP_X = [(0, 2), (2, 0), (1, 3), (3, 1)]
SWAP_CORE = [(0, 1), (1, 0), (2, 3), (3, 2)]


def bf16(values):
    return values.astype(jnp.bfloat16)


def f32(values):
    return values.astype(jnp.float32)


def matmul(left, right, dims=((1,), (0,))):
    return lax.dot_general(left, right, (dims, ((), ())), preferred_element_type=jnp.float32)


def swap_row(values):
    return lax.ppermute(values, "row", SWAP_ROW)


def swap_x(values):
    return lax.ppermute(values, "dp", SWAP_X)


def swap_core(values):
    return lax.ppermute(values, "dp", SWAP_CORE)


def pick(index, first, second):
    return jnp.where(index == 0, first, second)


def pair(index, mine, theirs, axis):
    return pick(
        index,
        jnp.concatenate([mine, theirs], axis=axis),
        jnp.concatenate([theirs, mine], axis=axis),
    )


def after(value, *earlier):
    return lax.optimization_barrier((value,) + earlier)[0]


def rotary_tables(positions):
    lane = jnp.arange(2 * HD, dtype=jnp.int32) % HD
    half_rot = ROT // 2
    frequency = jnp.exp(
        -math.log(rotary_base) * 2.0 * (lane % half_rot).astype(jnp.float32) / ROT
    )
    angle = positions[:, None] * frequency[None, :]
    turned = (lane < ROT)[None, :]
    sines = jnp.sin(angle)
    return (
        jnp.where(turned, jnp.cos(angle), 1.0),
        jnp.where((lane < half_rot)[None, :], -sines, 0.0),
        jnp.where(turned & (lane >= half_rot)[None, :], sines, 0.0),
    )


def turn(values, cosines, sines_low, sines_high):
    width = values.shape[1]
    half_rot = ROT // 2
    return (
        values * cosines
        + pltpu.roll(values, width - half_rot, 1) * sines_low
        + pltpu.roll(values, half_rot, 1) * sines_high
    )


def mixed_kernel(
    normed_ref, weight_ref, bias_ref, cos_ref, low_ref, high_ref, query_ref, keyval_ref
):
    cosines, low, high = cos_ref[...], low_ref[...], high_ref[...]
    rows, half = query_ref.shape
    first = lax.broadcasted_iota(jnp.int32, (rows, 2 * HD), 1) < HD
    scale = HD ** (-0.5)
    mixed = matmul(normed_ref[...], weight_ref[...]) + bias_ref[...]
    for at in range(half // (2 * HD)):
        tiles = [mixed[:, (3 * at + part) * 2 * HD : (3 * at + part + 1) * 2 * HD] for part in range(3)]
        query = jnp.where(first, tiles[0], tiles[1])
        key = jnp.where(first, pltpu.roll(tiles[0], HD, 1), pltpu.roll(tiles[2], HD, 1))
        value = jnp.where(first, tiles[1], tiles[2])
        here = slice(at * 2 * HD, (at + 1) * 2 * HD)
        query_ref[:, here] = bf16(f32(bf16(turn(query, cosines, low, high))) * scale)
        keyval_ref[:, here] = bf16(turn(key, cosines, low, high))
        keyval_ref[:, half + at * 2 * HD : half + (at + 1) * 2 * HD] = bf16(value)


def join_kernel(row_ref, dq_ref, dkv_ref, sent_ref, cos_ref, low_ref, high_ref, out_ref):
    cosines, low, high = cos_ref[...], -low_ref[...], -high_ref[...]
    rows = dq_ref.shape[0]
    half = dq_ref.shape[1]
    first = lax.broadcasted_iota(jnp.int32, (rows, 2 * HD), 1) < HD
    owner = row_ref[0] == 0
    for at in range(half // (2 * HD)):
        here = slice(at * 2 * HD, (at + 1) * 2 * HD)
        there = slice(half + at * 2 * HD, half + (at + 1) * 2 * HD)
        query = turn(dq_ref[:, here], cosines, low, high)
        key = dkv_ref[:, here] + jnp.where(owner, f32(sent_ref[:, here]), 0.0)
        value = dkv_ref[:, there] + jnp.where(owner, f32(sent_ref[:, there]), 0.0)
        key = pltpu.roll(turn(key, cosines, low, high), HD, 1)
        tiles = (jnp.where(first, query, key), jnp.where(first, value, query), jnp.where(first, key, value))
        for part in range(3):
            out_ref[:, (3 * at + part) * 2 * HD : (3 * at + part + 1) * 2 * HD] = bf16(tiles[part])


def tree_kernel(
    parent_ref, row_ref, query_ref, keyval_ref, trunk_ref, grad_ref,
    out_ref, dq_ref, dkv_ref, dtrunk_ref,
    keys, values, dkeys, dvalues,
):
    tree = pl.program_id(0)
    row = row_ref[0]
    rows, half = query_ref.shape
    trunk_len = trunk_ref.shape[0]
    segs = rows // SEG
    trunk_segs = trunk_len // SEG
    seg_count = parent_ref.shape[1]
    first_row = row == 0
    keys[...] = jnp.where(first_row, keyval_ref[:, :half], trunk_ref[:, :half])
    values[...] = jnp.where(first_row, keyval_ref[:, half:], trunk_ref[:, half:])
    dkeys[...] = jnp.zeros_like(dkeys)
    dvalues[...] = jnp.zeros_like(dvalues)
    lane = lax.broadcasted_iota(jnp.int32, (1, half), 1)
    causal = lax.broadcasted_iota(jnp.int32, (SEG, SEG), 0) >= lax.broadcasted_iota(
        jnp.int32, (SEG, SEG), 1
    )
    across = ((1,), (1,))
    down = ((0,), (0,))
    for seg in range(segs):
        here = slice(seg * SEG, (seg + 1) * SEG)
        above = parent_ref[tree, row * segs + seg]
        linked = [above == at for at in range(trunk_segs)]
        for _ in range(seg_count - 2):
            above = jnp.where(above >= 0, parent_ref[tree, jnp.maximum(above, 0)], -1)
            linked = [was | (above == at) for at, was in enumerate(linked)]
        bias = [jnp.where(is_linked, 0.0, masked_fill) for is_linked in linked]
        query, grad = query_ref[here, :], grad_ref[here, :]
        own_key, own_value = keyval_ref[here, :half], keyval_ref[here, half:]
        attended = jnp.zeros((SEG, half), jnp.float32)
        dquery = jnp.zeros((SEG, half), jnp.float32)
        dkey = jnp.zeros((SEG, half), jnp.float32)
        dvalue = jnp.zeros((SEG, half), jnp.float32)
        for head in range(half // HD):
            mine = (lane >= head * HD) & (lane < (head + 1) * HD)
            head_query = jnp.where(mine, query, jnp.zeros_like(query))
            head_grad = jnp.where(mine, grad, jnp.zeros_like(grad))
            scores = [
                matmul(head_query, keys[at * SEG : (at + 1) * SEG, :], across) + bias[at]
                for at in range(trunk_segs)
            ] + [jnp.where(causal, matmul(head_query, own_key, across), masked_fill)]
            top = functools.reduce(jnp.maximum, [jnp.max(s, axis=1, keepdims=True) for s in scores])
            powers = [jnp.exp(s - top) for s in scores]
            total = functools.reduce(jnp.add, [jnp.sum(p, axis=1, keepdims=True) for p in powers])
            probs = [p / total for p in powers]
            low = [bf16(p) for p in probs]
            blocks = [values[at * SEG : (at + 1) * SEG, :] for at in range(trunk_segs)] + [own_value]
            prob_grads = [matmul(head_grad, v, across) for v in blocks]
            delta = functools.reduce(
                jnp.add, [jnp.sum(p * g, axis=1, keepdims=True) for p, g in zip(probs, prob_grads)]
            )
            score_grads = [bf16(p * (g - delta)) for p, g in zip(probs, prob_grads)]
            head_out = functools.reduce(jnp.add, [matmul(p, v) for p, v in zip(low, blocks)])
            attended = jnp.where(mine, head_out, attended)
            key_blocks = [keys[at * SEG : (at + 1) * SEG, :] for at in range(trunk_segs)] + [own_key]
            head_dq = functools.reduce(jnp.add, [matmul(s, u) for s, u in zip(score_grads, key_blocks)])
            dquery = jnp.where(mine, head_dq, dquery)
            dkey = dkey + matmul(score_grads[-1], head_query, down)
            dvalue = dvalue + matmul(low[-1], head_grad, down)
            for at in range(trunk_segs):
                spot = slice(at * SEG, (at + 1) * SEG)
                dkeys[spot, :] += matmul(score_grads[at], head_query, down)
                dvalues[spot, :] += matmul(low[at], head_grad, down)
        out_ref[here, :] = bf16(attended)
        dq_ref[here, :] = dquery * HD ** (-0.5)
        dkv_ref[here, :half] = dkey
        dkv_ref[here, half:] = dvalue
    dtrunk_ref[:, :half] = bf16(dkeys[...])
    dtrunk_ref[:, half:] = bf16(dvalues[...])

    @pl.when(first_row)
    def _():
        dkv_ref[:, :half] += dkeys[...]
        dkv_ref[:, half:] += dvalues[...]


def store_blocks(place_ref, sides, full_ref, own_refs, plain_refs):
    row, slab = place_ref[1], place_ref[2]
    for side, values in enumerate(sides):
        width = values[0].shape[1]
        for source, value in enumerate(values):
            within = source % 2
            here = row == source // 2

            def put(refs):
                if len(refs) == 1:
                    refs[0][side, :, within * width : (within + 1) * width] = value
                else:
                    refs[within][side] = value

            @pl.when(here)
            def _():
                full_ref[side, :, within * width : (within + 1) * width] = value
                put(own_refs)

            @pl.when(jnp.logical_not(here))
            def _():
                put(plain_refs)
                at = (2 + jnp.where(slab == 0, within, 1 - within)) * width
                full_ref[side, :, pl.ds(pl.multiple_of(at, width), width)] = value


def gather_kernel(place_ref, mine_ref, theirs_ref, full_ref, own_ref, plain_ref):
    sides = [[ref[at] for at in range(ref.shape[0])] for ref in (mine_ref, theirs_ref)]
    store_blocks(place_ref, sides, full_ref, [own_ref], [plain_ref])


def norm_kernel(place_ref, gain_ref, bias_ref, mine_ref, theirs_ref, full_ref, *outs):
    normal_ref, scale_ref = outs[4:]
    sides = []
    for side, ref in enumerate((mine_ref, theirs_ref)):
        values = [f32(ref[at]) for at in range(ref.shape[0])]
        features = len(values) * values[0].shape[1]
        mean = functools.reduce(jnp.add, [jnp.sum(v, axis=1, keepdims=True) for v in values]) / features
        centred = [v - mean for v in values]
        square = functools.reduce(jnp.add, [jnp.sum(v * v, axis=1, keepdims=True) for v in centred])
        inv_scale = lax.rsqrt(square / features + norm_epsilon)
        normals = [v * inv_scale for v in centred]
        if side == 0:
            scale_ref[...] = inv_scale
            for source, normal in enumerate(normals):

                @pl.when(place_ref[0] == source)
                def _():
                    normal_ref[...] = normal

        sides.append(
            [
                bf16(normal * gain_ref[source : source + 1, :] + bias_ref[source : source + 1, :])
                for source, normal in enumerate(normals)
            ]
        )
    store_blocks(place_ref, sides, full_ref, outs[:2], outs[2:4])


def pair_rows(rows, width):
    return pl.BlockSpec((2, rows, width), lambda at, *_: (0, at, 0))


def gathered(place, mine, theirs, norm=None):
    blocks, count, width = mine.shape
    rows = SEG if norm is None else SEG // 2
    full = blocks * width
    in_specs = [pl.BlockSpec((blocks, rows, width), lambda at, *_: (0, at, 0))] * 2
    parts = [full // 2] * 2 if norm is None else [width] * 4
    out_specs = [pair_rows(rows, size) for size in [full] + parts]
    out_shape = [
        jax.ShapeDtypeStruct((2, count, size), jnp.bfloat16) for size in [full] + parts
    ]
    operands = [mine, theirs]
    if norm is not None:
        gain = [values.reshape(blocks, width) for values in norm]
        operands = gain + operands
        in_specs = [pl.BlockSpec((blocks, width), lambda at, *_: (0, 0))] * 2 + in_specs
        out_specs = out_specs + [row_block(rows, width), row_block(rows, 1)]
        out_shape = out_shape + [
            jax.ShapeDtypeStruct((count, width), jnp.float32),
            jax.ShapeDtypeStruct((count, 1), jnp.float32),
        ]
    results = pl.pallas_call(
        gather_kernel if norm is None else norm_kernel,
        grid_spec=pltpu.PrefetchScalarGridSpec(
            num_scalar_prefetch=1, grid=(count // rows,), in_specs=in_specs, out_specs=out_specs
        ),
        out_shape=out_shape,
        cost_estimate=pl.CostEstimate(flops=1, bytes_accessed=1, transcendentals=0),
        name="join_blocks" if norm is None else "norm_blocks",
    )(place, *operands)
    last = len(parts) + 1
    return [values.reshape(2 * count, -1) for values in results[:last]] + list(results[last:])


def stack_kernel(place_ref, terms_ref, arrived_ref, out_ref):
    row, slab = place_ref[1], place_ref[2]
    width = out_ref.shape[2]
    for spot in range(4):
        here = slice(spot * width, (spot + 1) * width)
        value = bf16(f32(terms_ref[:, here]) + f32(arrived_ref[:, here]))
        if spot < 2:
            out_ref[2 * row + spot] = value
        else:
            out_ref[2 * (1 - row) + jnp.where(slab == 0, spot - 2, 3 - spot)] = value


def stacked(place, terms, arrived, blocks):
    count, full = arrived.shape
    rows = SEG
    width = full // blocks
    return pl.pallas_call(
        stack_kernel,
        grid_spec=pltpu.PrefetchScalarGridSpec(
            num_scalar_prefetch=1,
            grid=(count // rows,),
            in_specs=[row_block(rows, full), row_block(rows, full)],
            out_specs=pl.BlockSpec((blocks, rows, width), lambda at, *_: (0, at, 0)),
        ),
        out_shape=jax.ShapeDtypeStruct((blocks, count, width), jnp.bfloat16),
        cost_estimate=pl.CostEstimate(flops=1, bytes_accessed=1, transcendentals=0),
        name="stack_blocks",
    )(place, terms, arrived)


def cast_rows_kernel(place_ref, master_ref, own_ref, send_ref):
    value = bf16(master_ref[...])
    own_ref[...] = value
    half = pl.num_programs(0) // 2

    @pl.when(pl.program_id(0) // half == place_ref[2])
    def _():
        send_ref[...] = value


def cast_cols_kernel(place_ref, master_ref, own_ref, send_ref):
    value = bf16(master_ref[...])
    own_ref[...] = value
    half = value.shape[1] // 2
    send_ref[...] = jnp.where(place_ref[2] == 0, value[:, :half], value[:, half:])


def cast_weight(place, master, axis):
    height, width = master.shape
    rows = min(2 * SEG, master.shape[0] // 4)
    if axis == 0:
        width = width // 2
        steps = height // rows
        half = steps // 2
        specs = [
            pl.BlockSpec((rows, width), lambda at, place_ref: (at, place_ref[3])),
            pl.BlockSpec((rows, width), lambda at, place_ref: (at, 0)),
            pl.BlockSpec(
                (rows, width), lambda at, place_ref: (jnp.clip(at - half * place_ref[2], 0, half - 1), 0)
            ),
        ]
        send = (height // 2, width)
        whole = (2 * height, width)
    else:
        height = height // 2
        steps = height // rows
        specs = [
            pl.BlockSpec((rows, width), lambda at, place_ref: (at + steps * place_ref[3], 0)),
            pl.BlockSpec((rows, width), lambda at, place_ref: (at, 0)),
            pl.BlockSpec((rows, width // 2), lambda at, place_ref: (at, 0)),
        ]
        send = (height, width // 2)
        whole = (height, 2 * width)
    return pl.pallas_call(
        cast_rows_kernel if axis == 0 else cast_cols_kernel,
        grid_spec=pltpu.PrefetchScalarGridSpec(
            num_scalar_prefetch=1, grid=(steps,), in_specs=specs[:1], out_specs=specs[1:]
        ),
        out_shape=[
            jax.ShapeDtypeStruct(whole, jnp.bfloat16),
            jax.ShapeDtypeStruct(send, jnp.bfloat16),
        ],
        cost_estimate=pl.CostEstimate(flops=1, bytes_accessed=1, transcendentals=0),
        name="cast_weight",
    )(place, master)


def settle_store(axis, place_ref, mine, theirs, out_ref):
    if axis == 0:
        out_ref[place_ref[3]] = mine
        out_ref[1 - place_ref[3]] = theirs
    else:
        width = mine.shape[1]
        first = place_ref[3] == 0
        out_ref[:, :width] = jnp.where(first, mine, theirs)
        out_ref[:, width:] = jnp.where(first, theirs, mine)


def settle_kernel(axis, place_ref, mine_ref, theirs_ref, *refs):
    settle_store(axis, place_ref, f32(mine_ref[...]), f32(theirs_ref[...]), refs[-1])


def settle_both_kernel(axis, place_ref, *refs):
    for at in range(2):

        @pl.when(pl.program_id(0) == at)
        def _():
            settle_store(axis, place_ref, f32(refs[2 * at][...]), f32(refs[2 * at + 1][...]), refs[-1])


def settle_both(place, first, last, shape, axis):
    rows, width = first[0].shape
    if axis == 0:
        shape = (2, shape[0] // 2, width)
        out_spec = pl.BlockSpec((2, rows, width), lambda at, *_: (0, at, 0))
    else:
        out_spec = pl.BlockSpec((rows, 2 * width), lambda at, *_: (at, 0))
    return pl.pallas_call(
        functools.partial(settle_both_kernel, axis),
        grid_spec=pltpu.PrefetchScalarGridSpec(
            num_scalar_prefetch=1,
            grid=(2,),
            in_specs=[pl.BlockSpec((rows, width), lambda *_: (0, 0))] * 4,
            out_specs=out_spec,
        ),
        out_shape=jax.ShapeDtypeStruct(shape, jnp.float32),
        cost_estimate=pl.CostEstimate(flops=1, bytes_accessed=1, transcendentals=0),
        name="settle_both",
    )(place, *first, *last)


def settle(place, mine, theirs, shape, axis, offset, dest=None):
    rows, width = mine.shape
    at = offset // rows
    whole = pl.BlockSpec((rows, width), lambda *_: (0, 0))
    if axis == 0:
        shape = (2, shape[0] // 2, width)
        out_spec = pl.BlockSpec((2, rows, width), lambda *_: (0, at, 0))
    else:
        out_spec = pl.BlockSpec((rows, 2 * width), lambda *_: (at, 0))
    in_specs = [whole, whole]
    operands = [place, mine, theirs]
    aliases = {}
    if dest is not None:
        in_specs.append(pl.BlockSpec(memory_space=pl.ANY))
        operands.append(dest)
        aliases = {3: 0}
    return pl.pallas_call(
        functools.partial(settle_kernel, axis),
        grid_spec=pltpu.PrefetchScalarGridSpec(
            num_scalar_prefetch=1, grid=(1,), in_specs=in_specs, out_specs=out_spec
        ),
        out_shape=jax.ShapeDtypeStruct(shape, jnp.float32),
        input_output_aliases=aliases,
        cost_estimate=pl.CostEstimate(flops=1, bytes_accessed=1, transcendentals=0),
        name="settle",
    )(*operands)


def row_block(rows, width):
    return pl.BlockSpec((rows, width), lambda at, *_: (at, 0))


def mixed_heads(normed, weight, bias, tables):
    count, depth = normed.shape
    width = weight.shape[1]
    rows = SEG
    return pl.pallas_call(
        mixed_kernel,
        grid=(count // rows,),
        in_specs=[
            row_block(rows, depth),
            pl.BlockSpec((depth, width), lambda at: (0, 0)),
            pl.BlockSpec((1, width), lambda at: (0, 0)),
        ]
        + [row_block(rows, 2 * HD)] * 3,
        out_specs=[row_block(rows, width // 3), row_block(rows, 2 * width // 3)],
        out_shape=[
            jax.ShapeDtypeStruct((count, width // 3), jnp.bfloat16),
            jax.ShapeDtypeStruct((count, 2 * width // 3), jnp.bfloat16),
        ],
        cost_estimate=pl.CostEstimate(flops=1, bytes_accessed=1, transcendentals=0),
        name="mixed_heads",
    )(normed, weight, bias.reshape(1, width), *tables)


def join_heads(row, dq, dkv, sent, tables):
    count, half = dq.shape
    rows = 2 * SEG
    return pl.pallas_call(
        join_kernel,
        grid_spec=pltpu.PrefetchScalarGridSpec(
            num_scalar_prefetch=1,
            grid=(count // rows,),
            in_specs=[row_block(rows, half), row_block(rows, 2 * half), row_block(rows, 2 * half)]
            + [row_block(rows, 2 * HD)] * 3,
            out_specs=row_block(rows, 3 * half),
        ),
        out_shape=jax.ShapeDtypeStruct((count, 3 * half), jnp.bfloat16),
        cost_estimate=pl.CostEstimate(flops=1, bytes_accessed=1, transcendentals=0),
        name="join_heads",
    )(row, dq, dkv, sent, *tables)


def tree_attention(parents, row, query, keyval, trunk, grad):
    trees = parents.shape[0]
    count, half = query.shape
    rows = count // trees
    keys = trunk.shape[0] // trees
    pairs = count * (keys + SEG) * (half // HD)
    return pl.pallas_call(
        tree_kernel,
        grid_spec=pltpu.PrefetchScalarGridSpec(
            num_scalar_prefetch=2,
            grid=(trees,),
            in_specs=[
                row_block(rows, half),
                row_block(rows, 2 * half),
                row_block(keys, 2 * half),
                row_block(rows, half),
            ],
            out_specs=[
                row_block(rows, half),
                row_block(rows, half),
                row_block(rows, 2 * half),
                row_block(keys, 2 * half),
            ],
            scratch_shapes=[pltpu.VMEM((keys, half), jnp.bfloat16)] * 2
            + [pltpu.VMEM((keys, half), jnp.float32)] * 2,
        ),
        out_shape=[
            jax.ShapeDtypeStruct((count, half), jnp.bfloat16),
            jax.ShapeDtypeStruct((count, half), jnp.float32),
            jax.ShapeDtypeStruct((count, 2 * half), jnp.float32),
            jax.ShapeDtypeStruct((trees * keys, 2 * half), jnp.bfloat16),
        ],
        cost_estimate=pl.CostEstimate(flops=1, bytes_accessed=1, transcendentals=0),
        name="tree_attention",
    )(parents, row, query, keyval, trunk, grad)


def paired_device(
    tokens,
    parent,
    depth,
    w_qkv,
    b_qkv,
    w_out,
    w_up,
    b_up,
    w_down,
    b_res,
    ln_gain,
    ln_bias,
    cotangent,
):
    count, width = tokens.shape
    row = lax.axis_index("row")
    col = lax.axis_index("col")
    core = lax.axis_index("dp") % 2
    slab = lax.axis_index("dp") // 2
    cols = lax.axis_size("col")
    half = 2 * width
    heads_width = w_out.shape[0] // 2
    hidden = w_up.shape[1] // 2
    place = jnp.stack([col, row, slab, core]).astype(jnp.int32)
    row_table = jnp.reshape(row, (1,)).astype(jnp.int32)
    down_dims = ((0,), (0,))
    across = ((1,), (1,))

    def part(values, at, size, axis):
        return lax.dynamic_slice_in_dim(values, at * size, size, axis)

    def exchange(stack):
        return lax.all_to_all(stack, "col", 0, 0, tiled=True)

    done = ()

    def step(run, *inputs):
        nonlocal done
        inputs, _ = lax.optimization_barrier((inputs, done))
        result = run(*inputs)
        done = result
        return result

    def wait(value):
        return step(lambda arrived: arrived, value)

    tokens_near = lax.all_gather(tokens, "col", axis=0)
    grad_stack = jnp.broadcast_to(cotangent[None], (cols,) + cotangent.shape)

    def ready(master, axis):
        whole, send = step(lambda weight: cast_weight(place, weight, axis), master)
        return whole, swap_row(send)

    def fill(whole, part_in, axis, last):
        at = whole.shape[axis] // 2 + (part_in.shape[axis] if last else 0)
        return step(lambda a, b: lax.dynamic_update_slice_in_dim(a, b, at, axis), whole, part_in)

    tables = jnp.concatenate([parent, depth], axis=0)
    tables = jnp.stack([tables, swap_core(tables)])
    parents = tables[:, 0]
    segs = count // SEG
    token = jnp.arange(count, dtype=jnp.int32)
    levels = jnp.zeros((2, count), jnp.float32)
    for seg in range(segs):
        level = lax.dynamic_slice_in_dim(tables[:, 1], row * segs + seg, 1, 1).astype(jnp.float32)
        levels = jnp.where((token // SEG == seg)[None, :], level, levels)
    positions = (levels * SEG + (token % SEG).astype(jnp.float32)[None, :]).reshape(2 * count)
    rotary = rotary_tables(positions)

    qkv_whole, qkv_row = ready(w_qkv, 0)
    up_whole, up_row = ready(w_up, 0)
    qkv_row = wait(qkv_row)
    qkv_x = swap_x(qkv_row)
    out_whole, out_row = ready(w_out, 1)
    down_whole, down_row = ready(w_down, 1)
    rotary = step(lambda *tables: tables, *rotary)
    qkv_whole = fill(qkv_whole, qkv_row, 0, False)
    up_row = wait(up_row)
    up_x = swap_x(up_row)
    qkv_x = wait(qkv_x)
    tokens_near = wait(tokens_near)
    tokens_far = swap_core(tokens_near)
    grad_near = exchange(after(grad_stack, tokens_near))
    up_whole = fill(up_whole, up_row, 0, False)
    normed, own_a, own_b, plain_a, plain_b, normal, inv_scale = step(
        lambda mine, theirs: gathered(place, mine, theirs, (ln_gain, ln_bias)), tokens_near, tokens_far
    )
    qkv_full = fill(qkv_whole, qkv_x, 0, True)
    query, keyval = step(
        lambda left, right: mixed_heads(left, right, part(b_qkv, core, 3 * heads_width, 0), rotary),
        normed, qkv_full,
    )
    trunk = lax.ppermute(keyval, "row", [(0, 1)])
    root = math.sqrt(2.0 / math.pi)

    def feed(left, right):
        hidden_up = matmul(left, right) + part(b_up, core, hidden, 0)
        squared = hidden_up * hidden_up
        bend = jnp.tanh(root * (hidden_up + 0.044715 * squared * hidden_up))
        return bf16(0.5 * hidden_up * (1.0 + bend)), bf16(
            0.5 * (1.0 + bend)
            + 0.5 * hidden_up * (1.0 - bend * bend) * root * (1.0 + 3.0 * 0.044715 * squared)
        )

    out_row = wait(out_row)
    out_x = swap_x(out_row)
    up_full = fill(up_whole, up_x, 0, True)
    down_row = wait(down_row)
    down_x = swap_x(down_row)
    activated, slope = step(feed, normed, up_full)
    out_whole = fill(out_whole, out_row, 1, False)
    down_whole = fill(down_whole, down_row, 1, False)
    out_full = fill(out_whole, out_x, 1, True)
    trunk = wait(trunk)
    grad_near = wait(grad_near)
    grad_far = swap_core(grad_near)
    grad, grad_own, grad_plain = step(lambda mine, theirs: gathered(place, mine, theirs), grad_near, grad_far)

    def cut(values, at):
        size = values.shape[1] // 2
        return values[:, at * size : (at + 1) * size]

    def leaving(left, right):
        return step(lambda a, b: bf16(matmul(a, b, down_dims)), left, right)

    def staying(left, right, sent):
        return step(lambda a, b, c: bf16(matmul(a, b, down_dims) + f32(c)), left, right, sent)

    def crossed(both, arrived):
        mine = step(lambda a, b: bf16(f32(a) + f32(b)), both, arrived)
        return mine, swap_core(mine)

    def settled(pieces, shape, axis, offset, dest):
        operands = pieces if dest is None else pieces + (dest,)
        return step(
            lambda mine, theirs, *rest: settle(place, mine, theirs, shape, axis, offset, *rest), *operands
        )

    down_sent_a = swap_row(leaving(cut(activated, 0), grad_plain))
    down_sent_b = swap_row(leaving(cut(activated, 1), grad_plain))
    out_heads = step(lambda a, b: bf16(matmul(a, b, across)), grad, out_full)
    attended, query_grad, own_grad, trunk_grad = step(
        lambda *operands: tree_attention(parents, row_table, *operands), query, keyval, trunk, out_heads
    )
    trunk_sent = lax.ppermute(trunk_grad, "row", [(1, 0)])
    down_both_a = staying(cut(activated, 0), grad_own, down_sent_a)
    down_cross_a = swap_x(down_both_a)
    down_full = fill(down_whole, down_x, 1, True)
    branch_terms = step(
        lambda a, b, c, d: bf16(matmul(a, b) + matmul(c, d)), attended, out_full, activated, down_full
    )
    branch_near = swap_core(branch_terms[count:])
    up_grad = step(lambda a, b, c: bf16(matmul(a, b, across) * f32(c)), grad, down_full, slope)
    up_sent_a = swap_row(leaving(plain_a, up_grad))
    down_both_b = staying(cut(activated, 1), grad_own, down_sent_b)
    down_cross_b = swap_x(down_both_b)
    up_sent_b = swap_row(leaving(plain_b, up_grad))
    down_a = crossed(down_both_a, down_cross_a)
    branch = lax.psum_scatter(
        step(lambda a, b: stacked(place, a, b, cols), branch_terms, branch_near), "col", tiled=False
    )
    mixed_grad = step(
        lambda *operands: join_heads(row_table, *operands, rotary), query_grad, own_grad, trunk_sent
    )
    qkv_sent_a = swap_row(leaving(plain_a, mixed_grad))
    down_b = crossed(down_both_b, down_cross_b)
    qkv_sent_b = swap_row(leaving(plain_b, mixed_grad))
    norm_terms = step(
        lambda a, b, c, d: bf16(matmul(a, b, across) + matmul(c, d, across)),
        mixed_grad, qkv_full, up_grad, up_full,
    )
    up_both_a = staying(own_a, up_grad, up_sent_a)
    up_cross_a = swap_x(up_both_a)
    norm_near = swap_core(step(lambda terms: terms[count:], norm_terms))
    output = step(lambda parts, block: bf16(f32(block) + f32(parts) + b_res), branch, tokens)
    norm_parts = exchange(step(lambda a, b: stacked(place, a, b, cols), norm_terms, norm_near))
    out_sent = swap_row(leaving(attended, grad_plain))
    down_grad = step(lambda first, last: settle_both(place, first, last, w_down.shape, 0), down_a, down_b)
    up_a = crossed(up_both_a, up_cross_a)
    up_both_b = staying(own_b, up_grad, up_sent_b)
    up_cross_b = swap_x(up_both_b)
    out_both = staying(attended, grad_own, out_sent)
    out_cross = swap_x(out_both)
    qkv_both_a = staying(own_a, mixed_grad, qkv_sent_a)
    qkv_cross_a = swap_x(qkv_both_a)
    up_b = crossed(up_both_b, up_cross_b)
    out_mine = crossed(out_both, out_cross)
    gain_here = part(ln_gain, col, width, 0)

    def norm_sums(parts):
        total = jnp.sum(f32(parts), axis=0)
        scaled = total * gain_here
        return (
            total,
            jnp.stack([jnp.sum(scaled, axis=1), jnp.sum(scaled * normal, axis=1)]),
            jnp.sum(total * normal, axis=0),
            jnp.sum(total, axis=0),
        )

    norm_grad, sums, gain_sum, shift_sum = step(norm_sums, norm_parts)
    up_weight_grad = step(lambda first, last: settle_both(place, first, last, w_up.shape, 1), up_a, up_b)

    def line_step(values, bit):
        return lax.ppermute(values, "col", [(at, at ^ bit) for at in range(cols)])

    small = jnp.concatenate(
        [
            jnp.sum(f32(up_grad), axis=0),
            jnp.sum(f32(mixed_grad), axis=0),
            jnp.sum(f32(cotangent), axis=0),
            gain_sum,
            shift_sum,
        ]
    ).reshape(-1, 128)
    shared_at = (hidden + 3 * heads_width) // 128
    res_at = width // 128
    sums_next = line_step(sums, 1)
    small_other = swap_core(small)
    sums, shared = step(
        lambda sums, arrived, small, other: (sums + arrived, (small + other)[shared_at:]),
        sums, sums_next, small, small_other,
    )
    sums_next = line_step(sums, 2)
    ends = shared[res_at:][None]
    ends_next = line_step(ends, 1)
    qkv_both_b = staying(own_b, mixed_grad, qkv_sent_b)
    qkv_cross_b = swap_x(qkv_both_b)
    ends = step(lambda ends, arrived: pair(col % 2, ends, arrived, 0), ends, ends_next)
    ends_next = line_step(ends, 2)
    qkv_a = crossed(qkv_both_a, qkv_cross_a)
    out_grad = settled(out_mine, w_out.shape, 0, 0, None)
    sums = (sums + sums_next) / (cols * width)
    tokens_grad = step(
        lambda sums, total: inv_scale
        * (total * gain_here - sums[0][:, None] - normal * sums[1][:, None])
        + f32(cotangent),
        sums, norm_grad,
    )

    def gather_small(small, other, shared, ends, arrived):
        return jnp.concatenate(
            [
                pair(core, small[: hidden // 128], other[: hidden // 128], 0),
                pair(core, small[hidden // 128 : shared_at], other[hidden // 128 : shared_at], 0),
                shared[:res_at],
                pair(col // 2, ends, arrived, 0).reshape(-1, 128),
            ]
        )

    small = step(gather_small, small, small_other, shared, ends, ends_next)
    small_next = swap_row(small)
    qkv_b = crossed(qkv_both_b, qkv_cross_b)
    small = step(jnp.add, small, small_next)
    small_next = swap_x(small)
    qkv_weight_grad = step(
        lambda first, last: settle_both(place, first, last, w_qkv.shape, 1), qkv_a, qkv_b
    )
    small = step(jnp.add, small, small_next)

    bounds = [0, 2 * hidden // 128, (2 * hidden + 6 * heads_width) // 128]
    bounds.append(bounds[-1] + res_at)
    up_bias_grad = small[: bounds[1]].reshape(-1)
    qkv_bias_grad = small[bounds[1] : bounds[2]].reshape(-1)
    res_bias_grad = small[bounds[2] : bounds[3]].reshape(-1)
    ends = small[bounds[3] :].reshape(cols, 2, width)
    gain_grad = ends[:, 0].reshape(-1)
    shift_grad = ends[:, 1].reshape(-1)
    return (
        output,
        tokens_grad,
        qkv_weight_grad,
        qkv_bias_grad,
        out_grad.reshape(w_out.shape),
        up_weight_grad,
        up_bias_grad,
        down_grad.reshape(w_down.shape),
        res_bias_grad,
        gain_grad,
        shift_grad,
    )


def solution(mesh):
    sizes = (mesh.shape["dp"], mesh.shape["row"], mesh.shape["col"])
    per_device = paired_device if sizes == (4, 2, 4) else general_device
    return jax.shard_map(
        per_device,
        mesh=mesh,
        in_specs=(
            P(("dp", "row"), "col"),
            P("dp", None),
            P("dp", None),
            P("row", "col"),
            P("col"),
            P("col", "row"),
            P("row", "col"),
            P("col"),
            P("col", "row"),
            P("col"),
            P(),
            P(),
            P(("dp", "row"), "col"),
        ),
        out_specs=(
            P(("dp", "row"), "col"),
            P(("dp", "row"), "col"),
            P("row", "col"),
            P("col"),
            P("col", "row"),
            P("row", "col"),
            P("col"),
            P("col", "row"),
            P("col"),
            P(),
            P(),
        ),
        check_vma=False,
    )
```

```python
import functools
import math

import jax
import jax.numpy as jnp
from jax import lax
from jax.experimental import pallas as pl
from jax.experimental.pallas import tpu as pltpu
from jax.sharding import PartitionSpec as P

HD = 64
ROT = 32
SEG = 256


norm_epsilon = 1e-05
masked_fill = -1e30
rotary_base = 10000.0


def precise_dot(left, right):
    return jnp.dot(left, right, precision=lax.Precision.HIGHEST, preferred_element_type=jnp.float32)


def ancestry(parent_row):
    seg_count = parent_row.shape[0]
    labels = jnp.arange(seg_count, dtype=jnp.int32)
    identity = jnp.eye(seg_count, dtype=jnp.float32)
    parent_hot = (parent_row[:, None] == labels[None, :]).astype(jnp.float32)

    def extend(rounds, reachable):
        return jnp.minimum(identity + precise_dot(parent_hot, reachable), 1.0)

    return lax.fori_loop(0, seg_count, extend, identity)


def rotate(values, cosines, sines):
    half_rot = ROT // 2
    former = values[..., :half_rot]
    latter = values[..., half_rot:ROT]
    return jnp.concatenate(
        [former * cosines - latter * sines, latter * cosines + former * sines, values[..., ROT:]],
        axis=-1,
    )


def angles_of(positions):
    frequency = jnp.exp(
        -math.log(rotary_base) * 2.0 * jnp.arange(ROT // 2, dtype=jnp.float32) / ROT
    )
    phase_angle = positions[:, None] * frequency[None, :]
    return (jnp.cos(phase_angle)[:, None, :], jnp.sin(phase_angle)[:, None, :])


def reorder_rows(gradient, row_count, dp_count):
    leading = gradient.shape[0]
    blocked = gradient.reshape(
        row_count, dp_count, leading // (row_count * dp_count), gradient.shape[1]
    )
    return jnp.transpose(blocked, (1, 0, 2, 3)).reshape(leading, gradient.shape[1])


def reorder_cols(gradient, row_count, dp_count):
    trailing = gradient.shape[1]
    blocked = gradient.reshape(
        gradient.shape[0], row_count, dp_count, trailing // (row_count * dp_count)
    )
    return jnp.transpose(blocked, (0, 2, 1, 3)).reshape(gradient.shape[0], trailing)


def general_device(
    tokens,
    parent,
    depth,
    w_qkv,
    b_qkv,
    w_out,
    w_up,
    b_up,
    w_down,
    b_res,
    ln_gain,
    ln_bias,
    cotangent,
):
    tok_rows = tokens.shape[0]
    col_width = tokens.shape[1]
    row_count = lax.axis_size("row")
    dp_count = lax.axis_size("dp")
    row_start = lax.axis_index("row") * tok_rows
    local_heads = w_out.shape[0] // HD
    seg_count = parent.shape[1]
    labels = jnp.arange(seg_count, dtype=jnp.int32)
    reachable = ancestry(parent[0])
    query_index = row_start + jnp.arange(tok_rows, dtype=jnp.int32)
    query_seg = query_index // SEG
    query_hot = (query_seg[:, None] == labels[None, :]).astype(jnp.float32)
    query_reach = precise_dot(query_hot, reachable)
    levels = precise_dot(query_hot, depth[0].astype(jnp.float32)[:, None])[:, 0]
    positions = levels * SEG + (query_index % SEG).astype(jnp.float32)
    cosines, sines = angles_of(positions)
    score_scale = HD ** (-0.5)

    def permit(key_len):
        key_index = jnp.arange(key_len, dtype=jnp.int32)
        key_seg = key_index // SEG
        key_hot = (key_seg[:, None] == labels[None, :]).astype(jnp.float32)
        linked = precise_dot(query_reach, key_hot.T) > 0.5
        return linked & (
            (query_seg[:, None] != key_seg[None, :]) | (query_index[:, None] >= key_index[None, :])
        )

    whole = lax.all_gather(tokens, "col", axis=1, tiled=True).astype(jnp.float32)
    centred = whole - jnp.mean(whole, axis=1, keepdims=True)
    inv_scale = lax.rsqrt(jnp.mean(centred * centred, axis=1, keepdims=True) + norm_epsilon)
    normal = centred * inv_scale
    normed = (normal * ln_gain + ln_bias).astype(jnp.bfloat16)
    qkv_full, up_full, out_full, down_full = (
        lax.all_gather(w_qkv.astype(jnp.bfloat16), "row", axis=0, tiled=True),
        lax.all_gather(w_up.astype(jnp.bfloat16), "row", axis=0, tiled=True),
        lax.all_gather(w_out.astype(jnp.bfloat16), "row", axis=1, tiled=True),
        lax.all_gather(w_down.astype(jnp.bfloat16), "row", axis=1, tiled=True),
    )
    mixed = (jnp.dot(normed, qkv_full, preferred_element_type=jnp.float32) + b_qkv).reshape(
        tok_rows, local_heads, 3, HD
    )

    def rotate_pair(query_pre, key_pre):
        return (rotate(query_pre, cosines, sines), rotate(key_pre, cosines, sines))

    rotated, rotate_back = jax.vjp(rotate_pair, mixed[:, :, 0], mixed[:, :, 1])
    queries = rotated[0].astype(jnp.bfloat16)
    key_rows = rotated[1].astype(jnp.bfloat16)
    value_rows = mixed[:, :, 2].astype(jnp.bfloat16)
    key_flat = key_rows.reshape(tok_rows, local_heads * HD)
    value_flat = value_rows.reshape(tok_rows, local_heads * HD)

    def scores_for(key_part):
        raw_scores = (
            jnp.einsum("qhe,khe->hqk", queries, key_part, preferred_element_type=jnp.float32)
            * score_scale
        )
        allowed = permit(key_part.shape[0])
        return (jnp.where(allowed[None], raw_scores, masked_fill), allowed)

    pieces = (
        lax.all_gather(key_flat, "row", axis=0, tiled=True),
        lax.all_gather(value_flat, "row", axis=0, tiled=True),
    )
    running_top = jnp.full((local_heads, tok_rows), masked_fill, jnp.float32)
    key_len = pieces[0].shape[0]
    key_part = pieces[0].reshape(key_len, local_heads, HD)
    value_part = pieces[1].reshape(key_len, local_heads, HD)
    scores, allowed = scores_for(key_part)
    new_top = jnp.maximum(running_top, jnp.max(scores, axis=2))
    exponent = jnp.where(allowed[None], jnp.exp(scores - new_top[:, :, None]), 0.0)
    running_sum = jnp.sum(exponent, axis=2)
    weighted = jnp.einsum(
        "hqk,khe->hqe",
        exponent.astype(jnp.bfloat16),
        value_part,
        preferred_element_type=jnp.float32,
    )
    running_top, running_sum, weighted = (new_top, running_sum, weighted)
    log_total = running_top + jnp.log(running_sum)
    attn_exact = weighted / running_sum[:, :, None]
    attended = (
        jnp.transpose(attn_exact, (1, 0, 2))
        .reshape(tok_rows, local_heads * HD)
        .astype(jnp.bfloat16)
    )
    hidden_up = jnp.dot(normed, up_full, preferred_element_type=jnp.float32) + b_up
    activated, gelu_back = jax.vjp(functools.partial(jax.nn.gelu, approximate=True), hidden_up)
    activated = activated.astype(jnp.bfloat16)
    branch_terms = jnp.dot(attended, out_full, preferred_element_type=jnp.float32) + jnp.dot(
        activated, down_full, preferred_element_type=jnp.float32
    )
    branch = lax.psum_scatter(
        branch_terms.astype(jnp.bfloat16), "col", scatter_dimension=1, tiled=True
    ).astype(jnp.float32)
    output = (tokens.astype(jnp.float32) + branch + b_res).astype(jnp.bfloat16)
    grad_full = lax.all_gather(cotangent, "col", axis=1, tiled=True)
    res_bias_grad = jnp.sum(cotangent.astype(jnp.float32), axis=0)
    down_grad = jnp.einsum("tf,td->fd", activated, grad_full, preferred_element_type=jnp.float32)
    out_grad = jnp.einsum("te,td->ed", attended, grad_full, preferred_element_type=jnp.float32)
    act_grad = jnp.einsum("td,fd->tf", grad_full, down_full, preferred_element_type=jnp.float32)
    up_grad = gelu_back(act_grad)[0].astype(jnp.bfloat16)
    attn_grad = jnp.einsum(
        "td,ed->te", grad_full, out_full, preferred_element_type=jnp.float32
    ).astype(jnp.bfloat16)
    up_bias_grad = jnp.sum(up_grad.astype(jnp.float32), axis=0)
    up_weight_grad = jnp.einsum("td,tf->df", normed, up_grad, preferred_element_type=jnp.float32)
    out_heads = attn_grad.reshape(tok_rows, local_heads, HD)
    delta_sum = jnp.einsum("qhe,hqe->hq", out_heads.astype(jnp.float32), attn_exact)
    pieces = (
        lax.all_gather(key_flat, "row", axis=0, tiled=True),
        lax.all_gather(value_flat, "row", axis=0, tiled=True),
    )
    key_len = pieces[0].shape[0]
    key_part = pieces[0].reshape(key_len, local_heads, HD)
    value_part = pieces[1].reshape(key_len, local_heads, HD)
    scores, allowed = scores_for(key_part)
    softmaxed = jnp.where(allowed[None], jnp.exp(scores - log_total[:, :, None]), 0.0)
    prob_grad = jnp.einsum(
        "qhe,khe->hqk", out_heads, value_part, preferred_element_type=jnp.float32
    )
    score_grad = (softmaxed * (prob_grad - delta_sum[:, :, None])).astype(jnp.bfloat16)
    query_grad = (
        jnp.einsum("hqk,khe->qhe", score_grad, key_part, preferred_element_type=jnp.float32)
        * score_scale
    )
    key_grad = (
        jnp.einsum("hqk,qhe->khe", score_grad, queries, preferred_element_type=jnp.float32)
        * score_scale
    )
    value_grad = jnp.einsum(
        "hqk,qhe->khe",
        softmaxed.astype(jnp.bfloat16),
        out_heads,
        preferred_element_type=jnp.float32,
    )
    stacked = jnp.stack([key_grad, value_grad], axis=1).reshape(key_len, 2 * local_heads * HD)
    pair_grad = stacked
    query_grad, pair_grad = (query_grad, pair_grad)
    own_pairs = (
        lax.psum_scatter(pair_grad.astype(jnp.bfloat16), "row", scatter_dimension=0, tiled=True)
        .astype(jnp.float32)
        .reshape(tok_rows, 2, local_heads, HD)
    )
    query_pre, key_pre = rotate_back((query_grad, own_pairs[:, 0]))
    mixed_grad = (
        jnp.stack([query_pre, key_pre, own_pairs[:, 1]], axis=2)
        .reshape(tok_rows, 3 * local_heads * HD)
        .astype(jnp.bfloat16)
    )
    qkv_bias_grad = jnp.sum(mixed_grad.astype(jnp.float32), axis=0)
    qkv_weight_grad = jnp.einsum(
        "td,tc->dc", normed, mixed_grad, preferred_element_type=jnp.float32
    )
    norm_part = jnp.einsum(
        "tc,dc->td", mixed_grad, qkv_full, preferred_element_type=jnp.float32
    ) + jnp.einsum("tf,df->td", up_grad, up_full, preferred_element_type=jnp.float32)
    norm_grad = lax.psum(norm_part.astype(jnp.bfloat16), "col").astype(jnp.float32)
    gain_grad = jnp.sum(norm_grad * normal, axis=0)
    shift_grad = jnp.sum(norm_grad, axis=0)
    scaled = norm_grad * ln_gain
    mean_scaled = jnp.mean(scaled, axis=1, keepdims=True)
    mean_mixed = jnp.mean(scaled * normal, axis=1, keepdims=True)
    col_start = lax.axis_index("col") * col_width
    scaled_share = lax.dynamic_slice_in_dim(scaled, col_start, col_width, 1)
    normal_share = lax.dynamic_slice_in_dim(normal, col_start, col_width, 1)
    tokens_grad = inv_scale * (
        scaled_share - mean_scaled - normal_share * mean_mixed
    ) + cotangent.astype(jnp.float32)
    qkv_bias_grad, up_bias_grad, res_bias_grad, gain_grad, shift_grad = (
        lax.psum(qkv_bias_grad.astype(jnp.bfloat16), ("dp", "row")).astype(jnp.float32),
        lax.psum(up_bias_grad.astype(jnp.bfloat16), ("dp", "row")).astype(jnp.float32),
        lax.psum(res_bias_grad.astype(jnp.bfloat16), ("dp", "row")).astype(jnp.float32),
        lax.psum(gain_grad.astype(jnp.bfloat16), ("dp", "row")).astype(jnp.float32),
        lax.psum(shift_grad.astype(jnp.bfloat16), ("dp", "row")).astype(jnp.float32),
    )
    pieces_now = (
        lax.psum_scatter(
            reorder_rows(qkv_weight_grad, row_count, dp_count).astype(jnp.bfloat16),
            ("dp", "row"),
            scatter_dimension=0,
            tiled=True,
        ).astype(jnp.float32),
        lax.psum_scatter(
            reorder_rows(up_weight_grad, row_count, dp_count).astype(jnp.bfloat16),
            ("dp", "row"),
            scatter_dimension=0,
            tiled=True,
        ).astype(jnp.float32),
        lax.psum_scatter(
            reorder_cols(out_grad, row_count, dp_count).astype(jnp.bfloat16),
            ("dp", "row"),
            scatter_dimension=1,
            tiled=True,
        ).astype(jnp.float32),
        lax.psum_scatter(
            reorder_cols(down_grad, row_count, dp_count).astype(jnp.bfloat16),
            ("dp", "row"),
            scatter_dimension=1,
            tiled=True,
        ).astype(jnp.float32),
    )
    qkv_weight_grad, up_weight_grad, out_grad, down_grad = (
        lax.all_gather(pieces_now[0].astype(jnp.bfloat16), "dp", axis=0, tiled=True).astype(
            jnp.float32
        ),
        lax.all_gather(pieces_now[1].astype(jnp.bfloat16), "dp", axis=0, tiled=True).astype(
            jnp.float32
        ),
        lax.all_gather(pieces_now[2].astype(jnp.bfloat16), "dp", axis=1, tiled=True).astype(
            jnp.float32
        ),
        lax.all_gather(pieces_now[3].astype(jnp.bfloat16), "dp", axis=1, tiled=True).astype(
            jnp.float32
        ),
    )
    return (
        output,
        tokens_grad,
        qkv_weight_grad,
        qkv_bias_grad,
        out_grad,
        up_weight_grad,
        up_bias_grad,
        down_grad,
        res_bias_grad,
        gain_grad,
        shift_grad,
    )


SWAP_ROW = [(0, 1), (1, 0)]
SWAP_X = [(0, 2), (2, 0), (1, 3), (3, 1)]
SWAP_CORE = [(0, 1), (1, 0), (2, 3), (3, 2)]


def bf16(values):
    return values.astype(jnp.bfloat16)


def f32(values):
    return values.astype(jnp.float32)


def matmul(left, right, dims=((1,), (0,))):
    return lax.dot_general(left, right, (dims, ((), ())), preferred_element_type=jnp.float32)


def swap_row(values):
    return lax.ppermute(values, "row", SWAP_ROW)


def swap_x(values):
    return lax.ppermute(values, "dp", SWAP_X)


def swap_core(values):
    return lax.ppermute(values, "dp", SWAP_CORE)


def pick(index, first, second):
    return jnp.where(index == 0, first, second)


def pair(index, mine, theirs, axis):
    return pick(
        index,
        jnp.concatenate([mine, theirs], axis=axis),
        jnp.concatenate([theirs, mine], axis=axis),
    )


def after(value, *earlier):
    return lax.optimization_barrier((value,) + earlier)[0]


def rotary_tables(positions):
    lane = jnp.arange(2 * HD, dtype=jnp.int32) % HD
    half_rot = ROT // 2
    frequency = jnp.exp(
        -math.log(rotary_base) * 2.0 * (lane % half_rot).astype(jnp.float32) / ROT
    )
    angle = positions[:, None] * frequency[None, :]
    turned = (lane < ROT)[None, :]
    sines = jnp.sin(angle)
    return (
        jnp.where(turned, jnp.cos(angle), 1.0),
        jnp.where((lane < half_rot)[None, :], -sines, 0.0),
        jnp.where(turned & (lane >= half_rot)[None, :], sines, 0.0),
    )


def turn(values, cosines, sines_low, sines_high):
    width = values.shape[1]
    half_rot = ROT // 2
    return (
        values * cosines
        + pltpu.roll(values, width - half_rot, 1) * sines_low
        + pltpu.roll(values, half_rot, 1) * sines_high
    )


def mixed_kernel(
    normed_ref, weight_ref, bias_ref, cos_ref, low_ref, high_ref, query_ref, keyval_ref
):
    cosines, low, high = cos_ref[...], low_ref[...], high_ref[...]
    rows, half = query_ref.shape
    first = lax.broadcasted_iota(jnp.int32, (rows, 2 * HD), 1) < HD
    scale = HD ** (-0.5)
    mixed = matmul(normed_ref[...], weight_ref[...]) + bias_ref[...]
    for at in range(half // (2 * HD)):
        tiles = [mixed[:, (3 * at + part) * 2 * HD : (3 * at + part + 1) * 2 * HD] for part in range(3)]
        query = jnp.where(first, tiles[0], tiles[1])
        key = jnp.where(first, pltpu.roll(tiles[0], HD, 1), pltpu.roll(tiles[2], HD, 1))
        value = jnp.where(first, tiles[1], tiles[2])
        here = slice(at * 2 * HD, (at + 1) * 2 * HD)
        query_ref[:, here] = bf16(f32(bf16(turn(query, cosines, low, high))) * scale)
        keyval_ref[:, here] = bf16(turn(key, cosines, low, high))
        keyval_ref[:, half + at * 2 * HD : half + (at + 1) * 2 * HD] = bf16(value)


def join_kernel(row_ref, dq_ref, dkv_ref, sent_ref, cos_ref, low_ref, high_ref, out_ref):
    cosines, low, high = cos_ref[...], -low_ref[...], -high_ref[...]
    rows = dq_ref.shape[0]
    half = dq_ref.shape[1]
    first = lax.broadcasted_iota(jnp.int32, (rows, 2 * HD), 1) < HD
    owner = row_ref[0] == 0
    for at in range(half // (2 * HD)):
        here = slice(at * 2 * HD, (at + 1) * 2 * HD)
        there = slice(half + at * 2 * HD, half + (at + 1) * 2 * HD)
        query = turn(dq_ref[:, here], cosines, low, high)
        key = dkv_ref[:, here] + jnp.where(owner, f32(sent_ref[:, here]), 0.0)
        value = dkv_ref[:, there] + jnp.where(owner, f32(sent_ref[:, there]), 0.0)
        key = pltpu.roll(turn(key, cosines, low, high), HD, 1)
        tiles = (jnp.where(first, query, key), jnp.where(first, value, query), jnp.where(first, key, value))
        for part in range(3):
            out_ref[:, (3 * at + part) * 2 * HD : (3 * at + part + 1) * 2 * HD] = bf16(tiles[part])


def tree_kernel(
    parent_ref, row_ref, query_ref, keyval_ref, trunk_ref, grad_ref,
    out_ref, dq_ref, dkv_ref, dtrunk_ref,
    keys, values, dkeys, dvalues,
):
    tree = pl.program_id(0)
    row = row_ref[0]
    rows, half = query_ref.shape
    trunk_len = trunk_ref.shape[0]
    segs = rows // SEG
    trunk_segs = trunk_len // SEG
    seg_count = parent_ref.shape[1]
    first_row = row == 0
    keys[...] = jnp.where(first_row, keyval_ref[:, :half], trunk_ref[:, :half])
    values[...] = jnp.where(first_row, keyval_ref[:, half:], trunk_ref[:, half:])
    dkeys[...] = jnp.zeros_like(dkeys)
    dvalues[...] = jnp.zeros_like(dvalues)
    lane = lax.broadcasted_iota(jnp.int32, (1, half), 1)
    causal = lax.broadcasted_iota(jnp.int32, (SEG, SEG), 0) >= lax.broadcasted_iota(
        jnp.int32, (SEG, SEG), 1
    )
    across = ((1,), (1,))
    down = ((0,), (0,))
    for seg in range(segs):
        here = slice(seg * SEG, (seg + 1) * SEG)
        above = parent_ref[tree, row * segs + seg]
        linked = [above == at for at in range(trunk_segs)]
        for _ in range(seg_count - 2):
            above = jnp.where(above >= 0, parent_ref[tree, jnp.maximum(above, 0)], -1)
            linked = [was | (above == at) for at, was in enumerate(linked)]
        bias = [jnp.where(is_linked, 0.0, masked_fill) for is_linked in linked]
        query, grad = query_ref[here, :], grad_ref[here, :]
        own_key, own_value = keyval_ref[here, :half], keyval_ref[here, half:]
        attended = jnp.zeros((SEG, half), jnp.float32)
        dquery = jnp.zeros((SEG, half), jnp.float32)
        dkey = jnp.zeros((SEG, half), jnp.float32)
        dvalue = jnp.zeros((SEG, half), jnp.float32)
        for head in range(half // HD):
            mine = (lane >= head * HD) & (lane < (head + 1) * HD)
            head_query = jnp.where(mine, query, jnp.zeros_like(query))
            head_grad = jnp.where(mine, grad, jnp.zeros_like(grad))
            scores = [
                matmul(head_query, keys[at * SEG : (at + 1) * SEG, :], across) + bias[at]
                for at in range(trunk_segs)
            ] + [jnp.where(causal, matmul(head_query, own_key, across), masked_fill)]
            top = functools.reduce(jnp.maximum, [jnp.max(s, axis=1, keepdims=True) for s in scores])
            powers = [jnp.exp(s - top) for s in scores]
            total = functools.reduce(jnp.add, [jnp.sum(p, axis=1, keepdims=True) for p in powers])
            probs = [p / total for p in powers]
            low = [bf16(p) for p in probs]
            blocks = [values[at * SEG : (at + 1) * SEG, :] for at in range(trunk_segs)] + [own_value]
            prob_grads = [matmul(head_grad, v, across) for v in blocks]
            delta = functools.reduce(
                jnp.add, [jnp.sum(p * g, axis=1, keepdims=True) for p, g in zip(probs, prob_grads)]
            )
            score_grads = [bf16(p * (g - delta)) for p, g in zip(probs, prob_grads)]
            head_out = functools.reduce(jnp.add, [matmul(p, v) for p, v in zip(low, blocks)])
            attended = jnp.where(mine, head_out, attended)
            key_blocks = [keys[at * SEG : (at + 1) * SEG, :] for at in range(trunk_segs)] + [own_key]
            head_dq = functools.reduce(jnp.add, [matmul(s, u) for s, u in zip(score_grads, key_blocks)])
            dquery = jnp.where(mine, head_dq, dquery)
            dkey = dkey + matmul(score_grads[-1], head_query, down)
            dvalue = dvalue + matmul(low[-1], head_grad, down)
            for at in range(trunk_segs):
                spot = slice(at * SEG, (at + 1) * SEG)
                dkeys[spot, :] += matmul(score_grads[at], head_query, down)
                dvalues[spot, :] += matmul(low[at], head_grad, down)
        out_ref[here, :] = bf16(attended)
        dq_ref[here, :] = dquery * HD ** (-0.5)
        dkv_ref[here, :half] = dkey
        dkv_ref[here, half:] = dvalue
    dtrunk_ref[:, :half] = bf16(dkeys[...])
    dtrunk_ref[:, half:] = bf16(dvalues[...])

    @pl.when(first_row)
    def _():
        dkv_ref[:, :half] += dkeys[...]
        dkv_ref[:, half:] += dvalues[...]


def store_blocks(place_ref, sides, full_ref, own_refs, plain_refs):
    row, slab = place_ref[1], place_ref[2]
    for side, values in enumerate(sides):
        width = values[0].shape[1]
        for source, value in enumerate(values):
            within = source % 2
            here = row == source // 2

            def put(refs):
                if len(refs) == 1:
                    refs[0][side, :, within * width : (within + 1) * width] = value
                else:
                    refs[within][side] = value

            @pl.when(here)
            def _():
                full_ref[side, :, within * width : (within + 1) * width] = value
                put(own_refs)

            @pl.when(jnp.logical_not(here))
            def _():
                put(plain_refs)
                at = (2 + jnp.where(slab == 0, within, 1 - within)) * width
                full_ref[side, :, pl.ds(pl.multiple_of(at, width), width)] = value


def gather_kernel(place_ref, mine_ref, theirs_ref, full_ref, own_ref, plain_ref):
    sides = [[ref[at] for at in range(ref.shape[0])] for ref in (mine_ref, theirs_ref)]
    store_blocks(place_ref, sides, full_ref, [own_ref], [plain_ref])


def norm_kernel(place_ref, gain_ref, bias_ref, mine_ref, theirs_ref, full_ref, *outs):
    normal_ref, scale_ref = outs[4:]
    sides = []
    for side, ref in enumerate((mine_ref, theirs_ref)):
        values = [f32(ref[at]) for at in range(ref.shape[0])]
        features = len(values) * values[0].shape[1]
        mean = functools.reduce(jnp.add, [jnp.sum(v, axis=1, keepdims=True) for v in values]) / features
        centred = [v - mean for v in values]
        square = functools.reduce(jnp.add, [jnp.sum(v * v, axis=1, keepdims=True) for v in centred])
        inv_scale = lax.rsqrt(square / features + norm_epsilon)
        normals = [v * inv_scale for v in centred]
        if side == 0:
            scale_ref[...] = inv_scale
            for source, normal in enumerate(normals):

                @pl.when(place_ref[0] == source)
                def _():
                    normal_ref[...] = normal

        sides.append(
            [
                bf16(normal * gain_ref[source : source + 1, :] + bias_ref[source : source + 1, :])
                for source, normal in enumerate(normals)
            ]
        )
    store_blocks(place_ref, sides, full_ref, outs[:2], outs[2:4])


def pair_rows(rows, width):
    return pl.BlockSpec((2, rows, width), lambda at, *_: (0, at, 0))


def gathered(place, mine, theirs, norm=None):
    blocks, count, width = mine.shape
    rows = SEG if norm is None else SEG // 2
    full = blocks * width
    in_specs = [pl.BlockSpec((blocks, rows, width), lambda at, *_: (0, at, 0))] * 2
    parts = [full // 2] * 2 if norm is None else [width] * 4
    out_specs = [pair_rows(rows, size) for size in [full] + parts]
    out_shape = [
        jax.ShapeDtypeStruct((2, count, size), jnp.bfloat16) for size in [full] + parts
    ]
    operands = [mine, theirs]
    if norm is not None:
        gain = [values.reshape(blocks, width) for values in norm]
        operands = gain + operands
        in_specs = [pl.BlockSpec((blocks, width), lambda at, *_: (0, 0))] * 2 + in_specs
        out_specs = out_specs + [row_block(rows, width), row_block(rows, 1)]
        out_shape = out_shape + [
            jax.ShapeDtypeStruct((count, width), jnp.float32),
            jax.ShapeDtypeStruct((count, 1), jnp.float32),
        ]
    results = pl.pallas_call(
        gather_kernel if norm is None else norm_kernel,
        grid_spec=pltpu.PrefetchScalarGridSpec(
            num_scalar_prefetch=1, grid=(count // rows,), in_specs=in_specs, out_specs=out_specs
        ),
        out_shape=out_shape,
        cost_estimate=pl.CostEstimate(flops=1, bytes_accessed=1, transcendentals=0),
        name="join_blocks" if norm is None else "norm_blocks",
    )(place, *operands)
    last = len(parts) + 1
    return [values.reshape(2 * count, -1) for values in results[:last]] + list(results[last:])


def stack_kernel(place_ref, terms_ref, arrived_ref, out_ref):
    row, slab = place_ref[1], place_ref[2]
    width = out_ref.shape[2]
    for spot in range(4):
        here = slice(spot * width, (spot + 1) * width)
        value = bf16(f32(terms_ref[:, here]) + f32(arrived_ref[:, here]))
        if spot < 2:
            out_ref[2 * row + spot] = value
        else:
            out_ref[2 * (1 - row) + jnp.where(slab == 0, spot - 2, 3 - spot)] = value


def stacked(place, terms, arrived, blocks):
    count, full = arrived.shape
    rows = SEG
    width = full // blocks
    return pl.pallas_call(
        stack_kernel,
        grid_spec=pltpu.PrefetchScalarGridSpec(
            num_scalar_prefetch=1,
            grid=(count // rows,),
            in_specs=[row_block(rows, full), row_block(rows, full)],
            out_specs=pl.BlockSpec((blocks, rows, width), lambda at, *_: (0, at, 0)),
        ),
        out_shape=jax.ShapeDtypeStruct((blocks, count, width), jnp.bfloat16),
        cost_estimate=pl.CostEstimate(flops=1, bytes_accessed=1, transcendentals=0),
        name="stack_blocks",
    )(place, terms, arrived)


def cast_rows_kernel(place_ref, master_ref, own_ref, send_ref):
    value = bf16(master_ref[...])
    own_ref[...] = value
    half = pl.num_programs(0) // 2

    @pl.when(pl.program_id(0) // half == place_ref[2])
    def _():
        send_ref[...] = value


def cast_cols_kernel(place_ref, master_ref, own_ref, send_ref):
    value = bf16(master_ref[...])
    own_ref[...] = value
    half = value.shape[1] // 2
    send_ref[...] = jnp.where(place_ref[2] == 0, value[:, :half], value[:, half:])


def cast_weight(place, master, axis):
    height, width = master.shape
    rows = min(2 * SEG, master.shape[0] // 4)
    if axis == 0:
        width = width // 2
        steps = height // rows
        half = steps // 2
        specs = [
            pl.BlockSpec((rows, width), lambda at, place_ref: (at, place_ref[3])),
            pl.BlockSpec((rows, width), lambda at, place_ref: (at, 0)),
            pl.BlockSpec(
                (rows, width), lambda at, place_ref: (jnp.clip(at - half * place_ref[2], 0, half - 1), 0)
            ),
        ]
        send = (height // 2, width)
        whole = (2 * height, width)
    else:
        height = height // 2
        steps = height // rows
        specs = [
            pl.BlockSpec((rows, width), lambda at, place_ref: (at + steps * place_ref[3], 0)),
            pl.BlockSpec((rows, width), lambda at, place_ref: (at, 0)),
            pl.BlockSpec((rows, width // 2), lambda at, place_ref: (at, 0)),
        ]
        send = (height, width // 2)
        whole = (height, 2 * width)
    return pl.pallas_call(
        cast_rows_kernel if axis == 0 else cast_cols_kernel,
        grid_spec=pltpu.PrefetchScalarGridSpec(
            num_scalar_prefetch=1, grid=(steps,), in_specs=specs[:1], out_specs=specs[1:]
        ),
        out_shape=[
            jax.ShapeDtypeStruct(whole, jnp.bfloat16),
            jax.ShapeDtypeStruct(send, jnp.bfloat16),
        ],
        cost_estimate=pl.CostEstimate(flops=1, bytes_accessed=1, transcendentals=0),
        name="cast_weight",
    )(place, master)


def settle_store(axis, place_ref, mine, theirs, out_ref):
    if axis == 0:
        out_ref[place_ref[3]] = mine
        out_ref[1 - place_ref[3]] = theirs
    else:
        width = mine.shape[1]
        first = place_ref[3] == 0
        out_ref[:, :width] = jnp.where(first, mine, theirs)
        out_ref[:, width:] = jnp.where(first, theirs, mine)


def settle_kernel(axis, place_ref, mine_ref, theirs_ref, *refs):
    settle_store(axis, place_ref, f32(mine_ref[...]), f32(theirs_ref[...]), refs[-1])


def settle_both_kernel(axis, place_ref, *refs):
    for at in range(2):

        @pl.when(pl.program_id(0) == at)
        def _():
            settle_store(axis, place_ref, f32(refs[2 * at][...]), f32(refs[2 * at + 1][...]), refs[-1])


def settle_both(place, first, last, shape, axis):
    rows, width = first[0].shape
    if axis == 0:
        shape = (2, shape[0] // 2, width)
        out_spec = pl.BlockSpec((2, rows, width), lambda at, *_: (0, at, 0))
    else:
        out_spec = pl.BlockSpec((rows, 2 * width), lambda at, *_: (at, 0))
    return pl.pallas_call(
        functools.partial(settle_both_kernel, axis),
        grid_spec=pltpu.PrefetchScalarGridSpec(
            num_scalar_prefetch=1,
            grid=(2,),
            in_specs=[pl.BlockSpec((rows, width), lambda *_: (0, 0))] * 4,
            out_specs=out_spec,
        ),
        out_shape=jax.ShapeDtypeStruct(shape, jnp.float32),
        cost_estimate=pl.CostEstimate(flops=1, bytes_accessed=1, transcendentals=0),
        name="settle_both",
    )(place, *first, *last)


def settle(place, mine, theirs, shape, axis, offset, dest=None):
    rows, width = mine.shape
    at = offset // rows
    whole = pl.BlockSpec((rows, width), lambda *_: (0, 0))
    if axis == 0:
        shape = (2, shape[0] // 2, width)
        out_spec = pl.BlockSpec((2, rows, width), lambda *_: (0, at, 0))
    else:
        out_spec = pl.BlockSpec((rows, 2 * width), lambda *_: (at, 0))
    in_specs = [whole, whole]
    operands = [place, mine, theirs]
    aliases = {}
    if dest is not None:
        in_specs.append(pl.BlockSpec(memory_space=pl.ANY))
        operands.append(dest)
        aliases = {3: 0}
    return pl.pallas_call(
        functools.partial(settle_kernel, axis),
        grid_spec=pltpu.PrefetchScalarGridSpec(
            num_scalar_prefetch=1, grid=(1,), in_specs=in_specs, out_specs=out_spec
        ),
        out_shape=jax.ShapeDtypeStruct(shape, jnp.float32),
        input_output_aliases=aliases,
        cost_estimate=pl.CostEstimate(flops=1, bytes_accessed=1, transcendentals=0),
        name="settle",
    )(*operands)


def row_block(rows, width):
    return pl.BlockSpec((rows, width), lambda at, *_: (at, 0))


def mixed_heads(normed, weight, bias, tables):
    count, depth = normed.shape
    width = weight.shape[1]
    rows = SEG
    return pl.pallas_call(
        mixed_kernel,
        grid=(count // rows,),
        in_specs=[
            row_block(rows, depth),
            pl.BlockSpec((depth, width), lambda at: (0, 0)),
            pl.BlockSpec((1, width), lambda at: (0, 0)),
        ]
        + [row_block(rows, 2 * HD)] * 3,
        out_specs=[row_block(rows, width // 3), row_block(rows, 2 * width // 3)],
        out_shape=[
            jax.ShapeDtypeStruct((count, width // 3), jnp.bfloat16),
            jax.ShapeDtypeStruct((count, 2 * width // 3), jnp.bfloat16),
        ],
        cost_estimate=pl.CostEstimate(flops=1, bytes_accessed=1, transcendentals=0),
        name="mixed_heads",
    )(normed, weight, bias.reshape(1, width), *tables)


def join_heads(row, dq, dkv, sent, tables):
    count, half = dq.shape
    rows = 2 * SEG
    return pl.pallas_call(
        join_kernel,
        grid_spec=pltpu.PrefetchScalarGridSpec(
            num_scalar_prefetch=1,
            grid=(count // rows,),
            in_specs=[row_block(rows, half), row_block(rows, 2 * half), row_block(rows, 2 * half)]
            + [row_block(rows, 2 * HD)] * 3,
            out_specs=row_block(rows, 3 * half),
        ),
        out_shape=jax.ShapeDtypeStruct((count, 3 * half), jnp.bfloat16),
        cost_estimate=pl.CostEstimate(flops=1, bytes_accessed=1, transcendentals=0),
        name="join_heads",
    )(row, dq, dkv, sent, *tables)


def tree_attention(parents, row, query, keyval, trunk, grad):
    trees = parents.shape[0]
    count, half = query.shape
    rows = count // trees
    keys = trunk.shape[0] // trees
    pairs = count * (keys + SEG) * (half // HD)
    return pl.pallas_call(
        tree_kernel,
        grid_spec=pltpu.PrefetchScalarGridSpec(
            num_scalar_prefetch=2,
            grid=(trees,),
            in_specs=[
                row_block(rows, half),
                row_block(rows, 2 * half),
                row_block(keys, 2 * half),
                row_block(rows, half),
            ],
            out_specs=[
                row_block(rows, half),
                row_block(rows, half),
                row_block(rows, 2 * half),
                row_block(keys, 2 * half),
            ],
            scratch_shapes=[pltpu.VMEM((keys, half), jnp.bfloat16)] * 2
            + [pltpu.VMEM((keys, half), jnp.float32)] * 2,
        ),
        out_shape=[
            jax.ShapeDtypeStruct((count, half), jnp.bfloat16),
            jax.ShapeDtypeStruct((count, half), jnp.float32),
            jax.ShapeDtypeStruct((count, 2 * half), jnp.float32),
            jax.ShapeDtypeStruct((trees * keys, 2 * half), jnp.bfloat16),
        ],
        cost_estimate=pl.CostEstimate(flops=1, bytes_accessed=1, transcendentals=0),
        name="tree_attention",
    )(parents, row, query, keyval, trunk, grad)


def paired_device(
    tokens,
    parent,
    depth,
    w_qkv,
    b_qkv,
    w_out,
    w_up,
    b_up,
    w_down,
    b_res,
    ln_gain,
    ln_bias,
    cotangent,
):
    count, width = tokens.shape
    row = lax.axis_index("row")
    col = lax.axis_index("col")
    core = lax.axis_index("dp") % 2
    slab = lax.axis_index("dp") // 2
    cols = lax.axis_size("col")
    half = 2 * width
    heads_width = w_out.shape[0] // 2
    hidden = w_up.shape[1] // 2
    place = jnp.stack([col, row, slab, core]).astype(jnp.int32)
    row_table = jnp.reshape(row, (1,)).astype(jnp.int32)
    down_dims = ((0,), (0,))
    across = ((1,), (1,))

    def part(values, at, size, axis):
        return lax.dynamic_slice_in_dim(values, at * size, size, axis)

    def exchange(stack):
        return lax.all_to_all(stack, "col", 0, 0, tiled=True)

    done = ()

    def step(run, *inputs):
        nonlocal done
        inputs, _ = lax.optimization_barrier((inputs, done))
        result = run(*inputs)
        done = result
        return result

    def wait(value):
        return step(lambda arrived: arrived, value)

    tokens_near = lax.all_gather(tokens, "col", axis=0)
    grad_stack = jnp.broadcast_to(cotangent[None], (cols,) + cotangent.shape)

    def ready(master, axis):
        whole, send = step(lambda weight: cast_weight(place, weight, axis), master)
        return whole, swap_row(send)

    def fill(whole, part_in, axis, last):
        at = whole.shape[axis] // 2 + (part_in.shape[axis] if last else 0)
        return step(lambda a, b: lax.dynamic_update_slice_in_dim(a, b, at, axis), whole, part_in)

    tables = jnp.concatenate([parent, depth], axis=0)
    tables = jnp.stack([tables, swap_core(tables)])
    parents = tables[:, 0]
    segs = count // SEG
    token = jnp.arange(count, dtype=jnp.int32)
    levels = jnp.zeros((2, count), jnp.float32)
    for seg in range(segs):
        level = lax.dynamic_slice_in_dim(tables[:, 1], row * segs + seg, 1, 1).astype(jnp.float32)
        levels = jnp.where((token // SEG == seg)[None, :], level, levels)
    positions = (levels * SEG + (token % SEG).astype(jnp.float32)[None, :]).reshape(2 * count)
    rotary = rotary_tables(positions)

    qkv_whole, qkv_row = ready(w_qkv, 0)
    up_whole, up_row = ready(w_up, 0)
    qkv_row = wait(qkv_row)
    qkv_x = swap_x(qkv_row)
    out_whole, out_row = ready(w_out, 1)
    down_whole, down_row = ready(w_down, 1)
    rotary = step(lambda *tables: tables, *rotary)
    qkv_whole = fill(qkv_whole, qkv_row, 0, False)
    up_row = wait(up_row)
    up_x = swap_x(up_row)
    qkv_x = wait(qkv_x)
    tokens_near = wait(tokens_near)
    tokens_far = swap_core(tokens_near)
    grad_near = exchange(after(grad_stack, tokens_near))
    up_whole = fill(up_whole, up_row, 0, False)
    normed, own_a, own_b, plain_a, plain_b, normal, inv_scale = step(
        lambda mine, theirs: gathered(place, mine, theirs, (ln_gain, ln_bias)), tokens_near, tokens_far
    )
    qkv_full = fill(qkv_whole, qkv_x, 0, True)
    query, keyval = step(
        lambda left, right: mixed_heads(left, right, part(b_qkv, core, 3 * heads_width, 0), rotary),
        normed, qkv_full,
    )
    trunk = lax.ppermute(keyval, "row", [(0, 1)])
    root = math.sqrt(2.0 / math.pi)

    def feed(left, right):
        hidden_up = matmul(left, right) + part(b_up, core, hidden, 0)
        squared = hidden_up * hidden_up
        bend = jnp.tanh(root * (hidden_up + 0.044715 * squared * hidden_up))
        return bf16(0.5 * hidden_up * (1.0 + bend)), bf16(
            0.5 * (1.0 + bend)
            + 0.5 * hidden_up * (1.0 - bend * bend) * root * (1.0 + 3.0 * 0.044715 * squared)
        )

    out_row = wait(out_row)
    out_x = swap_x(out_row)
    up_full = fill(up_whole, up_x, 0, True)
    down_row = wait(down_row)
    down_x = swap_x(down_row)
    activated, slope = step(feed, normed, up_full)
    out_whole = fill(out_whole, out_row, 1, False)
    down_whole = fill(down_whole, down_row, 1, False)
    out_full = fill(out_whole, out_x, 1, True)
    trunk = wait(trunk)
    grad_near = wait(grad_near)
    grad_far = swap_core(grad_near)
    grad, grad_own, grad_plain = step(lambda mine, theirs: gathered(place, mine, theirs), grad_near, grad_far)

    def cut(values, at):
        size = values.shape[1] // 2
        return values[:, at * size : (at + 1) * size]

    def leaving(left, right):
        return step(lambda a, b: bf16(matmul(a, b, down_dims)), left, right)

    def staying(left, right, sent):
        return step(lambda a, b, c: bf16(matmul(a, b, down_dims) + f32(c)), left, right, sent)

    def crossed(both, arrived):
        mine = step(lambda a, b: bf16(f32(a) + f32(b)), both, arrived)
        return mine, swap_core(mine)

    def settled(pieces, shape, axis, offset, dest):
        operands = pieces if dest is None else pieces + (dest,)
        return step(
            lambda mine, theirs, *rest: settle(place, mine, theirs, shape, axis, offset, *rest), *operands
        )

    down_sent_a = swap_row(leaving(cut(activated, 0), grad_plain))
    down_sent_b = swap_row(leaving(cut(activated, 1), grad_plain))
    out_heads = step(lambda a, b: bf16(matmul(a, b, across)), grad, out_full)
    attended, query_grad, own_grad, trunk_grad = step(
        lambda *operands: tree_attention(parents, row_table, *operands), query, keyval, trunk, out_heads
    )
    trunk_sent = lax.ppermute(trunk_grad, "row", [(1, 0)])
    down_both_a = staying(cut(activated, 0), grad_own, down_sent_a)
    down_cross_a = swap_x(down_both_a)
    down_full = fill(down_whole, down_x, 1, True)
    branch_terms = step(
        lambda a, b, c, d: bf16(matmul(a, b) + matmul(c, d)), attended, out_full, activated, down_full
    )
    branch_near = swap_core(branch_terms[count:])
    up_grad = step(lambda a, b, c: bf16(matmul(a, b, across) * f32(c)), grad, down_full, slope)
    up_sent_a = swap_row(leaving(plain_a, up_grad))
    down_both_b = staying(cut(activated, 1), grad_own, down_sent_b)
    down_cross_b = swap_x(down_both_b)
    up_sent_b = swap_row(leaving(plain_b, up_grad))
    down_a = crossed(down_both_a, down_cross_a)
    branch = lax.psum_scatter(
        step(lambda a, b: stacked(place, a, b, cols), branch_terms, branch_near), "col", tiled=False
    )
    mixed_grad = step(
        lambda *operands: join_heads(row_table, *operands, rotary), query_grad, own_grad, trunk_sent
    )
    qkv_sent_a = swap_row(leaving(plain_a, mixed_grad))
    down_b = crossed(down_both_b, down_cross_b)
    qkv_sent_b = swap_row(leaving(plain_b, mixed_grad))
    norm_terms = step(
        lambda a, b, c, d: bf16(matmul(a, b, across) + matmul(c, d, across)),
        mixed_grad, qkv_full, up_grad, up_full,
    )
    up_both_a = staying(own_a, up_grad, up_sent_a)
    up_cross_a = swap_x(up_both_a)
    norm_near = swap_core(step(lambda terms: terms[count:], norm_terms))
    output = step(lambda parts, block: bf16(f32(block) + f32(parts) + b_res), branch, tokens)
    norm_parts = exchange(step(lambda a, b: stacked(place, a, b, cols), norm_terms, norm_near))
    down_grad = step(lambda first, last: settle_both(place, first, last, w_down.shape, 0), down_a, down_b)
    up_a = crossed(up_both_a, up_cross_a)
    up_both_b = staying(own_b, up_grad, up_sent_b)
    up_cross_b = swap_x(up_both_b)
    qkv_both_a = staying(own_a, mixed_grad, qkv_sent_a)
    qkv_cross_a = swap_x(qkv_both_a)
    out_sent = swap_row(leaving(attended, grad_plain))
    up_b = crossed(up_both_b, up_cross_b)
    qkv_both_b = staying(own_b, mixed_grad, qkv_sent_b)
    qkv_cross_b = swap_x(qkv_both_b)
    gain_here = part(ln_gain, col, width, 0)

    def norm_sums(parts):
        total = jnp.sum(f32(parts), axis=0)
        scaled = total * gain_here
        return (
            total,
            jnp.stack([jnp.sum(scaled, axis=1), jnp.sum(scaled * normal, axis=1)]),
            jnp.sum(total * normal, axis=0),
            jnp.sum(total, axis=0),
        )

    norm_grad, sums, gain_sum, shift_sum = step(norm_sums, norm_parts)
    up_weight_grad = step(lambda first, last: settle_both(place, first, last, w_up.shape, 1), up_a, up_b)

    def line_step(values, bit):
        return lax.ppermute(values, "col", [(at, at ^ bit) for at in range(cols)])

    small = jnp.concatenate(
        [
            jnp.sum(f32(up_grad), axis=0),
            jnp.sum(f32(mixed_grad), axis=0),
            jnp.sum(f32(cotangent), axis=0),
            gain_sum,
            shift_sum,
        ]
    ).reshape(-1, 128)
    shared_at = (hidden + 3 * heads_width) // 128
    res_at = width // 128
    sums_next = line_step(sums, 1)
    small_other = swap_core(small)
    qkv_a = crossed(qkv_both_a, qkv_cross_a)
    sums, shared = step(
        lambda sums, arrived, small, other: (sums + arrived, (small + other)[shared_at:]),
        sums, sums_next, small, small_other,
    )
    sums_next = line_step(sums, 2)
    ends = shared[res_at:][None]
    ends_next = line_step(ends, 1)
    out_both = staying(attended, grad_own, out_sent)
    out_cross = swap_x(out_both)
    ends = step(lambda ends, arrived: pair(col % 2, ends, arrived, 0), ends, ends_next)
    ends_next = line_step(ends, 2)
    qkv_weight_grad = settled(qkv_a, w_qkv.shape, 1, 0, None)
    sums = (sums + sums_next) / (cols * width)
    tokens_grad = step(
        lambda sums, total: inv_scale
        * (total * gain_here - sums[0][:, None] - normal * sums[1][:, None])
        + f32(cotangent),
        sums, norm_grad,
    )

    def gather_small(small, other, shared, ends, arrived):
        return jnp.concatenate(
            [
                pair(core, small[: hidden // 128], other[: hidden // 128], 0),
                pair(core, small[hidden // 128 : shared_at], other[hidden // 128 : shared_at], 0),
                shared[:res_at],
                pair(col // 2, ends, arrived, 0).reshape(-1, 128),
            ]
        )

    small = step(gather_small, small, small_other, shared, ends, ends_next)
    small_next = swap_row(small)
    qkv_b = crossed(qkv_both_b, qkv_cross_b)
    small = step(jnp.add, small, small_next)
    small_next = swap_x(small)
    qkv_weight_grad = settled(qkv_b, w_qkv.shape, 1, qkv_both_a.shape[0], qkv_weight_grad)
    out_mine = crossed(out_both, out_cross)
    out_grad = settled(out_mine, w_out.shape, 0, 0, None)
    small = step(jnp.add, small, small_next)

    bounds = [0, 2 * hidden // 128, (2 * hidden + 6 * heads_width) // 128]
    bounds.append(bounds[-1] + res_at)
    up_bias_grad = small[: bounds[1]].reshape(-1)
    qkv_bias_grad = small[bounds[1] : bounds[2]].reshape(-1)
    res_bias_grad = small[bounds[2] : bounds[3]].reshape(-1)
    ends = small[bounds[3] :].reshape(cols, 2, width)
    gain_grad = ends[:, 0].reshape(-1)
    shift_grad = ends[:, 1].reshape(-1)
    return (
        output,
        tokens_grad,
        qkv_weight_grad,
        qkv_bias_grad,
        out_grad.reshape(w_out.shape),
        up_weight_grad,
        up_bias_grad,
        down_grad.reshape(w_down.shape),
        res_bias_grad,
        gain_grad,
        shift_grad,
    )


def solution(mesh):
    sizes = (mesh.shape["dp"], mesh.shape["row"], mesh.shape["col"])
    per_device = paired_device if sizes == (4, 2, 4) else general_device
    return jax.shard_map(
        per_device,
        mesh=mesh,
        in_specs=(
            P(("dp", "row"), "col"),
            P("dp", None),
            P("dp", None),
            P("row", "col"),
            P("col"),
            P("col", "row"),
            P("row", "col"),
            P("col"),
            P("col", "row"),
            P("col"),
            P(),
            P(),
            P(("dp", "row"), "col"),
        ),
        out_specs=(
            P(("dp", "row"), "col"),
            P(("dp", "row"), "col"),
            P("row", "col"),
            P("col"),
            P("col", "row"),
            P("row", "col"),
            P("col"),
            P("col", "row"),
            P("col"),
            P(),
            P(),
        ),
        check_vma=False,
    )
```
